32 devices in a mesh: grp: 2 (over y), inner: 8 (over z, x), outer: 2 (over core).
Axes of the slice: x: 2, y: 2, z: 4, core: 2. Of those that a mesh axis runs over, the one named last changes fastest.
Arguments:
- tokens: bfloat16 [4, 6144, 4096], P(('grp', 'outer'), 'inner'), parts along dimension 0, may hold values from -6 to 6
- w_in: bfloat16 [4096, 1536], P('inner'), may hold values from -0.09375 to 0.09375
- w_dt: bfloat16 [4096, 16], P('inner'), may hold values from -0.09375 to 0.09375
- conv_w: float32 [4, 1536], replicated, may hold values from -0.6 to 0.6
- conv_b: float32 [1536], replicated, may hold values from -0.5 to 0.5
- dt_bias: float32 [16], replicated, may hold values from -2 to 0
- a_log: float32 [16], replicated
- d_skip: float32 [16], replicated, may hold values from 0.5 to 8
- norm_gain: float32 [1024], replicated, may hold values from 0.1 to 1.9
Outputs:
- mixed: bfloat16 [4, 6144, 1024], P(('grp', 'outer'), 'inner'), parts along dimension 0
- entry_states: float32 [4, 8, 16, 64, 256], P(('grp', 'outer'), 'inner'), parts along dimension 0
The draws below stay inside these ranges and needn't reach their ends.
There are 2 independent parts, one for each index of `grp`. The reference program is written for one: setup_inputs(seed, part) draws one part's arguments, and reference() takes and returns one part's arrays. A program takes and returns all parts, laid end to end along the dimension named above; an argument that names none is the same for every part. Nothing has to cross between parts.
All inputs are finite; a program needn't handle non-finite values.
Results may differ from the reference program's by a relative error of at most 0.004.
Values may be sent and summed in bfloat16 or wider, within the bound.
A program may use at most 192 MiB of HBM per device.

```python
import math
from functools import partial
import jax
import jax.numpy as jnp
from jax import lax

D = 4096
HEADS = 16
P_SIZE = 64
N = 256
CONV = 4
TOK_DEV = 768
HP = 1024
XBC = 1536
BLOCKS = 2
SPANS = 8
BLOCK_LEN = 6144


def draw_a_log(key, part):
    chain_len = BLOCKS * BLOCK_LEN
    slowest = jnp.log(0.25 / chain_len)
    fastest = jnp.log(1.0 / 30.0)
    first_key = jax.random.fold_in(key, 0)
    spread = jax.random.uniform(first_key, (HEADS,), jnp.float32)
    return jnp.log(2.5) + slowest + spread * (fastest - slowest)


def levels(own_key, shape, cuts, smallest, high):
    loudness, own = 1.0, jax.random.fold_in(own_key, 6)
    for axis_at, parts in cuts:
        draws = jnp.exp(jax.random.uniform(jax.random.fold_in(own, axis_at), (parts,), jnp.float32, smallest / len(cuts), high / len(cuts)))
        loudness = loudness * jnp.repeat(draws, shape[axis_at] // parts).reshape([-1 if axis == axis_at else 1 for axis in range(len(shape))])
    return loudness


def bell_draw(stream_key, dims, scale, reach, pieces=(), held_as=jnp.bfloat16):
    values = jax.random.normal(stream_key, dims, jnp.float32) * scale
    if len(pieces) > 0:
        values = levels(stream_key, dims, pieces, -0.22, 0.18) * values
    return jnp.clip(values, min=-reach, max=reach).astype(held_as)


def setup_inputs(seed: int = 0, part: int = 0) -> dict:
    arg_keys = jax.random.split(jax.random.key(seed), 10)
    own_keys = jax.random.split(jax.random.fold_in(arg_keys[9], part), 10)
    tokens = bell_draw(own_keys[0], (BLOCKS, BLOCK_LEN, D), 1.0, 6.0, ((0, 2), (1, 8)))
    w_in = bell_draw(arg_keys[1], (D, XBC), D ** -0.5, 0.09375, ((0, 8),))
    w_dt = bell_draw(arg_keys[2], (D, HEADS), D ** -0.5, 0.09375, ((0, 8),))
    conv_w = jnp.clip(jax.random.uniform(arg_keys[3], (CONV, XBC), jnp.float32, -0.6, 0.6), -0.6, 0.6)
    conv_b = jnp.clip(jax.random.uniform(arg_keys[4], (XBC,), jnp.float32, -0.5, 0.5), -0.5, 0.5)
    dt_bias = jnp.clip(jax.random.uniform(arg_keys[5], (HEADS,), jnp.float32, -2.0, 0.0), -2.0, 0.0)
    a_log = draw_a_log(jax.random.fold_in(arg_keys[9], 71), part)
    d_skip = jnp.clip(jnp.exp(jax.random.uniform(arg_keys[7], (HEADS,), jnp.float32, math.log(0.5), math.log(8.0))), 0.5, 8.0)
    norm_gain = jnp.clip(1.0 + 0.18 * jax.random.normal(arg_keys[8], (HP,), jnp.float32), 0.1, 1.9)
    return dict(tokens=tokens, w_in=w_in, w_dt=w_dt, conv_w=conv_w, conv_b=conv_b, dt_bias=dt_bias, a_log=a_log, d_skip=d_skip, norm_gain=norm_gain)


EPSILON = 1e-05

def rounded(values):
    return lax.optimization_barrier(values.astype(jnp.bfloat16)).astype(jnp.float32)

def prepare_span(projected, dt_raw, tail_rows, conv_w, conv_b, dt_bias, a_log):
    length = projected.shape[0]
    padded = jnp.concatenate([tail_rows, projected], axis=0).astype(jnp.float32)
    conv_sum = conv_b[None, :] + conv_w[0][None, :] * padded[0:length]
    for offset in range(1, CONV):
        conv_sum = conv_sum + conv_w[offset][None, :] * padded[offset:offset + length]
    conv_out = jax.nn.silu(conv_sum).astype(jnp.bfloat16)
    inputs = conv_out[:, :HEADS * P_SIZE].reshape(length, HEADS, P_SIZE).transpose(1, 0, 2)
    b_rows = conv_out[:, HEADS * P_SIZE:HEADS * P_SIZE + N]
    c_rows = conv_out[:, HEADS * P_SIZE + N:]
    step_size = jax.nn.softplus(dt_raw.astype(jnp.float32) + dt_bias[None, :]).T
    log_decay = jnp.cumsum(step_size * (-jnp.exp(a_log))[:, None], axis=1)
    return (inputs, b_rows, c_rows, step_size, log_decay)

def span_state(inputs, b_rows, step_size, log_decay):
    final_log = log_decay[:, -1:]
    weighted = rounded((jnp.exp(final_log - log_decay) * step_size)[:, :, None] * inputs.astype(jnp.float32))
    contrib = jnp.einsum('hqp,qn->hpn', weighted, b_rows.astype(jnp.float32))
    return (jnp.exp(log_decay[:, -1]), contrib)

def head_rows(c_rows, scores, operands):
    log_h, input_h, step_h, entry_h, skip_h, gain_h = operands
    length = log_h.shape[0]
    row_ids = lax.broadcasted_iota(jnp.int32, (length, length), 0)
    col_ids = lax.broadcasted_iota(jnp.int32, (length, length), 1)
    causal = col_ids <= row_ids
    log_gap = jnp.where(causal, log_h[:, None] - log_h[None, :], 0.0)
    mixing = jnp.where(causal, scores * jnp.exp(log_gap), 0.0).astype(jnp.bfloat16)
    driven = (step_h[:, None] * input_h.astype(jnp.float32)).astype(jnp.bfloat16)
    output = jnp.dot(mixing, driven, preferred_element_type=jnp.float32)
    carried = jnp.dot(c_rows, entry_h.astype(jnp.bfloat16).T, preferred_element_type=jnp.float32)
    output = output + jnp.exp(log_h)[:, None] * carried + skip_h * input_h.astype(jnp.float32)
    inv_rms = lax.rsqrt(lax.optimization_barrier(jnp.mean(output * output, axis=1, keepdims=True)) + EPSILON)
    return output * inv_rms * gain_h[None, :]

def span_output(inputs, b_rows, c_rows, step_size, log_decay, entry_state, d_skip, norm_gain):
    scores = jnp.dot(c_rows, b_rows.T, preferred_element_type=jnp.float32)
    head_gains = norm_gain.reshape(HEADS, P_SIZE)
    per_head = lax.map(partial(head_rows, c_rows, scores), (log_decay, inputs, step_size, entry_state, d_skip, head_gains))
    return per_head.transpose(1, 0, 2).reshape(inputs.shape[1], HEADS * P_SIZE).astype(jnp.bfloat16)

def reference(tokens, w_in, w_dt, conv_w, conv_b, dt_bias, a_log, d_skip, norm_gain):
    ranges = tokens.reshape(BLOCKS * SPANS, TOK_DEV, D)
    start_state = jnp.zeros((HEADS, P_SIZE, N), jnp.float32)
    start_tail = jnp.zeros((CONV - 1, HEADS * P_SIZE + 2 * N), jnp.bfloat16)

    def advance(carried_in, token_block):
        current, tail_rows = carried_in
        projected = jnp.dot(token_block, w_in, preferred_element_type=jnp.float32).astype(jnp.bfloat16)
        dt_raw = jnp.dot(token_block, w_dt, preferred_element_type=jnp.float32).astype(jnp.bfloat16)
        inputs, b_rows, c_rows, step_size, log_decay = prepare_span(projected, dt_raw, tail_rows, conv_w, conv_b, dt_bias, a_log)
        decay_total, contrib = span_state(inputs, b_rows, step_size, log_decay)
        output = span_output(inputs, b_rows, c_rows, step_size, log_decay, current, d_skip, norm_gain)
        next_state = decay_total[:, None, None] * current + contrib
        return ((next_state, projected[TOK_DEV - CONV + 1:]), (output, current))
    last_carry, stacked = lax.scan(advance, (start_state, start_tail), ranges)
    outputs, entries = stacked
    return (outputs.reshape(BLOCKS, BLOCK_LEN, HEADS * P_SIZE), entries.reshape(BLOCKS, SPANS, HEADS, P_SIZE, N))
```

```python
from functools import partial

import jax
import jax.numpy as jnp
from jax import lax
from jax.experimental import pallas as pl
from jax.experimental.pallas import tpu as pltpu
from jax.sharding import PartitionSpec as P

HEADS = 16
P_SIZE = 64
N = 256
CONV = 4
HP = HEADS * P_SIZE
CHUNK = 256
EPSILON = 1e-05
MESH = pl.DeviceIdType.MESH
F32 = jnp.float32
BF16 = jnp.bfloat16
LAST = (((1,), (1,)), ((), ()))
FIRST = (((0,), (0,)), ((), ()))


def expand(values, spread):
    high = values.astype(BF16)
    low = (values - high.astype(F32)).astype(BF16)
    return jnp.dot(high, spread, preferred_element_type=F32) + jnp.dot(
        low, spread, preferred_element_type=F32
    )


def scan_kernel(
    n_in, ndev,
    proj, tail, dt_raw, conv_w, conv_b, dt_bias, a_log, d_skip, gain,
    mixed, entry_out,
    gain_s, bias_row, skip_row, pad, conv, log_s, log_t, step_s, y, states,
    send1, recv1, send2, recv2, dec_send, dec_recv,
    ss1, rs1, ss2, rs2, ssd, rsd,
):
    length = proj.shape[0]
    chunks = length // CHUNK
    rows = HP // ndev
    me = lax.axis_index("outer") * n_in + lax.axis_index("inner")

    def place(g):
        return {"inner": lax.rem(g, n_in), "outer": lax.div(g, n_in)}

    barrier = pltpu.get_barrier_semaphore()

    def greet(k, carry):
        pl.semaphore_signal(
            barrier, inc=1, device_id=place(lax.rem(me + k, ndev)), device_id_type=MESH
        )
        return carry

    lax.fori_loop(1, ndev, greet, 0)

    head_id = lax.broadcasted_iota(jnp.int32, (HEADS, HP), 0)
    col_head = lax.broadcasted_iota(jnp.int32, (HEADS, HP), 1) // P_SIZE
    spread = (head_id == col_head).astype(F32).astype(BF16)

    bias_row[...] = conv_b[...].reshape(1, conv_b.shape[0])
    gain_s[...] = gain[...].reshape(1, HP)
    skip = d_skip[...].reshape(1, HEADS)
    skip_high = skip.astype(BF16).astype(F32)
    skip_row[...] = expand(skip - skip_high, spread) + jnp.dot(
        skip_high.astype(BF16), spread, preferred_element_type=F32
    )
    step_size = jax.nn.softplus(dt_raw[...].astype(F32) + dt_bias[...].reshape(1, HEADS))
    scaled = step_size * (-jnp.exp(a_log[...].reshape(1, HEADS)))
    row_id = lax.broadcasted_iota(jnp.int32, (CHUNK, CHUNK), 0)
    col_id = lax.broadcasted_iota(jnp.int32, (CHUNK, CHUNK), 1)
    causal = col_id <= row_id
    lower = causal.astype(F32)
    step_s[...] = step_size
    before = jnp.zeros((1, HEADS), F32)
    for c in range(chunks):
        part = jnp.dot(
            lower,
            scaled[c * CHUNK : (c + 1) * CHUNK],
            preferred_element_type=F32,
            precision=lax.Precision.HIGHEST,
        ) + before
        log_s[c * CHUNK : (c + 1) * CHUNK] = part
        before = part[CHUNK - 1 : CHUNK]
    log_t[...] = jnp.transpose(log_s[...])
    dec_send[...] = jnp.broadcast_to(jnp.exp(log_t[:, length - 1 : length]), (HEADS, 128))

    pad[0:8] = tail[...].astype(F32)[8:16]
    pad[8:] = proj[...].astype(F32)
    wide = 256
    blocks = proj.shape[1] // wide

    def conv_block(t, carry):
        i, j = lax.div(t, blocks), lax.rem(t, blocks)
        cols = pl.ds(pl.multiple_of(j * wide, wide), wide)
        window = pad[pl.ds(pl.multiple_of(i * 128, 128), 136), cols]
        total = bias_row[:, cols]
        for k in range(CONV):
            total = total + conv_w[k : k + 1, cols] * window[5 + k : 5 + k + 128]
        conv[pl.ds(pl.multiple_of(i * 128, 128), 128), cols] = (
            total * jax.nn.sigmoid(total)
        ).astype(BF16)
        return carry

    row_blocks = length // 128

    def conv_column(j):
        def one(i, carry):
            return conv_block(i * blocks + j, carry)

        lax.fori_loop(0, row_blocks, one, 0)

    conv_column(HP // wide)

    def weighted_sum(stop):
        final = log_s[stop - 1 : stop]
        factor = jnp.exp(final - log_s[0:stop]) * step_s[0:stop]
        weighted = (expand(factor, spread) * conv[0:stop, 0:HP].astype(F32)).astype(BF16)
        return lax.dot_general(
            weighted, conv[0:stop, HP : HP + N], FIRST, preferred_element_type=F32
        )

    dec_recv[me] = dec_send[...]

    def decay_copy(g):
        return pltpu.make_async_remote_copy(
            src_ref=dec_send, dst_ref=dec_recv.at[me], send_sem=ssd.at[g],
            recv_sem=rsd.at[me], device_id=place(g), device_id_type=MESH,
        )

    def first_copy(g):
        return pltpu.make_async_remote_copy(
            src_ref=send1.at[g], dst_ref=recv1.at[me], send_sem=ss1.at[g],
            recv_sem=rs1.at[me], device_id=place(g), device_id_type=MESH,
        )

    def second_copy(g):
        return pltpu.make_async_remote_copy(
            src_ref=send2.at[g], dst_ref=recv2.at[me], send_sem=ss2.at[g],
            recv_sem=rs2.at[me], device_id=place(g), device_id_type=MESH,
        )

    pl.semaphore_wait(barrier, ndev - 1)

    def send_decay(k, carry):
        decay_copy(lax.rem(me + k, ndev)).start()
        return carry

    lax.fori_loop(1, ndev, send_decay, 0)

    groups = HP // wide
    owners = ndev // groups
    own_group = lax.div(me, owners)
    factor = jnp.exp(log_s[length - 1 : length] - log_s[...]) * step_s[...]

    def spread_of(j):
        head = lax.broadcasted_iota(jnp.int32, (HEADS, wide), 0)
        col = lax.broadcasted_iota(jnp.int32, (HEADS, wide), 1) // P_SIZE
        return (head == col + j * (wide // P_SIZE)).astype(F32).astype(BF16)

    def first_group(i, carry):
        j = lax.rem(own_group + 1 + i, groups)
        conv_column(j)
        cols = pl.ds(pl.multiple_of(j * wide, wide), wide)
        weighted = (expand(factor, spread_of(j)) * conv[:, cols].astype(F32)).astype(BF16)
        part = lax.dot_general(
            weighted, conv[:, HP : HP + N], FIRST, preferred_element_type=F32
        )
        send1[pl.ds(j * owners, owners)] = part.reshape(owners, rows, N).astype(BF16)

        def send_one(k, inner):
            g = j * owners + k

            @pl.when(g != me)
            def _():
                first_copy(g).start()

            return inner

        return lax.fori_loop(0, owners, send_one, carry)

    lax.fori_loop(0, groups, first_group, 0)
    recv1[me] = send1[me]
    conv_column(HP // wide + 1)

    states[0] = jnp.zeros((HP, N), BF16)
    for c in range(1, chunks):
        states[c] = weighted_sum(c * CHUNK).astype(BF16)

    def local_chunk(c, carry):
        start = pl.multiple_of(c * CHUNK, CHUNK)
        here = pl.ds(start, CHUNK)
        log_c = log_s[here]
        reached = log_s[pl.ds(pl.multiple_of(jnp.maximum(start - 8, 0), 8), 8)][7:8]
        reached = jnp.where(c > 0, reached, 0.0)
        c_rows = conv[here, HP + N :]
        b_rows = conv[here, HP : HP + N]
        scores = lax.dot_general(c_rows, b_rows, LAST, preferred_element_type=F32)
        scores = jnp.where(causal, scores, 0.0)
        x_rows = conv[here, 0:HP].astype(F32)
        driven = (expand(step_s[here], spread) * x_rows).astype(BF16)
        inter = lax.dot_general(c_rows, states[c], LAST, preferred_element_type=F32)
        y[here] = expand(jnp.exp(log_c - reached), spread) * inter + skip_row[...] * x_rows
        for h in range(0, HEADS, 2):
            pieces = []
            for k in (h, h + 1):
                gap = jnp.minimum(log_c[:, k : k + 1] - log_t[k : k + 1, here], 0.0)
                mixing = (scores * jnp.exp(gap)).astype(BF16)
                pieces.append(
                    jnp.dot(
                        mixing,
                        driven[:, k * P_SIZE : (k + 1) * P_SIZE],
                        preferred_element_type=F32,
                    )
                )
            both = slice(h * P_SIZE, (h + 2) * P_SIZE)
            y[here, both] = y[here, both] + jnp.concatenate(pieces, axis=1)
        return carry

    lax.fori_loop(0, chunks, local_chunk, 0)

    own_head = lax.div(me * rows, P_SIZE)

    def wait_from(copy_of, r):
        copy_of(r).wait_recv()

    def arrive(buffer, sems, r):
        pltpu.make_async_remote_copy(
            src_ref=buffer.at[r], dst_ref=buffer.at[r], send_sem=sems.at[r],
            recv_sem=sems.at[r], device_id=place(r), device_id_type=MESH,
        ).wait_recv()

    def advance(r, state):
        send2[r] = state.astype(BF16)

        @pl.when(r != me)
        def _():
            arrive(dec_recv, rsd, r)
            arrive(recv1, rs1, r)

        decay = dec_recv[r, pl.ds(own_head, 1), :]
        decay = jnp.concatenate([decay, decay], axis=1)
        return decay * state + recv1[r].astype(F32)

    lax.fori_loop(0, ndev, advance, jnp.zeros((rows, N), F32))

    def send_second(k, carry):
        second_copy(lax.rem(me + k, ndev)).start()
        return carry

    lax.fori_loop(1, ndev, send_second, 0)
    recv2[me] = send2[me]

    reach = jnp.exp(log_s[...])

    def last_group(i, carry):
        j = lax.rem(own_group + groups - 1 - i, groups)

        def wait_one(k, inner):
            g = j * owners + k

            @pl.when(g != me)
            def _():
                arrive(recv2, rs2, g)

            return inner

        lax.fori_loop(0, owners, wait_one, 0)
        cols = pl.ds(pl.multiple_of(j * wide, wide), wide)
        entry = recv2[pl.ds(j * owners, owners)].astype(F32).reshape(wide, N)
        entry_out[cols] = entry
        carried = lax.dot_general(
            conv[:, HP + N :], entry.astype(BF16), LAST, preferred_element_type=F32
        )
        spread_j = spread_of(j)
        out = y[:, cols] + expand(reach, spread_j) * carried
        square = out * out
        high = square.astype(BF16)
        low = (square - high.astype(F32)).astype(BF16)
        sums = lax.dot_general(high, spread_j, LAST, preferred_element_type=F32)
        sums = sums + lax.dot_general(low, spread_j, LAST, preferred_element_type=F32)
        inv_rms = lax.rsqrt(sums * (1.0 / P_SIZE) + EPSILON)
        mixed[:, cols] = (out * expand(inv_rms, spread_j) * gain_s[:, cols]).astype(BF16)
        return carry

    lax.fori_loop(0, groups, last_group, 0)

    def finish(k, carry):
        g = lax.rem(me + k, ndev)
        decay_copy(g).wait_send()
        first_copy(g).wait_send()
        second_copy(g).wait_send()
        return carry

    lax.fori_loop(1, ndev, finish, 0)


def run_scan(projected, tail, dt_raw, conv_w, conv_b, dt_bias, a_log, d_skip, norm_gain):
    n_in, n_out = lax.axis_size("inner"), lax.axis_size("outer")
    ndev = n_in * n_out
    length, xbc = projected.shape
    rows = HP // ndev
    dma = pltpu.SemaphoreType.DMA((ndev,))
    vmem = pl.BlockSpec(memory_space=pltpu.VMEM)
    return pl.pallas_call(
        partial(scan_kernel, n_in, ndev),
        out_shape=(
            jax.ShapeDtypeStruct((length, HP), BF16),
            jax.ShapeDtypeStruct((HP, N), F32),
        ),
        in_specs=[vmem] * 9,
        out_specs=(vmem, vmem),
        scratch_shapes=[
            pltpu.VMEM((1, HP), F32),
            pltpu.VMEM((1, xbc), F32),
            pltpu.VMEM((1, HP), F32),
            pltpu.VMEM((length + 8, xbc), F32),
            pltpu.VMEM((length, xbc), BF16),
            pltpu.VMEM((length, HEADS), F32),
            pltpu.VMEM((HEADS, length), F32),
            pltpu.VMEM((length, HEADS), F32),
            pltpu.VMEM((length, HP), F32),
            pltpu.VMEM((length // CHUNK, HP, N), BF16),
            pltpu.VMEM((ndev, rows, N), BF16),
            pltpu.VMEM((ndev, rows, N), BF16),
            pltpu.VMEM((ndev, rows, N), BF16),
            pltpu.VMEM((ndev, rows, N), BF16),
            pltpu.VMEM((HEADS, 128), F32),
            pltpu.VMEM((ndev, HEADS, 128), F32),
            dma, dma, dma, dma, dma, dma,
        ],
        compiler_params=pltpu.CompilerParams(
            collective_id=1, has_side_effects=True, vmem_limit_bytes=60 * 2**20
        ),
        name="scan",
    )(
        projected, tail, dt_raw, conv_w, conv_b, dt_bias, a_log, d_skip, norm_gain,
    )


def project_kernel(
    n, n_out,
    tokens, w_in, w_dt,
    proj, tail, dt_out,
    tok, held, total, held_dt,
    ring_s, ring_r, side_s, side_r, core_s, core_r, dt_s, dt_r, misc, tail_s, tail_r,
):
    length, depth = tokens.shape
    local, xbc = w_in.shape
    half = xbc // 2
    quarter = half // 2
    lanes = 128
    streams = quarter // lanes
    wide = 256
    tiles = half // wide
    third = (local * 5 // 16) // 16 * 16
    ring_rows = local - third
    tail_rows = tok.shape[0] - length
    block = held_dt.shape[2]
    ndev = n * n_out
    me = lax.axis_index("inner")
    core = lax.axis_index("outer")
    grp = lax.axis_index("grp")
    rank = core * n + me
    odd = lax.rem(me, 2)
    pos = jnp.where(odd == 0, lax.div(me, 2), n - lax.div(me + 1, 2))

    def index_at(q):
        q = lax.rem(q + 2 * n, n)
        return jnp.where(q < n // 2, 2 * q, 2 * n - 1 - 2 * q)

    def place(g):
        return {"inner": lax.rem(g, n), "outer": lax.div(g, n)}

    barrier = pltpu.get_barrier_semaphore()

    def greet(k, carry):
        pl.semaphore_signal(
            barrier, inc=1, device_id=place(lax.rem(rank + k, ndev)), device_id_type=MESH
        )
        return carry

    lax.fori_loop(1, ndev, greet, 0)
    pl.semaphore_signal(barrier, inc=1, device_id={"grp": 1 - grp}, device_id_type=MESH)

    def own_rows(owner):
        return pl.ds(pl.multiple_of(owner * local, 16), local)

    load_tok = pltpu.make_async_copy(tokens, tok.at[pl.ds(0, length)], misc.at[0])
    load_w = [
        pltpu.make_async_copy(
            w_in.at[:, pl.ds(d * half, half)], held.at[d, own_rows(me)], misc.at[1 + d]
        )
        for d in range(2)
    ]
    for copy in load_w:
        copy.start()
    load_tok.start()
    held_dt[me] = w_dt[...]

    @pl.when(rank == 0)
    def _():
        tok[length:] = jnp.zeros((tail_rows, depth), BF16)

    def ring_copy(d, t, s):
        owner = index_at(pos - (s - 1)) if d == 0 else index_at(pos + (s - 1))
        target = index_at(pos + 1) if d == 0 else index_at(pos - 1)
        rows = pl.ds(pl.multiple_of(owner * local + grp * third, 16), ring_rows)
        cols = pl.ds(pl.multiple_of(core * quarter + t * lanes, lanes), lanes)
        part = held.at[d, rows, cols]
        return pltpu.make_async_remote_copy(
            src_ref=part, dst_ref=part, send_sem=ring_s.at[d, t, s],
            recv_sem=ring_r.at[d, t, s], device_id={"inner": target}, device_id_type=MESH,
        )

    def owner_of(d, s):
        return index_at(pos - s) if d == 0 else index_at(pos + s)

    def chunk_cols(which, t):
        return pl.ds(pl.multiple_of(which * quarter + t * lanes, lanes), lanes)

    def side_rows(d, s, which):
        start = owner_of(d, s) * local + which * ring_rows
        return pl.ds(pl.multiple_of(start, 16), third)

    def side_between(d, t, s, which):
        part = held.at[d, side_rows(d, s, which), chunk_cols(core, t)]
        return pltpu.make_async_remote_copy(
            src_ref=part, dst_ref=part, send_sem=side_s.at[d, t, s],
            recv_sem=side_r.at[d, t, s], device_id={"grp": 1 - grp}, device_id_type=MESH,
        )

    def core_between(d, t, s, which):
        part = held.at[d, own_rows(owner_of(d, s)), chunk_cols(which, t)]
        return pltpu.make_async_remote_copy(
            src_ref=part, dst_ref=part, send_sem=core_s.at[d, t, s],
            recv_sem=core_r.at[d, t, s], device_id={"outer": 1 - core}, device_id_type=MESH,
        )

    def side_copy(d, t, s):
        return side_between(d, t, s, grp)

    def core_copy(d, t, s):
        return core_between(d, t, s, core)

    def ring_arrival(d, t, s):
        start = owner_of(d, s) * local + grp * third
        rows = pl.ds(pl.multiple_of(start, 16), ring_rows)
        part = held.at[d, rows, chunk_cols(core, t)]
        pltpu.make_async_remote_copy(
            src_ref=part, dst_ref=part, send_sem=ring_s.at[d, t, s],
            recv_sem=ring_r.at[d, t, s], device_id={"inner": index_at(pos + 1)},
            device_id_type=MESH,
        ).wait_recv()

    def side_arrival(d, t, s):
        side_between(d, t, s, 1 - grp).wait_recv()

    def core_arrival(d, t, s):
        core_between(d, t, s, 1 - core).wait_recv()

    def dt_copy(k):
        peer = lax.rem(me + k, n)
        return pltpu.make_async_remote_copy(
            src_ref=w_dt, dst_ref=held_dt.at[me], send_sem=dt_s.at[k],
            recv_sem=dt_r.at[me], device_id={"inner": peer}, device_id_type=MESH,
        )

    def dt_arrival(k):
        peer = lax.rem(me + k, n)
        pltpu.make_async_remote_copy(
            src_ref=w_dt, dst_ref=held_dt.at[peer], send_sem=dt_s.at[k],
            recv_sem=dt_r.at[peer], device_id={"inner": peer}, device_id_type=MESH,
        ).wait_recv()

    def tail_copy():
        return pltpu.make_async_remote_copy(
            src_ref=tokens.at[pl.ds(length - tail_rows, tail_rows)],
            dst_ref=tok.at[pl.ds(length, tail_rows)], send_sem=tail_s,
            recv_sem=tail_r, device_id=place(lax.rem(rank + 1, ndev)), device_id_type=MESH,
        )

    pl.semaphore_wait(barrier, ndev)

    @pl.when(rank < ndev - 1)
    def _():
        tail_copy().start()

    for d in range(2):
        load_w[d].wait()
        for t in range(streams):
            ring_copy(d, t, 1).start()

    def send_dt(k, carry):
        dt_copy(k).start()
        return carry

    lax.fori_loop(1, n, send_dt, 0)
    load_tok.wait()

    @pl.when(rank > 0)
    def _():
        tail_copy().wait_recv()

    incremental = local % 128 == 0

    def multiply_tile(d, lhs_cols, rhs_rows, first, j):
        cols = pl.ds(pl.multiple_of(j * wide, wide), wide)
        product = jnp.dot(
            tok[:, lhs_cols], held[d, rhs_rows, cols], preferred_element_type=F32
        )
        at = d * tiles + j
        if first:
            total[at] = product
        else:
            total[at] = total[at] + product

    def multiply(d, lhs_cols, rhs_rows, first):
        def tile(j, carry):
            multiply_tile(d, lhs_cols, rhs_rows, first, j)
            return carry

        lax.fori_loop(0, tiles, tile, 0)

    def project_dt():
        def arrived(k, carry):
            dt_arrival(k)
            return carry

        lax.fori_loop(1, n, arrived, 0)
        together = block // local

        def add(j, sums):
            cols = pl.ds(pl.multiple_of(j * block, block), block)
            piece = held_dt[j * together]
            for m in range(1, together):
                piece = piece + held_dt[j * together + m]
            return sums + lax.dot_general(
                tok[0:length, cols], piece, LAST, preferred_element_type=F32
            )

        sums = lax.fori_loop(0, depth // block, add, jnp.zeros((length, HEADS), F32))
        dt_out[...] = sums.astype(BF16)

    def step(s, carry):
        @pl.when(s >= 3)
        def _():
            for t in range(streams):
                for d in range(2):
                    core_arrival(d, t, s - 2)

        def part(t, inner):
            @pl.when(s < n)
            def _():
                for d in range(2):
                    ring_arrival(d, t, s)

                    @pl.when(s < n - 1)
                    def _():
                        ring_copy(d, t, s + 1).start()

                    side_copy(d, t, s).start()

            @pl.when((s >= 2) & (s <= n))
            def _():
                for d in range(2):
                    side_arrival(d, t, s - 1)
                    core_copy(d, t, s - 1).start()

            if incremental:
                for d in range(2):
                    owner = owner_of(d, s - 2)
                    at = pl.ds(pl.multiple_of(owner * local, 128), local)

                    @pl.when(s == 2)
                    def _():
                        multiply_tile(d, at, at, True, t)

                    @pl.when(s > 2)
                    def _():
                        multiply_tile(d, at, at, False, t)

            return inner

        lax.fori_loop(0, streams, part, 0)

        @pl.when(s == 1)
        def _():
            project_dt()

        return carry

    lax.fori_loop(1, n + 2, step, 0)
    if not incremental:
        for d in range(2):
            multiply(d, slice(0, 512), slice(0, 512), True)

            def more(j, carry):
                at = pl.ds(pl.multiple_of(j * 512, 512), 512)
                multiply(d, at, at, False)
                return carry

            lax.fori_loop(1, depth // 512, more, 0)

    for j in range(2 * tiles):
        cols = slice(j * wide, (j + 1) * wide)
        proj[:, cols] = total[j, 0:length].astype(BF16)
        tail[:, cols] = total[j, length:].astype(BF16)

    def drain(s, carry):
        for d in range(2):
            for t in range(streams):
                ring_copy(d, t, s).wait_send()
                side_copy(d, t, s).wait_send()
                core_copy(d, t, s).wait_send()
        dt_copy(s).wait_send()
        return carry

    lax.fori_loop(1, n, drain, 0)

    @pl.when(rank < ndev - 1)
    def _():
        tail_copy().wait_send()


def run_project(tokens, w_in, w_dt):
    n, n_out = lax.axis_size("inner"), lax.axis_size("outer")
    length, depth = tokens.shape
    local, xbc = w_in.shape
    block = max(local, 128)
    tail_rows = 16
    dt_block = w_dt.T
    if block != local:
        start = lax.rem(lax.axis_index("inner") * local, block)
        dt_block = lax.dynamic_update_slice(
            jnp.zeros((HEADS, block), BF16), dt_block, (jnp.int32(0), start)
        )
    streams = xbc // 4 // 128
    dma = pltpu.SemaphoreType.DMA
    vmem = pl.BlockSpec(memory_space=pltpu.VMEM)
    whole = pl.BlockSpec(memory_space=pl.ANY)
    return pl.pallas_call(
        partial(project_kernel, n, n_out),
        out_shape=(
            jax.ShapeDtypeStruct((length, xbc), BF16),
            jax.ShapeDtypeStruct((tail_rows, xbc), BF16),
            jax.ShapeDtypeStruct((length, HEADS), BF16),
        ),
        in_specs=[whole, whole, vmem],
        out_specs=(vmem, vmem, vmem),
        scratch_shapes=[
            pltpu.VMEM((length + tail_rows, depth), BF16),
            pltpu.VMEM((2, depth, xbc // 2), BF16),
            pltpu.VMEM((xbc // 256, length + tail_rows, 256), F32),
            pltpu.VMEM((n, HEADS, block), BF16),
            dma((2, streams, n)), dma((2, streams, n)),
            dma((2, streams, n)), dma((2, streams, n)),
            dma((2, streams, n)), dma((2, streams, n)),
            dma((n,)), dma((n,)), dma((3,)), dma(()), dma(()),
        ],
        compiler_params=pltpu.CompilerParams(
            collective_id=2, has_side_effects=True, vmem_limit_bytes=60 * 2**20
        ),
        name="project",
    )(tokens, w_in, dt_block)


def fused_kernel(
    n, n_out,
    tokens, w_in, w_dt, conv_w, conv_b, dt_bias, a_log, d_skip, gain,
    mixed, entry_out,
    tok, held, total, held_dt, dt_acc, half_w, bias_row, gain_s, skip_row,
    conv, log_s, log_t, step_s, fac_s, reach_s, edge, scores, mix_s, local_s, y,
    send1, recv1, prefix, mid_send, mid_recv, start, send2, recv2, dec_send, dec_recv,
    ring_s, ring_r, side_s, side_r, core_s, core_r, dt_s, dt_r, misc, tail_s, tail_r,
    ss1, rs1, ssm, rsm, ss2, rs2, ssd, rsd,
):
    length, depth = tokens.shape
    local, xbc = w_in.shape
    tail_rows = tok.shape[0] - length
    wide, lanes = 256, 128
    blocks = xbc // wide
    groups = HP // wide
    early = groups
    late = blocks - early
    steps = n // 2
    half = local // 2
    third = (half * 5 // 16) // 16 * 16
    ring_rows = half - third
    chunks = length // CHUNK
    ndev = n * n_out
    team = ndev // 2
    own_heads = HEADS // team
    rows = own_heads * P_SIZE
    owners = team // groups
    me = lax.axis_index("inner")
    core = lax.axis_index("outer")
    grp = lax.axis_index("grp")
    rank = core * n + me
    odd = lax.rem(me, 2)
    pos = jnp.where(odd == 0, lax.div(me, 2), n - lax.div(me + 1, 2))
    upper = lax.div(me, n // 2)
    base = upper * (n // 2)
    own = (me - base) * n_out + core
    slot = core * (n // 2) + me - base

    def index_at(q):
        q = lax.rem(q + 2 * n, n)
        return jnp.where(q < n // 2, 2 * q, 2 * n - 1 - 2 * q)

    def place(g):
        return {"inner": lax.rem(g, n), "outer": lax.div(g, n)}

    barrier = pltpu.get_barrier_semaphore()

    def greet(k, carry):
        pl.semaphore_signal(
            barrier, inc=1, device_id=place(lax.rem(rank + k, ndev)), device_id_type=MESH
        )
        return carry

    lax.fori_loop(1, ndev, greet, 0)
    pl.semaphore_signal(barrier, inc=1, device_id={"grp": 1 - grp}, device_id_type=MESH)

    own_rows = pl.ds(pl.multiple_of(me * local, local), local)

    def natural(q):
        return groups if q == 0 else (blocks - 1 if q == blocks - 1 else q - 1)

    load_tok = pltpu.make_async_copy(
        tokens, tok.at[pl.ds(tail_rows, length)], misc.at[blocks]
    )
    load_w = [
        pltpu.make_async_copy(
            w_in.at[:, pl.ds(natural(q) * wide, wide)],
            held.at[q, own_rows], misc.at[q],
        )
        for q in range(blocks)
    ]
    for copy in load_w:
        copy.start()
    load_tok.start()
    held_dt[me] = w_dt[...]

    @pl.when(rank == 0)
    def _():
        tok[0:tail_rows] = jnp.zeros((tail_rows, depth), BF16)

    def owner_of(d, s):
        return index_at(pos - s) if d == 0 else index_at(pos + s)

    def columns(d, whole):
        return slice(0, wide) if whole else slice(d * lanes, (d + 1) * lanes)

    def ring_between(d, q, s, source, whole):
        start = owner_of(d, source) * local + core * half + grp * third
        part = held.at[q, pl.ds(pl.multiple_of(start, 16), ring_rows), columns(d, whole)]
        target = index_at(pos + 1) if d == 0 else index_at(pos - 1)
        return pltpu.make_async_remote_copy(
            src_ref=part, dst_ref=part, send_sem=ring_s.at[d, q, s],
            recv_sem=ring_r.at[d, q, s], device_id={"inner": target}, device_id_type=MESH,
        )

    def ring_copy(d, q, s, whole):
        return ring_between(d, q, s, s - 1, whole)

    def side_between(d, q, s, which, whole):
        start = owner_of(d, s) * local + core * half + which * ring_rows
        part = held.at[q, pl.ds(pl.multiple_of(start, 16), third), columns(d, whole)]
        return pltpu.make_async_remote_copy(
            src_ref=part, dst_ref=part, send_sem=side_s.at[d, q, s],
            recv_sem=side_r.at[d, q, s], device_id={"grp": 1 - grp}, device_id_type=MESH,
        )

    def core_between(d, q, s, which, whole):
        start = owner_of(d, s) * local + which * half
        part = held.at[q, pl.ds(pl.multiple_of(start, 16), half), columns(d, whole)]
        return pltpu.make_async_remote_copy(
            src_ref=part, dst_ref=part, send_sem=core_s.at[d, q, s],
            recv_sem=core_r.at[d, q, s], device_id={"outer": 1 - core}, device_id_type=MESH,
        )

    def dt_copy(k):
        peer = lax.rem(me + k, n)
        return pltpu.make_async_remote_copy(
            src_ref=w_dt, dst_ref=held_dt.at[me], send_sem=dt_s.at[k],
            recv_sem=dt_r.at[me], device_id={"inner": peer}, device_id_type=MESH,
        )

    def dt_arrival(k):
        peer = lax.rem(me + k, n)
        pltpu.make_async_remote_copy(
            src_ref=w_dt, dst_ref=held_dt.at[peer], send_sem=dt_s.at[k],
            recv_sem=dt_r.at[peer], device_id={"inner": peer}, device_id_type=MESH,
        ).wait_recv()

    def tail_copy():
        return pltpu.make_async_remote_copy(
            src_ref=tokens.at[pl.ds(length - tail_rows, tail_rows)],
            dst_ref=tok.at[pl.ds(0, tail_rows)], send_sem=tail_s,
            recv_sem=tail_r, device_id=place(lax.rem(rank + 1, ndev)), device_id_type=MESH,
        )

    def decay_copy(g):
        return pltpu.make_async_remote_copy(
            src_ref=dec_send, dst_ref=dec_recv.at[rank], send_sem=ssd.at[g],
            recv_sem=rsd.at[rank], device_id=place(g), device_id_type=MESH,
        )

    def member(o):
        return {"inner": base + lax.div(o, n_out), "outer": lax.rem(o, n_out)}

    def member_at(k):
        return {"inner": base + lax.rem(k, n // 2), "outer": lax.div(k, n // 2)}

    def first_copy(o):
        return pltpu.make_async_remote_copy(
            src_ref=send1.at[o], dst_ref=recv1.at[slot], send_sem=ss1.at[o],
            recv_sem=rs1.at[slot], device_id=member(o), device_id_type=MESH,
        )

    def mid_copy(k):
        return pltpu.make_async_remote_copy(
            src_ref=mid_send.at[k], dst_ref=mid_recv.at[k], send_sem=ssm.at[k],
            recv_sem=rsm.at[k], device_id={"inner": me + n // 2 - upper * n},
            device_id_type=MESH,
        )

    def second_copy(k):
        return pltpu.make_async_remote_copy(
            src_ref=send2.at[k], dst_ref=recv2.at[own], send_sem=ss2.at[k],
            recv_sem=rs2.at[own], device_id=member_at(k), device_id_type=MESH,
        )

    def arrive(buffer, sems, r, peer):
        pltpu.make_async_remote_copy(
            src_ref=buffer.at[r], dst_ref=buffer.at[r], send_sem=sems.at[r],
            recv_sem=sems.at[r], device_id=peer, device_id_type=MESH,
        ).wait_recv()

    half_w[...] = conv_w[...] * 0.5
    bias_row[...] = conv_b[...].reshape(1, xbc) * 0.5
    gain_s[...] = gain[...].reshape(1, HP)

    def spread_of(j, count):
        head = lax.rem(lax.broadcasted_iota(jnp.int32, (count, wide), 0), HEADS)
        col = lax.broadcasted_iota(jnp.int32, (count, wide), 1) // P_SIZE
        return (head == col + j * (wide // P_SIZE)).astype(F32).astype(BF16)

    def split(values):
        high = values.astype(BF16).astype(F32)
        lane = lax.broadcasted_iota(jnp.int32, values.shape, 1)
        return jnp.where(lane < HEADS, high, values - high).astype(BF16)

    skip = d_skip[...].reshape(1, HEADS)
    skip_high = skip.astype(BF16).astype(F32)
    for j in range(groups):
        skip_row[:, j * wide : (j + 1) * wide] = expand(
            skip - skip_high, spread_of(j, HEADS)
        ) + jnp.dot(skip_high.astype(BF16), spread_of(j, HEADS), preferred_element_type=F32)

    pl.semaphore_wait(barrier, ndev)

    @pl.when(rank < ndev - 1)
    def _():
        tail_copy().start()

    def send_dt(k, carry):
        dt_copy(k).start()
        return carry

    lax.fori_loop(1, n, send_dt, 0)
    for q in range(early):
        load_w[q].wait()
        for d in range(2):
            ring_copy(d, q, 1, True).start()
    for q in range(early, blocks):
        load_w[q].wait()
    load_tok.wait()

    def multiply(q, shards, first):
        product = None if first else total[q]
        for owner in shards:
            at = pl.ds(pl.multiple_of(owner * local, local), local)
            term = jnp.dot(tok[:, at], held[q, at, :], preferred_element_type=F32)
            product = term if product is None else product + term
        total[q] = product

    first_part = early * steps
    all_parts = blocks * steps
    side_lag, core_lag = 3, 4

    def item(i):
        behind = i - first_part
        is_early = i < first_part
        q = jnp.where(is_early, lax.rem(i, early), early + lax.rem(jnp.maximum(behind, 0), late))
        s = jnp.where(is_early, lax.div(i, early), lax.div(jnp.maximum(behind, 0), late)) + 1
        return q, s

    def exchange(i):
        q, s = item(i)

        @pl.when((i < all_parts) & (s < steps))
        def _():
            for d in range(2):
                ring_between(d, q, s, s, True).wait_recv()

                @pl.when(s < steps - 1)
                def _():
                    ring_copy(d, q, s + 1, True).start()

                @pl.when(s == steps - 1)
                def _():
                    ring_copy(d, q, s + 1, False).start()

                side_between(d, q, s, grp, True).start()

        @pl.when((i < all_parts) & (s == steps))
        def _():
            for d in range(2):
                ring_between(d, q, s, s, False).wait_recv()
                side_between(d, q, s, grp, False).start()

        for k in range(late):
            @pl.when(i == first_part - early - 1 + 2 * k)
            def _():
                for d in range(2):
                    ring_copy(d, early + k, 1, True).start()

        q, s = item(jnp.maximum(i - side_lag, 0))
        for whole in (True, False):
            @pl.when((i >= side_lag) & (i < all_parts + side_lag) & ((s < steps) == whole))
            def _():
                for d in range(2):
                    side_between(d, q, s, 1 - grp, whole).wait_recv()
                    core_between(d, q, s, core, whole).start()

    def accumulate(i):
        q, s = item(jnp.maximum(i - core_lag, 0))

        @pl.when((i >= core_lag) & (s < steps))
        def _():
            for d in range(2):
                core_between(d, q, s, 1 - core, True).wait_recv()
            multiply(q, [owner_of(0, s), owner_of(1, s)], False)

        @pl.when((i >= core_lag) & (s == steps))
        def _():
            for d in range(2):
                core_between(d, q, s, 1 - core, False).wait_recv()
            multiply(q, [owner_of(0, s)], False)

        @pl.when((i < early) | (i == 6) | (i == 10))
        def _():
            multiply(jnp.where(i < early, i, early + lax.div(jnp.maximum(i - 6, 0), 4)), [me], True)

    def add_dt(k):
        @pl.when(k != me)
        def _():
            dt_arrival(lax.rem(k - me + n, n))

        cols = pl.ds(pl.multiple_of(k * local, local), local)
        part = lax.dot_general(
            tok[tail_rows:, cols], held_dt[k], LAST, preferred_element_type=F32
        )

        @pl.when(k == 0)
        def _():
            dt_acc[...] = part

        @pl.when(k > 0)
        def _():
            dt_acc[...] = dt_acc[...] + part

    def early_part(i, carry):
        exchange(i)

        @pl.when((i == 0) & (rank > 0))
        def _():
            tail_copy().wait_recv()

        accumulate(i)

        @pl.when(i < n)
        def _():
            add_dt(i)

        return carry

    lax.fori_loop(0, 10, early_part, 0)

    row_id = lax.broadcasted_iota(jnp.int32, (CHUNK, CHUNK), 0)
    col_id = lax.broadcasted_iota(jnp.int32, (CHUNK, CHUNK), 1)
    causal = col_id <= row_id
    dt_raw = dt_acc[...].astype(BF16).astype(F32)
    step_one = jax.nn.softplus(dt_raw + dt_bias[...].reshape(1, HEADS))
    scaled = step_one * (-jnp.exp(a_log[...].reshape(1, HEADS)))
    scaled = jnp.concatenate([scaled, scaled], axis=1)
    step_size = jnp.concatenate([step_one, step_one], axis=1)
    before = jnp.zeros((1, 2 * HEADS), F32)
    lower = causal.astype(F32)
    for c in range(chunks):
        here = slice(c * CHUNK, (c + 1) * CHUNK)
        part = jnp.dot(
            lower, scaled[here], preferred_element_type=F32,
            precision=lax.Precision.HIGHEST,
        ) + before
        log_s[here] = part
        reach_s[here] = split(jnp.exp(part - before))
        before = part[CHUNK - 1 : CHUNK]
        fac_s[here] = split(jnp.exp(before - part) * step_size[here])
    flat = jnp.transpose(log_s[...])[0:HEADS]
    log_t[...] = jnp.transpose(log_s[...] - jnp.log(step_size))[0:HEADS]
    ends = [flat[:, (c + 1) * CHUNK - 1 : (c + 1) * CHUNK] for c in range(chunks)]
    dec_send[...] = jnp.broadcast_to(jnp.exp(ends[chunks - 1]), (HEADS, 128))
    dec_recv[rank] = dec_send[...]

    def tall_of(column):
        column = jnp.broadcast_to(column, (HEADS, 128)).reshape(HEADS, 1, 128)
        return jnp.broadcast_to(column, (HEADS, P_SIZE, 128)).reshape(HP, 128)

    for c in range(1, chunks):
        edge[0, c - 1] = tall_of(jnp.exp(ends[c] - ends[c - 1]))
        edge[1, c - 1] = tall_of(jnp.exp(ends[c - 1]))

    def send_decay(k, carry):
        decay_copy(lax.rem(rank + k, ndev)).start()
        return carry

    lax.fori_loop(1, ndev, send_decay, 0)

    def conv_column(block):
        q = jnp.where(block < groups, block + 1, (blocks - 1) * (block - groups))
        cols = pl.ds(pl.multiple_of(block * wide, wide), wide)

        def one(i, carry):
            start = pl.multiple_of(i * 128, 128)
            window = total[q, pl.ds(pl.multiple_of(start + tail_rows - 8, 8), 136), :]
            window = window.astype(BF16).astype(F32)
            acc = bias_row[:, cols]
            for k in range(CONV):
                acc = acc + half_w[k : k + 1, cols] * window[5 + k : 5 + k + 128]
            conv[pl.ds(start, 128), cols] = (acc + acc * jnp.tanh(acc)).astype(BF16)
            return carry

        lax.fori_loop(0, length // 128, one, 0)

    def score_all():
        def one(c, carry):
            here = pl.ds(pl.multiple_of(c * CHUNK, CHUNK), CHUNK)
            product = lax.dot_general(
                conv[here, HP + N :], conv[here, HP : HP + N], LAST,
                preferred_element_type=F32,
            )
            scores[c] = jnp.where(causal, product, 0.0)
            return carry

        lax.fori_loop(0, chunks, one, 0)

    heads_each = HEADS // groups

    def mix(c, j):
        here = pl.ds(pl.multiple_of(c * CHUNK, CHUNK), CHUNK)
        log_c = log_s[here]
        for k in range(heads_each):
            h = j * heads_each + k
            gap = jnp.minimum(log_c[:, h : h + 1] - log_t[h : h + 1, here], 60.0)
            mix_s[h, c] = (scores[c] * jnp.exp(gap)).astype(BF16)

    def contribute(j):
        cols = pl.ds(pl.multiple_of(j * wide, wide), wide)
        spread = spread_of(j, 2 * HEADS)
        state = None
        for c in range(chunks):
            here = slice(c * CHUNK, (c + 1) * CHUNK)
            factor = jnp.dot(fac_s[here], spread, preferred_element_type=F32)
            weighted = (factor * conv[here, cols].astype(F32)).astype(BF16)
            part = lax.dot_general(
                weighted, conv[here, HP : HP + N], FIRST, preferred_element_type=F32
            )
            if c > 0:
                local_s[c - 1, cols] = state
                scale = edge[0, c - 1, cols, :]
                part = part + jnp.concatenate([scale, scale], axis=1) * state
            state = part
        send1[pl.ds(j * owners, owners)] = state.reshape(owners, rows, N).astype(BF16)

        def send_one(k, inner):
            o = j * owners + k

            @pl.when(o != own)
            def _():
                first_copy(o).start()

            return inner

        lax.fori_loop(0, owners, send_one, 0)

    def inside(j):
        cols = pl.ds(pl.multiple_of(j * wide, wide), wide)
        lane = lax.broadcasted_iota(jnp.int32, (1, wide), 1) // P_SIZE

        def one(c, carry):
            here = pl.ds(pl.multiple_of(c * CHUNK, CHUNK), CHUNK)
            x_rows = conv[here, cols]
            acc = skip_row[:, cols] * x_rows.astype(F32)
            for k in range(heads_each):
                keep = (lane == k).astype(F32).astype(BF16)
                acc = acc + jnp.dot(
                    mix_s[j * heads_each + k, c], x_rows * keep, preferred_element_type=F32
                )
            y[here, cols] = acc
            return carry

        lax.fori_loop(0, chunks, one, 0)

    heads_at = pl.ds(own * own_heads, own_heads)

    def decay_of(k, half_of):
        row = dec_recv[lax.div(k, n // 2) * n + half_of * (n // 2) + lax.rem(k, n // 2), heads_at, :]
        return jnp.concatenate([row, row], axis=1).reshape(own_heads, 1, N)

    shape = (own_heads, P_SIZE, N)

    def combine():
        recv1[slot] = send1[own]
        for c in range(2):
            def one(m, state):
                k = c * (n // 2) + m
                prefix[k] = state.reshape(rows, N)

                @pl.when(k != slot)
                def _():
                    arrive(recv1, rs1, k, member_at(k))

                return decay_of(k, upper) * state + recv1[k].astype(F32).reshape(shape)

            state = lax.fori_loop(0, n // 2, one, jnp.zeros(shape, F32))
            mid_send[c] = state.reshape(rows, N).astype(BF16)

            @pl.when(upper * c == 0)
            def _():
                mid_copy(c).start()

    def product_of(c, half_of):
        result = decay_of(c * (n // 2), half_of)
        for m in range(1, n // 2):
            result = result * decay_of(c * (n // 2) + m, half_of)
        return result

    def distribute():
        mid_copy(0).wait_recv()

        @pl.when(upper == 1)
        def _():
            mid_copy(1).wait_recv()

        middle = mid_recv[0].astype(F32).reshape(shape)
        ours = mid_send[0].astype(F32).reshape(shape)
        is_upper = upper == 1
        lower_sum = jnp.where(is_upper, middle, ours)
        upper_sum = jnp.where(is_upper, ours, middle)
        block_end = product_of(0, 1) * lower_sum + upper_sum
        @pl.when(is_upper)
        def _():
            start[0] = middle
            start[1] = product_of(1, 0) * block_end + mid_recv[1].astype(F32).reshape(shape)

        @pl.when(upper == 0)
        def _():
            start[0] = jnp.zeros(shape, F32)
            start[1] = block_end

        for c in range(2):
            def one(m, state):
                k = c * (n // 2) + m
                value = prefix[k].reshape(shape) + state
                send2[k] = value.reshape(rows, N).astype(BF16)

                @pl.when(k != slot)
                def _():
                    second_copy(k).start()

                return decay_of(k, upper) * state

            lax.fori_loop(0, n // 2, one, start[c])
        recv2[own] = send2[slot]

    def late_part(i, carry):
        exchange(i)
        accumulate(i)
        ready = first_part + core_lag

        @pl.when(i == ready)
        def _():
            conv_column(groups)

        @pl.when((i >= ready) & (i < ready + groups - 1))
        def _():
            conv_column(i - ready)
            contribute(i - ready)

        return carry

    lax.fori_loop(10, all_parts + core_lag, late_part, 0)

    def others(k, carry):
        r = lax.rem(rank + k, ndev)
        arrive(dec_recv, rsd, r, place(r))
        return carry

    lax.fori_loop(1, ndev, others, 0)
    is_last = own >= (groups - 1) * owners

    @pl.when(jnp.logical_not(is_last))
    def _():
        combine()

    conv_column(groups - 1)
    contribute(groups - 1)
    conv_column(groups + 1)
    score_all()

    def mix_all(c, carry):
        for j in range(groups // 2):
            mix(c, j)
        return carry

    lax.fori_loop(0, chunks, mix_all, 0)

    @pl.when(jnp.logical_not(is_last))
    def _():
        distribute()

    @pl.when(is_last)
    def _():
        combine()

    def mix_rest(c, carry):
        for j in range(groups // 2, groups):
            mix(c, j)
        return carry

    lax.fori_loop(0, chunks, mix_rest, 0)

    def fill(j, carry):
        inside(j)
        return carry

    lax.fori_loop(0, groups // 2, fill, 0)

    @pl.when(is_last)
    def _():
        distribute()

    lax.fori_loop(groups // 2, groups, fill, 0)

    row_head = lax.broadcasted_iota(jnp.int32, (wide, wide), 0) // P_SIZE
    col_head = lax.broadcasted_iota(jnp.int32, (wide, wide), 1) // P_SIZE
    same = (row_head == col_head).astype(F32).astype(BF16)

    def finish_group(j, carry):

        def wait_one(k, inner):
            o = j * owners + k

            @pl.when(o != own)
            def _():
                arrive(recv2, rs2, o, member(o))

            return inner

        lax.fori_loop(0, owners, wait_one, 0)
        cols = pl.ds(pl.multiple_of(j * wide, wide), wide)
        entry = recv2[pl.ds(j * owners, owners)].astype(F32).reshape(wide, N)
        entry_out[cols] = entry
        spread = spread_of(j, 2 * HEADS)
        for c in range(chunks):
            here = slice(c * CHUNK, (c + 1) * CHUNK)
            state = entry
            if c > 0:
                scale = edge[1, c - 1, cols, :]
                state = local_s[c - 1, cols] + jnp.concatenate([scale, scale], axis=1) * entry
            carried = lax.dot_general(
                conv[here, HP + N :], state.astype(BF16), LAST, preferred_element_type=F32
            )
            reach = jnp.dot(reach_s[here], spread, preferred_element_type=F32)
            out = y[here, cols] + reach * carried
            square = (out * out).astype(BF16)
            sums = jnp.dot(square, same, preferred_element_type=F32)
            inv_rms = lax.rsqrt(sums * (1.0 / P_SIZE) + EPSILON)
            mixed[here, cols] = (out * inv_rms * gain_s[:, cols]).astype(BF16)
        return carry

    lax.fori_loop(0, groups, finish_group, 0)

    def drain(q, carry):
        for d in range(2):
            for s in range(1, steps + 1):
                whole = s < steps
                ring_copy(d, q, s, whole).wait_send()
                side_between(d, q, s, grp, whole).wait_send()
                core_between(d, q, s, core, whole).wait_send()
        return carry

    lax.fori_loop(0, blocks, drain, 0)

    def drain_dt(k, carry):
        dt_copy(k).wait_send()
        return carry

    lax.fori_loop(1, n, drain_dt, 0)

    def drain_decay(k, carry):
        decay_copy(lax.rem(rank + k, ndev)).wait_send()
        return carry

    lax.fori_loop(1, ndev, drain_decay, 0)

    def drain_state(k, carry):
        @pl.when(k != own)
        def _():
            first_copy(k).wait_send()

        @pl.when(k != slot)
        def _():
            second_copy(k).wait_send()

        return carry

    lax.fori_loop(0, team, drain_state, 0)
    mid_copy(0).wait_send()

    @pl.when(upper == 0)
    def _():
        mid_copy(1).wait_send()

    @pl.when(rank < ndev - 1)
    def _():
        tail_copy().wait_send()


def run_fused(tokens, w_in, w_dt, conv_w, conv_b, dt_bias, a_log, d_skip, norm_gain):
    n, n_out = lax.axis_size("inner"), lax.axis_size("outer")
    ndev = n * n_out
    length, depth = tokens.shape
    local, xbc = w_in.shape
    team = ndev // 2
    rows = HP // team
    tail_rows = 16
    blocks = xbc // 256
    chunks = length // CHUNK
    dma = pltpu.SemaphoreType.DMA
    vmem = pl.BlockSpec(memory_space=pltpu.VMEM)
    whole = pl.BlockSpec(memory_space=pl.ANY)
    weight_sems = [dma((2, blocks, n // 2 + 1))] * 6
    pair_sems = [dma((team,))] * 2
    swap_sems = [dma((2,))] * 2
    rank_sems = [dma((ndev,))] * 2
    return pl.pallas_call(
        partial(fused_kernel, n, n_out),
        out_shape=(
            jax.ShapeDtypeStruct((length, HP), BF16),
            jax.ShapeDtypeStruct((HP, N), F32),
        ),
        in_specs=[whole, whole] + [vmem] * 7,
        out_specs=(vmem, vmem),
        scratch_shapes=[
            pltpu.VMEM((length + tail_rows, depth), BF16),
            pltpu.VMEM((blocks, depth, 256), BF16),
            pltpu.VMEM((blocks, length + tail_rows, 256), F32),
            pltpu.VMEM((n, HEADS, local), BF16),
            pltpu.VMEM((length, HEADS), F32),
            pltpu.VMEM((CONV, xbc), F32),
            pltpu.VMEM((1, xbc), F32),
            pltpu.VMEM((1, HP), F32),
            pltpu.VMEM((1, HP), F32),
            pltpu.VMEM((length, xbc), BF16),
            pltpu.VMEM((length, 2 * HEADS), F32),
            pltpu.VMEM((HEADS, length), F32),
            pltpu.VMEM((length, 2 * HEADS), F32),
            pltpu.VMEM((length, 2 * HEADS), BF16),
            pltpu.VMEM((length, 2 * HEADS), BF16),
            pltpu.VMEM((2, chunks - 1, HP, 128), F32),
            pltpu.VMEM((chunks, CHUNK, CHUNK), F32),
            pltpu.VMEM((HEADS, chunks, CHUNK, CHUNK), BF16),
            pltpu.VMEM((chunks - 1, HP, N), F32),
            pltpu.VMEM((length, HP), F32),
            pltpu.VMEM((team, rows, N), BF16),
            pltpu.VMEM((team, rows, N), BF16),
            pltpu.VMEM((team, rows, N), F32),
            pltpu.VMEM((2, rows, N), BF16),
            pltpu.VMEM((2, rows, N), BF16),
            pltpu.VMEM((2, rows // P_SIZE, P_SIZE, N), F32),
            pltpu.VMEM((team, rows, N), BF16),
            pltpu.VMEM((team, rows, N), BF16),
            pltpu.VMEM((HEADS, 128), F32),
            pltpu.VMEM((ndev, HEADS, 128), F32),
            *weight_sems,
            dma((n,)), dma((n,)), dma((blocks + 1,)), dma(()), dma(()),
            *pair_sems, *swap_sems, *pair_sems, *rank_sems,
        ],
        compiler_params=pltpu.CompilerParams(
            collective_id=3, has_side_effects=True, vmem_limit_bytes=62 * 2**20
        ),
        name="fused",
    )(
        tokens, w_in, w_dt.T, conv_w, conv_b, dt_bias, a_log, d_skip, norm_gain,
    )


def per_device(tokens, w_in, w_dt, conv_w, conv_b, dt_bias, a_log, d_skip, norm_gain):
    own_rows = tokens.reshape(tokens.shape[1], tokens.shape[2])
    row_count = own_rows.shape[0]
    if w_in.shape[0] % 512 == 0 and lax.axis_size("inner") == 8:
        mixed, entry = run_fused(
            own_rows, w_in, w_dt, conv_w, conv_b, dt_bias, a_log, d_skip, norm_gain
        )
    else:
        projected, tail, dt_raw = run_project(own_rows, w_in, w_dt)
        mixed, entry = run_scan(
            projected, tail, dt_raw, conv_w, conv_b, dt_bias, a_log, d_skip, norm_gain
        )
    return (
        mixed.reshape(1, row_count, HP),
        entry.reshape(1, 1, HEADS, P_SIZE, N),
    )


def solution(mesh):
    placed = (
        P(("grp", "outer"), "inner", None),
        P("inner", None),
        P("inner", None),
        P(), P(), P(), P(), P(), P(),
    )
    return jax.shard_map(
        per_device,
        mesh=mesh,
        in_specs=placed,
        out_specs=(
            P(("grp", "outer"), "inner", None),
            P(("grp", "outer"), "inner", None, None, None),
        ),
        check_vma=False,
    )
```

```python
from functools import partial

import jax
import jax.numpy as jnp
from jax import lax
from jax.experimental import pallas as pl
from jax.experimental.pallas import tpu as pltpu
from jax.sharding import PartitionSpec as P

HEADS = 16
P_SIZE = 64
N = 256
CONV = 4
HP = HEADS * P_SIZE
CHUNK = 256
EPSILON = 1e-05
MESH = pl.DeviceIdType.MESH
F32 = jnp.float32
BF16 = jnp.bfloat16
LAST = (((1,), (1,)), ((), ()))
FIRST = (((0,), (0,)), ((), ()))


def expand(values, spread):
    high = values.astype(BF16)
    low = (values - high.astype(F32)).astype(BF16)
    return jnp.dot(high, spread, preferred_element_type=F32) + jnp.dot(
        low, spread, preferred_element_type=F32
    )


def scan_kernel(
    n_in, ndev,
    proj, tail, dt_raw, conv_w, conv_b, dt_bias, a_log, d_skip, gain,
    mixed, entry_out,
    gain_s, bias_row, skip_row, pad, conv, log_s, log_t, step_s, y, states,
    send1, recv1, send2, recv2, dec_send, dec_recv,
    ss1, rs1, ss2, rs2, ssd, rsd,
):
    length = proj.shape[0]
    chunks = length // CHUNK
    rows = HP // ndev
    me = lax.axis_index("outer") * n_in + lax.axis_index("inner")

    def place(g):
        return {"inner": lax.rem(g, n_in), "outer": lax.div(g, n_in)}

    barrier = pltpu.get_barrier_semaphore()

    def greet(k, carry):
        pl.semaphore_signal(
            barrier, inc=1, device_id=place(lax.rem(me + k, ndev)), device_id_type=MESH
        )
        return carry

    lax.fori_loop(1, ndev, greet, 0)

    head_id = lax.broadcasted_iota(jnp.int32, (HEADS, HP), 0)
    col_head = lax.broadcasted_iota(jnp.int32, (HEADS, HP), 1) // P_SIZE
    spread = (head_id == col_head).astype(F32).astype(BF16)

    bias_row[...] = conv_b[...].reshape(1, conv_b.shape[0])
    gain_s[...] = gain[...].reshape(1, HP)
    skip = d_skip[...].reshape(1, HEADS)
    skip_high = skip.astype(BF16).astype(F32)
    skip_row[...] = expand(skip - skip_high, spread) + jnp.dot(
        skip_high.astype(BF16), spread, preferred_element_type=F32
    )
    step_size = jax.nn.softplus(dt_raw[...].astype(F32) + dt_bias[...].reshape(1, HEADS))
    scaled = step_size * (-jnp.exp(a_log[...].reshape(1, HEADS)))
    row_id = lax.broadcasted_iota(jnp.int32, (CHUNK, CHUNK), 0)
    col_id = lax.broadcasted_iota(jnp.int32, (CHUNK, CHUNK), 1)
    causal = col_id <= row_id
    lower = causal.astype(F32)
    step_s[...] = step_size
    before = jnp.zeros((1, HEADS), F32)
    for c in range(chunks):
        part = jnp.dot(
            lower,
            scaled[c * CHUNK : (c + 1) * CHUNK],
            preferred_element_type=F32,
            precision=lax.Precision.HIGHEST,
        ) + before
        log_s[c * CHUNK : (c + 1) * CHUNK] = part
        before = part[CHUNK - 1 : CHUNK]
    log_t[...] = jnp.transpose(log_s[...])
    dec_send[...] = jnp.broadcast_to(jnp.exp(log_t[:, length - 1 : length]), (HEADS, 128))

    pad[0:8] = tail[...].astype(F32)[8:16]
    pad[8:] = proj[...].astype(F32)
    wide = 256
    blocks = proj.shape[1] // wide

    def conv_block(t, carry):
        i, j = lax.div(t, blocks), lax.rem(t, blocks)
        cols = pl.ds(pl.multiple_of(j * wide, wide), wide)
        window = pad[pl.ds(pl.multiple_of(i * 128, 128), 136), cols]
        total = bias_row[:, cols]
        for k in range(CONV):
            total = total + conv_w[k : k + 1, cols] * window[5 + k : 5 + k + 128]
        conv[pl.ds(pl.multiple_of(i * 128, 128), 128), cols] = (
            total * jax.nn.sigmoid(total)
        ).astype(BF16)
        return carry

    row_blocks = length // 128

    def conv_column(j):
        def one(i, carry):
            return conv_block(i * blocks + j, carry)

        lax.fori_loop(0, row_blocks, one, 0)

    conv_column(HP // wide)

    def weighted_sum(stop):
        final = log_s[stop - 1 : stop]
        factor = jnp.exp(final - log_s[0:stop]) * step_s[0:stop]
        weighted = (expand(factor, spread) * conv[0:stop, 0:HP].astype(F32)).astype(BF16)
        return lax.dot_general(
            weighted, conv[0:stop, HP : HP + N], FIRST, preferred_element_type=F32
        )

    dec_recv[me] = dec_send[...]

    def decay_copy(g):
        return pltpu.make_async_remote_copy(
            src_ref=dec_send, dst_ref=dec_recv.at[me], send_sem=ssd.at[g],
            recv_sem=rsd.at[me], device_id=place(g), device_id_type=MESH,
        )

    def first_copy(g):
        return pltpu.make_async_remote_copy(
            src_ref=send1.at[g], dst_ref=recv1.at[me], send_sem=ss1.at[g],
            recv_sem=rs1.at[me], device_id=place(g), device_id_type=MESH,
        )

    def second_copy(g):
        return pltpu.make_async_remote_copy(
            src_ref=send2.at[g], dst_ref=recv2.at[me], send_sem=ss2.at[g],
            recv_sem=rs2.at[me], device_id=place(g), device_id_type=MESH,
        )

    pl.semaphore_wait(barrier, ndev - 1)

    def send_decay(k, carry):
        decay_copy(lax.rem(me + k, ndev)).start()
        return carry

    lax.fori_loop(1, ndev, send_decay, 0)

    groups = HP // wide
    owners = ndev // groups
    own_group = lax.div(me, owners)
    factor = jnp.exp(log_s[length - 1 : length] - log_s[...]) * step_s[...]

    def spread_of(j):
        head = lax.broadcasted_iota(jnp.int32, (HEADS, wide), 0)
        col = lax.broadcasted_iota(jnp.int32, (HEADS, wide), 1) // P_SIZE
        return (head == col + j * (wide // P_SIZE)).astype(F32).astype(BF16)

    def first_group(i, carry):
        j = lax.rem(own_group + 1 + i, groups)
        conv_column(j)
        cols = pl.ds(pl.multiple_of(j * wide, wide), wide)
        weighted = (expand(factor, spread_of(j)) * conv[:, cols].astype(F32)).astype(BF16)
        part = lax.dot_general(
            weighted, conv[:, HP : HP + N], FIRST, preferred_element_type=F32
        )
        send1[pl.ds(j * owners, owners)] = part.reshape(owners, rows, N).astype(BF16)

        def send_one(k, inner):
            g = j * owners + k

            @pl.when(g != me)
            def _():
                first_copy(g).start()

            return inner

        return lax.fori_loop(0, owners, send_one, carry)

    lax.fori_loop(0, groups, first_group, 0)
    recv1[me] = send1[me]
    conv_column(HP // wide + 1)

    states[0] = jnp.zeros((HP, N), BF16)
    for c in range(1, chunks):
        states[c] = weighted_sum(c * CHUNK).astype(BF16)

    def local_chunk(c, carry):
        start = pl.multiple_of(c * CHUNK, CHUNK)
        here = pl.ds(start, CHUNK)
        log_c = log_s[here]
        reached = log_s[pl.ds(pl.multiple_of(jnp.maximum(start - 8, 0), 8), 8)][7:8]
        reached = jnp.where(c > 0, reached, 0.0)
        c_rows = conv[here, HP + N :]
        b_rows = conv[here, HP : HP + N]
        scores = lax.dot_general(c_rows, b_rows, LAST, preferred_element_type=F32)
        scores = jnp.where(causal, scores, 0.0)
        x_rows = conv[here, 0:HP].astype(F32)
        driven = (expand(step_s[here], spread) * x_rows).astype(BF16)
        inter = lax.dot_general(c_rows, states[c], LAST, preferred_element_type=F32)
        y[here] = expand(jnp.exp(log_c - reached), spread) * inter + skip_row[...] * x_rows
        for h in range(0, HEADS, 2):
            pieces = []
            for k in (h, h + 1):
                gap = jnp.minimum(log_c[:, k : k + 1] - log_t[k : k + 1, here], 0.0)
                mixing = (scores * jnp.exp(gap)).astype(BF16)
                pieces.append(
                    jnp.dot(
                        mixing,
                        driven[:, k * P_SIZE : (k + 1) * P_SIZE],
                        preferred_element_type=F32,
                    )
                )
            both = slice(h * P_SIZE, (h + 2) * P_SIZE)
            y[here, both] = y[here, both] + jnp.concatenate(pieces, axis=1)
        return carry

    lax.fori_loop(0, chunks, local_chunk, 0)

    own_head = lax.div(me * rows, P_SIZE)

    def wait_from(copy_of, r):
        copy_of(r).wait_recv()

    def arrive(buffer, sems, r):
        pltpu.make_async_remote_copy(
            src_ref=buffer.at[r], dst_ref=buffer.at[r], send_sem=sems.at[r],
            recv_sem=sems.at[r], device_id=place(r), device_id_type=MESH,
        ).wait_recv()

    def advance(r, state):
        send2[r] = state.astype(BF16)

        @pl.when(r != me)
        def _():
            arrive(dec_recv, rsd, r)
            arrive(recv1, rs1, r)

        decay = dec_recv[r, pl.ds(own_head, 1), :]
        decay = jnp.concatenate([decay, decay], axis=1)
        return decay * state + recv1[r].astype(F32)

    lax.fori_loop(0, ndev, advance, jnp.zeros((rows, N), F32))

    def send_second(k, carry):
        second_copy(lax.rem(me + k, ndev)).start()
        return carry

    lax.fori_loop(1, ndev, send_second, 0)
    recv2[me] = send2[me]

    reach = jnp.exp(log_s[...])

    def last_group(i, carry):
        j = lax.rem(own_group + groups - 1 - i, groups)

        def wait_one(k, inner):
            g = j * owners + k

            @pl.when(g != me)
            def _():
                arrive(recv2, rs2, g)

            return inner

        lax.fori_loop(0, owners, wait_one, 0)
        cols = pl.ds(pl.multiple_of(j * wide, wide), wide)
        entry = recv2[pl.ds(j * owners, owners)].astype(F32).reshape(wide, N)
        entry_out[cols] = entry
        carried = lax.dot_general(
            conv[:, HP + N :], entry.astype(BF16), LAST, preferred_element_type=F32
        )
        spread_j = spread_of(j)
        out = y[:, cols] + expand(reach, spread_j) * carried
        square = out * out
        high = square.astype(BF16)
        low = (square - high.astype(F32)).astype(BF16)
        sums = lax.dot_general(high, spread_j, LAST, preferred_element_type=F32)
        sums = sums + lax.dot_general(low, spread_j, LAST, preferred_element_type=F32)
        inv_rms = lax.rsqrt(sums * (1.0 / P_SIZE) + EPSILON)
        mixed[:, cols] = (out * expand(inv_rms, spread_j) * gain_s[:, cols]).astype(BF16)
        return carry

    lax.fori_loop(0, groups, last_group, 0)

    def finish(k, carry):
        g = lax.rem(me + k, ndev)
        decay_copy(g).wait_send()
        first_copy(g).wait_send()
        second_copy(g).wait_send()
        return carry

    lax.fori_loop(1, ndev, finish, 0)


def run_scan(projected, tail, dt_raw, conv_w, conv_b, dt_bias, a_log, d_skip, norm_gain):
    n_in, n_out = lax.axis_size("inner"), lax.axis_size("outer")
    ndev = n_in * n_out
    length, xbc = projected.shape
    rows = HP // ndev
    dma = pltpu.SemaphoreType.DMA((ndev,))
    vmem = pl.BlockSpec(memory_space=pltpu.VMEM)
    return pl.pallas_call(
        partial(scan_kernel, n_in, ndev),
        out_shape=(
            jax.ShapeDtypeStruct((length, HP), BF16),
            jax.ShapeDtypeStruct((HP, N), F32),
        ),
        in_specs=[vmem] * 9,
        out_specs=(vmem, vmem),
        scratch_shapes=[
            pltpu.VMEM((1, HP), F32),
            pltpu.VMEM((1, xbc), F32),
            pltpu.VMEM((1, HP), F32),
            pltpu.VMEM((length + 8, xbc), F32),
            pltpu.VMEM((length, xbc), BF16),
            pltpu.VMEM((length, HEADS), F32),
            pltpu.VMEM((HEADS, length), F32),
            pltpu.VMEM((length, HEADS), F32),
            pltpu.VMEM((length, HP), F32),
            pltpu.VMEM((length // CHUNK, HP, N), BF16),
            pltpu.VMEM((ndev, rows, N), BF16),
            pltpu.VMEM((ndev, rows, N), BF16),
            pltpu.VMEM((ndev, rows, N), BF16),
            pltpu.VMEM((ndev, rows, N), BF16),
            pltpu.VMEM((HEADS, 128), F32),
            pltpu.VMEM((ndev, HEADS, 128), F32),
            dma, dma, dma, dma, dma, dma,
        ],
        compiler_params=pltpu.CompilerParams(
            collective_id=1, has_side_effects=True, vmem_limit_bytes=60 * 2**20
        ),
        name="scan",
    )(
        projected, tail, dt_raw, conv_w, conv_b, dt_bias, a_log, d_skip, norm_gain,
    )


def project_kernel(
    n, n_out,
    tokens, w_in, w_dt,
    proj, tail, dt_out,
    tok, held, total, held_dt,
    ring_s, ring_r, side_s, side_r, core_s, core_r, dt_s, dt_r, misc, tail_s, tail_r,
):
    length, depth = tokens.shape
    local, xbc = w_in.shape
    half = xbc // 2
    quarter = half // 2
    lanes = 128
    streams = quarter // lanes
    wide = 256
    tiles = half // wide
    third = (local * 5 // 16) // 16 * 16
    ring_rows = local - third
    tail_rows = tok.shape[0] - length
    block = held_dt.shape[2]
    ndev = n * n_out
    me = lax.axis_index("inner")
    core = lax.axis_index("outer")
    grp = lax.axis_index("grp")
    rank = core * n + me
    odd = lax.rem(me, 2)
    pos = jnp.where(odd == 0, lax.div(me, 2), n - lax.div(me + 1, 2))

    def index_at(q):
        q = lax.rem(q + 2 * n, n)
        return jnp.where(q < n // 2, 2 * q, 2 * n - 1 - 2 * q)

    def place(g):
        return {"inner": lax.rem(g, n), "outer": lax.div(g, n)}

    barrier = pltpu.get_barrier_semaphore()

    def greet(k, carry):
        pl.semaphore_signal(
            barrier, inc=1, device_id=place(lax.rem(rank + k, ndev)), device_id_type=MESH
        )
        return carry

    lax.fori_loop(1, ndev, greet, 0)
    pl.semaphore_signal(barrier, inc=1, device_id={"grp": 1 - grp}, device_id_type=MESH)

    def own_rows(owner):
        return pl.ds(pl.multiple_of(owner * local, 16), local)

    load_tok = pltpu.make_async_copy(tokens, tok.at[pl.ds(0, length)], misc.at[0])
    load_w = [
        pltpu.make_async_copy(
            w_in.at[:, pl.ds(d * half, half)], held.at[d, own_rows(me)], misc.at[1 + d]
        )
        for d in range(2)
    ]
    for copy in load_w:
        copy.start()
    load_tok.start()
    held_dt[me] = w_dt[...]

    @pl.when(rank == 0)
    def _():
        tok[length:] = jnp.zeros((tail_rows, depth), BF16)

    def ring_copy(d, t, s):
        owner = index_at(pos - (s - 1)) if d == 0 else index_at(pos + (s - 1))
        target = index_at(pos + 1) if d == 0 else index_at(pos - 1)
        rows = pl.ds(pl.multiple_of(owner * local + grp * third, 16), ring_rows)
        cols = pl.ds(pl.multiple_of(core * quarter + t * lanes, lanes), lanes)
        part = held.at[d, rows, cols]
        return pltpu.make_async_remote_copy(
            src_ref=part, dst_ref=part, send_sem=ring_s.at[d, t, s],
            recv_sem=ring_r.at[d, t, s], device_id={"inner": target}, device_id_type=MESH,
        )

    def owner_of(d, s):
        return index_at(pos - s) if d == 0 else index_at(pos + s)

    def chunk_cols(which, t):
        return pl.ds(pl.multiple_of(which * quarter + t * lanes, lanes), lanes)

    def side_rows(d, s, which):
        start = owner_of(d, s) * local + which * ring_rows
        return pl.ds(pl.multiple_of(start, 16), third)

    def side_between(d, t, s, which):
        part = held.at[d, side_rows(d, s, which), chunk_cols(core, t)]
        return pltpu.make_async_remote_copy(
            src_ref=part, dst_ref=part, send_sem=side_s.at[d, t, s],
            recv_sem=side_r.at[d, t, s], device_id={"grp": 1 - grp}, device_id_type=MESH,
        )

    def core_between(d, t, s, which):
        part = held.at[d, own_rows(owner_of(d, s)), chunk_cols(which, t)]
        return pltpu.make_async_remote_copy(
            src_ref=part, dst_ref=part, send_sem=core_s.at[d, t, s],
            recv_sem=core_r.at[d, t, s], device_id={"outer": 1 - core}, device_id_type=MESH,
        )

    def side_copy(d, t, s):
        return side_between(d, t, s, grp)

    def core_copy(d, t, s):
        return core_between(d, t, s, core)

    def ring_arrival(d, t, s):
        start = owner_of(d, s) * local + grp * third
        rows = pl.ds(pl.multiple_of(start, 16), ring_rows)
        part = held.at[d, rows, chunk_cols(core, t)]
        pltpu.make_async_remote_copy(
            src_ref=part, dst_ref=part, send_sem=ring_s.at[d, t, s],
            recv_sem=ring_r.at[d, t, s], device_id={"inner": index_at(pos + 1)},
            device_id_type=MESH,
        ).wait_recv()

    def side_arrival(d, t, s):
        side_between(d, t, s, 1 - grp).wait_recv()

    def core_arrival(d, t, s):
        core_between(d, t, s, 1 - core).wait_recv()

    def dt_copy(k):
        peer = lax.rem(me + k, n)
        return pltpu.make_async_remote_copy(
            src_ref=w_dt, dst_ref=held_dt.at[me], send_sem=dt_s.at[k],
            recv_sem=dt_r.at[me], device_id={"inner": peer}, device_id_type=MESH,
        )

    def dt_arrival(k):
        peer = lax.rem(me + k, n)
        pltpu.make_async_remote_copy(
            src_ref=w_dt, dst_ref=held_dt.at[peer], send_sem=dt_s.at[k],
            recv_sem=dt_r.at[peer], device_id={"inner": peer}, device_id_type=MESH,
        ).wait_recv()

    def tail_copy():
        return pltpu.make_async_remote_copy(
            src_ref=tokens.at[pl.ds(length - tail_rows, tail_rows)],
            dst_ref=tok.at[pl.ds(length, tail_rows)], send_sem=tail_s,
            recv_sem=tail_r, device_id=place(lax.rem(rank + 1, ndev)), device_id_type=MESH,
        )

    pl.semaphore_wait(barrier, ndev)

    @pl.when(rank < ndev - 1)
    def _():
        tail_copy().start()

    for d in range(2):
        load_w[d].wait()
        for t in range(streams):
            ring_copy(d, t, 1).start()

    def send_dt(k, carry):
        dt_copy(k).start()
        return carry

    lax.fori_loop(1, n, send_dt, 0)
    load_tok.wait()

    @pl.when(rank > 0)
    def _():
        tail_copy().wait_recv()

    incremental = local % 128 == 0

    def multiply_tile(d, lhs_cols, rhs_rows, first, j):
        cols = pl.ds(pl.multiple_of(j * wide, wide), wide)
        product = jnp.dot(
            tok[:, lhs_cols], held[d, rhs_rows, cols], preferred_element_type=F32
        )
        at = d * tiles + j
        if first:
            total[at] = product
        else:
            total[at] = total[at] + product

    def multiply(d, lhs_cols, rhs_rows, first):
        def tile(j, carry):
            multiply_tile(d, lhs_cols, rhs_rows, first, j)
            return carry

        lax.fori_loop(0, tiles, tile, 0)

    def project_dt():
        def arrived(k, carry):
            dt_arrival(k)
            return carry

        lax.fori_loop(1, n, arrived, 0)
        together = block // local

        def add(j, sums):
            cols = pl.ds(pl.multiple_of(j * block, block), block)
            piece = held_dt[j * together]
            for m in range(1, together):
                piece = piece + held_dt[j * together + m]
            return sums + lax.dot_general(
                tok[0:length, cols], piece, LAST, preferred_element_type=F32
            )

        sums = lax.fori_loop(0, depth // block, add, jnp.zeros((length, HEADS), F32))
        dt_out[...] = sums.astype(BF16)

    def step(s, carry):
        @pl.when(s >= 3)
        def _():
            for t in range(streams):
                for d in range(2):
                    core_arrival(d, t, s - 2)

        def part(t, inner):
            @pl.when(s < n)
            def _():
                for d in range(2):
                    ring_arrival(d, t, s)

                    @pl.when(s < n - 1)
                    def _():
                        ring_copy(d, t, s + 1).start()

                    side_copy(d, t, s).start()

            @pl.when((s >= 2) & (s <= n))
            def _():
                for d in range(2):
                    side_arrival(d, t, s - 1)
                    core_copy(d, t, s - 1).start()

            if incremental:
                for d in range(2):
                    owner = owner_of(d, s - 2)
                    at = pl.ds(pl.multiple_of(owner * local, 128), local)

                    @pl.when(s == 2)
                    def _():
                        multiply_tile(d, at, at, True, t)

                    @pl.when(s > 2)
                    def _():
                        multiply_tile(d, at, at, False, t)

            return inner

        lax.fori_loop(0, streams, part, 0)

        @pl.when(s == 1)
        def _():
            project_dt()

        return carry

    lax.fori_loop(1, n + 2, step, 0)
    if not incremental:
        for d in range(2):
            multiply(d, slice(0, 512), slice(0, 512), True)

            def more(j, carry):
                at = pl.ds(pl.multiple_of(j * 512, 512), 512)
                multiply(d, at, at, False)
                return carry

            lax.fori_loop(1, depth // 512, more, 0)

    for j in range(2 * tiles):
        cols = slice(j * wide, (j + 1) * wide)
        proj[:, cols] = total[j, 0:length].astype(BF16)
        tail[:, cols] = total[j, length:].astype(BF16)

    def drain(s, carry):
        for d in range(2):
            for t in range(streams):
                ring_copy(d, t, s).wait_send()
                side_copy(d, t, s).wait_send()
                core_copy(d, t, s).wait_send()
        dt_copy(s).wait_send()
        return carry

    lax.fori_loop(1, n, drain, 0)

    @pl.when(rank < ndev - 1)
    def _():
        tail_copy().wait_send()


def run_project(tokens, w_in, w_dt):
    n, n_out = lax.axis_size("inner"), lax.axis_size("outer")
    length, depth = tokens.shape
    local, xbc = w_in.shape
    block = max(local, 128)
    tail_rows = 16
    dt_block = w_dt.T
    if block != local:
        start = lax.rem(lax.axis_index("inner") * local, block)
        dt_block = lax.dynamic_update_slice(
            jnp.zeros((HEADS, block), BF16), dt_block, (jnp.int32(0), start)
        )
    streams = xbc // 4 // 128
    dma = pltpu.SemaphoreType.DMA
    vmem = pl.BlockSpec(memory_space=pltpu.VMEM)
    whole = pl.BlockSpec(memory_space=pl.ANY)
    return pl.pallas_call(
        partial(project_kernel, n, n_out),
        out_shape=(
            jax.ShapeDtypeStruct((length, xbc), BF16),
            jax.ShapeDtypeStruct((tail_rows, xbc), BF16),
            jax.ShapeDtypeStruct((length, HEADS), BF16),
        ),
        in_specs=[whole, whole, vmem],
        out_specs=(vmem, vmem, vmem),
        scratch_shapes=[
            pltpu.VMEM((length + tail_rows, depth), BF16),
            pltpu.VMEM((2, depth, xbc // 2), BF16),
            pltpu.VMEM((xbc // 256, length + tail_rows, 256), F32),
            pltpu.VMEM((n, HEADS, block), BF16),
            dma((2, streams, n)), dma((2, streams, n)),
            dma((2, streams, n)), dma((2, streams, n)),
            dma((2, streams, n)), dma((2, streams, n)),
            dma((n,)), dma((n,)), dma((3,)), dma(()), dma(()),
        ],
        compiler_params=pltpu.CompilerParams(
            collective_id=2, has_side_effects=True, vmem_limit_bytes=60 * 2**20
        ),
        name="project",
    )(tokens, w_in, dt_block)


def fused_kernel(
    n, n_out,
    tokens, w_in, w_dt, conv_w_in, conv_b_in, dt_bias_in, a_log_in, d_skip_in, gain_in,
    mixed_out, entry_all,
    conv_w, conv_b, dt_bias, a_log, d_skip, gain, mixed, entry_out,
    tok, held, total, held_dt, dt_acc, half_w, bias_row, gain_s, skip_row,
    conv, log_s, log_t, step_s, fac_s, reach_s, edge, scores, mix_s, local_s, y,
    send1, recv1, prefix, mid_send, mid_recv, start, send2, recv2, dec_send, dec_recv,
    ring_s, ring_r, side_s, side_r, core_s, core_r, dt_s, dt_r, misc, tail_s, tail_r,
    ss1, rs1, ssm, rsm, ss2, rs2, ssd, rsd, small, out_sems,
):
    length, depth = tokens.shape
    local, xbc = w_in.shape
    tail_rows = tok.shape[0] - length
    wide, lanes = 256, 128
    blocks = xbc // wide
    groups = HP // wide
    early = groups
    late = blocks - early
    steps = n // 2
    half = local // 2
    third = (half * 5 // 16) // 16 * 16
    ring_rows = half - third
    chunks = length // CHUNK
    ndev = n * n_out
    team = ndev // 2
    rows = wide // team
    me = lax.axis_index("inner")
    core = lax.axis_index("outer")
    grp = lax.axis_index("grp")
    rank = core * n + me
    odd = lax.rem(me, 2)
    pos = jnp.where(odd == 0, lax.div(me, 2), n - lax.div(me + 1, 2))
    upper = lax.div(me, n // 2)
    base = upper * (n // 2)
    own = (me - base) * n_out + core
    slot = core * (n // 2) + me - base

    def index_at(q):
        q = lax.rem(q + 2 * n, n)
        return jnp.where(q < n // 2, 2 * q, 2 * n - 1 - 2 * q)

    def place(g):
        return {"inner": lax.rem(g, n), "outer": lax.div(g, n)}

    barrier = pltpu.get_barrier_semaphore()

    def greet(k, carry):
        pl.semaphore_signal(
            barrier, inc=1, device_id=place(lax.rem(rank + k, ndev)), device_id_type=MESH
        )
        return carry

    lax.fori_loop(1, ndev, greet, 0)
    pl.semaphore_signal(barrier, inc=1, device_id={"grp": 1 - grp}, device_id_type=MESH)

    own_rows = pl.ds(pl.multiple_of(me * local, local), local)

    def natural(q):
        return groups if q == 0 else (blocks - 1 if q == blocks - 1 else q - 1)

    load_tok = pltpu.make_async_copy(
        tokens, tok.at[pl.ds(tail_rows, length)], misc.at[blocks]
    )
    load_w = [
        pltpu.make_async_copy(
            w_in.at[:, pl.ds(natural(q) * wide, wide)],
            held.at[q, own_rows], misc.at[q],
        )
        for q in range(blocks)
    ]
    for copy in load_w:
        copy.start()
    load_small = [
        pltpu.make_async_copy(source, target, small.at[k])
        for k, (source, target) in enumerate((
            (w_dt, held_dt.at[me]), (conv_w_in, conv_w), (conv_b_in, conv_b),
            (dt_bias_in, dt_bias), (a_log_in, a_log), (d_skip_in, d_skip), (gain_in, gain),
        ))
    ]
    for copy in load_small:
        copy.start()
    load_tok.start()

    @pl.when(rank == 0)
    def _():
        tok[0:tail_rows] = jnp.zeros((tail_rows, depth), BF16)

    def owner_of(d, s):
        return index_at(pos - s) if d == 0 else index_at(pos + s)

    def columns(d, whole):
        return slice(0, wide) if whole else slice(d * lanes, (d + 1) * lanes)

    def ring_between(d, q, s, source, whole):
        start = owner_of(d, source) * local + core * half + grp * third
        part = held.at[q, pl.ds(pl.multiple_of(start, 16), ring_rows), columns(d, whole)]
        target = index_at(pos + 1) if d == 0 else index_at(pos - 1)
        return pltpu.make_async_remote_copy(
            src_ref=part, dst_ref=part, send_sem=ring_s.at[d, q, s],
            recv_sem=ring_r.at[d, q, s], device_id={"inner": target}, device_id_type=MESH,
        )

    def ring_copy(d, q, s, whole):
        return ring_between(d, q, s, s - 1, whole)

    def side_between(d, q, s, which, whole):
        start = owner_of(d, s) * local + core * half + which * ring_rows
        part = held.at[q, pl.ds(pl.multiple_of(start, 16), third), columns(d, whole)]
        return pltpu.make_async_remote_copy(
            src_ref=part, dst_ref=part, send_sem=side_s.at[d, q, s],
            recv_sem=side_r.at[d, q, s], device_id={"grp": 1 - grp}, device_id_type=MESH,
        )

    def core_between(d, q, s, which, whole):
        start = owner_of(d, s) * local + which * half
        part = held.at[q, pl.ds(pl.multiple_of(start, 16), half), columns(d, whole)]
        return pltpu.make_async_remote_copy(
            src_ref=part, dst_ref=part, send_sem=core_s.at[d, q, s],
            recv_sem=core_r.at[d, q, s], device_id={"outer": 1 - core}, device_id_type=MESH,
        )

    def dt_copy(k):
        peer = lax.rem(me + k, n)
        return pltpu.make_async_remote_copy(
            src_ref=w_dt, dst_ref=held_dt.at[me], send_sem=dt_s.at[k],
            recv_sem=dt_r.at[me], device_id={"inner": peer}, device_id_type=MESH,
        )

    def dt_arrival(k):
        peer = lax.rem(me + k, n)
        pltpu.make_async_remote_copy(
            src_ref=w_dt, dst_ref=held_dt.at[peer], send_sem=dt_s.at[k],
            recv_sem=dt_r.at[peer], device_id={"inner": peer}, device_id_type=MESH,
        ).wait_recv()

    def tail_copy():
        return pltpu.make_async_remote_copy(
            src_ref=tokens.at[pl.ds(length - tail_rows, tail_rows)],
            dst_ref=tok.at[pl.ds(0, tail_rows)], send_sem=tail_s,
            recv_sem=tail_r, device_id=place(lax.rem(rank + 1, ndev)), device_id_type=MESH,
        )

    def decay_copy(g):
        return pltpu.make_async_remote_copy(
            src_ref=dec_send, dst_ref=dec_recv.at[rank], send_sem=ssd.at[g],
            recv_sem=rsd.at[rank], device_id=place(g), device_id_type=MESH,
        )

    def member(o):
        return {"inner": base + lax.div(o, n_out), "outer": lax.rem(o, n_out)}

    def member_at(k):
        return {"inner": base + lax.rem(k, n // 2), "outer": lax.div(k, n // 2)}

    def first_copy(j, o):
        return pltpu.make_async_remote_copy(
            src_ref=send1.at[j, o], dst_ref=recv1.at[j, slot], send_sem=ss1.at[j, o],
            recv_sem=rs1.at[j, slot], device_id=member(o), device_id_type=MESH,
        )

    def first_arrival(j, k):
        pltpu.make_async_remote_copy(
            src_ref=send1.at[j, k], dst_ref=recv1.at[j, k], send_sem=ss1.at[j, k],
            recv_sem=rs1.at[j, k], device_id=member_at(k), device_id_type=MESH,
        ).wait_recv()

    batches = [slice(0, groups - 1), slice(groups - 1, groups)]

    def mid_copy(b, c):
        return pltpu.make_async_remote_copy(
            src_ref=mid_send.at[c, batches[b]], dst_ref=mid_recv.at[c, batches[b]],
            send_sem=ssm.at[b, c], recv_sem=rsm.at[b, c],
            device_id={"inner": me + n // 2 - upper * n}, device_id_type=MESH,
        )

    def second_copy(b, k):
        return pltpu.make_async_remote_copy(
            src_ref=send2.at[k, batches[b]], dst_ref=recv2.at[own, batches[b]],
            send_sem=ss2.at[b, k], recv_sem=rs2.at[b, own],
            device_id=member_at(k), device_id_type=MESH,
        )

    def second_arrival(b, o):
        pltpu.make_async_remote_copy(
            src_ref=send2.at[o, batches[b]], dst_ref=recv2.at[o, batches[b]],
            send_sem=ss2.at[b, o], recv_sem=rs2.at[b, o],
            device_id=member(o), device_id_type=MESH,
        ).wait_recv()

    def arrive(buffer, sems, r, peer):
        pltpu.make_async_remote_copy(
            src_ref=buffer.at[r], dst_ref=buffer.at[r], send_sem=sems.at[r],
            recv_sem=sems.at[r], device_id=peer, device_id_type=MESH,
        ).wait_recv()

    for copy in load_small:
        copy.wait()

    half_w[...] = conv_w[...] * 0.5
    bias_row[...] = conv_b[...].reshape(1, xbc) * 0.5
    gain_s[...] = gain[...].reshape(1, HP)

    def spread_of(j, count):
        head = lax.rem(lax.broadcasted_iota(jnp.int32, (count, wide), 0), HEADS)
        col = lax.broadcasted_iota(jnp.int32, (count, wide), 1) // P_SIZE
        return (head == col + j * (wide // P_SIZE)).astype(F32).astype(BF16)

    def split(values):
        high = values.astype(BF16).astype(F32)
        lane = lax.broadcasted_iota(jnp.int32, values.shape, 1)
        return jnp.where(lane < HEADS, high, values - high).astype(BF16)

    skip = d_skip[...].reshape(1, HEADS)
    skip_high = skip.astype(BF16).astype(F32)
    for j in range(groups):
        skip_row[:, j * wide : (j + 1) * wide] = expand(
            skip - skip_high, spread_of(j, HEADS)
        ) + jnp.dot(skip_high.astype(BF16), spread_of(j, HEADS), preferred_element_type=F32)

    pl.semaphore_wait(barrier, ndev)

    @pl.when(rank < ndev - 1)
    def _():
        tail_copy().start()

    def send_dt(k, carry):
        dt_copy(k).start()
        return carry

    lax.fori_loop(1, n, send_dt, 0)
    for q in range(early):
        load_w[q].wait()
        for d in range(2):
            ring_copy(d, q, 1, True).start()
    for q in range(early, blocks):
        load_w[q].wait()
    load_tok.wait()

    def multiply(q, shards, first):
        product = None if first else total[q]
        for owner in shards:
            at = pl.ds(pl.multiple_of(owner * local, local), local)
            term = jnp.dot(tok[:, at], held[q, at, :], preferred_element_type=F32)
            product = term if product is None else product + term
        total[q] = product

    first_part = early * steps
    all_parts = blocks * steps
    side_lag, core_lag = 3, 4

    def item(i):
        behind = i - first_part
        is_early = i < first_part
        q = jnp.where(is_early, lax.rem(i, early), early + lax.rem(jnp.maximum(behind, 0), late))
        s = jnp.where(is_early, lax.div(i, early), lax.div(jnp.maximum(behind, 0), late)) + 1
        return q, s

    def exchange(i):
        q, s = item(i)

        @pl.when((i < all_parts) & (s < steps))
        def _():
            for d in range(2):
                ring_between(d, q, s, s, True).wait_recv()

                @pl.when(s < steps - 1)
                def _():
                    ring_copy(d, q, s + 1, True).start()

                @pl.when(s == steps - 1)
                def _():
                    ring_copy(d, q, s + 1, False).start()

                side_between(d, q, s, grp, True).start()

        @pl.when((i < all_parts) & (s == steps))
        def _():
            for d in range(2):
                ring_between(d, q, s, s, False).wait_recv()
                side_between(d, q, s, grp, False).start()

        for k in range(late):
            @pl.when(i == first_part - early - 1 + 2 * k)
            def _():
                for d in range(2):
                    ring_copy(d, early + k, 1, True).start()

        q, s = item(jnp.maximum(i - side_lag, 0))
        for whole in (True, False):
            @pl.when((i >= side_lag) & (i < all_parts + side_lag) & ((s < steps) == whole))
            def _():
                for d in range(2):
                    side_between(d, q, s, 1 - grp, whole).wait_recv()
                    core_between(d, q, s, core, whole).start()

    def accumulate(i):
        q, s = item(jnp.maximum(i - core_lag, 0))

        @pl.when((i >= core_lag) & (s < steps))
        def _():
            for d in range(2):
                core_between(d, q, s, 1 - core, True).wait_recv()
            multiply(q, [owner_of(0, s), owner_of(1, s)], False)

        @pl.when((i >= core_lag) & (s == steps))
        def _():
            for d in range(2):
                core_between(d, q, s, 1 - core, False).wait_recv()
            multiply(q, [owner_of(0, s)], False)

        @pl.when((i < early) | (i == 6) | (i == 10))
        def _():
            multiply(jnp.where(i < early, i, early + lax.div(jnp.maximum(i - 6, 0), 4)), [me], True)

    def add_dt(k):
        @pl.when(k != me)
        def _():
            dt_arrival(lax.rem(k - me + n, n))

        cols = pl.ds(pl.multiple_of(k * local, local), local)
        part = lax.dot_general(
            tok[tail_rows:, cols], held_dt[k], LAST, preferred_element_type=F32
        )

        @pl.when(k == 0)
        def _():
            dt_acc[...] = part

        @pl.when(k > 0)
        def _():
            dt_acc[...] = dt_acc[...] + part

    def early_part(i, carry):
        exchange(i)

        @pl.when((i == 0) & (rank > 0))
        def _():
            tail_copy().wait_recv()

        accumulate(i)

        @pl.when(i < n)
        def _():
            add_dt(i)

        return carry

    lax.fori_loop(0, 10, early_part, 0)

    row_id = lax.broadcasted_iota(jnp.int32, (CHUNK, CHUNK), 0)
    col_id = lax.broadcasted_iota(jnp.int32, (CHUNK, CHUNK), 1)
    causal = col_id <= row_id
    dt_raw = dt_acc[...].astype(BF16).astype(F32)
    step_one = jax.nn.softplus(dt_raw + dt_bias[...].reshape(1, HEADS))
    scaled = step_one * (-jnp.exp(a_log[...].reshape(1, HEADS)))
    scaled = jnp.concatenate([scaled, scaled], axis=1)
    step_size = jnp.concatenate([step_one, step_one], axis=1)
    before = jnp.zeros((1, 2 * HEADS), F32)
    lower = causal.astype(F32)
    for c in range(chunks):
        here = slice(c * CHUNK, (c + 1) * CHUNK)
        part = jnp.dot(
            lower, scaled[here], preferred_element_type=F32,
            precision=lax.Precision.HIGHEST,
        ) + before
        log_s[here] = part
        reach_s[here] = split(jnp.exp(part - before))
        before = part[CHUNK - 1 : CHUNK]
        fac_s[here] = split(jnp.exp(before - part) * step_size[here])
    flat = jnp.transpose(log_s[...])[0:HEADS]
    log_t[...] = jnp.transpose(log_s[...] - jnp.log(step_size))[0:HEADS]
    ends = [flat[:, (c + 1) * CHUNK - 1 : (c + 1) * CHUNK] for c in range(chunks)]
    dec_send[...] = jnp.broadcast_to(jnp.exp(ends[chunks - 1]), (HEADS, 128))
    dec_recv[rank] = dec_send[...]

    def tall_of(column):
        column = jnp.broadcast_to(column, (HEADS, 128)).reshape(HEADS, 1, 128)
        return jnp.broadcast_to(column, (HEADS, P_SIZE, 128)).reshape(HP, 128)

    for c in range(1, chunks):
        edge[0, c - 1] = tall_of(jnp.exp(ends[c] - ends[c - 1]))
        edge[1, c - 1] = tall_of(jnp.exp(ends[c - 1]))

    def send_decay(k, carry):
        decay_copy(lax.rem(rank + k, ndev)).start()
        return carry

    lax.fori_loop(1, ndev, send_decay, 0)

    def conv_column(block):
        q = jnp.where(block < groups, block + 1, (blocks - 1) * (block - groups))
        cols = pl.ds(pl.multiple_of(block * wide, wide), wide)

        def one(i, carry):
            start = pl.multiple_of(i * 128, 128)
            window = total[q, pl.ds(pl.multiple_of(start + tail_rows - 8, 8), 136), :]
            window = window.astype(BF16).astype(F32)
            acc = bias_row[:, cols]
            for k in range(CONV):
                acc = acc + half_w[k : k + 1, cols] * window[5 + k : 5 + k + 128]
            conv[pl.ds(start, 128), cols] = (acc + acc * jnp.tanh(acc)).astype(BF16)
            return carry

        lax.fori_loop(0, length // 128, one, 0)

    def score_all():
        def one(c, carry):
            here = pl.ds(pl.multiple_of(c * CHUNK, CHUNK), CHUNK)
            product = lax.dot_general(
                conv[here, HP + N :], conv[here, HP : HP + N], LAST,
                preferred_element_type=F32,
            )
            scores[c] = jnp.where(causal, product, 0.0)
            return carry

        lax.fori_loop(0, chunks, one, 0)

    heads_each = HEADS // groups

    def mix(c, j):
        here = pl.ds(pl.multiple_of(c * CHUNK, CHUNK), CHUNK)
        log_c = log_s[here]
        for k in range(heads_each):
            h = j * heads_each + k
            gap = jnp.minimum(log_c[:, h : h + 1] - log_t[h : h + 1, here], 60.0)
            mix_s[h, c] = (scores[c] * jnp.exp(gap)).astype(BF16)

    def contribute(j):
        cols = pl.ds(pl.multiple_of(j * wide, wide), wide)
        spread = spread_of(j, 2 * HEADS)
        state = None
        for c in range(chunks):
            here = slice(c * CHUNK, (c + 1) * CHUNK)
            factor = jnp.dot(fac_s[here], spread, preferred_element_type=F32)
            weighted = (factor * conv[here, cols].astype(F32)).astype(BF16)
            part = lax.dot_general(
                weighted, conv[here, HP : HP + N], FIRST, preferred_element_type=F32
            )
            if c > 0:
                local_s[c - 1, cols] = state
                scale = edge[0, c - 1, cols, :]
                part = part + jnp.concatenate([scale, scale], axis=1) * state
            state = part
        send1[j] = state.reshape(team, rows, N).astype(BF16)

        def send_one(o, inner):
            @pl.when(o != own)
            def _():
                first_copy(j, o).start()

            return inner

        lax.fori_loop(0, team, send_one, 0)

    def inside(j):
        cols = pl.ds(pl.multiple_of(j * wide, wide), wide)
        lane = lax.broadcasted_iota(jnp.int32, (1, wide), 1) // P_SIZE

        def one(c, carry):
            here = pl.ds(pl.multiple_of(c * CHUNK, CHUNK), CHUNK)
            x_rows = conv[here, cols]
            acc = skip_row[:, cols] * x_rows.astype(F32)
            for k in range(heads_each):
                keep = (lane == k).astype(F32).astype(BF16)
                acc = acc + jnp.dot(
                    mix_s[j * heads_each + k, c], x_rows * keep, preferred_element_type=F32
                )
            y[here, cols] = acc
            return carry

        lax.fori_loop(0, chunks, one, 0)

    def decay_of(k, half_of, j):
        r = lax.div(k, n // 2) * n + half_of * (n // 2) + lax.rem(k, n // 2)
        head = j * heads_each + lax.div(own * rows, P_SIZE)
        row = dec_recv[r, pl.ds(head, 1), :]
        return jnp.concatenate([row, row], axis=1)

    def combine(b):
        for j in range(groups)[batches[b]]:
            recv1[j, slot] = send1[j, own]

            def arrived(k, carry):
                @pl.when(k != slot)
                def _():
                    first_arrival(j, k)

                return carry

            lax.fori_loop(0, team, arrived, 0)
            for c in range(2):
                state = jnp.zeros((rows, N), F32)
                for m in range(n // 2):
                    k = c * (n // 2) + m
                    prefix[j, k] = state
                    state = decay_of(k, upper, j) * state + recv1[j, k].astype(F32)
                mid_send[c, j] = state.astype(BF16)
        mid_copy(b, 0).start()

        @pl.when(upper == 0)
        def _():
            mid_copy(b, 1).start()

    def product_of(c, half_of, j):
        result = decay_of(c * (n // 2), half_of, j)
        for m in range(1, n // 2):
            result = result * decay_of(c * (n // 2) + m, half_of, j)
        return result

    def distribute(b):
        mid_copy(b, 0).wait_recv()

        @pl.when(upper == 1)
        def _():
            mid_copy(b, 1).wait_recv()

        is_upper = upper == 1
        for j in range(groups)[batches[b]]:
            middle = mid_recv[0, j].astype(F32)
            ours = mid_send[0, j].astype(F32)
            lower_sum = jnp.where(is_upper, middle, ours)
            upper_sum = jnp.where(is_upper, ours, middle)
            block_end = product_of(0, 1, j) * lower_sum + upper_sum

            @pl.when(is_upper)
            def _():
                start[0, j] = middle
                start[1, j] = product_of(1, 0, j) * block_end + mid_recv[1, j].astype(F32)

            @pl.when(upper == 0)
            def _():
                start[0, j] = jnp.zeros((rows, N), F32)
                start[1, j] = block_end

        for k in range(team):
            for j in range(groups)[batches[b]]:
                state = start[k // (n // 2), j]
                send2[k, j] = (prefix[j, k] + state).astype(BF16)
                start[k // (n // 2), j] = decay_of(k, upper, j) * state

            @pl.when(k != slot)
            def _():
                second_copy(b, k).start()

        recv2[own, batches[b]] = send2[slot, batches[b]]

    def late_part(i, carry):
        exchange(i)
        accumulate(i)
        ready = first_part + core_lag

        @pl.when(i == ready)
        def _():
            conv_column(groups)

        @pl.when((i >= ready) & (i < ready + groups - 1))
        def _():
            conv_column(i - ready)
            contribute(i - ready)

        @pl.when(i == ready + groups - 1)
        def _():
            others()

        @pl.when(i == all_parts + 1)
        def _():
            combine(0)

        @pl.when(i == all_parts + core_lag - late)
        def _():
            conv_column(groups - 1)
            contribute(groups - 1)

        return carry

    def others():
        def one(k, carry):
            r = lax.rem(rank + k, ndev)
            arrive(dec_recv, rsd, r, place(r))
            return carry

        lax.fori_loop(1, ndev, one, 0)

    lax.fori_loop(10, all_parts + core_lag, late_part, 0)

    conv_column(groups + 1)
    score_all()

    def fill(j, carry):
        for k in range(groups):
            @pl.when(j == k)
            def _():
                def one(c, inner):
                    mix(c, k)
                    return inner

                lax.fori_loop(0, chunks, one, 0)

        inside(j)
        return carry

    lax.fori_loop(0, 1, fill, 0)
    distribute(0)
    lax.fori_loop(1, 2, fill, 0)
    combine(1)
    lax.fori_loop(2, groups, fill, 0)

    row_head = lax.broadcasted_iota(jnp.int32, (wide, wide), 0) // P_SIZE
    col_head = lax.broadcasted_iota(jnp.int32, (wide, wide), 1) // P_SIZE
    same = (row_head == col_head).astype(F32).astype(BF16)

    def out_copies(j):
        cols = pl.ds(pl.multiple_of(j * wide, wide), wide)
        return [
            pltpu.make_async_copy(
                mixed.at[:, cols], mixed_out.at[:, cols], out_sems.at[0, j]
            ),
            pltpu.make_async_copy(
                entry_out.at[cols], entry_all.at[cols], out_sems.at[1, j]
            ),
        ]

    def finish_group(j, carry):
        cols = pl.ds(pl.multiple_of(j * wide, wide), wide)
        entry = jnp.concatenate([recv2[o, j] for o in range(team)], axis=0).astype(F32)
        entry_out[cols] = entry
        spread = spread_of(j, 2 * HEADS)
        for c in range(chunks):
            here = slice(c * CHUNK, (c + 1) * CHUNK)
            state = entry
            if c > 0:
                scale = edge[1, c - 1, cols, :]
                state = local_s[c - 1, cols] + jnp.concatenate([scale, scale], axis=1) * entry
            carried = lax.dot_general(
                conv[here, HP + N :], state.astype(BF16), LAST, preferred_element_type=F32
            )
            reach = jnp.dot(reach_s[here], spread, preferred_element_type=F32)
            out = y[here, cols] + reach * carried
            square = (out * out).astype(BF16)
            sums = jnp.dot(square, same, preferred_element_type=F32)
            inv_rms = lax.rsqrt(sums * (1.0 / P_SIZE) + EPSILON)
            mixed[here, cols] = (out * inv_rms * gain_s[:, cols]).astype(BF16)
        for copy in out_copies(j):
            copy.start()
        return carry

    def wait_second(b):
        def one(o, carry):
            @pl.when(o != own)
            def _():
                second_arrival(b, o)

            return carry

        lax.fori_loop(0, team, one, 0)

    distribute(1)
    wait_second(0)
    lax.fori_loop(0, groups - 1, finish_group, 0)
    wait_second(1)
    lax.fori_loop(groups - 1, groups, finish_group, 0)

    def drain_out(j, carry):
        for copy in out_copies(j):
            copy.wait()
        return carry

    def drain(q, carry):
        for d in range(2):
            for s in range(1, steps + 1):
                whole = s < steps
                ring_copy(d, q, s, whole).wait_send()
                side_between(d, q, s, grp, whole).wait_send()
                core_between(d, q, s, core, whole).wait_send()
        return carry

    lax.fori_loop(0, blocks, drain, 0)

    def drain_dt(k, carry):
        dt_copy(k).wait_send()
        return carry

    lax.fori_loop(1, n, drain_dt, 0)

    def drain_decay(k, carry):
        decay_copy(lax.rem(rank + k, ndev)).wait_send()
        return carry

    lax.fori_loop(1, ndev, drain_decay, 0)

    def drain_state(k, carry):
        @pl.when(k != own)
        def _():
            for j in range(groups):
                first_copy(j, k).wait_send()

        @pl.when(k != slot)
        def _():
            for b in range(2):
                second_copy(b, k).wait_send()

        return carry

    lax.fori_loop(0, team, drain_state, 0)
    for b in range(2):
        mid_copy(b, 0).wait_send()

    @pl.when(upper == 0)
    def _():
        for b in range(2):
            mid_copy(b, 1).wait_send()

    @pl.when(rank < ndev - 1)
    def _():
        tail_copy().wait_send()

    lax.fori_loop(0, groups, drain_out, 0)


def run_fused(tokens, w_in, w_dt, conv_w, conv_b, dt_bias, a_log, d_skip, norm_gain):
    n, n_out = lax.axis_size("inner"), lax.axis_size("outer")
    ndev = n * n_out
    length, depth = tokens.shape
    local, xbc = w_in.shape
    team = ndev // 2
    groups = HP // 256
    rows = 256 // team
    tail_rows = 16
    blocks = xbc // 256
    chunks = length // CHUNK
    dma = pltpu.SemaphoreType.DMA
    whole = pl.BlockSpec(memory_space=pl.ANY)
    weight_sems = [dma((2, blocks, n // 2 + 1))] * 6
    first_sems = [dma((groups, team))] * 2
    swap_sems = [dma((2, 2))] * 2
    second_sems = [dma((2, team))] * 2
    rank_sems = [dma((ndev,))] * 2
    return pl.pallas_call(
        partial(fused_kernel, n, n_out),
        out_shape=(
            jax.ShapeDtypeStruct((length, HP), BF16),
            jax.ShapeDtypeStruct((HP, N), F32),
        ),
        in_specs=[whole] * 9,
        out_specs=(whole, whole),
        scratch_shapes=[
            pltpu.VMEM((CONV, xbc), F32), pltpu.VMEM((xbc,), F32),
            pltpu.VMEM((HEADS,), F32), pltpu.VMEM((HEADS,), F32),
            pltpu.VMEM((HEADS,), F32), pltpu.VMEM((HP,), F32),
            pltpu.VMEM((length, HP), BF16), pltpu.VMEM((HP, N), F32),
            pltpu.VMEM((length + tail_rows, depth), BF16),
            pltpu.VMEM((blocks, depth, 256), BF16),
            pltpu.VMEM((blocks, length + tail_rows, 256), F32),
            pltpu.VMEM((n, HEADS, local), BF16),
            pltpu.VMEM((length, HEADS), F32),
            pltpu.VMEM((CONV, xbc), F32),
            pltpu.VMEM((1, xbc), F32),
            pltpu.VMEM((1, HP), F32),
            pltpu.VMEM((1, HP), F32),
            pltpu.VMEM((length, xbc), BF16),
            pltpu.VMEM((length, 2 * HEADS), F32),
            pltpu.VMEM((HEADS, length), F32),
            pltpu.VMEM((length, 2 * HEADS), F32),
            pltpu.VMEM((length, 2 * HEADS), BF16),
            pltpu.VMEM((length, 2 * HEADS), BF16),
            pltpu.VMEM((2, chunks - 1, HP, 128), F32),
            pltpu.VMEM((chunks, CHUNK, CHUNK), F32),
            pltpu.VMEM((HEADS, chunks, CHUNK, CHUNK), BF16),
            pltpu.VMEM((chunks - 1, HP, N), F32),
            pltpu.VMEM((length, HP), F32),
            pltpu.VMEM((groups, team, rows, N), BF16),
            pltpu.VMEM((groups, team, rows, N), BF16),
            pltpu.VMEM((groups, team, rows, N), F32),
            pltpu.VMEM((2, groups, rows, N), BF16),
            pltpu.VMEM((2, groups, rows, N), BF16),
            pltpu.VMEM((2, groups, rows, N), F32),
            pltpu.VMEM((team, groups, rows, N), BF16),
            pltpu.VMEM((team, groups, rows, N), BF16),
            pltpu.VMEM((HEADS, 128), F32),
            pltpu.VMEM((ndev, HEADS, 128), F32),
            *weight_sems,
            dma((n,)), dma((n,)), dma((blocks + 1,)), dma(()), dma(()),
            *first_sems, *swap_sems, *second_sems, *rank_sems, dma((7,)), dma((2, groups)),
        ],
        compiler_params=pltpu.CompilerParams(
            collective_id=3, has_side_effects=True, vmem_limit_bytes=62 * 2**20
        ),
        name="fused",
    )(
        tokens, w_in, w_dt.T, conv_w, conv_b, dt_bias, a_log, d_skip, norm_gain,
    )


def hand_over_kernel(
    mixed, entry, mixed_out, entry_out, held_m, held_e, in_sems, out_sems
):
    parts = in_sems.shape[1]
    loads, stores = [], []
    arrays = ((mixed, held_m, mixed_out), (entry, held_e, entry_out))
    for i, (source, held, target) in enumerate(arrays):
        rows = source.shape[0] // parts
        for k in range(parts):
            at = pl.ds(k * rows, rows)
            loads.append(pltpu.make_async_copy(source.at[at], held.at[at], in_sems.at[i, k]))
            stores.append(pltpu.make_async_copy(held.at[at], target.at[at], out_sems.at[i, k]))
    for load in loads:
        load.start()
    for load, store in zip(loads, stores):
        load.wait()
        store.start()
    for store in stores:
        store.wait()


def hand_over(mixed, entry):
    whole = pl.BlockSpec(memory_space=pl.ANY)
    sems = pltpu.SemaphoreType.DMA((2, 4))
    return pl.pallas_call(
        hand_over_kernel,
        out_shape=(
            jax.ShapeDtypeStruct(mixed.shape, mixed.dtype),
            jax.ShapeDtypeStruct(entry.shape, entry.dtype),
        ),
        in_specs=[whole, whole],
        out_specs=(whole, whole),
        scratch_shapes=[
            pltpu.VMEM(mixed.shape, mixed.dtype), pltpu.VMEM(entry.shape, entry.dtype),
            sems, sems,
        ],
        name="hand_over",
    )(mixed, entry)


def per_device(tokens, w_in, w_dt, conv_w, conv_b, dt_bias, a_log, d_skip, norm_gain):
    own_rows = tokens.reshape(tokens.shape[1], tokens.shape[2])
    row_count = own_rows.shape[0]
    if w_in.shape[0] % 512 == 0 and lax.axis_size("inner") == 8:
        mixed, entry = run_fused(
            own_rows, w_in, w_dt, conv_w, conv_b, dt_bias, a_log, d_skip, norm_gain
        )
        mixed, entry = hand_over(mixed, entry)
    else:
        projected, tail, dt_raw = run_project(own_rows, w_in, w_dt)
        mixed, entry = run_scan(
            projected, tail, dt_raw, conv_w, conv_b, dt_bias, a_log, d_skip, norm_gain
        )
    return (
        mixed.reshape(1, row_count, HP),
        entry.reshape(1, 1, HEADS, P_SIZE, N),
    )


def solution(mesh):
    placed = (
        P(("grp", "outer"), "inner", None),
        P("inner", None),
        P("inner", None),
        P(), P(), P(), P(), P(), P(),
    )
    return jax.shard_map(
        per_device,
        mesh=mesh,
        in_specs=placed,
        out_specs=(
            P(("grp", "outer"), "inner", None),
            P(("grp", "outer"), "inner", None, None, None),
        ),
        check_vma=False,
    )
```

```python
from functools import partial

import jax
import jax.numpy as jnp
from jax import lax
from jax.experimental import pallas as pl
from jax.experimental.pallas import tpu as pltpu
from jax.sharding import PartitionSpec as P

HEADS = 16
P_SIZE = 64
N = 256
CONV = 4
HP = HEADS * P_SIZE
CHUNK = 256
EPSILON = 1e-05
MESH = pl.DeviceIdType.MESH
F32 = jnp.float32
BF16 = jnp.bfloat16
LAST = (((1,), (1,)), ((), ()))
FIRST = (((0,), (0,)), ((), ()))


def expand(values, spread):
    high = values.astype(BF16)
    low = (values - high.astype(F32)).astype(BF16)
    return jnp.dot(high, spread, preferred_element_type=F32) + jnp.dot(
        low, spread, preferred_element_type=F32
    )


def scan_kernel(
    n_in, ndev,
    proj, tail, dt_raw, conv_w, conv_b, dt_bias, a_log, d_skip, gain,
    mixed, entry_out,
    gain_s, bias_row, skip_row, pad, conv, log_s, log_t, step_s, y, states,
    send1, recv1, send2, recv2, dec_send, dec_recv,
    ss1, rs1, ss2, rs2, ssd, rsd,
):
    length = proj.shape[0]
    chunks = length // CHUNK
    rows = HP // ndev
    me = lax.axis_index("outer") * n_in + lax.axis_index("inner")

    def place(g):
        return {"inner": lax.rem(g, n_in), "outer": lax.div(g, n_in)}

    barrier = pltpu.get_barrier_semaphore()

    def greet(k, carry):
        pl.semaphore_signal(
            barrier, inc=1, device_id=place(lax.rem(me + k, ndev)), device_id_type=MESH
        )
        return carry

    lax.fori_loop(1, ndev, greet, 0)

    head_id = lax.broadcasted_iota(jnp.int32, (HEADS, HP), 0)
    col_head = lax.broadcasted_iota(jnp.int32, (HEADS, HP), 1) // P_SIZE
    spread = (head_id == col_head).astype(F32).astype(BF16)

    bias_row[...] = conv_b[...].reshape(1, conv_b.shape[0])
    gain_s[...] = gain[...].reshape(1, HP)
    skip = d_skip[...].reshape(1, HEADS)
    skip_high = skip.astype(BF16).astype(F32)
    skip_row[...] = expand(skip - skip_high, spread) + jnp.dot(
        skip_high.astype(BF16), spread, preferred_element_type=F32
    )
    step_size = jax.nn.softplus(dt_raw[...].astype(F32) + dt_bias[...].reshape(1, HEADS))
    scaled = step_size * (-jnp.exp(a_log[...].reshape(1, HEADS)))
    row_id = lax.broadcasted_iota(jnp.int32, (CHUNK, CHUNK), 0)
    col_id = lax.broadcasted_iota(jnp.int32, (CHUNK, CHUNK), 1)
    causal = col_id <= row_id
    lower = causal.astype(F32)
    step_s[...] = step_size
    before = jnp.zeros((1, HEADS), F32)
    for c in range(chunks):
        part = jnp.dot(
            lower,
            scaled[c * CHUNK : (c + 1) * CHUNK],
            preferred_element_type=F32,
            precision=lax.Precision.HIGHEST,
        ) + before
        log_s[c * CHUNK : (c + 1) * CHUNK] = part
        before = part[CHUNK - 1 : CHUNK]
    log_t[...] = jnp.transpose(log_s[...])
    dec_send[...] = jnp.broadcast_to(jnp.exp(log_t[:, length - 1 : length]), (HEADS, 128))

    pad[0:8] = tail[...].astype(F32)[8:16]
    pad[8:] = proj[...].astype(F32)
    wide = 256
    blocks = proj.shape[1] // wide

    def conv_block(t, carry):
        i, j = lax.div(t, blocks), lax.rem(t, blocks)
        cols = pl.ds(pl.multiple_of(j * wide, wide), wide)
        window = pad[pl.ds(pl.multiple_of(i * 128, 128), 136), cols]
        total = bias_row[:, cols]
        for k in range(CONV):
            total = total + conv_w[k : k + 1, cols] * window[5 + k : 5 + k + 128]
        conv[pl.ds(pl.multiple_of(i * 128, 128), 128), cols] = (
            total * jax.nn.sigmoid(total)
        ).astype(BF16)
        return carry

    row_blocks = length // 128

    def conv_column(j):
        def one(i, carry):
            return conv_block(i * blocks + j, carry)

        lax.fori_loop(0, row_blocks, one, 0)

    conv_column(HP // wide)

    def weighted_sum(stop):
        final = log_s[stop - 1 : stop]
        factor = jnp.exp(final - log_s[0:stop]) * step_s[0:stop]
        weighted = (expand(factor, spread) * conv[0:stop, 0:HP].astype(F32)).astype(BF16)
        return lax.dot_general(
            weighted, conv[0:stop, HP : HP + N], FIRST, preferred_element_type=F32
        )

    dec_recv[me] = dec_send[...]

    def decay_copy(g):
        return pltpu.make_async_remote_copy(
            src_ref=dec_send, dst_ref=dec_recv.at[me], send_sem=ssd.at[g],
            recv_sem=rsd.at[me], device_id=place(g), device_id_type=MESH,
        )

    def first_copy(g):
        return pltpu.make_async_remote_copy(
            src_ref=send1.at[g], dst_ref=recv1.at[me], send_sem=ss1.at[g],
            recv_sem=rs1.at[me], device_id=place(g), device_id_type=MESH,
        )

    def second_copy(g):
        return pltpu.make_async_remote_copy(
            src_ref=send2.at[g], dst_ref=recv2.at[me], send_sem=ss2.at[g],
            recv_sem=rs2.at[me], device_id=place(g), device_id_type=MESH,
        )

    pl.semaphore_wait(barrier, ndev - 1)

    def send_decay(k, carry):
        decay_copy(lax.rem(me + k, ndev)).start()
        return carry

    lax.fori_loop(1, ndev, send_decay, 0)

    groups = HP // wide
    owners = ndev // groups
    own_group = lax.div(me, owners)
    factor = jnp.exp(log_s[length - 1 : length] - log_s[...]) * step_s[...]

    def spread_of(j):
        head = lax.broadcasted_iota(jnp.int32, (HEADS, wide), 0)
        col = lax.broadcasted_iota(jnp.int32, (HEADS, wide), 1) // P_SIZE
        return (head == col + j * (wide // P_SIZE)).astype(F32).astype(BF16)

    def first_group(i, carry):
        j = lax.rem(own_group + 1 + i, groups)
        conv_column(j)
        cols = pl.ds(pl.multiple_of(j * wide, wide), wide)
        weighted = (expand(factor, spread_of(j)) * conv[:, cols].astype(F32)).astype(BF16)
        part = lax.dot_general(
            weighted, conv[:, HP : HP + N], FIRST, preferred_element_type=F32
        )
        send1[pl.ds(j * owners, owners)] = part.reshape(owners, rows, N).astype(BF16)

        def send_one(k, inner):
            g = j * owners + k

            @pl.when(g != me)
            def _():
                first_copy(g).start()

            return inner

        return lax.fori_loop(0, owners, send_one, carry)

    lax.fori_loop(0, groups, first_group, 0)
    recv1[me] = send1[me]
    conv_column(HP // wide + 1)

    states[0] = jnp.zeros((HP, N), BF16)
    for c in range(1, chunks):
        states[c] = weighted_sum(c * CHUNK).astype(BF16)

    def local_chunk(c, carry):
        start = pl.multiple_of(c * CHUNK, CHUNK)
        here = pl.ds(start, CHUNK)
        log_c = log_s[here]
        reached = log_s[pl.ds(pl.multiple_of(jnp.maximum(start - 8, 0), 8), 8)][7:8]
        reached = jnp.where(c > 0, reached, 0.0)
        c_rows = conv[here, HP + N :]
        b_rows = conv[here, HP : HP + N]
        scores = lax.dot_general(c_rows, b_rows, LAST, preferred_element_type=F32)
        scores = jnp.where(causal, scores, 0.0)
        x_rows = conv[here, 0:HP].astype(F32)
        driven = (expand(step_s[here], spread) * x_rows).astype(BF16)
        inter = lax.dot_general(c_rows, states[c], LAST, preferred_element_type=F32)
        y[here] = expand(jnp.exp(log_c - reached), spread) * inter + skip_row[...] * x_rows
        for h in range(0, HEADS, 2):
            pieces = []
            for k in (h, h + 1):
                gap = jnp.minimum(log_c[:, k : k + 1] - log_t[k : k + 1, here], 0.0)
                mixing = (scores * jnp.exp(gap)).astype(BF16)
                pieces.append(
                    jnp.dot(
                        mixing,
                        driven[:, k * P_SIZE : (k + 1) * P_SIZE],
                        preferred_element_type=F32,
                    )
                )
            both = slice(h * P_SIZE, (h + 2) * P_SIZE)
            y[here, both] = y[here, both] + jnp.concatenate(pieces, axis=1)
        return carry

    lax.fori_loop(0, chunks, local_chunk, 0)

    own_head = lax.div(me * rows, P_SIZE)

    def wait_from(copy_of, r):
        copy_of(r).wait_recv()

    def arrive(buffer, sems, r):
        pltpu.make_async_remote_copy(
            src_ref=buffer.at[r], dst_ref=buffer.at[r], send_sem=sems.at[r],
            recv_sem=sems.at[r], device_id=place(r), device_id_type=MESH,
        ).wait_recv()

    def advance(r, state):
        send2[r] = state.astype(BF16)

        @pl.when(r != me)
        def _():
            arrive(dec_recv, rsd, r)
            arrive(recv1, rs1, r)

        decay = dec_recv[r, pl.ds(own_head, 1), :]
        decay = jnp.concatenate([decay, decay], axis=1)
        return decay * state + recv1[r].astype(F32)

    lax.fori_loop(0, ndev, advance, jnp.zeros((rows, N), F32))

    def send_second(k, carry):
        second_copy(lax.rem(me + k, ndev)).start()
        return carry

    lax.fori_loop(1, ndev, send_second, 0)
    recv2[me] = send2[me]

    reach = jnp.exp(log_s[...])

    def last_group(i, carry):
        j = lax.rem(own_group + groups - 1 - i, groups)

        def wait_one(k, inner):
            g = j * owners + k

            @pl.when(g != me)
            def _():
                arrive(recv2, rs2, g)

            return inner

        lax.fori_loop(0, owners, wait_one, 0)
        cols = pl.ds(pl.multiple_of(j * wide, wide), wide)
        entry = recv2[pl.ds(j * owners, owners)].astype(F32).reshape(wide, N)
        entry_out[cols] = entry
        carried = lax.dot_general(
            conv[:, HP + N :], entry.astype(BF16), LAST, preferred_element_type=F32
        )
        spread_j = spread_of(j)
        out = y[:, cols] + expand(reach, spread_j) * carried
        square = out * out
        high = square.astype(BF16)
        low = (square - high.astype(F32)).astype(BF16)
        sums = lax.dot_general(high, spread_j, LAST, preferred_element_type=F32)
        sums = sums + lax.dot_general(low, spread_j, LAST, preferred_element_type=F32)
        inv_rms = lax.rsqrt(sums * (1.0 / P_SIZE) + EPSILON)
        mixed[:, cols] = (out * expand(inv_rms, spread_j) * gain_s[:, cols]).astype(BF16)
        return carry

    lax.fori_loop(0, groups, last_group, 0)

    def finish(k, carry):
        g = lax.rem(me + k, ndev)
        decay_copy(g).wait_send()
        first_copy(g).wait_send()
        second_copy(g).wait_send()
        return carry

    lax.fori_loop(1, ndev, finish, 0)


def run_scan(projected, tail, dt_raw, conv_w, conv_b, dt_bias, a_log, d_skip, norm_gain):
    n_in, n_out = lax.axis_size("inner"), lax.axis_size("outer")
    ndev = n_in * n_out
    length, xbc = projected.shape
    rows = HP // ndev
    dma = pltpu.SemaphoreType.DMA((ndev,))
    vmem = pl.BlockSpec(memory_space=pltpu.VMEM)
    return pl.pallas_call(
        partial(scan_kernel, n_in, ndev),
        out_shape=(
            jax.ShapeDtypeStruct((length, HP), BF16),
            jax.ShapeDtypeStruct((HP, N), F32),
        ),
        in_specs=[vmem] * 9,
        out_specs=(vmem, vmem),
        scratch_shapes=[
            pltpu.VMEM((1, HP), F32),
            pltpu.VMEM((1, xbc), F32),
            pltpu.VMEM((1, HP), F32),
            pltpu.VMEM((length + 8, xbc), F32),
            pltpu.VMEM((length, xbc), BF16),
            pltpu.VMEM((length, HEADS), F32),
            pltpu.VMEM((HEADS, length), F32),
            pltpu.VMEM((length, HEADS), F32),
            pltpu.VMEM((length, HP), F32),
            pltpu.VMEM((length // CHUNK, HP, N), BF16),
            pltpu.VMEM((ndev, rows, N), BF16),
            pltpu.VMEM((ndev, rows, N), BF16),
            pltpu.VMEM((ndev, rows, N), BF16),
            pltpu.VMEM((ndev, rows, N), BF16),
            pltpu.VMEM((HEADS, 128), F32),
            pltpu.VMEM((ndev, HEADS, 128), F32),
            dma, dma, dma, dma, dma, dma,
        ],
        compiler_params=pltpu.CompilerParams(
            collective_id=1, has_side_effects=True, vmem_limit_bytes=60 * 2**20
        ),
        name="scan",
    )(
        projected, tail, dt_raw, conv_w, conv_b, dt_bias, a_log, d_skip, norm_gain,
    )


def project_kernel(
    n, n_out,
    tokens, w_in, w_dt,
    proj, tail, dt_out,
    tok, held, total, held_dt,
    ring_s, ring_r, side_s, side_r, core_s, core_r, dt_s, dt_r, misc, tail_s, tail_r,
):
    length, depth = tokens.shape
    local, xbc = w_in.shape
    half = xbc // 2
    quarter = half // 2
    lanes = 128
    streams = quarter // lanes
    wide = 256
    tiles = half // wide
    third = (local * 5 // 16) // 16 * 16
    ring_rows = local - third
    tail_rows = tok.shape[0] - length
    block = held_dt.shape[2]
    ndev = n * n_out
    me = lax.axis_index("inner")
    core = lax.axis_index("outer")
    grp = lax.axis_index("grp")
    rank = core * n + me
    odd = lax.rem(me, 2)
    pos = jnp.where(odd == 0, lax.div(me, 2), n - lax.div(me + 1, 2))

    def index_at(q):
        q = lax.rem(q + 2 * n, n)
        return jnp.where(q < n // 2, 2 * q, 2 * n - 1 - 2 * q)

    def place(g):
        return {"inner": lax.rem(g, n), "outer": lax.div(g, n)}

    barrier = pltpu.get_barrier_semaphore()

    def greet(k, carry):
        pl.semaphore_signal(
            barrier, inc=1, device_id=place(lax.rem(rank + k, ndev)), device_id_type=MESH
        )
        return carry

    lax.fori_loop(1, ndev, greet, 0)
    pl.semaphore_signal(barrier, inc=1, device_id={"grp": 1 - grp}, device_id_type=MESH)

    def own_rows(owner):
        return pl.ds(pl.multiple_of(owner * local, 16), local)

    load_tok = pltpu.make_async_copy(tokens, tok.at[pl.ds(0, length)], misc.at[0])
    load_w = [
        pltpu.make_async_copy(
            w_in.at[:, pl.ds(d * half, half)], held.at[d, own_rows(me)], misc.at[1 + d]
        )
        for d in range(2)
    ]
    for copy in load_w:
        copy.start()
    load_tok.start()
    held_dt[me] = w_dt[...]

    @pl.when(rank == 0)
    def _():
        tok[length:] = jnp.zeros((tail_rows, depth), BF16)

    def ring_copy(d, t, s):
        owner = index_at(pos - (s - 1)) if d == 0 else index_at(pos + (s - 1))
        target = index_at(pos + 1) if d == 0 else index_at(pos - 1)
        rows = pl.ds(pl.multiple_of(owner * local + grp * third, 16), ring_rows)
        cols = pl.ds(pl.multiple_of(core * quarter + t * lanes, lanes), lanes)
        part = held.at[d, rows, cols]
        return pltpu.make_async_remote_copy(
            src_ref=part, dst_ref=part, send_sem=ring_s.at[d, t, s],
            recv_sem=ring_r.at[d, t, s], device_id={"inner": target}, device_id_type=MESH,
        )

    def owner_of(d, s):
        return index_at(pos - s) if d == 0 else index_at(pos + s)

    def chunk_cols(which, t):
        return pl.ds(pl.multiple_of(which * quarter + t * lanes, lanes), lanes)

    def side_rows(d, s, which):
        start = owner_of(d, s) * local + which * ring_rows
        return pl.ds(pl.multiple_of(start, 16), third)

    def side_between(d, t, s, which):
        part = held.at[d, side_rows(d, s, which), chunk_cols(core, t)]
        return pltpu.make_async_remote_copy(
            src_ref=part, dst_ref=part, send_sem=side_s.at[d, t, s],
            recv_sem=side_r.at[d, t, s], device_id={"grp": 1 - grp}, device_id_type=MESH,
        )

    def core_between(d, t, s, which):
        part = held.at[d, own_rows(owner_of(d, s)), chunk_cols(which, t)]
        return pltpu.make_async_remote_copy(
            src_ref=part, dst_ref=part, send_sem=core_s.at[d, t, s],
            recv_sem=core_r.at[d, t, s], device_id={"outer": 1 - core}, device_id_type=MESH,
        )

    def side_copy(d, t, s):
        return side_between(d, t, s, grp)

    def core_copy(d, t, s):
        return core_between(d, t, s, core)

    def ring_arrival(d, t, s):
        start = owner_of(d, s) * local + grp * third
        rows = pl.ds(pl.multiple_of(start, 16), ring_rows)
        part = held.at[d, rows, chunk_cols(core, t)]
        pltpu.make_async_remote_copy(
            src_ref=part, dst_ref=part, send_sem=ring_s.at[d, t, s],
            recv_sem=ring_r.at[d, t, s], device_id={"inner": index_at(pos + 1)},
            device_id_type=MESH,
        ).wait_recv()

    def side_arrival(d, t, s):
        side_between(d, t, s, 1 - grp).wait_recv()

    def core_arrival(d, t, s):
        core_between(d, t, s, 1 - core).wait_recv()

    def dt_copy(k):
        peer = lax.rem(me + k, n)
        return pltpu.make_async_remote_copy(
            src_ref=w_dt, dst_ref=held_dt.at[me], send_sem=dt_s.at[k],
            recv_sem=dt_r.at[me], device_id={"inner": peer}, device_id_type=MESH,
        )

    def dt_arrival(k):
        peer = lax.rem(me + k, n)
        pltpu.make_async_remote_copy(
            src_ref=w_dt, dst_ref=held_dt.at[peer], send_sem=dt_s.at[k],
            recv_sem=dt_r.at[peer], device_id={"inner": peer}, device_id_type=MESH,
        ).wait_recv()

    def tail_copy():
        return pltpu.make_async_remote_copy(
            src_ref=tokens.at[pl.ds(length - tail_rows, tail_rows)],
            dst_ref=tok.at[pl.ds(length, tail_rows)], send_sem=tail_s,
            recv_sem=tail_r, device_id=place(lax.rem(rank + 1, ndev)), device_id_type=MESH,
        )

    pl.semaphore_wait(barrier, ndev)

    @pl.when(rank < ndev - 1)
    def _():
        tail_copy().start()

    for d in range(2):
        load_w[d].wait()
        for t in range(streams):
            ring_copy(d, t, 1).start()

    def send_dt(k, carry):
        dt_copy(k).start()
        return carry

    lax.fori_loop(1, n, send_dt, 0)
    load_tok.wait()

    @pl.when(rank > 0)
    def _():
        tail_copy().wait_recv()

    incremental = local % 128 == 0

    def multiply_tile(d, lhs_cols, rhs_rows, first, j):
        cols = pl.ds(pl.multiple_of(j * wide, wide), wide)
        product = jnp.dot(
            tok[:, lhs_cols], held[d, rhs_rows, cols], preferred_element_type=F32
        )
        at = d * tiles + j
        if first:
            total[at] = product
        else:
            total[at] = total[at] + product

    def multiply(d, lhs_cols, rhs_rows, first):
        def tile(j, carry):
            multiply_tile(d, lhs_cols, rhs_rows, first, j)
            return carry

        lax.fori_loop(0, tiles, tile, 0)

    def project_dt():
        def arrived(k, carry):
            dt_arrival(k)
            return carry

        lax.fori_loop(1, n, arrived, 0)
        together = block // local

        def add(j, sums):
            cols = pl.ds(pl.multiple_of(j * block, block), block)
            piece = held_dt[j * together]
            for m in range(1, together):
                piece = piece + held_dt[j * together + m]
            return sums + lax.dot_general(
                tok[0:length, cols], piece, LAST, preferred_element_type=F32
            )

        sums = lax.fori_loop(0, depth // block, add, jnp.zeros((length, HEADS), F32))
        dt_out[...] = sums.astype(BF16)

    def step(s, carry):
        @pl.when(s >= 3)
        def _():
            for t in range(streams):
                for d in range(2):
                    core_arrival(d, t, s - 2)

        def part(t, inner):
            @pl.when(s < n)
            def _():
                for d in range(2):
                    ring_arrival(d, t, s)

                    @pl.when(s < n - 1)
                    def _():
                        ring_copy(d, t, s + 1).start()

                    side_copy(d, t, s).start()

            @pl.when((s >= 2) & (s <= n))
            def _():
                for d in range(2):
                    side_arrival(d, t, s - 1)
                    core_copy(d, t, s - 1).start()

            if incremental:
                for d in range(2):
                    owner = owner_of(d, s - 2)
                    at = pl.ds(pl.multiple_of(owner * local, 128), local)

                    @pl.when(s == 2)
                    def _():
                        multiply_tile(d, at, at, True, t)

                    @pl.when(s > 2)
                    def _():
                        multiply_tile(d, at, at, False, t)

            return inner

        lax.fori_loop(0, streams, part, 0)

        @pl.when(s == 1)
        def _():
            project_dt()

        return carry

    lax.fori_loop(1, n + 2, step, 0)
    if not incremental:
        for d in range(2):
            multiply(d, slice(0, 512), slice(0, 512), True)

            def more(j, carry):
                at = pl.ds(pl.multiple_of(j * 512, 512), 512)
                multiply(d, at, at, False)
                return carry

            lax.fori_loop(1, depth // 512, more, 0)

    for j in range(2 * tiles):
        cols = slice(j * wide, (j + 1) * wide)
        proj[:, cols] = total[j, 0:length].astype(BF16)
        tail[:, cols] = total[j, length:].astype(BF16)

    def drain(s, carry):
        for d in range(2):
            for t in range(streams):
                ring_copy(d, t, s).wait_send()
                side_copy(d, t, s).wait_send()
                core_copy(d, t, s).wait_send()
        dt_copy(s).wait_send()
        return carry

    lax.fori_loop(1, n, drain, 0)

    @pl.when(rank < ndev - 1)
    def _():
        tail_copy().wait_send()


def run_project(tokens, w_in, w_dt):
    n, n_out = lax.axis_size("inner"), lax.axis_size("outer")
    length, depth = tokens.shape
    local, xbc = w_in.shape
    block = max(local, 128)
    tail_rows = 16
    dt_block = w_dt.T
    if block != local:
        start = lax.rem(lax.axis_index("inner") * local, block)
        dt_block = lax.dynamic_update_slice(
            jnp.zeros((HEADS, block), BF16), dt_block, (jnp.int32(0), start)
        )
    streams = xbc // 4 // 128
    dma = pltpu.SemaphoreType.DMA
    vmem = pl.BlockSpec(memory_space=pltpu.VMEM)
    whole = pl.BlockSpec(memory_space=pl.ANY)
    return pl.pallas_call(
        partial(project_kernel, n, n_out),
        out_shape=(
            jax.ShapeDtypeStruct((length, xbc), BF16),
            jax.ShapeDtypeStruct((tail_rows, xbc), BF16),
            jax.ShapeDtypeStruct((length, HEADS), BF16),
        ),
        in_specs=[whole, whole, vmem],
        out_specs=(vmem, vmem, vmem),
        scratch_shapes=[
            pltpu.VMEM((length + tail_rows, depth), BF16),
            pltpu.VMEM((2, depth, xbc // 2), BF16),
            pltpu.VMEM((xbc // 256, length + tail_rows, 256), F32),
            pltpu.VMEM((n, HEADS, block), BF16),
            dma((2, streams, n)), dma((2, streams, n)),
            dma((2, streams, n)), dma((2, streams, n)),
            dma((2, streams, n)), dma((2, streams, n)),
            dma((n,)), dma((n,)), dma((3,)), dma(()), dma(()),
        ],
        compiler_params=pltpu.CompilerParams(
            collective_id=2, has_side_effects=True, vmem_limit_bytes=60 * 2**20
        ),
        name="project",
    )(tokens, w_in, dt_block)


def fused_kernel(
    n, n_out,
    tokens, w_in, w_dt, conv_w_in, conv_b_in, dt_bias_in, a_log_in, d_skip_in, gain_in,
    mixed_out, entry_all,
    conv_w, conv_b, dt_bias, a_log, d_skip, gain, mixed, entry_out,
    tok, held, total, held_dt, dt_acc, half_w, bias_row, gain_s, skip_row,
    conv, log_s, log_t, step_s, fac_s, reach_s, edge, scores, mix_s, local_s, y,
    send1, recv1, prefix, mid_send, mid_recv, start, send2, recv2, dec_send, dec_recv,
    ring_s, ring_r, side_s, side_r, core_s, core_r, dt_s, dt_r, misc, tail_s, tail_r,
    ss1, rs1, ssm, rsm, ss2, rs2, ssd, rsd, small, out_sems,
):
    length, depth = tokens.shape
    local, xbc = w_in.shape
    tail_rows = tok.shape[0] - length
    wide, lanes = 256, 128
    blocks = xbc // wide
    groups = HP // wide
    early = groups
    late = blocks - early
    steps = n // 2
    half = local // 2
    third = (half * 5 // 16) // 16 * 16
    chunks = length // CHUNK
    ndev = n * n_out
    team = ndev // 2
    rows = wide // team
    me = lax.axis_index("inner")
    core = lax.axis_index("outer")
    grp = lax.axis_index("grp")
    rank = core * n + me
    odd = lax.rem(me, 2)
    pos = jnp.where(odd == 0, lax.div(me, 2), n - lax.div(me + 1, 2))
    upper = lax.div(me, n // 2)
    base = upper * (n // 2)
    own = (me - base) * n_out + core
    slot = core * (n // 2) + me - base

    def index_at(q):
        q = lax.rem(q + 2 * n, n)
        return jnp.where(q < n // 2, 2 * q, 2 * n - 1 - 2 * q)

    def place(g):
        return {"inner": lax.rem(g, n), "outer": lax.div(g, n)}

    barrier = pltpu.get_barrier_semaphore()

    def greet(k, carry):
        pl.semaphore_signal(
            barrier, inc=1, device_id=place(lax.rem(rank + k, ndev)), device_id_type=MESH
        )
        return carry

    lax.fori_loop(1, ndev, greet, 0)
    pl.semaphore_signal(barrier, inc=1, device_id={"grp": 1 - grp}, device_id_type=MESH)

    own_rows = pl.ds(pl.multiple_of(me * local, local), local)

    def natural(q):
        return groups if q == 0 else (blocks - 1 if q == blocks - 1 else q - 1)

    load_tok = pltpu.make_async_copy(
        tokens, tok.at[pl.ds(tail_rows, length)], misc.at[blocks]
    )
    load_w = [
        pltpu.make_async_copy(
            w_in.at[:, pl.ds(natural(q) * wide, wide)],
            held.at[q, own_rows], misc.at[q],
        )
        for q in range(blocks)
    ]
    for copy in load_w:
        copy.start()
    load_small = [
        pltpu.make_async_copy(source, target, small.at[k])
        for k, (source, target) in enumerate((
            (w_dt, held_dt.at[me]), (conv_w_in, conv_w), (conv_b_in, conv_b),
            (dt_bias_in, dt_bias), (a_log_in, a_log), (d_skip_in, d_skip), (gain_in, gain),
        ))
    ]
    for copy in load_small:
        copy.start()
    load_tok.start()

    @pl.when(rank == 0)
    def _():
        tok[0:tail_rows] = jnp.zeros((tail_rows, depth), BF16)

    def owner_of(d, s):
        return index_at(pos - s) if d == 0 else index_at(pos + s)

    def share(whole):
        return third if whole else half // 2

    def columns(d, whole):
        return slice(0, wide) if whole else slice(d * lanes, (d + 1) * lanes)

    def ring_between(d, q, s, source, whole):
        start = owner_of(d, source) * local + core * half + grp * share(whole)
        span = pl.ds(pl.multiple_of(start, 16), half - share(whole))
        part = held.at[q, span, columns(d, whole)]
        target = index_at(pos + 1) if d == 0 else index_at(pos - 1)
        return pltpu.make_async_remote_copy(
            src_ref=part, dst_ref=part, send_sem=ring_s.at[d, q, s],
            recv_sem=ring_r.at[d, q, s], device_id={"inner": target}, device_id_type=MESH,
        )

    def ring_copy(d, q, s, whole):
        return ring_between(d, q, s, s - 1, whole)

    def side_between(d, q, s, which, whole):
        start = owner_of(d, s) * local + core * half + which * (half - share(whole))
        span = pl.ds(pl.multiple_of(start, 16), share(whole))
        part = held.at[q, span, columns(d, whole)]
        return pltpu.make_async_remote_copy(
            src_ref=part, dst_ref=part, send_sem=side_s.at[d, q, s],
            recv_sem=side_r.at[d, q, s], device_id={"grp": 1 - grp}, device_id_type=MESH,
        )

    def core_between(d, q, s, which, whole):
        start = owner_of(d, s) * local + which * half
        part = held.at[q, pl.ds(pl.multiple_of(start, 16), half), columns(d, whole)]
        return pltpu.make_async_remote_copy(
            src_ref=part, dst_ref=part, send_sem=core_s.at[d, q, s],
            recv_sem=core_r.at[d, q, s], device_id={"outer": 1 - core}, device_id_type=MESH,
        )

    def dt_copy(k):
        peer = lax.rem(me + k, n)
        return pltpu.make_async_remote_copy(
            src_ref=w_dt, dst_ref=held_dt.at[me], send_sem=dt_s.at[k],
            recv_sem=dt_r.at[me], device_id={"inner": peer}, device_id_type=MESH,
        )

    def dt_arrival(k):
        peer = lax.rem(me + k, n)
        pltpu.make_async_remote_copy(
            src_ref=w_dt, dst_ref=held_dt.at[peer], send_sem=dt_s.at[k],
            recv_sem=dt_r.at[peer], device_id={"inner": peer}, device_id_type=MESH,
        ).wait_recv()

    def tail_copy():
        return pltpu.make_async_remote_copy(
            src_ref=tokens.at[pl.ds(length - tail_rows, tail_rows)],
            dst_ref=tok.at[pl.ds(0, tail_rows)], send_sem=tail_s,
            recv_sem=tail_r, device_id=place(lax.rem(rank + 1, ndev)), device_id_type=MESH,
        )

    def decay_copy(g):
        return pltpu.make_async_remote_copy(
            src_ref=dec_send, dst_ref=dec_recv.at[rank], send_sem=ssd.at[g],
            recv_sem=rsd.at[rank], device_id=place(g), device_id_type=MESH,
        )

    def member(o):
        return {"inner": base + lax.div(o, n_out), "outer": lax.rem(o, n_out)}

    def member_at(k):
        return {"inner": base + lax.rem(k, n // 2), "outer": lax.div(k, n // 2)}

    def first_copy(j, o):
        return pltpu.make_async_remote_copy(
            src_ref=send1.at[j, o], dst_ref=recv1.at[j, slot], send_sem=ss1.at[j, o],
            recv_sem=rs1.at[j, slot], device_id=member(o), device_id_type=MESH,
        )

    def first_arrival(j, k):
        pltpu.make_async_remote_copy(
            src_ref=send1.at[j, k], dst_ref=recv1.at[j, k], send_sem=ss1.at[j, k],
            recv_sem=rs1.at[j, k], device_id=member_at(k), device_id_type=MESH,
        ).wait_recv()

    batches = [slice(0, groups - 1), slice(groups - 1, groups)]

    def mid_copy(b, c):
        return pltpu.make_async_remote_copy(
            src_ref=mid_send.at[c, batches[b]], dst_ref=mid_recv.at[c, batches[b]],
            send_sem=ssm.at[b, c], recv_sem=rsm.at[b, c],
            device_id={"inner": me + n // 2 - upper * n}, device_id_type=MESH,
        )

    def second_copy(b, k):
        return pltpu.make_async_remote_copy(
            src_ref=send2.at[k, batches[b]], dst_ref=recv2.at[own, batches[b]],
            send_sem=ss2.at[b, k], recv_sem=rs2.at[b, own],
            device_id=member_at(k), device_id_type=MESH,
        )

    def second_arrival(b, o):
        pltpu.make_async_remote_copy(
            src_ref=send2.at[o, batches[b]], dst_ref=recv2.at[o, batches[b]],
            send_sem=ss2.at[b, o], recv_sem=rs2.at[b, o],
            device_id=member(o), device_id_type=MESH,
        ).wait_recv()

    def arrive(buffer, sems, r, peer):
        pltpu.make_async_remote_copy(
            src_ref=buffer.at[r], dst_ref=buffer.at[r], send_sem=sems.at[r],
            recv_sem=sems.at[r], device_id=peer, device_id_type=MESH,
        ).wait_recv()

    for copy in load_small:
        copy.wait()

    half_w[...] = conv_w[...] * 0.5
    bias_row[...] = conv_b[...].reshape(1, xbc) * 0.5
    gain_s[...] = gain[...].reshape(1, HP)

    def spread_of(j, count):
        head = lax.rem(lax.broadcasted_iota(jnp.int32, (count, wide), 0), HEADS)
        col = lax.broadcasted_iota(jnp.int32, (count, wide), 1) // P_SIZE
        return (head == col + j * (wide // P_SIZE)).astype(F32).astype(BF16)

    def split(values):
        high = values.astype(BF16).astype(F32)
        lane = lax.broadcasted_iota(jnp.int32, values.shape, 1)
        return jnp.where(lane < HEADS, high, values - high).astype(BF16)

    skip = d_skip[...].reshape(1, HEADS)
    skip_high = skip.astype(BF16).astype(F32)
    for j in range(groups):
        skip_row[:, j * wide : (j + 1) * wide] = expand(
            skip - skip_high, spread_of(j, HEADS)
        ) + jnp.dot(skip_high.astype(BF16), spread_of(j, HEADS), preferred_element_type=F32)

    pl.semaphore_wait(barrier, ndev)

    @pl.when(rank < ndev - 1)
    def _():
        tail_copy().start()

    def send_dt(k, carry):
        dt_copy(k).start()
        return carry

    lax.fori_loop(1, n, send_dt, 0)
    for q in range(early):
        load_w[q].wait()
        for d in range(2):
            ring_copy(d, q, 1, True).start()
    for q in range(early, blocks):
        load_w[q].wait()
    load_tok.wait()

    def multiply(q, shards, first):
        product = None if first else total[q]
        for owner in shards:
            at = pl.ds(pl.multiple_of(owner * local, local), local)
            term = jnp.dot(tok[:, at], held[q, at, :], preferred_element_type=F32)
            product = term if product is None else product + term
        total[q] = product

    all_parts = blocks * steps
    side_lag, core_lag = 3, 4
    second, third_turn = early, 2 * early + 1
    fifth = third_turn + (steps - 2) * blocks

    def item(i):
        full = jnp.maximum(i - third_turn, 0)
        t = jnp.where(i < second, 1, jnp.where(i < third_turn, 2, 3 + lax.div(full, blocks)))
        q = jnp.where(
            i < second, i, jnp.where(i < third_turn, i - second, lax.rem(full, blocks))
        )
        t = jnp.where(i < fifth, t, jnp.where(i < fifth + 2, steps + 1, steps + 2))
        q = jnp.where(i < fifth, q, jnp.where(i < fifth + 1, early, early + 1))
        return q, t - jnp.maximum(q - early + 1, 0)

    def exchange(i):
        q, s = item(i)

        @pl.when((i < all_parts) & (s < steps))
        def _():
            for d in range(2):
                ring_between(d, q, s, s, True).wait_recv()

                @pl.when(s < steps - 1)
                def _():
                    ring_copy(d, q, s + 1, True).start()

                @pl.when(s == steps - 1)
                def _():
                    ring_copy(d, q, s + 1, False).start()

                side_between(d, q, s, grp, True).start()

        @pl.when((i < all_parts) & (s == steps))
        def _():
            for d in range(2):
                ring_between(d, q, s, s, False).wait_recv()
                side_between(d, q, s, grp, False).start()

        for k in range(late):
            @pl.when(i == (early - 1, 2 * early)[k])
            def _():
                for d in range(2):
                    ring_copy(d, early + k, 1, True).start()

        q, s = item(jnp.maximum(i - side_lag, 0))
        for whole in (True, False):
            @pl.when((i >= side_lag) & (i < all_parts + side_lag) & ((s < steps) == whole))
            def _():
                for d in range(2):
                    side_between(d, q, s, 1 - grp, whole).wait_recv()
                    core_between(d, q, s, core, whole).start()

    def accumulate(i):
        q, s = item(jnp.maximum(i - core_lag, 0))

        @pl.when((i >= core_lag) & (s < steps))
        def _():
            for d in range(2):
                core_between(d, q, s, 1 - core, True).wait_recv()
            multiply(q, [owner_of(0, s), owner_of(1, s)], False)

        @pl.when((i >= core_lag) & (s == steps))
        def _():
            for d in range(2):
                core_between(d, q, s, 1 - core, False).wait_recv()
            multiply(q, [owner_of(0, s)], False)

        @pl.when((i < early) | (i == 6) | (i == 10))
        def _():
            multiply(jnp.where(i < early, i, early + lax.div(jnp.maximum(i - 6, 0), 4)), [me], True)

    def add_dt(k):
        @pl.when(k != me)
        def _():
            dt_arrival(lax.rem(k - me + n, n))

        cols = pl.ds(pl.multiple_of(k * local, local), local)
        part = lax.dot_general(
            tok[tail_rows:, cols], held_dt[k], LAST, preferred_element_type=F32
        )

        @pl.when(k == 0)
        def _():
            dt_acc[...] = part

        @pl.when(k > 0)
        def _():
            dt_acc[...] = dt_acc[...] + part

    def early_part(i, carry):
        exchange(i)

        @pl.when((i == 0) & (rank > 0))
        def _():
            tail_copy().wait_recv()

        accumulate(i)

        @pl.when(i < n)
        def _():
            add_dt(i)

        return carry

    lax.fori_loop(0, 10, early_part, 0)

    row_id = lax.broadcasted_iota(jnp.int32, (CHUNK, CHUNK), 0)
    col_id = lax.broadcasted_iota(jnp.int32, (CHUNK, CHUNK), 1)
    causal = col_id <= row_id
    dt_raw = dt_acc[...].astype(BF16).astype(F32)
    step_one = jax.nn.softplus(dt_raw + dt_bias[...].reshape(1, HEADS))
    scaled = step_one * (-jnp.exp(a_log[...].reshape(1, HEADS)))
    scaled = jnp.concatenate([scaled, scaled], axis=1)
    step_size = jnp.concatenate([step_one, step_one], axis=1)
    before = jnp.zeros((1, 2 * HEADS), F32)
    lower = causal.astype(F32)
    for c in range(chunks):
        here = slice(c * CHUNK, (c + 1) * CHUNK)
        part = jnp.dot(
            lower, scaled[here], preferred_element_type=F32,
            precision=lax.Precision.HIGHEST,
        ) + before
        log_s[here] = part
        reach_s[here] = split(jnp.exp(part - before))
        before = part[CHUNK - 1 : CHUNK]
        fac_s[here] = split(jnp.exp(before - part) * step_size[here])
    flat = jnp.transpose(log_s[...])[0:HEADS]
    log_t[...] = jnp.transpose(log_s[...] - jnp.log(step_size))[0:HEADS]
    ends = [flat[:, (c + 1) * CHUNK - 1 : (c + 1) * CHUNK] for c in range(chunks)]
    dec_send[...] = jnp.broadcast_to(jnp.exp(ends[chunks - 1]), (HEADS, 128))
    dec_recv[rank] = dec_send[...]

    def tall_of(column):
        column = jnp.broadcast_to(column, (HEADS, 128)).reshape(HEADS, 1, 128)
        return jnp.broadcast_to(column, (HEADS, P_SIZE, 128)).reshape(HP, 128)

    for c in range(1, chunks):
        edge[0, c - 1] = tall_of(jnp.exp(ends[c] - ends[c - 1]))
        edge[1, c - 1] = tall_of(jnp.exp(ends[c - 1]))

    def send_decay(k, carry):
        decay_copy(lax.rem(rank + k, ndev)).start()
        return carry

    lax.fori_loop(1, ndev, send_decay, 0)

    def conv_column(block):
        q = jnp.where(block < groups, block + 1, (blocks - 1) * (block - groups))
        cols = pl.ds(pl.multiple_of(block * wide, wide), wide)

        def one(i, carry):
            start = pl.multiple_of(i * 128, 128)
            window = total[q, pl.ds(pl.multiple_of(start + tail_rows - 8, 8), 136), :]
            window = window.astype(BF16).astype(F32)
            acc = bias_row[:, cols]
            for k in range(CONV):
                acc = acc + half_w[k : k + 1, cols] * window[5 + k : 5 + k + 128]
            conv[pl.ds(start, 128), cols] = (acc + acc * jnp.tanh(acc)).astype(BF16)
            return carry

        lax.fori_loop(0, length // 128, one, 0)

    def score_all():
        def one(c, carry):
            here = pl.ds(pl.multiple_of(c * CHUNK, CHUNK), CHUNK)
            product = lax.dot_general(
                conv[here, HP + N :], conv[here, HP : HP + N], LAST,
                preferred_element_type=F32,
            )
            scores[c] = jnp.where(causal, product, 0.0)
            return carry

        lax.fori_loop(0, chunks, one, 0)

    heads_each = HEADS // groups

    def mix(c, j):
        here = pl.ds(pl.multiple_of(c * CHUNK, CHUNK), CHUNK)
        log_c = log_s[here]
        for k in range(heads_each):
            h = j * heads_each + k
            gap = jnp.minimum(log_c[:, h : h + 1] - log_t[h : h + 1, here], 60.0)
            mix_s[h, c] = (scores[c] * jnp.exp(gap)).astype(BF16)

    def contribute(j):
        cols = pl.ds(pl.multiple_of(j * wide, wide), wide)
        spread = spread_of(j, 2 * HEADS)
        state = None
        for c in range(chunks):
            here = slice(c * CHUNK, (c + 1) * CHUNK)
            factor = jnp.dot(fac_s[here], spread, preferred_element_type=F32)
            weighted = (factor * conv[here, cols].astype(F32)).astype(BF16)
            part = lax.dot_general(
                weighted, conv[here, HP : HP + N], FIRST, preferred_element_type=F32
            )
            if c > 0:
                local_s[c - 1, cols] = state
                scale = edge[0, c - 1, cols, :]
                part = part + jnp.concatenate([scale, scale], axis=1) * state
            state = part
        send1[j] = state.reshape(team, rows, N).astype(BF16)

        def send_one(o, inner):
            @pl.when(o != own)
            def _():
                first_copy(j, o).start()

            return inner

        lax.fori_loop(0, team, send_one, 0)

    def inside(j):
        cols = pl.ds(pl.multiple_of(j * wide, wide), wide)
        lane = lax.broadcasted_iota(jnp.int32, (1, wide), 1) // P_SIZE

        def one(c, carry):
            here = pl.ds(pl.multiple_of(c * CHUNK, CHUNK), CHUNK)
            x_rows = conv[here, cols]
            acc = skip_row[:, cols] * x_rows.astype(F32)
            for k in range(heads_each):
                keep = (lane == k).astype(F32).astype(BF16)
                acc = acc + jnp.dot(
                    mix_s[j * heads_each + k, c], x_rows * keep, preferred_element_type=F32
                )
            y[here, cols] = acc
            return carry

        lax.fori_loop(0, chunks, one, 0)

    def decay_of(k, half_of, j):
        r = lax.div(k, n // 2) * n + half_of * (n // 2) + lax.rem(k, n // 2)
        head = j * heads_each + lax.div(own * rows, P_SIZE)
        row = dec_recv[r, pl.ds(head, 1), :]
        return jnp.concatenate([row, row], axis=1)

    def combine(b):
        for j in range(groups)[batches[b]]:
            recv1[j, slot] = send1[j, own]

            def arrived(k, carry):
                @pl.when(k != slot)
                def _():
                    first_arrival(j, k)

                return carry

            lax.fori_loop(0, team, arrived, 0)
            for c in range(2):
                state = jnp.zeros((rows, N), F32)
                for m in range(n // 2):
                    k = c * (n // 2) + m
                    prefix[j, k] = state
                    state = decay_of(k, upper, j) * state + recv1[j, k].astype(F32)
                mid_send[c, j] = state.astype(BF16)
        mid_copy(b, 0).start()

        @pl.when(upper == 0)
        def _():
            mid_copy(b, 1).start()

    def product_of(c, half_of, j):
        result = decay_of(c * (n // 2), half_of, j)
        for m in range(1, n // 2):
            result = result * decay_of(c * (n // 2) + m, half_of, j)
        return result

    def distribute(b):
        mid_copy(b, 0).wait_recv()

        @pl.when(upper == 1)
        def _():
            mid_copy(b, 1).wait_recv()

        is_upper = upper == 1
        for j in range(groups)[batches[b]]:
            middle = mid_recv[0, j].astype(F32)
            ours = mid_send[0, j].astype(F32)
            lower_sum = jnp.where(is_upper, middle, ours)
            upper_sum = jnp.where(is_upper, ours, middle)
            block_end = product_of(0, 1, j) * lower_sum + upper_sum

            @pl.when(is_upper)
            def _():
                start[0, j] = middle
                start[1, j] = product_of(1, 0, j) * block_end + mid_recv[1, j].astype(F32)

            @pl.when(upper == 0)
            def _():
                start[0, j] = jnp.zeros((rows, N), F32)
                start[1, j] = block_end

        for k in range(team):
            for j in range(groups)[batches[b]]:
                state = start[k // (n // 2), j]
                send2[k, j] = (prefix[j, k] + state).astype(BF16)
                start[k // (n // 2), j] = decay_of(k, upper, j) * state

            @pl.when(k != slot)
            def _():
                second_copy(b, k).start()

        recv2[own, batches[b]] = send2[slot, batches[b]]

    def late_part(i, carry):
        exchange(i)
        accumulate(i)
        ready = fifth - blocks + core_lag + 1

        @pl.when(i == ready - 1)
        def _():
            conv_column(groups)

        @pl.when((i >= ready) & (i < ready + groups - 1))
        def _():
            conv_column(i - ready)
            contribute(i - ready)

        @pl.when(i == ready + groups - 1)
        def _():
            others()

        @pl.when(i == all_parts + 2)
        def _():
            combine(0)

        @pl.when(i == fifth + core_lag)
        def _():
            conv_column(groups - 1)
            contribute(groups - 1)

        return carry

    def others():
        def one(k, carry):
            r = lax.rem(rank + k, ndev)
            arrive(dec_recv, rsd, r, place(r))
            return carry

        lax.fori_loop(1, ndev, one, 0)

    lax.fori_loop(10, all_parts + core_lag, late_part, 0)

    conv_column(groups + 1)
    score_all()

    def fill(j, carry):
        for k in range(groups):
            @pl.when(j == k)
            def _():
                def one(c, inner):
                    mix(c, k)
                    return inner

                lax.fori_loop(0, chunks, one, 0)

        inside(j)
        return carry

    combine(1)
    lax.fori_loop(0, 1, fill, 0)
    distribute(0)
    lax.fori_loop(1, groups - 1, fill, 0)
    distribute(1)
    lax.fori_loop(groups - 1, groups, fill, 0)

    row_head = lax.broadcasted_iota(jnp.int32, (wide, wide), 0) // P_SIZE
    col_head = lax.broadcasted_iota(jnp.int32, (wide, wide), 1) // P_SIZE
    same = (row_head == col_head).astype(F32).astype(BF16)

    def out_copies(j):
        cols = pl.ds(pl.multiple_of(j * wide, wide), wide)
        return [
            pltpu.make_async_copy(
                mixed.at[:, cols], mixed_out.at[:, cols], out_sems.at[0, j]
            ),
            pltpu.make_async_copy(
                entry_out.at[cols], entry_all.at[cols], out_sems.at[1, j]
            ),
        ]

    def finish_group(j, carry):
        cols = pl.ds(pl.multiple_of(j * wide, wide), wide)
        entry = jnp.concatenate([recv2[o, j] for o in range(team)], axis=0).astype(F32)
        entry_out[cols] = entry.astype(BF16)
        spread = spread_of(j, 2 * HEADS)
        for c in range(chunks):
            here = slice(c * CHUNK, (c + 1) * CHUNK)
            state = entry
            if c > 0:
                scale = edge[1, c - 1, cols, :]
                state = local_s[c - 1, cols] + jnp.concatenate([scale, scale], axis=1) * entry
            carried = lax.dot_general(
                conv[here, HP + N :], state.astype(BF16), LAST, preferred_element_type=F32
            )
            reach = jnp.dot(reach_s[here], spread, preferred_element_type=F32)
            out = y[here, cols] + reach * carried
            square = (out * out).astype(BF16)
            sums = jnp.dot(square, same, preferred_element_type=F32)
            inv_rms = lax.rsqrt(sums * (1.0 / P_SIZE) + EPSILON)
            mixed[here, cols] = (out * inv_rms * gain_s[:, cols]).astype(BF16)
        for copy in out_copies(j):
            copy.start()
        return carry

    def wait_second(b):
        def one(o, carry):
            @pl.when(o != own)
            def _():
                second_arrival(b, o)

            return carry

        lax.fori_loop(0, team, one, 0)

    wait_second(0)
    lax.fori_loop(0, groups - 1, finish_group, 0)
    wait_second(1)
    lax.fori_loop(groups - 1, groups, finish_group, 0)

    def drain_out(j, carry):
        for copy in out_copies(j):
            copy.wait()
        return carry

    def drain(q, carry):
        for d in range(2):
            for s in range(1, steps + 1):
                whole = s < steps
                ring_copy(d, q, s, whole).wait_send()
                side_between(d, q, s, grp, whole).wait_send()
                core_between(d, q, s, core, whole).wait_send()
        return carry

    lax.fori_loop(0, blocks, drain, 0)

    def drain_dt(k, carry):
        dt_copy(k).wait_send()
        return carry

    lax.fori_loop(1, n, drain_dt, 0)

    def drain_decay(k, carry):
        decay_copy(lax.rem(rank + k, ndev)).wait_send()
        return carry

    lax.fori_loop(1, ndev, drain_decay, 0)

    def drain_state(k, carry):
        @pl.when(k != own)
        def _():
            for j in range(groups):
                first_copy(j, k).wait_send()

        @pl.when(k != slot)
        def _():
            for b in range(2):
                second_copy(b, k).wait_send()

        return carry

    lax.fori_loop(0, team, drain_state, 0)
    for b in range(2):
        mid_copy(b, 0).wait_send()

    @pl.when(upper == 0)
    def _():
        for b in range(2):
            mid_copy(b, 1).wait_send()

    @pl.when(rank < ndev - 1)
    def _():
        tail_copy().wait_send()

    lax.fori_loop(0, groups, drain_out, 0)


def run_fused(tokens, w_in, w_dt, conv_w, conv_b, dt_bias, a_log, d_skip, norm_gain):
    n, n_out = lax.axis_size("inner"), lax.axis_size("outer")
    ndev = n * n_out
    length, depth = tokens.shape
    local, xbc = w_in.shape
    team = ndev // 2
    groups = HP // 256
    rows = 256 // team
    tail_rows = 16
    blocks = xbc // 256
    chunks = length // CHUNK
    dma = pltpu.SemaphoreType.DMA
    whole = pl.BlockSpec(memory_space=pl.ANY)
    weight_sems = [dma((2, blocks, n // 2 + 1))] * 6
    first_sems = [dma((groups, team))] * 2
    swap_sems = [dma((2, 2))] * 2
    second_sems = [dma((2, team))] * 2
    rank_sems = [dma((ndev,))] * 2
    return pl.pallas_call(
        partial(fused_kernel, n, n_out),
        out_shape=(
            jax.ShapeDtypeStruct((length, HP), BF16),
            jax.ShapeDtypeStruct((HP, N), BF16),
        ),
        in_specs=[whole] * 9,
        out_specs=(whole, whole),
        scratch_shapes=[
            pltpu.VMEM((CONV, xbc), F32), pltpu.VMEM((xbc,), F32),
            pltpu.VMEM((HEADS,), F32), pltpu.VMEM((HEADS,), F32),
            pltpu.VMEM((HEADS,), F32), pltpu.VMEM((HP,), F32),
            pltpu.VMEM((length, HP), BF16), pltpu.VMEM((HP, N), BF16),
            pltpu.VMEM((length + tail_rows, depth), BF16),
            pltpu.VMEM((blocks, depth, 256), BF16),
            pltpu.VMEM((blocks, length + tail_rows, 256), F32),
            pltpu.VMEM((n, HEADS, local), BF16),
            pltpu.VMEM((length, HEADS), F32),
            pltpu.VMEM((CONV, xbc), F32),
            pltpu.VMEM((1, xbc), F32),
            pltpu.VMEM((1, HP), F32),
            pltpu.VMEM((1, HP), F32),
            pltpu.VMEM((length, xbc), BF16),
            pltpu.VMEM((length, 2 * HEADS), F32),
            pltpu.VMEM((HEADS, length), F32),
            pltpu.VMEM((length, 2 * HEADS), F32),
            pltpu.VMEM((length, 2 * HEADS), BF16),
            pltpu.VMEM((length, 2 * HEADS), BF16),
            pltpu.VMEM((2, chunks - 1, HP, 128), F32),
            pltpu.VMEM((chunks, CHUNK, CHUNK), F32),
            pltpu.VMEM((HEADS, chunks, CHUNK, CHUNK), BF16),
            pltpu.VMEM((chunks - 1, HP, N), F32),
            pltpu.VMEM((length, HP), F32),
            pltpu.VMEM((groups, team, rows, N), BF16),
            pltpu.VMEM((groups, team, rows, N), BF16),
            pltpu.VMEM((groups, team, rows, N), F32),
            pltpu.VMEM((2, groups, rows, N), BF16),
            pltpu.VMEM((2, groups, rows, N), BF16),
            pltpu.VMEM((2, groups, rows, N), F32),
            pltpu.VMEM((team, groups, rows, N), BF16),
            pltpu.VMEM((team, groups, rows, N), BF16),
            pltpu.VMEM((HEADS, 128), F32),
            pltpu.VMEM((ndev, HEADS, 128), F32),
            *weight_sems,
            dma((n,)), dma((n,)), dma((blocks + 1,)), dma(()), dma(()),
            *first_sems, *swap_sems, *second_sems, *rank_sems, dma((7,)), dma((2, groups)),
        ],
        compiler_params=pltpu.CompilerParams(
            collective_id=3, has_side_effects=True, vmem_limit_bytes=62 * 2**20
        ),
        name="fused",
    )(
        tokens, w_in, w_dt.T, conv_w, conv_b, dt_bias, a_log, d_skip, norm_gain,
    )


def hand_over_kernel(
    mixed, entry, mixed_out, entry_out, held_m, held_e, wide_e, in_sems, out_sems
):
    parts = in_sems.shape[1]
    loads, stores = [], []
    arrays = ((entry, held_e, wide_e, entry_out), (mixed, held_m, held_m, mixed_out))
    for i, (source, held, ready, target) in enumerate(arrays):
        rows = source.shape[0] // parts
        for k in range(parts):
            at = pl.ds(k * rows, rows)
            loads.append(pltpu.make_async_copy(source.at[at], held.at[at], in_sems.at[i, k]))
            stores.append(pltpu.make_async_copy(ready.at[at], target.at[at], out_sems.at[i, k]))
    for load in loads:
        load.start()
    rows = entry.shape[0] // parts
    for k, (load, store) in enumerate(zip(loads, stores)):
        load.wait()
        if k < parts:
            at = slice(k * rows, (k + 1) * rows)
            wide_e[at] = held_e[at].astype(F32)
        store.start()
    for store in stores:
        store.wait()


def hand_over(mixed, entry):
    whole = pl.BlockSpec(memory_space=pl.ANY)
    sems = pltpu.SemaphoreType.DMA((2, 4))
    return pl.pallas_call(
        hand_over_kernel,
        out_shape=(
            jax.ShapeDtypeStruct(mixed.shape, mixed.dtype),
            jax.ShapeDtypeStruct(entry.shape, F32),
        ),
        in_specs=[whole, whole],
        out_specs=(whole, whole),
        scratch_shapes=[
            pltpu.VMEM(mixed.shape, mixed.dtype), pltpu.VMEM(entry.shape, entry.dtype),
            pltpu.VMEM(entry.shape, F32), sems, sems,
        ],
        name="hand_over",
    )(mixed, entry)


def per_device(tokens, w_in, w_dt, conv_w, conv_b, dt_bias, a_log, d_skip, norm_gain):
    own_rows = tokens.reshape(tokens.shape[1], tokens.shape[2])
    row_count = own_rows.shape[0]
    if w_in.shape[0] % 512 == 0 and lax.axis_size("inner") == 8:
        mixed, entry = run_fused(
            own_rows, w_in, w_dt, conv_w, conv_b, dt_bias, a_log, d_skip, norm_gain
        )
        mixed, entry = hand_over(mixed, entry)
    else:
        projected, tail, dt_raw = run_project(own_rows, w_in, w_dt)
        mixed, entry = run_scan(
            projected, tail, dt_raw, conv_w, conv_b, dt_bias, a_log, d_skip, norm_gain
        )
    return (
        mixed.reshape(1, row_count, HP),
        entry.reshape(1, 1, HEADS, P_SIZE, N),
    )


def solution(mesh):
    placed = (
        P(("grp", "outer"), "inner", None),
        P("inner", None),
        P("inner", None),
        P(), P(), P(), P(), P(), P(),
    )
    return jax.shard_map(
        per_device,
        mesh=mesh,
        in_specs=placed,
        out_specs=(
            P(("grp", "outer"), "inner", None),
            P(("grp", "outer"), "inner", None, None, None),
        ),
        check_vma=False,
    )
```

```python
from functools import partial

import jax
import jax.numpy as jnp
from jax import lax
from jax.experimental import pallas as pl
from jax.experimental.pallas import tpu as pltpu
from jax.sharding import PartitionSpec as P

HEADS = 16
P_SIZE = 64
N = 256
CONV = 4
HP = HEADS * P_SIZE
CHUNK = 256
EPSILON = 1e-05
MESH = pl.DeviceIdType.MESH
F32 = jnp.float32
BF16 = jnp.bfloat16
LAST = (((1,), (1,)), ((), ()))
FIRST = (((0,), (0,)), ((), ()))


def expand(values, spread):
    high = values.astype(BF16)
    low = (values - high.astype(F32)).astype(BF16)
    return jnp.dot(high, spread, preferred_element_type=F32) + jnp.dot(
        low, spread, preferred_element_type=F32
    )


def scan_kernel(
    n_in, ndev,
    proj, tail, dt_raw, conv_w, conv_b, dt_bias, a_log, d_skip, gain,
    mixed, entry_out,
    gain_s, bias_row, skip_row, pad, conv, log_s, log_t, step_s, y, states,
    send1, recv1, send2, recv2, dec_send, dec_recv,
    ss1, rs1, ss2, rs2, ssd, rsd,
):
    length = proj.shape[0]
    chunks = length // CHUNK
    rows = HP // ndev
    me = lax.axis_index("outer") * n_in + lax.axis_index("inner")

    def place(g):
        return {"inner": lax.rem(g, n_in), "outer": lax.div(g, n_in)}

    barrier = pltpu.get_barrier_semaphore()

    def greet(k, carry):
        pl.semaphore_signal(
            barrier, inc=1, device_id=place(lax.rem(me + k, ndev)), device_id_type=MESH
        )
        return carry

    lax.fori_loop(1, ndev, greet, 0)

    head_id = lax.broadcasted_iota(jnp.int32, (HEADS, HP), 0)
    col_head = lax.broadcasted_iota(jnp.int32, (HEADS, HP), 1) // P_SIZE
    spread = (head_id == col_head).astype(F32).astype(BF16)

    bias_row[...] = conv_b[...].reshape(1, conv_b.shape[0])
    gain_s[...] = gain[...].reshape(1, HP)
    skip = d_skip[...].reshape(1, HEADS)
    skip_high = skip.astype(BF16).astype(F32)
    skip_row[...] = expand(skip - skip_high, spread) + jnp.dot(
        skip_high.astype(BF16), spread, preferred_element_type=F32
    )
    step_size = jax.nn.softplus(dt_raw[...].astype(F32) + dt_bias[...].reshape(1, HEADS))
    scaled = step_size * (-jnp.exp(a_log[...].reshape(1, HEADS)))
    row_id = lax.broadcasted_iota(jnp.int32, (CHUNK, CHUNK), 0)
    col_id = lax.broadcasted_iota(jnp.int32, (CHUNK, CHUNK), 1)
    causal = col_id <= row_id
    lower = causal.astype(F32)
    step_s[...] = step_size
    before = jnp.zeros((1, HEADS), F32)
    for c in range(chunks):
        part = jnp.dot(
            lower,
            scaled[c * CHUNK : (c + 1) * CHUNK],
            preferred_element_type=F32,
            precision=lax.Precision.HIGHEST,
        ) + before
        log_s[c * CHUNK : (c + 1) * CHUNK] = part
        before = part[CHUNK - 1 : CHUNK]
    log_t[...] = jnp.transpose(log_s[...])
    dec_send[...] = jnp.broadcast_to(jnp.exp(log_t[:, length - 1 : length]), (HEADS, 128))

    pad[0:8] = tail[...].astype(F32)[8:16]
    pad[8:] = proj[...].astype(F32)
    wide = 256
    blocks = proj.shape[1] // wide

    def conv_block(t, carry):
        i, j = lax.div(t, blocks), lax.rem(t, blocks)
        cols = pl.ds(pl.multiple_of(j * wide, wide), wide)
        window = pad[pl.ds(pl.multiple_of(i * 128, 128), 136), cols]
        total = bias_row[:, cols]
        for k in range(CONV):
            total = total + conv_w[k : k + 1, cols] * window[5 + k : 5 + k + 128]
        conv[pl.ds(pl.multiple_of(i * 128, 128), 128), cols] = (
            total * jax.nn.sigmoid(total)
        ).astype(BF16)
        return carry

    row_blocks = length // 128

    def conv_column(j):
        def one(i, carry):
            return conv_block(i * blocks + j, carry)

        lax.fori_loop(0, row_blocks, one, 0)

    conv_column(HP // wide)

    def weighted_sum(stop):
        final = log_s[stop - 1 : stop]
        factor = jnp.exp(final - log_s[0:stop]) * step_s[0:stop]
        weighted = (expand(factor, spread) * conv[0:stop, 0:HP].astype(F32)).astype(BF16)
        return lax.dot_general(
            weighted, conv[0:stop, HP : HP + N], FIRST, preferred_element_type=F32
        )

    dec_recv[me] = dec_send[...]

    def decay_copy(g):
        return pltpu.make_async_remote_copy(
            src_ref=dec_send, dst_ref=dec_recv.at[me], send_sem=ssd.at[g],
            recv_sem=rsd.at[me], device_id=place(g), device_id_type=MESH,
        )

    def first_copy(g):
        return pltpu.make_async_remote_copy(
            src_ref=send1.at[g], dst_ref=recv1.at[me], send_sem=ss1.at[g],
            recv_sem=rs1.at[me], device_id=place(g), device_id_type=MESH,
        )

    def second_copy(g):
        return pltpu.make_async_remote_copy(
            src_ref=send2.at[g], dst_ref=recv2.at[me], send_sem=ss2.at[g],
            recv_sem=rs2.at[me], device_id=place(g), device_id_type=MESH,
        )

    pl.semaphore_wait(barrier, ndev - 1)

    def send_decay(k, carry):
        decay_copy(lax.rem(me + k, ndev)).start()
        return carry

    lax.fori_loop(1, ndev, send_decay, 0)

    groups = HP // wide
    owners = ndev // groups
    own_group = lax.div(me, owners)
    factor = jnp.exp(log_s[length - 1 : length] - log_s[...]) * step_s[...]

    def spread_of(j):
        head = lax.broadcasted_iota(jnp.int32, (HEADS, wide), 0)
        col = lax.broadcasted_iota(jnp.int32, (HEADS, wide), 1) // P_SIZE
        return (head == col + j * (wide // P_SIZE)).astype(F32).astype(BF16)

    def first_group(i, carry):
        j = lax.rem(own_group + 1 + i, groups)
        conv_column(j)
        cols = pl.ds(pl.multiple_of(j * wide, wide), wide)
        weighted = (expand(factor, spread_of(j)) * conv[:, cols].astype(F32)).astype(BF16)
        part = lax.dot_general(
            weighted, conv[:, HP : HP + N], FIRST, preferred_element_type=F32
        )
        send1[pl.ds(j * owners, owners)] = part.reshape(owners, rows, N).astype(BF16)

        def send_one(k, inner):
            g = j * owners + k

            @pl.when(g != me)
            def _():
                first_copy(g).start()

            return inner

        return lax.fori_loop(0, owners, send_one, carry)

    lax.fori_loop(0, groups, first_group, 0)
    recv1[me] = send1[me]
    conv_column(HP // wide + 1)

    states[0] = jnp.zeros((HP, N), BF16)
    for c in range(1, chunks):
        states[c] = weighted_sum(c * CHUNK).astype(BF16)

    def local_chunk(c, carry):
        start = pl.multiple_of(c * CHUNK, CHUNK)
        here = pl.ds(start, CHUNK)
        log_c = log_s[here]
        reached = log_s[pl.ds(pl.multiple_of(jnp.maximum(start - 8, 0), 8), 8)][7:8]
        reached = jnp.where(c > 0, reached, 0.0)
        c_rows = conv[here, HP + N :]
        b_rows = conv[here, HP : HP + N]
        scores = lax.dot_general(c_rows, b_rows, LAST, preferred_element_type=F32)
        scores = jnp.where(causal, scores, 0.0)
        x_rows = conv[here, 0:HP].astype(F32)
        driven = (expand(step_s[here], spread) * x_rows).astype(BF16)
        inter = lax.dot_general(c_rows, states[c], LAST, preferred_element_type=F32)
        y[here] = expand(jnp.exp(log_c - reached), spread) * inter + skip_row[...] * x_rows
        for h in range(0, HEADS, 2):
            pieces = []
            for k in (h, h + 1):
                gap = jnp.minimum(log_c[:, k : k + 1] - log_t[k : k + 1, here], 0.0)
                mixing = (scores * jnp.exp(gap)).astype(BF16)
                pieces.append(
                    jnp.dot(
                        mixing,
                        driven[:, k * P_SIZE : (k + 1) * P_SIZE],
                        preferred_element_type=F32,
                    )
                )
            both = slice(h * P_SIZE, (h + 2) * P_SIZE)
            y[here, both] = y[here, both] + jnp.concatenate(pieces, axis=1)
        return carry

    lax.fori_loop(0, chunks, local_chunk, 0)

    own_head = lax.div(me * rows, P_SIZE)

    def wait_from(copy_of, r):
        copy_of(r).wait_recv()

    def arrive(buffer, sems, r):
        pltpu.make_async_remote_copy(
            src_ref=buffer.at[r], dst_ref=buffer.at[r], send_sem=sems.at[r],
            recv_sem=sems.at[r], device_id=place(r), device_id_type=MESH,
        ).wait_recv()

    def advance(r, state):
        send2[r] = state.astype(BF16)

        @pl.when(r != me)
        def _():
            arrive(dec_recv, rsd, r)
            arrive(recv1, rs1, r)

        decay = dec_recv[r, pl.ds(own_head, 1), :]
        decay = jnp.concatenate([decay, decay], axis=1)
        return decay * state + recv1[r].astype(F32)

    lax.fori_loop(0, ndev, advance, jnp.zeros((rows, N), F32))

    def send_second(k, carry):
        second_copy(lax.rem(me + k, ndev)).start()
        return carry

    lax.fori_loop(1, ndev, send_second, 0)
    recv2[me] = send2[me]

    reach = jnp.exp(log_s[...])

    def last_group(i, carry):
        j = lax.rem(own_group + groups - 1 - i, groups)

        def wait_one(k, inner):
            g = j * owners + k

            @pl.when(g != me)
            def _():
                arrive(recv2, rs2, g)

            return inner

        lax.fori_loop(0, owners, wait_one, 0)
        cols = pl.ds(pl.multiple_of(j * wide, wide), wide)
        entry = recv2[pl.ds(j * owners, owners)].astype(F32).reshape(wide, N)
        entry_out[cols] = entry
        carried = lax.dot_general(
            conv[:, HP + N :], entry.astype(BF16), LAST, preferred_element_type=F32
        )
        spread_j = spread_of(j)
        out = y[:, cols] + expand(reach, spread_j) * carried
        square = out * out
        high = square.astype(BF16)
        low = (square - high.astype(F32)).astype(BF16)
        sums = lax.dot_general(high, spread_j, LAST, preferred_element_type=F32)
        sums = sums + lax.dot_general(low, spread_j, LAST, preferred_element_type=F32)
        inv_rms = lax.rsqrt(sums * (1.0 / P_SIZE) + EPSILON)
        mixed[:, cols] = (out * expand(inv_rms, spread_j) * gain_s[:, cols]).astype(BF16)
        return carry

    lax.fori_loop(0, groups, last_group, 0)

    def finish(k, carry):
        g = lax.rem(me + k, ndev)
        decay_copy(g).wait_send()
        first_copy(g).wait_send()
        second_copy(g).wait_send()
        return carry

    lax.fori_loop(1, ndev, finish, 0)


def run_scan(projected, tail, dt_raw, conv_w, conv_b, dt_bias, a_log, d_skip, norm_gain):
    n_in, n_out = lax.axis_size("inner"), lax.axis_size("outer")
    ndev = n_in * n_out
    length, xbc = projected.shape
    rows = HP // ndev
    dma = pltpu.SemaphoreType.DMA((ndev,))
    vmem = pl.BlockSpec(memory_space=pltpu.VMEM)
    return pl.pallas_call(
        partial(scan_kernel, n_in, ndev),
        out_shape=(
            jax.ShapeDtypeStruct((length, HP), BF16),
            jax.ShapeDtypeStruct((HP, N), F32),
        ),
        in_specs=[vmem] * 9,
        out_specs=(vmem, vmem),
        scratch_shapes=[
            pltpu.VMEM((1, HP), F32),
            pltpu.VMEM((1, xbc), F32),
            pltpu.VMEM((1, HP), F32),
            pltpu.VMEM((length + 8, xbc), F32),
            pltpu.VMEM((length, xbc), BF16),
            pltpu.VMEM((length, HEADS), F32),
            pltpu.VMEM((HEADS, length), F32),
            pltpu.VMEM((length, HEADS), F32),
            pltpu.VMEM((length, HP), F32),
            pltpu.VMEM((length // CHUNK, HP, N), BF16),
            pltpu.VMEM((ndev, rows, N), BF16),
            pltpu.VMEM((ndev, rows, N), BF16),
            pltpu.VMEM((ndev, rows, N), BF16),
            pltpu.VMEM((ndev, rows, N), BF16),
            pltpu.VMEM((HEADS, 128), F32),
            pltpu.VMEM((ndev, HEADS, 128), F32),
            dma, dma, dma, dma, dma, dma,
        ],
        compiler_params=pltpu.CompilerParams(
            collective_id=1, has_side_effects=True, vmem_limit_bytes=60 * 2**20
        ),
        name="scan",
    )(
        projected, tail, dt_raw, conv_w, conv_b, dt_bias, a_log, d_skip, norm_gain,
    )


def project_kernel(
    n, n_out,
    tokens, w_in, w_dt,
    proj, tail, dt_out,
    tok, held, total, held_dt,
    ring_s, ring_r, side_s, side_r, core_s, core_r, dt_s, dt_r, misc, tail_s, tail_r,
):
    length, depth = tokens.shape
    local, xbc = w_in.shape
    half = xbc // 2
    quarter = half // 2
    lanes = 128
    streams = quarter // lanes
    wide = 256
    tiles = half // wide
    third = (local * 5 // 16) // 16 * 16
    ring_rows = local - third
    tail_rows = tok.shape[0] - length
    block = held_dt.shape[2]
    ndev = n * n_out
    me = lax.axis_index("inner")
    core = lax.axis_index("outer")
    grp = lax.axis_index("grp")
    rank = core * n + me
    odd = lax.rem(me, 2)
    pos = jnp.where(odd == 0, lax.div(me, 2), n - lax.div(me + 1, 2))

    def index_at(q):
        q = lax.rem(q + 2 * n, n)
        return jnp.where(q < n // 2, 2 * q, 2 * n - 1 - 2 * q)

    def place(g):
        return {"inner": lax.rem(g, n), "outer": lax.div(g, n)}

    barrier = pltpu.get_barrier_semaphore()

    def greet(k, carry):
        pl.semaphore_signal(
            barrier, inc=1, device_id=place(lax.rem(rank + k, ndev)), device_id_type=MESH
        )
        return carry

    lax.fori_loop(1, ndev, greet, 0)
    pl.semaphore_signal(barrier, inc=1, device_id={"grp": 1 - grp}, device_id_type=MESH)

    def own_rows(owner):
        return pl.ds(pl.multiple_of(owner * local, 16), local)

    load_tok = pltpu.make_async_copy(tokens, tok.at[pl.ds(0, length)], misc.at[0])
    load_w = [
        pltpu.make_async_copy(
            w_in.at[:, pl.ds(d * half, half)], held.at[d, own_rows(me)], misc.at[1 + d]
        )
        for d in range(2)
    ]
    for copy in load_w:
        copy.start()
    load_tok.start()
    held_dt[me] = w_dt[...]

    @pl.when(rank == 0)
    def _():
        tok[length:] = jnp.zeros((tail_rows, depth), BF16)

    def ring_copy(d, t, s):
        owner = index_at(pos - (s - 1)) if d == 0 else index_at(pos + (s - 1))
        target = index_at(pos + 1) if d == 0 else index_at(pos - 1)
        rows = pl.ds(pl.multiple_of(owner * local + grp * third, 16), ring_rows)
        cols = pl.ds(pl.multiple_of(core * quarter + t * lanes, lanes), lanes)
        part = held.at[d, rows, cols]
        return pltpu.make_async_remote_copy(
            src_ref=part, dst_ref=part, send_sem=ring_s.at[d, t, s],
            recv_sem=ring_r.at[d, t, s], device_id={"inner": target}, device_id_type=MESH,
        )

    def owner_of(d, s):
        return index_at(pos - s) if d == 0 else index_at(pos + s)

    def chunk_cols(which, t):
        return pl.ds(pl.multiple_of(which * quarter + t * lanes, lanes), lanes)

    def side_rows(d, s, which):
        start = owner_of(d, s) * local + which * ring_rows
        return pl.ds(pl.multiple_of(start, 16), third)

    def side_between(d, t, s, which):
        part = held.at[d, side_rows(d, s, which), chunk_cols(core, t)]
        return pltpu.make_async_remote_copy(
            src_ref=part, dst_ref=part, send_sem=side_s.at[d, t, s],
            recv_sem=side_r.at[d, t, s], device_id={"grp": 1 - grp}, device_id_type=MESH,
        )

    def core_between(d, t, s, which):
        part = held.at[d, own_rows(owner_of(d, s)), chunk_cols(which, t)]
        return pltpu.make_async_remote_copy(
            src_ref=part, dst_ref=part, send_sem=core_s.at[d, t, s],
            recv_sem=core_r.at[d, t, s], device_id={"outer": 1 - core}, device_id_type=MESH,
        )

    def side_copy(d, t, s):
        return side_between(d, t, s, grp)

    def core_copy(d, t, s):
        return core_between(d, t, s, core)

    def ring_arrival(d, t, s):
        start = owner_of(d, s) * local + grp * third
        rows = pl.ds(pl.multiple_of(start, 16), ring_rows)
        part = held.at[d, rows, chunk_cols(core, t)]
        pltpu.make_async_remote_copy(
            src_ref=part, dst_ref=part, send_sem=ring_s.at[d, t, s],
            recv_sem=ring_r.at[d, t, s], device_id={"inner": index_at(pos + 1)},
            device_id_type=MESH,
        ).wait_recv()

    def side_arrival(d, t, s):
        side_between(d, t, s, 1 - grp).wait_recv()

    def core_arrival(d, t, s):
        core_between(d, t, s, 1 - core).wait_recv()

    def dt_copy(k):
        peer = lax.rem(me + k, n)
        return pltpu.make_async_remote_copy(
            src_ref=w_dt, dst_ref=held_dt.at[me], send_sem=dt_s.at[k],
            recv_sem=dt_r.at[me], device_id={"inner": peer}, device_id_type=MESH,
        )

    def dt_arrival(k):
        peer = lax.rem(me + k, n)
        pltpu.make_async_remote_copy(
            src_ref=w_dt, dst_ref=held_dt.at[peer], send_sem=dt_s.at[k],
            recv_sem=dt_r.at[peer], device_id={"inner": peer}, device_id_type=MESH,
        ).wait_recv()

    def tail_copy():
        return pltpu.make_async_remote_copy(
            src_ref=tokens.at[pl.ds(length - tail_rows, tail_rows)],
            dst_ref=tok.at[pl.ds(length, tail_rows)], send_sem=tail_s,
            recv_sem=tail_r, device_id=place(lax.rem(rank + 1, ndev)), device_id_type=MESH,
        )

    pl.semaphore_wait(barrier, ndev)

    @pl.when(rank < ndev - 1)
    def _():
        tail_copy().start()

    for d in range(2):
        load_w[d].wait()
        for t in range(streams):
            ring_copy(d, t, 1).start()

    def send_dt(k, carry):
        dt_copy(k).start()
        return carry

    lax.fori_loop(1, n, send_dt, 0)
    load_tok.wait()

    @pl.when(rank > 0)
    def _():
        tail_copy().wait_recv()

    incremental = local % 128 == 0

    def multiply_tile(d, lhs_cols, rhs_rows, first, j):
        cols = pl.ds(pl.multiple_of(j * wide, wide), wide)
        product = jnp.dot(
            tok[:, lhs_cols], held[d, rhs_rows, cols], preferred_element_type=F32
        )
        at = d * tiles + j
        if first:
            total[at] = product
        else:
            total[at] = total[at] + product

    def multiply(d, lhs_cols, rhs_rows, first):
        def tile(j, carry):
            multiply_tile(d, lhs_cols, rhs_rows, first, j)
            return carry

        lax.fori_loop(0, tiles, tile, 0)

    def project_dt():
        def arrived(k, carry):
            dt_arrival(k)
            return carry

        lax.fori_loop(1, n, arrived, 0)
        together = block // local

        def add(j, sums):
            cols = pl.ds(pl.multiple_of(j * block, block), block)
            piece = held_dt[j * together]
            for m in range(1, together):
                piece = piece + held_dt[j * together + m]
            return sums + lax.dot_general(
                tok[0:length, cols], piece, LAST, preferred_element_type=F32
            )

        sums = lax.fori_loop(0, depth // block, add, jnp.zeros((length, HEADS), F32))
        dt_out[...] = sums.astype(BF16)

    def step(s, carry):
        @pl.when(s >= 3)
        def _():
            for t in range(streams):
                for d in range(2):
                    core_arrival(d, t, s - 2)

        def part(t, inner):
            @pl.when(s < n)
            def _():
                for d in range(2):
                    ring_arrival(d, t, s)

                    @pl.when(s < n - 1)
                    def _():
                        ring_copy(d, t, s + 1).start()

                    side_copy(d, t, s).start()

            @pl.when((s >= 2) & (s <= n))
            def _():
                for d in range(2):
                    side_arrival(d, t, s - 1)
                    core_copy(d, t, s - 1).start()

            if incremental:
                for d in range(2):
                    owner = owner_of(d, s - 2)
                    at = pl.ds(pl.multiple_of(owner * local, 128), local)

                    @pl.when(s == 2)
                    def _():
                        multiply_tile(d, at, at, True, t)

                    @pl.when(s > 2)
                    def _():
                        multiply_tile(d, at, at, False, t)

            return inner

        lax.fori_loop(0, streams, part, 0)

        @pl.when(s == 1)
        def _():
            project_dt()

        return carry

    lax.fori_loop(1, n + 2, step, 0)
    if not incremental:
        for d in range(2):
            multiply(d, slice(0, 512), slice(0, 512), True)

            def more(j, carry):
                at = pl.ds(pl.multiple_of(j * 512, 512), 512)
                multiply(d, at, at, False)
                return carry

            lax.fori_loop(1, depth // 512, more, 0)

    for j in range(2 * tiles):
        cols = slice(j * wide, (j + 1) * wide)
        proj[:, cols] = total[j, 0:length].astype(BF16)
        tail[:, cols] = total[j, length:].astype(BF16)

    def drain(s, carry):
        for d in range(2):
            for t in range(streams):
                ring_copy(d, t, s).wait_send()
                side_copy(d, t, s).wait_send()
                core_copy(d, t, s).wait_send()
        dt_copy(s).wait_send()
        return carry

    lax.fori_loop(1, n, drain, 0)

    @pl.when(rank < ndev - 1)
    def _():
        tail_copy().wait_send()


def run_project(tokens, w_in, w_dt):
    n, n_out = lax.axis_size("inner"), lax.axis_size("outer")
    length, depth = tokens.shape
    local, xbc = w_in.shape
    block = max(local, 128)
    tail_rows = 16
    dt_block = w_dt.T
    if block != local:
        start = lax.rem(lax.axis_index("inner") * local, block)
        dt_block = lax.dynamic_update_slice(
            jnp.zeros((HEADS, block), BF16), dt_block, (jnp.int32(0), start)
        )
    streams = xbc // 4 // 128
    dma = pltpu.SemaphoreType.DMA
    vmem = pl.BlockSpec(memory_space=pltpu.VMEM)
    whole = pl.BlockSpec(memory_space=pl.ANY)
    return pl.pallas_call(
        partial(project_kernel, n, n_out),
        out_shape=(
            jax.ShapeDtypeStruct((length, xbc), BF16),
            jax.ShapeDtypeStruct((tail_rows, xbc), BF16),
            jax.ShapeDtypeStruct((length, HEADS), BF16),
        ),
        in_specs=[whole, whole, vmem],
        out_specs=(vmem, vmem, vmem),
        scratch_shapes=[
            pltpu.VMEM((length + tail_rows, depth), BF16),
            pltpu.VMEM((2, depth, xbc // 2), BF16),
            pltpu.VMEM((xbc // 256, length + tail_rows, 256), F32),
            pltpu.VMEM((n, HEADS, block), BF16),
            dma((2, streams, n)), dma((2, streams, n)),
            dma((2, streams, n)), dma((2, streams, n)),
            dma((2, streams, n)), dma((2, streams, n)),
            dma((n,)), dma((n,)), dma((3,)), dma(()), dma(()),
        ],
        compiler_params=pltpu.CompilerParams(
            collective_id=2, has_side_effects=True, vmem_limit_bytes=60 * 2**20
        ),
        name="project",
    )(tokens, w_in, dt_block)


def fused_kernel(
    n, n_out,
    tokens, w_in, w_dt, conv_w_in, conv_b_in, dt_bias_in, a_log_in, d_skip_in, gain_in,
    mixed_out, entry_all,
    conv_w, conv_b, dt_bias, a_log, d_skip, gain, mixed, entry_out,
    tail_rows_in, tail_send, tail_recv, decays,
    tok, held, total, held_dt, dt_acc, half_w, bias_row, gain_s, skip_row,
    conv, log_s, log_t, step_s, fac_s, reach_s, edge, scores, mix_s, local_s, y,
    send1, recv1, prefix, mid_send, mid_recv, start, send2, recv2, dec_send, dec_recv,
    ring_s, ring_r, side_s, side_r, core_s, core_r, dt_s, dt_r, dc_s, dc_r, misc, tail_s, tail_r,
    ss1, rs1, ssm, rsm, ss2, rs2, ssd, rsd, small, out_sems,
):
    length, depth = tokens.shape
    local, xbc = w_in.shape
    tail_rows = tok.shape[0] - length
    wide, lanes = 256, 128
    blocks = xbc // wide
    groups = HP // wide
    early = groups
    late = blocks - early
    steps = n // 2
    half = local // 2
    third = (half * 5 // 16) // 16 * 16
    chunks = length // CHUNK
    ndev = n * n_out
    team = ndev // 2
    rows = wide // team
    me = lax.axis_index("inner")
    core = lax.axis_index("outer")
    grp = lax.axis_index("grp")
    rank = core * n + me
    odd = lax.rem(me, 2)
    pos = jnp.where(odd == 0, lax.div(me, 2), n - lax.div(me + 1, 2))
    upper = lax.div(me, n // 2)
    base = upper * (n // 2)
    own = (me - base) * n_out + core
    slot = core * (n // 2) + me - base

    def index_at(q):
        q = lax.rem(q + 2 * n, n)
        return jnp.where(q < n // 2, 2 * q, 2 * n - 1 - 2 * q)

    def place(g):
        return {"inner": lax.rem(g, n), "outer": lax.div(g, n)}

    barrier = pltpu.get_barrier_semaphore()

    def greet(k, carry):
        pl.semaphore_signal(
            barrier, inc=1, device_id=place(lax.rem(rank + k, ndev)), device_id_type=MESH
        )
        return carry

    lax.fori_loop(1, ndev, greet, 0)
    pl.semaphore_signal(barrier, inc=1, device_id={"grp": 1 - grp}, device_id_type=MESH)

    own_rows = pl.ds(pl.multiple_of(me * local, local), local)

    def natural(q):
        return groups if q == 0 else (blocks - 1 if q == blocks - 1 else q - 1)

    load_tok = pltpu.make_async_copy(
        tokens, tok.at[pl.ds(tail_rows, length)], misc.at[blocks]
    )
    load_w = [
        pltpu.make_async_copy(
            w_in.at[:, pl.ds(natural(q) * wide, wide)],
            held.at[q, own_rows], misc.at[q],
        )
        for q in range(blocks)
    ]
    for copy in load_w:
        copy.start()
    load_small = [
        pltpu.make_async_copy(source, target, small.at[k])
        for k, (source, target) in enumerate((
            (w_dt, held_dt.at[me]), (conv_w_in, conv_w), (conv_b_in, conv_b),
            (dt_bias_in, dt_bias), (a_log_in, a_log), (d_skip_in, d_skip), (gain_in, gain),
            (tokens.at[pl.ds(length - tail_rows, tail_rows)], tail_rows_in),
        ))
    ]
    for copy in load_small:
        copy.start()

    @pl.when(rank == 0)
    def _():
        tok[0:tail_rows] = jnp.zeros((tail_rows, depth), BF16)

    def owner_of(d, s):
        return index_at(pos - s) if d == 0 else index_at(pos + s)

    def share(whole):
        return third if whole else half // 2

    def columns(d, whole):
        return slice(0, wide) if whole else slice(d * lanes, (d + 1) * lanes)

    def ring_between(d, q, s, source, whole):
        start = owner_of(d, source) * local + core * half + grp * share(whole)
        span = pl.ds(pl.multiple_of(start, 16), half - share(whole))
        part = held.at[q, span, columns(d, whole)]
        target = index_at(pos + 1) if d == 0 else index_at(pos - 1)
        return pltpu.make_async_remote_copy(
            src_ref=part, dst_ref=part, send_sem=ring_s.at[d, q, s],
            recv_sem=ring_r.at[d, q, s], device_id={"inner": target}, device_id_type=MESH,
        )

    def ring_copy(d, q, s, whole):
        return ring_between(d, q, s, s - 1, whole)

    def side_between(d, q, s, which, whole):
        start = owner_of(d, s) * local + core * half + which * (half - share(whole))
        span = pl.ds(pl.multiple_of(start, 16), share(whole))
        part = held.at[q, span, columns(d, whole)]
        return pltpu.make_async_remote_copy(
            src_ref=part, dst_ref=part, send_sem=side_s.at[d, q, s],
            recv_sem=side_r.at[d, q, s], device_id={"grp": 1 - grp}, device_id_type=MESH,
        )

    def core_between(d, q, s, which, whole):
        start = owner_of(d, s) * local + which * half
        part = held.at[q, pl.ds(pl.multiple_of(start, 16), half), columns(d, whole)]
        return pltpu.make_async_remote_copy(
            src_ref=part, dst_ref=part, send_sem=core_s.at[d, q, s],
            recv_sem=core_r.at[d, q, s], device_id={"outer": 1 - core}, device_id_type=MESH,
        )

    def dt_part(owner, which):
        return held_dt.at[owner, :, pl.ds(pl.multiple_of(which * half, 128), half)]

    def dt_copy(k):
        peer = lax.rem(me + k, n)
        return pltpu.make_async_remote_copy(
            src_ref=dt_part(me, core), dst_ref=dt_part(me, core), send_sem=dt_s.at[k],
            recv_sem=dt_r.at[me], device_id={"inner": peer}, device_id_type=MESH,
        )

    def dt_arrival(k):
        peer = lax.rem(me + k, n)
        pltpu.make_async_remote_copy(
            src_ref=dt_part(peer, core), dst_ref=dt_part(peer, core), send_sem=dt_s.at[k],
            recv_sem=dt_r.at[peer], device_id={"inner": peer}, device_id_type=MESH,
        ).wait_recv()

    def dt_core(owner, which):
        return pltpu.make_async_remote_copy(
            src_ref=dt_part(owner, which), dst_ref=dt_part(owner, which),
            send_sem=dc_s.at[owner], recv_sem=dc_r.at[owner],
            device_id={"outer": 1 - core}, device_id_type=MESH,
        )

    def tail_copy():
        return pltpu.make_async_remote_copy(
            src_ref=tail_send, dst_ref=tail_recv, send_sem=tail_s,
            recv_sem=tail_r, device_id=place(lax.rem(rank + 1, ndev)), device_id_type=MESH,
        )

    def decay_copy(g):
        return pltpu.make_async_remote_copy(
            src_ref=dec_send, dst_ref=dec_recv.at[rank], send_sem=ssd.at[g],
            recv_sem=rsd.at[rank], device_id=place(g), device_id_type=MESH,
        )

    def member(o):
        return {"inner": base + lax.div(o, n_out), "outer": lax.rem(o, n_out)}

    def member_at(k):
        return {"inner": base + lax.rem(k, n // 2), "outer": lax.div(k, n // 2)}

    def first_copy(j, o):
        return pltpu.make_async_remote_copy(
            src_ref=send1.at[j, o], dst_ref=recv1.at[j, slot], send_sem=ss1.at[j, o],
            recv_sem=rs1.at[j, slot], device_id=member(o), device_id_type=MESH,
        )

    def first_arrival(j, k):
        pltpu.make_async_remote_copy(
            src_ref=send1.at[j, k], dst_ref=recv1.at[j, k], send_sem=ss1.at[j, k],
            recv_sem=rs1.at[j, k], device_id=member_at(k), device_id_type=MESH,
        ).wait_recv()

    batches = [slice(0, groups - 1), slice(groups - 1, groups)]

    def mid_copy(b, c):
        return pltpu.make_async_remote_copy(
            src_ref=mid_send.at[c, batches[b]], dst_ref=mid_recv.at[c, batches[b]],
            send_sem=ssm.at[b, c], recv_sem=rsm.at[b, c],
            device_id={"inner": me + n // 2 - upper * n}, device_id_type=MESH,
        )

    def second_copy(b, k):
        return pltpu.make_async_remote_copy(
            src_ref=send2.at[k, batches[b]], dst_ref=recv2.at[own, batches[b]],
            send_sem=ss2.at[b, k], recv_sem=rs2.at[b, own],
            device_id=member_at(k), device_id_type=MESH,
        )

    def second_arrival(b, o):
        pltpu.make_async_remote_copy(
            src_ref=send2.at[o, batches[b]], dst_ref=recv2.at[o, batches[b]],
            send_sem=ss2.at[b, o], recv_sem=rs2.at[b, o],
            device_id=member(o), device_id_type=MESH,
        ).wait_recv()

    def arrive(buffer, sems, r, peer):
        pltpu.make_async_remote_copy(
            src_ref=buffer.at[r], dst_ref=buffer.at[r], send_sem=sems.at[r],
            recv_sem=sems.at[r], device_id=peer, device_id_type=MESH,
        ).wait_recv()

    for copy in load_small:
        copy.wait()

    kept = tail_rows_in[...].astype(F32)[tail_rows - CONV :]
    part_cols = depth // CONV
    tail_send[...] = jnp.concatenate(
        [kept[:, k * part_cols : (k + 1) * part_cols] for k in range(CONV)], axis=0
    ).astype(BF16)

    half_w[...] = conv_w[...] * 0.5
    bias_row[...] = conv_b[...].reshape(1, xbc) * 0.5
    gain_s[...] = gain[...].reshape(1, HP)

    def spread_of(j, count):
        head = lax.rem(lax.broadcasted_iota(jnp.int32, (count, wide), 0), HEADS)
        col = lax.broadcasted_iota(jnp.int32, (count, wide), 1) // P_SIZE
        return (head == col + j * (wide // P_SIZE)).astype(F32).astype(BF16)

    def split(values):
        high = values.astype(BF16).astype(F32)
        lane = lax.broadcasted_iota(jnp.int32, values.shape, 1)
        return jnp.where(lane < HEADS, high, values - high).astype(BF16)

    skip = d_skip[...].reshape(1, HEADS)
    skip_high = skip.astype(BF16).astype(F32)
    for j in range(groups):
        skip_row[:, j * wide : (j + 1) * wide] = expand(
            skip - skip_high, spread_of(j, HEADS)
        ) + jnp.dot(skip_high.astype(BF16), spread_of(j, HEADS), preferred_element_type=F32)

    pl.semaphore_wait(barrier, ndev)

    @pl.when(rank < ndev - 1)
    def _():
        tail_copy().start()

    def send_dt(k, carry):
        dt_copy(k).start()
        return carry

    lax.fori_loop(1, n, send_dt, 0)
    for q in range(early):
        load_w[q].wait()
        for d in range(2):
            ring_copy(d, q, 1, True).start()
    load_tok.start()
    for q in range(early, blocks):
        load_w[q].wait()

    def multiply(q, shards, first):
        product = None if first else total[q]
        for owner in shards:
            at = pl.ds(pl.multiple_of(owner * local, local), local)
            term = jnp.dot(tok[:, at], held[q, at, :], preferred_element_type=F32)
            product = term if product is None else product + term
        total[q] = product

    all_parts = blocks * steps
    side_lag, core_lag = 3, 4
    second, third_turn = early, 2 * early + 1
    fifth = third_turn + (steps - 2) * blocks

    def item(i):
        full = jnp.maximum(i - third_turn, 0)
        t = jnp.where(i < second, 1, jnp.where(i < third_turn, 2, 3 + lax.div(full, blocks)))
        q = jnp.where(
            i < second, i, jnp.where(i < third_turn, i - second, lax.rem(full, blocks))
        )
        t = jnp.where(i < fifth, t, jnp.where(i < fifth + 2, steps + 1, steps + 2))
        q = jnp.where(i < fifth, q, jnp.where(i < fifth + 1, early, early + 1))
        return q, t - jnp.maximum(q - early + 1, 0)

    def exchange(i):
        q, s = item(i)

        @pl.when((i < all_parts) & (s < steps))
        def _():
            for d in range(2):
                ring_between(d, q, s, s, True).wait_recv()

                @pl.when(s < steps - 1)
                def _():
                    ring_copy(d, q, s + 1, True).start()

                @pl.when(s == steps - 1)
                def _():
                    ring_copy(d, q, s + 1, False).start()

                side_between(d, q, s, grp, True).start()

        @pl.when((i < all_parts) & (s == steps))
        def _():
            for d in range(2):
                ring_between(d, q, s, s, False).wait_recv()
                side_between(d, q, s, grp, False).start()

        for k in range(late):
            @pl.when(i == (early - 1, 2 * early)[k])
            def _():
                for d in range(2):
                    ring_copy(d, early + k, 1, True).start()

        q, s = item(jnp.maximum(i - side_lag, 0))
        for whole in (True, False):
            @pl.when((i >= side_lag) & (i < all_parts + side_lag) & ((s < steps) == whole))
            def _():
                for d in range(2):
                    side_between(d, q, s, 1 - grp, whole).wait_recv()
                    core_between(d, q, s, core, whole).start()

    def accumulate(i):
        q, s = item(jnp.maximum(i - core_lag, 0))

        @pl.when((i >= core_lag) & (s < steps))
        def _():
            for d in range(2):
                core_between(d, q, s, 1 - core, True).wait_recv()
            multiply(q, [owner_of(0, s), owner_of(1, s)], False)

        @pl.when((i >= core_lag) & (s == steps))
        def _():
            for d in range(2):
                core_between(d, q, s, 1 - core, False).wait_recv()
            multiply(q, [owner_of(0, s)], False)

        @pl.when((i < early) | (i == 6) | (i == 10))
        def _():
            multiply(jnp.where(i < early, i, early + lax.div(jnp.maximum(i - 6, 0), 4)), [me], True)

    def add_dt(k):
        @pl.when(k != me)
        def _():
            dt_core(k, 1 - core).wait_recv()

        cols = pl.ds(pl.multiple_of(k * local, local), local)
        part = lax.dot_general(
            tok[tail_rows:, cols], held_dt[k], LAST, preferred_element_type=F32
        )

        @pl.when(k == 0)
        def _():
            dt_acc[...] = part

        @pl.when(k > 0)
        def _():
            dt_acc[...] = dt_acc[...] + part

    def early_part(i, carry):
        exchange(i)

        @pl.when((i == 0) & (rank > 0))
        def _():
            tail_copy().wait_recv()
            for k in range(CONV):
                rows_k = tail_recv[...].astype(F32)[k * CONV : (k + 1) * CONV]
                above = jnp.zeros((tail_rows - CONV, part_cols), F32)
                tok[0:tail_rows, k * part_cols : (k + 1) * part_cols] = jnp.concatenate(
                    [above, rows_k], axis=0
                ).astype(BF16)

        @pl.when(i == 0)
        def _():
            load_tok.wait()

        accumulate(i)

        @pl.when((i < n) & (i != me))
        def _():
            dt_arrival(lax.rem(i - me + n, n))
            dt_core(i, core).start()

        @pl.when(i >= 2)
        def _():
            add_dt(i - 2)

        return carry

    lax.fori_loop(0, 10, early_part, 0)

    row_id = lax.broadcasted_iota(jnp.int32, (CHUNK, CHUNK), 0)
    col_id = lax.broadcasted_iota(jnp.int32, (CHUNK, CHUNK), 1)
    causal = col_id <= row_id
    dt_raw = dt_acc[...].astype(BF16).astype(F32)
    step_one = jax.nn.softplus(dt_raw + dt_bias[...].reshape(1, HEADS))
    scaled = step_one * (-jnp.exp(a_log[...].reshape(1, HEADS)))
    scaled = jnp.concatenate([scaled, scaled], axis=1)
    step_size = jnp.concatenate([step_one, step_one], axis=1)
    before = jnp.zeros((1, 2 * HEADS), F32)
    lower = causal.astype(F32)
    for c in range(chunks):
        here = slice(c * CHUNK, (c + 1) * CHUNK)
        part = jnp.dot(
            lower, scaled[here], preferred_element_type=F32,
            precision=lax.Precision.HIGHEST,
        ) + before
        log_s[here] = part
        reach_s[here] = split(jnp.exp(part - before))
        before = part[CHUNK - 1 : CHUNK]
        fac_s[here] = split(jnp.exp(before - part) * step_size[here])
    flat = jnp.transpose(log_s[...])[0:HEADS]
    log_t[...] = jnp.transpose(log_s[...] - jnp.log(step_size))[0:HEADS]
    ends = [flat[:, (c + 1) * CHUNK - 1 : (c + 1) * CHUNK] for c in range(chunks)]
    dec_send[...] = jnp.zeros((1, 128), F32)
    dec_send[:, 0 : 2 * HEADS] = jnp.exp(before)
    dec_recv[rank] = dec_send[...]

    def tall_of(column):
        column = jnp.broadcast_to(column, (HEADS, 128)).reshape(HEADS, 1, 128)
        return jnp.broadcast_to(column, (HEADS, P_SIZE, 128)).reshape(HP, 128)

    for c in range(1, chunks):
        edge[0, c - 1] = tall_of(jnp.exp(ends[c] - ends[c - 1]))
        edge[1, c - 1] = tall_of(jnp.exp(ends[c - 1]))

    def send_decay(k, carry):
        decay_copy(lax.rem(rank + k, ndev)).start()
        return carry

    lax.fori_loop(1, ndev, send_decay, 0)

    def conv_column(block):
        q = jnp.where(block < groups, block + 1, (blocks - 1) * (block - groups))
        cols = pl.ds(pl.multiple_of(block * wide, wide), wide)

        def one(i, carry):
            start = pl.multiple_of(i * 128, 128)
            window = total[q, pl.ds(pl.multiple_of(start + tail_rows - 8, 8), 136), :]
            window = window.astype(BF16).astype(F32)
            acc = bias_row[:, cols]
            for k in range(CONV):
                acc = acc + half_w[k : k + 1, cols] * window[5 + k : 5 + k + 128]
            conv[pl.ds(start, 128), cols] = (acc + acc * jnp.tanh(acc)).astype(BF16)
            return carry

        lax.fori_loop(0, length // 128, one, 0)

    def score_all():
        def one(c, carry):
            here = pl.ds(pl.multiple_of(c * CHUNK, CHUNK), CHUNK)
            product = lax.dot_general(
                conv[here, HP + N :], conv[here, HP : HP + N], LAST,
                preferred_element_type=F32,
            )
            scores[c] = jnp.where(causal, product, 0.0)
            return carry

        lax.fori_loop(0, chunks, one, 0)

    heads_each = HEADS // groups

    def mix(c, j):
        here = pl.ds(pl.multiple_of(c * CHUNK, CHUNK), CHUNK)
        log_c = log_s[here]
        for k in range(heads_each):
            h = j * heads_each + k
            gap = jnp.minimum(log_c[:, h : h + 1] - log_t[h : h + 1, here], 60.0)
            mix_s[h, c] = (scores[c] * jnp.exp(gap)).astype(BF16)

    def contribute(j):
        cols = pl.ds(pl.multiple_of(j * wide, wide), wide)
        spread = spread_of(j, 2 * HEADS)
        state = None
        for c in range(chunks):
            here = slice(c * CHUNK, (c + 1) * CHUNK)
            factor = jnp.dot(fac_s[here], spread, preferred_element_type=F32)
            weighted = (factor * conv[here, cols].astype(F32)).astype(BF16)
            part = lax.dot_general(
                weighted, conv[here, HP : HP + N], FIRST, preferred_element_type=F32
            )
            if c > 0:
                local_s[c - 1, cols] = state
                scale = edge[0, c - 1, cols, :]
                part = part + jnp.concatenate([scale, scale], axis=1) * state
            state = part
        send1[j] = state.reshape(team, rows, N).astype(BF16)

        def send_one(o, inner):
            @pl.when(o != own)
            def _():
                first_copy(j, o).start()

            return inner

        lax.fori_loop(0, team, send_one, 0)

    def inside(j):
        cols = pl.ds(pl.multiple_of(j * wide, wide), wide)
        lane = lax.broadcasted_iota(jnp.int32, (1, wide), 1) // P_SIZE

        def one(c, carry):
            here = pl.ds(pl.multiple_of(c * CHUNK, CHUNK), CHUNK)
            x_rows = conv[here, cols]
            acc = skip_row[:, cols] * x_rows.astype(F32)
            for k in range(heads_each):
                keep = (lane == k).astype(F32).astype(BF16)
                acc = acc + jnp.dot(
                    mix_s[j * heads_each + k, c], x_rows * keep, preferred_element_type=F32
                )
            y[here, cols] = acc
            return carry

        lax.fori_loop(0, chunks, one, 0)

    def decay_of(k, half_of, j):
        r = lax.div(k, n // 2) * n + half_of * (n // 2) + lax.rem(k, n // 2)
        return decays[j, pl.ds(r, 1), :]

    def combine(b):
        for j in range(groups)[batches[b]]:
            recv1[j, slot] = send1[j, own]

            def arrived(k, carry):
                @pl.when(k != slot)
                def _():
                    first_arrival(j, k)

                return carry

            lax.fori_loop(0, team, arrived, 0)
            for c in range(2):
                state = jnp.zeros((rows, N), F32)
                for m in range(n // 2):
                    k = c * (n // 2) + m
                    prefix[j, k] = state
                    state = decay_of(k, upper, j) * state + recv1[j, k].astype(F32)
                mid_send[c, j] = state.astype(BF16)
        mid_copy(b, 0).start()

        @pl.when(upper == 0)
        def _():
            mid_copy(b, 1).start()

    def product_of(c, half_of, j):
        result = decay_of(c * (n // 2), half_of, j)
        for m in range(1, n // 2):
            result = result * decay_of(c * (n // 2) + m, half_of, j)
        return result

    def distribute(b):
        mid_copy(b, 0).wait_recv()

        @pl.when(upper == 1)
        def _():
            mid_copy(b, 1).wait_recv()

        is_upper = upper == 1
        for j in range(groups)[batches[b]]:
            middle = mid_recv[0, j].astype(F32)
            ours = mid_send[0, j].astype(F32)
            lower_sum = jnp.where(is_upper, middle, ours)
            upper_sum = jnp.where(is_upper, ours, middle)
            block_end = product_of(0, 1, j) * lower_sum + upper_sum

            @pl.when(is_upper)
            def _():
                start[0, j] = middle
                start[1, j] = product_of(1, 0, j) * block_end + mid_recv[1, j].astype(F32)

            @pl.when(upper == 0)
            def _():
                start[0, j] = jnp.zeros((rows, N), F32)
                start[1, j] = block_end

        for k in range(team):
            for j in range(groups)[batches[b]]:
                state = start[k // (n // 2), j]
                send2[k, j] = (prefix[j, k] + state).astype(BF16)
                start[k // (n // 2), j] = decay_of(k, upper, j) * state

            @pl.when(k != slot)
            def _():
                second_copy(b, k).start()

        recv2[own, batches[b]] = send2[slot, batches[b]]

    def late_part(i, carry):
        exchange(i)
        accumulate(i)
        ready = fifth - blocks + core_lag + 1

        @pl.when(i == ready - 1)
        def _():
            conv_column(groups)

        @pl.when((i >= ready) & (i < ready + groups - 1))
        def _():
            conv_column(i - ready)
            contribute(i - ready)

        @pl.when(i == ready + groups - 1)
        def _():
            others()

        @pl.when(i == all_parts + 2)
        def _():
            combine(0)

        @pl.when(i == fifth + core_lag)
        def _():
            conv_column(groups - 1)
            contribute(groups - 1)

        return carry

    def others():
        def one(k, carry):
            r = lax.rem(rank + k, ndev)
            arrive(dec_recv, rsd, r, place(r))
            return carry

        lax.fori_loop(1, ndev, one, 0)
        every = jnp.concatenate([dec_recv[r] for r in range(ndev)], axis=0)
        lane = lax.broadcasted_iota(jnp.int32, (ndev, 128), 1)
        for j in range(groups):
            head = j * heads_each + lax.div(own * rows, P_SIZE)
            column = jnp.sum(jnp.where(lane == head, every, 0.0), axis=1, keepdims=True)
            decays[j] = jnp.broadcast_to(column, (ndev, N))

    lax.fori_loop(10, all_parts + core_lag, late_part, 0)

    conv_column(groups + 1)
    score_all()

    def fill(j, carry):
        for k in range(groups):
            @pl.when(j == k)
            def _():
                def one(c, inner):
                    mix(c, k)
                    return inner

                lax.fori_loop(0, chunks, one, 0)

        inside(j)
        return carry

    combine(1)
    lax.fori_loop(0, 1, fill, 0)
    distribute(0)
    lax.fori_loop(1, groups - 1, fill, 0)
    distribute(1)
    lax.fori_loop(groups - 1, groups, fill, 0)

    row_head = lax.broadcasted_iota(jnp.int32, (wide, wide), 0) // P_SIZE
    col_head = lax.broadcasted_iota(jnp.int32, (wide, wide), 1) // P_SIZE
    same = (row_head == col_head).astype(F32).astype(BF16)

    def out_copies(j):
        cols = pl.ds(pl.multiple_of(j * wide, wide), wide)
        return [
            pltpu.make_async_copy(
                mixed.at[:, cols], mixed_out.at[:, cols], out_sems.at[0, j]
            ),
            pltpu.make_async_copy(
                entry_out.at[cols], entry_all.at[cols], out_sems.at[1, j]
            ),
        ]

    def finish_group(j, carry):
        cols = pl.ds(pl.multiple_of(j * wide, wide), wide)
        entry = jnp.concatenate([recv2[o, j] for o in range(team)], axis=0).astype(F32)
        entry_out[cols] = entry.astype(BF16)
        spread = spread_of(j, 2 * HEADS)
        for c in range(chunks):
            here = slice(c * CHUNK, (c + 1) * CHUNK)
            state = entry
            if c > 0:
                scale = edge[1, c - 1, cols, :]
                state = local_s[c - 1, cols] + jnp.concatenate([scale, scale], axis=1) * entry
            carried = lax.dot_general(
                conv[here, HP + N :], state.astype(BF16), LAST, preferred_element_type=F32
            )
            reach = jnp.dot(reach_s[here], spread, preferred_element_type=F32)
            out = y[here, cols] + reach * carried
            square = (out * out).astype(BF16)
            sums = jnp.dot(square, same, preferred_element_type=F32)
            inv_rms = lax.rsqrt(sums * (1.0 / P_SIZE) + EPSILON)
            mixed[here, cols] = (out * inv_rms * gain_s[:, cols]).astype(BF16)
        for copy in out_copies(j):
            copy.start()
        return carry

    def wait_second(b):
        def one(o, carry):
            @pl.when(o != own)
            def _():
                second_arrival(b, o)

            return carry

        lax.fori_loop(0, team, one, 0)

    wait_second(0)
    lax.fori_loop(0, groups - 1, finish_group, 0)
    wait_second(1)
    lax.fori_loop(groups - 1, groups, finish_group, 0)

    def drain_out(j, carry):
        for copy in out_copies(j):
            copy.wait()
        return carry

    def drain(q, carry):
        for d in range(2):
            for s in range(1, steps + 1):
                whole = s < steps
                ring_copy(d, q, s, whole).wait_send()
                side_between(d, q, s, grp, whole).wait_send()
                core_between(d, q, s, core, whole).wait_send()
        return carry

    lax.fori_loop(0, blocks, drain, 0)

    def drain_dt(k, carry):
        dt_copy(k).wait_send()
        dt_core(lax.rem(me + k, n), core).wait_send()
        return carry

    lax.fori_loop(1, n, drain_dt, 0)

    def drain_decay(k, carry):
        decay_copy(lax.rem(rank + k, ndev)).wait_send()
        return carry

    lax.fori_loop(1, ndev, drain_decay, 0)

    def drain_state(k, carry):
        @pl.when(k != own)
        def _():
            for j in range(groups):
                first_copy(j, k).wait_send()

        @pl.when(k != slot)
        def _():
            for b in range(2):
                second_copy(b, k).wait_send()

        return carry

    lax.fori_loop(0, team, drain_state, 0)
    for b in range(2):
        mid_copy(b, 0).wait_send()

    @pl.when(upper == 0)
    def _():
        for b in range(2):
            mid_copy(b, 1).wait_send()

    @pl.when(rank < ndev - 1)
    def _():
        tail_copy().wait_send()

    lax.fori_loop(0, groups, drain_out, 0)


def run_fused(tokens, w_in, w_dt, conv_w, conv_b, dt_bias, a_log, d_skip, norm_gain):
    n, n_out = lax.axis_size("inner"), lax.axis_size("outer")
    ndev = n * n_out
    length, depth = tokens.shape
    local, xbc = w_in.shape
    team = ndev // 2
    groups = HP // 256
    rows = 256 // team
    tail_rows = 16
    blocks = xbc // 256
    chunks = length // CHUNK
    dma = pltpu.SemaphoreType.DMA
    whole = pl.BlockSpec(memory_space=pl.ANY)
    weight_sems = [dma((2, blocks, n // 2 + 1))] * 6
    first_sems = [dma((groups, team))] * 2
    swap_sems = [dma((2, 2))] * 2
    second_sems = [dma((2, team))] * 2
    rank_sems = [dma((ndev,))] * 2
    return pl.pallas_call(
        partial(fused_kernel, n, n_out),
        out_shape=(
            jax.ShapeDtypeStruct((length, HP), BF16),
            jax.ShapeDtypeStruct((HP, N), BF16),
        ),
        in_specs=[whole] * 9,
        out_specs=(whole, whole),
        scratch_shapes=[
            pltpu.VMEM((CONV, xbc), F32), pltpu.VMEM((xbc,), F32),
            pltpu.VMEM((HEADS,), F32), pltpu.VMEM((HEADS,), F32),
            pltpu.VMEM((HEADS,), F32), pltpu.VMEM((HP,), F32),
            pltpu.VMEM((length, HP), BF16), pltpu.VMEM((HP, N), BF16),
            pltpu.VMEM((tail_rows, depth), BF16),
            pltpu.VMEM((tail_rows, depth // 4), BF16),
            pltpu.VMEM((tail_rows, depth // 4), BF16),
            pltpu.VMEM((groups, ndev, N), F32),
            pltpu.VMEM((length + tail_rows, depth), BF16),
            pltpu.VMEM((blocks, depth, 256), BF16),
            pltpu.VMEM((blocks, length + tail_rows, 256), F32),
            pltpu.VMEM((n, HEADS, local), BF16),
            pltpu.VMEM((length, HEADS), F32),
            pltpu.VMEM((CONV, xbc), F32),
            pltpu.VMEM((1, xbc), F32),
            pltpu.VMEM((1, HP), F32),
            pltpu.VMEM((1, HP), F32),
            pltpu.VMEM((length, xbc), BF16),
            pltpu.VMEM((length, 2 * HEADS), F32),
            pltpu.VMEM((HEADS, length), F32),
            pltpu.VMEM((length, 2 * HEADS), F32),
            pltpu.VMEM((length, 2 * HEADS), BF16),
            pltpu.VMEM((length, 2 * HEADS), BF16),
            pltpu.VMEM((2, chunks - 1, HP, 128), F32),
            pltpu.VMEM((chunks, CHUNK, CHUNK), F32),
            pltpu.VMEM((HEADS, chunks, CHUNK, CHUNK), BF16),
            pltpu.VMEM((chunks - 1, HP, N), F32),
            pltpu.VMEM((length, HP), F32),
            pltpu.VMEM((groups, team, rows, N), BF16),
            pltpu.VMEM((groups, team, rows, N), BF16),
            pltpu.VMEM((groups, team, rows, N), F32),
            pltpu.VMEM((2, groups, rows, N), BF16),
            pltpu.VMEM((2, groups, rows, N), BF16),
            pltpu.VMEM((2, groups, rows, N), F32),
            pltpu.VMEM((team, groups, rows, N), BF16),
            pltpu.VMEM((team, groups, rows, N), BF16),
            pltpu.VMEM((1, 128), F32),
            pltpu.VMEM((ndev, 1, 128), F32),
            *weight_sems,
            dma((n,)), dma((n,)), dma((n,)), dma((n,)), dma((blocks + 1,)), dma(()), dma(()),
            *first_sems, *swap_sems, *second_sems, *rank_sems, dma((8,)), dma((2, groups)),
        ],
        compiler_params=pltpu.CompilerParams(
            collective_id=3, has_side_effects=True, vmem_limit_bytes=62 * 2**20
        ),
        name="fused",
    )(
        tokens, w_in, w_dt.T, conv_w, conv_b, dt_bias, a_log, d_skip, norm_gain,
    )


def hand_over_kernel(
    mixed, entry, mixed_out, entry_out, held_m, held_e, wide_e, in_sems, out_sems
):
    parts = in_sems.shape[1]
    loads, stores = [], []
    arrays = ((entry, held_e, wide_e, entry_out), (mixed, held_m, held_m, mixed_out))
    for i, (source, held, ready, target) in enumerate(arrays):
        rows = source.shape[0] // parts
        for k in range(parts):
            at = pl.ds(k * rows, rows)
            loads.append(pltpu.make_async_copy(source.at[at], held.at[at], in_sems.at[i, k]))
            stores.append(pltpu.make_async_copy(ready.at[at], target.at[at], out_sems.at[i, k]))
    for load in loads:
        load.start()
    rows = entry.shape[0] // parts
    for k, (load, store) in enumerate(zip(loads, stores)):
        load.wait()
        if k < parts:
            at = slice(k * rows, (k + 1) * rows)
            wide_e[at] = held_e[at].astype(F32)
        store.start()
    for store in stores:
        store.wait()


def hand_over(mixed, entry):
    whole = pl.BlockSpec(memory_space=pl.ANY)
    sems = pltpu.SemaphoreType.DMA((2, 4))
    return pl.pallas_call(
        hand_over_kernel,
        out_shape=(
            jax.ShapeDtypeStruct(mixed.shape, mixed.dtype),
            jax.ShapeDtypeStruct(entry.shape, F32),
        ),
        in_specs=[whole, whole],
        out_specs=(whole, whole),
        scratch_shapes=[
            pltpu.VMEM(mixed.shape, mixed.dtype), pltpu.VMEM(entry.shape, entry.dtype),
            pltpu.VMEM(entry.shape, F32), sems, sems,
        ],
        name="hand_over",
    )(mixed, entry)


def per_device(tokens, w_in, w_dt, conv_w, conv_b, dt_bias, a_log, d_skip, norm_gain):
    own_rows = tokens.reshape(tokens.shape[1], tokens.shape[2])
    row_count = own_rows.shape[0]
    if w_in.shape[0] % 512 == 0 and lax.axis_size("inner") == 8:
        mixed, entry = run_fused(
            own_rows, w_in, w_dt, conv_w, conv_b, dt_bias, a_log, d_skip, norm_gain
        )
        mixed, entry = hand_over(mixed, entry)
    else:
        projected, tail, dt_raw = run_project(own_rows, w_in, w_dt)
        mixed, entry = run_scan(
            projected, tail, dt_raw, conv_w, conv_b, dt_bias, a_log, d_skip, norm_gain
        )
    return (
        mixed.reshape(1, row_count, HP),
        entry.reshape(1, 1, HEADS, P_SIZE, N),
    )


def solution(mesh):
    placed = (
        P(("grp", "outer"), "inner", None),
        P("inner", None),
        P("inner", None),
        P(), P(), P(), P(), P(), P(),
    )
    return jax.shard_map(
        per_device,
        mesh=mesh,
        in_specs=placed,
        out_specs=(
            P(("grp", "outer"), "inner", None),
            P(("grp", "outer"), "inner", None, None, None),
        ),
        check_vma=False,
    )
```

```python
from functools import partial

import jax
import jax.numpy as jnp
from jax import lax
from jax.experimental import pallas as pl
from jax.experimental.pallas import tpu as pltpu
from jax.sharding import PartitionSpec as P

HEADS = 16
P_SIZE = 64
N = 256
CONV = 4
HP = HEADS * P_SIZE
CHUNK = 256
EPSILON = 1e-05
MESH = pl.DeviceIdType.MESH
F32 = jnp.float32
BF16 = jnp.bfloat16
LAST = (((1,), (1,)), ((), ()))
FIRST = (((0,), (0,)), ((), ()))


def expand(values, spread):
    high = values.astype(BF16)
    low = (values - high.astype(F32)).astype(BF16)
    return jnp.dot(high, spread, preferred_element_type=F32) + jnp.dot(
        low, spread, preferred_element_type=F32
    )


def scan_kernel(
    n_in, ndev,
    proj, tail, dt_raw, conv_w, conv_b, dt_bias, a_log, d_skip, gain,
    mixed, entry_out,
    gain_s, bias_row, skip_row, pad, conv, log_s, log_t, step_s, y, states,
    send1, recv1, send2, recv2, dec_send, dec_recv,
    ss1, rs1, ss2, rs2, ssd, rsd,
):
    length = proj.shape[0]
    chunks = length // CHUNK
    rows = HP // ndev
    me = lax.axis_index("outer") * n_in + lax.axis_index("inner")

    def place(g):
        return {"inner": lax.rem(g, n_in), "outer": lax.div(g, n_in)}

    barrier = pltpu.get_barrier_semaphore()

    def greet(k, carry):
        pl.semaphore_signal(
            barrier, inc=1, device_id=place(lax.rem(me + k, ndev)), device_id_type=MESH
        )
        return carry

    lax.fori_loop(1, ndev, greet, 0)

    head_id = lax.broadcasted_iota(jnp.int32, (HEADS, HP), 0)
    col_head = lax.broadcasted_iota(jnp.int32, (HEADS, HP), 1) // P_SIZE
    spread = (head_id == col_head).astype(F32).astype(BF16)

    bias_row[...] = conv_b[...].reshape(1, conv_b.shape[0])
    gain_s[...] = gain[...].reshape(1, HP)
    skip = d_skip[...].reshape(1, HEADS)
    skip_high = skip.astype(BF16).astype(F32)
    skip_row[...] = expand(skip - skip_high, spread) + jnp.dot(
        skip_high.astype(BF16), spread, preferred_element_type=F32
    )
    step_size = jax.nn.softplus(dt_raw[...].astype(F32) + dt_bias[...].reshape(1, HEADS))
    scaled = step_size * (-jnp.exp(a_log[...].reshape(1, HEADS)))
    row_id = lax.broadcasted_iota(jnp.int32, (CHUNK, CHUNK), 0)
    col_id = lax.broadcasted_iota(jnp.int32, (CHUNK, CHUNK), 1)
    causal = col_id <= row_id
    lower = causal.astype(F32)
    step_s[...] = step_size
    before = jnp.zeros((1, HEADS), F32)
    for c in range(chunks):
        part = jnp.dot(
            lower,
            scaled[c * CHUNK : (c + 1) * CHUNK],
            preferred_element_type=F32,
            precision=lax.Precision.HIGHEST,
        ) + before
        log_s[c * CHUNK : (c + 1) * CHUNK] = part
        before = part[CHUNK - 1 : CHUNK]
    log_t[...] = jnp.transpose(log_s[...])
    dec_send[...] = jnp.broadcast_to(jnp.exp(log_t[:, length - 1 : length]), (HEADS, 128))

    pad[0:8] = tail[...].astype(F32)[8:16]
    pad[8:] = proj[...].astype(F32)
    wide = 256
    blocks = proj.shape[1] // wide

    def conv_block(t, carry):
        i, j = lax.div(t, blocks), lax.rem(t, blocks)
        cols = pl.ds(pl.multiple_of(j * wide, wide), wide)
        window = pad[pl.ds(pl.multiple_of(i * 128, 128), 136), cols]
        total = bias_row[:, cols]
        for k in range(CONV):
            total = total + conv_w[k : k + 1, cols] * window[5 + k : 5 + k + 128]
        conv[pl.ds(pl.multiple_of(i * 128, 128), 128), cols] = (
            total * jax.nn.sigmoid(total)
        ).astype(BF16)
        return carry

    row_blocks = length // 128

    def conv_column(j):
        def one(i, carry):
            return conv_block(i * blocks + j, carry)

        lax.fori_loop(0, row_blocks, one, 0)

    conv_column(HP // wide)

    def weighted_sum(stop):
        final = log_s[stop - 1 : stop]
        factor = jnp.exp(final - log_s[0:stop]) * step_s[0:stop]
        weighted = (expand(factor, spread) * conv[0:stop, 0:HP].astype(F32)).astype(BF16)
        return lax.dot_general(
            weighted, conv[0:stop, HP : HP + N], FIRST, preferred_element_type=F32
        )

    dec_recv[me] = dec_send[...]

    def decay_copy(g):
        return pltpu.make_async_remote_copy(
            src_ref=dec_send, dst_ref=dec_recv.at[me], send_sem=ssd.at[g],
            recv_sem=rsd.at[me], device_id=place(g), device_id_type=MESH,
        )

    def first_copy(g):
        return pltpu.make_async_remote_copy(
            src_ref=send1.at[g], dst_ref=recv1.at[me], send_sem=ss1.at[g],
            recv_sem=rs1.at[me], device_id=place(g), device_id_type=MESH,
        )

    def second_copy(g):
        return pltpu.make_async_remote_copy(
            src_ref=send2.at[g], dst_ref=recv2.at[me], send_sem=ss2.at[g],
            recv_sem=rs2.at[me], device_id=place(g), device_id_type=MESH,
        )

    pl.semaphore_wait(barrier, ndev - 1)

    def send_decay(k, carry):
        decay_copy(lax.rem(me + k, ndev)).start()
        return carry

    lax.fori_loop(1, ndev, send_decay, 0)

    groups = HP // wide
    owners = ndev // groups
    own_group = lax.div(me, owners)
    factor = jnp.exp(log_s[length - 1 : length] - log_s[...]) * step_s[...]

    def spread_of(j):
        head = lax.broadcasted_iota(jnp.int32, (HEADS, wide), 0)
        col = lax.broadcasted_iota(jnp.int32, (HEADS, wide), 1) // P_SIZE
        return (head == col + j * (wide // P_SIZE)).astype(F32).astype(BF16)

    def first_group(i, carry):
        j = lax.rem(own_group + 1 + i, groups)
        conv_column(j)
        cols = pl.ds(pl.multiple_of(j * wide, wide), wide)
        weighted = (expand(factor, spread_of(j)) * conv[:, cols].astype(F32)).astype(BF16)
        part = lax.dot_general(
            weighted, conv[:, HP : HP + N], FIRST, preferred_element_type=F32
        )
        send1[pl.ds(j * owners, owners)] = part.reshape(owners, rows, N).astype(BF16)

        def send_one(k, inner):
            g = j * owners + k

            @pl.when(g != me)
            def _():
                first_copy(g).start()

            return inner

        return lax.fori_loop(0, owners, send_one, carry)

    lax.fori_loop(0, groups, first_group, 0)
    recv1[me] = send1[me]
    conv_column(HP // wide + 1)

    states[0] = jnp.zeros((HP, N), BF16)
    for c in range(1, chunks):
        states[c] = weighted_sum(c * CHUNK).astype(BF16)

    def local_chunk(c, carry):
        start = pl.multiple_of(c * CHUNK, CHUNK)
        here = pl.ds(start, CHUNK)
        log_c = log_s[here]
        reached = log_s[pl.ds(pl.multiple_of(jnp.maximum(start - 8, 0), 8), 8)][7:8]
        reached = jnp.where(c > 0, reached, 0.0)
        c_rows = conv[here, HP + N :]
        b_rows = conv[here, HP : HP + N]
        scores = lax.dot_general(c_rows, b_rows, LAST, preferred_element_type=F32)
        scores = jnp.where(causal, scores, 0.0)
        x_rows = conv[here, 0:HP].astype(F32)
        driven = (expand(step_s[here], spread) * x_rows).astype(BF16)
        inter = lax.dot_general(c_rows, states[c], LAST, preferred_element_type=F32)
        y[here] = expand(jnp.exp(log_c - reached), spread) * inter + skip_row[...] * x_rows
        for h in range(0, HEADS, 2):
            pieces = []
            for k in (h, h + 1):
                gap = jnp.minimum(log_c[:, k : k + 1] - log_t[k : k + 1, here], 0.0)
                mixing = (scores * jnp.exp(gap)).astype(BF16)
                pieces.append(
                    jnp.dot(
                        mixing,
                        driven[:, k * P_SIZE : (k + 1) * P_SIZE],
                        preferred_element_type=F32,
                    )
                )
            both = slice(h * P_SIZE, (h + 2) * P_SIZE)
            y[here, both] = y[here, both] + jnp.concatenate(pieces, axis=1)
        return carry

    lax.fori_loop(0, chunks, local_chunk, 0)

    own_head = lax.div(me * rows, P_SIZE)

    def wait_from(copy_of, r):
        copy_of(r).wait_recv()

    def arrive(buffer, sems, r):
        pltpu.make_async_remote_copy(
            src_ref=buffer.at[r], dst_ref=buffer.at[r], send_sem=sems.at[r],
            recv_sem=sems.at[r], device_id=place(r), device_id_type=MESH,
        ).wait_recv()

    def advance(r, state):
        send2[r] = state.astype(BF16)

        @pl.when(r != me)
        def _():
            arrive(dec_recv, rsd, r)
            arrive(recv1, rs1, r)

        decay = dec_recv[r, pl.ds(own_head, 1), :]
        decay = jnp.concatenate([decay, decay], axis=1)
        return decay * state + recv1[r].astype(F32)

    lax.fori_loop(0, ndev, advance, jnp.zeros((rows, N), F32))

    def send_second(k, carry):
        second_copy(lax.rem(me + k, ndev)).start()
        return carry

    lax.fori_loop(1, ndev, send_second, 0)
    recv2[me] = send2[me]

    reach = jnp.exp(log_s[...])

    def last_group(i, carry):
        j = lax.rem(own_group + groups - 1 - i, groups)

        def wait_one(k, inner):
            g = j * owners + k

            @pl.when(g != me)
            def _():
                arrive(recv2, rs2, g)

            return inner

        lax.fori_loop(0, owners, wait_one, 0)
        cols = pl.ds(pl.multiple_of(j * wide, wide), wide)
        entry = recv2[pl.ds(j * owners, owners)].astype(F32).reshape(wide, N)
        entry_out[cols] = entry
        carried = lax.dot_general(
            conv[:, HP + N :], entry.astype(BF16), LAST, preferred_element_type=F32
        )
        spread_j = spread_of(j)
        out = y[:, cols] + expand(reach, spread_j) * carried
        square = out * out
        high = square.astype(BF16)
        low = (square - high.astype(F32)).astype(BF16)
        sums = lax.dot_general(high, spread_j, LAST, preferred_element_type=F32)
        sums = sums + lax.dot_general(low, spread_j, LAST, preferred_element_type=F32)
        inv_rms = lax.rsqrt(sums * (1.0 / P_SIZE) + EPSILON)
        mixed[:, cols] = (out * expand(inv_rms, spread_j) * gain_s[:, cols]).astype(BF16)
        return carry

    lax.fori_loop(0, groups, last_group, 0)

    def finish(k, carry):
        g = lax.rem(me + k, ndev)
        decay_copy(g).wait_send()
        first_copy(g).wait_send()
        second_copy(g).wait_send()
        return carry

    lax.fori_loop(1, ndev, finish, 0)


def run_scan(projected, tail, dt_raw, conv_w, conv_b, dt_bias, a_log, d_skip, norm_gain):
    n_in, n_out = lax.axis_size("inner"), lax.axis_size("outer")
    ndev = n_in * n_out
    length, xbc = projected.shape
    rows = HP // ndev
    dma = pltpu.SemaphoreType.DMA((ndev,))
    vmem = pl.BlockSpec(memory_space=pltpu.VMEM)
    return pl.pallas_call(
        partial(scan_kernel, n_in, ndev),
        out_shape=(
            jax.ShapeDtypeStruct((length, HP), BF16),
            jax.ShapeDtypeStruct((HP, N), F32),
        ),
        in_specs=[vmem] * 9,
        out_specs=(vmem, vmem),
        scratch_shapes=[
            pltpu.VMEM((1, HP), F32),
            pltpu.VMEM((1, xbc), F32),
            pltpu.VMEM((1, HP), F32),
            pltpu.VMEM((length + 8, xbc), F32),
            pltpu.VMEM((length, xbc), BF16),
            pltpu.VMEM((length, HEADS), F32),
            pltpu.VMEM((HEADS, length), F32),
            pltpu.VMEM((length, HEADS), F32),
            pltpu.VMEM((length, HP), F32),
            pltpu.VMEM((length // CHUNK, HP, N), BF16),
            pltpu.VMEM((ndev, rows, N), BF16),
            pltpu.VMEM((ndev, rows, N), BF16),
            pltpu.VMEM((ndev, rows, N), BF16),
            pltpu.VMEM((ndev, rows, N), BF16),
            pltpu.VMEM((HEADS, 128), F32),
            pltpu.VMEM((ndev, HEADS, 128), F32),
            dma, dma, dma, dma, dma, dma,
        ],
        compiler_params=pltpu.CompilerParams(
            collective_id=1, has_side_effects=True, vmem_limit_bytes=60 * 2**20
        ),
        name="scan",
    )(
        projected, tail, dt_raw, conv_w, conv_b, dt_bias, a_log, d_skip, norm_gain,
    )


def project_kernel(
    n, n_out,
    tokens, w_in, w_dt,
    proj, tail, dt_out,
    tok, held, total, held_dt,
    ring_s, ring_r, side_s, side_r, core_s, core_r, dt_s, dt_r, misc, tail_s, tail_r,
):
    length, depth = tokens.shape
    local, xbc = w_in.shape
    half = xbc // 2
    quarter = half // 2
    lanes = 128
    streams = quarter // lanes
    wide = 256
    tiles = half // wide
    third = (local * 5 // 16) // 16 * 16
    ring_rows = local - third
    tail_rows = tok.shape[0] - length
    block = held_dt.shape[2]
    ndev = n * n_out
    me = lax.axis_index("inner")
    core = lax.axis_index("outer")
    grp = lax.axis_index("grp")
    rank = core * n + me
    odd = lax.rem(me, 2)
    pos = jnp.where(odd == 0, lax.div(me, 2), n - lax.div(me + 1, 2))

    def index_at(q):
        q = lax.rem(q + 2 * n, n)
        return jnp.where(q < n // 2, 2 * q, 2 * n - 1 - 2 * q)

    def place(g):
        return {"inner": lax.rem(g, n), "outer": lax.div(g, n)}

    barrier = pltpu.get_barrier_semaphore()

    def greet(k, carry):
        pl.semaphore_signal(
            barrier, inc=1, device_id=place(lax.rem(rank + k, ndev)), device_id_type=MESH
        )
        return carry

    lax.fori_loop(1, ndev, greet, 0)
    pl.semaphore_signal(barrier, inc=1, device_id={"grp": 1 - grp}, device_id_type=MESH)

    def own_rows(owner):
        return pl.ds(pl.multiple_of(owner * local, 16), local)

    load_tok = pltpu.make_async_copy(tokens, tok.at[pl.ds(0, length)], misc.at[0])
    load_w = [
        pltpu.make_async_copy(
            w_in.at[:, pl.ds(d * half, half)], held.at[d, own_rows(me)], misc.at[1 + d]
        )
        for d in range(2)
    ]
    for copy in load_w:
        copy.start()
    load_tok.start()
    held_dt[me] = w_dt[...]

    @pl.when(rank == 0)
    def _():
        tok[length:] = jnp.zeros((tail_rows, depth), BF16)

    def ring_copy(d, t, s):
        owner = index_at(pos - (s - 1)) if d == 0 else index_at(pos + (s - 1))
        target = index_at(pos + 1) if d == 0 else index_at(pos - 1)
        rows = pl.ds(pl.multiple_of(owner * local + grp * third, 16), ring_rows)
        cols = pl.ds(pl.multiple_of(core * quarter + t * lanes, lanes), lanes)
        part = held.at[d, rows, cols]
        return pltpu.make_async_remote_copy(
            src_ref=part, dst_ref=part, send_sem=ring_s.at[d, t, s],
            recv_sem=ring_r.at[d, t, s], device_id={"inner": target}, device_id_type=MESH,
        )

    def owner_of(d, s):
        return index_at(pos - s) if d == 0 else index_at(pos + s)

    def chunk_cols(which, t):
        return pl.ds(pl.multiple_of(which * quarter + t * lanes, lanes), lanes)

    def side_rows(d, s, which):
        start = owner_of(d, s) * local + which * ring_rows
        return pl.ds(pl.multiple_of(start, 16), third)

    def side_between(d, t, s, which):
        part = held.at[d, side_rows(d, s, which), chunk_cols(core, t)]
        return pltpu.make_async_remote_copy(
            src_ref=part, dst_ref=part, send_sem=side_s.at[d, t, s],
            recv_sem=side_r.at[d, t, s], device_id={"grp": 1 - grp}, device_id_type=MESH,
        )

    def core_between(d, t, s, which):
        part = held.at[d, own_rows(owner_of(d, s)), chunk_cols(which, t)]
        return pltpu.make_async_remote_copy(
            src_ref=part, dst_ref=part, send_sem=core_s.at[d, t, s],
            recv_sem=core_r.at[d, t, s], device_id={"outer": 1 - core}, device_id_type=MESH,
        )

    def side_copy(d, t, s):
        return side_between(d, t, s, grp)

    def core_copy(d, t, s):
        return core_between(d, t, s, core)

    def ring_arrival(d, t, s):
        start = owner_of(d, s) * local + grp * third
        rows = pl.ds(pl.multiple_of(start, 16), ring_rows)
        part = held.at[d, rows, chunk_cols(core, t)]
        pltpu.make_async_remote_copy(
            src_ref=part, dst_ref=part, send_sem=ring_s.at[d, t, s],
            recv_sem=ring_r.at[d, t, s], device_id={"inner": index_at(pos + 1)},
            device_id_type=MESH,
        ).wait_recv()

    def side_arrival(d, t, s):
        side_between(d, t, s, 1 - grp).wait_recv()

    def core_arrival(d, t, s):
        core_between(d, t, s, 1 - core).wait_recv()

    def dt_copy(k):
        peer = lax.rem(me + k, n)
        return pltpu.make_async_remote_copy(
            src_ref=w_dt, dst_ref=held_dt.at[me], send_sem=dt_s.at[k],
            recv_sem=dt_r.at[me], device_id={"inner": peer}, device_id_type=MESH,
        )

    def dt_arrival(k):
        peer = lax.rem(me + k, n)
        pltpu.make_async_remote_copy(
            src_ref=w_dt, dst_ref=held_dt.at[peer], send_sem=dt_s.at[k],
            recv_sem=dt_r.at[peer], device_id={"inner": peer}, device_id_type=MESH,
        ).wait_recv()

    def tail_copy():
        return pltpu.make_async_remote_copy(
            src_ref=tokens.at[pl.ds(length - tail_rows, tail_rows)],
            dst_ref=tok.at[pl.ds(length, tail_rows)], send_sem=tail_s,
            recv_sem=tail_r, device_id=place(lax.rem(rank + 1, ndev)), device_id_type=MESH,
        )

    pl.semaphore_wait(barrier, ndev)

    @pl.when(rank < ndev - 1)
    def _():
        tail_copy().start()

    for d in range(2):
        load_w[d].wait()
        for t in range(streams):
            ring_copy(d, t, 1).start()

    def send_dt(k, carry):
        dt_copy(k).start()
        return carry

    lax.fori_loop(1, n, send_dt, 0)
    load_tok.wait()

    @pl.when(rank > 0)
    def _():
        tail_copy().wait_recv()

    incremental = local % 128 == 0

    def multiply_tile(d, lhs_cols, rhs_rows, first, j):
        cols = pl.ds(pl.multiple_of(j * wide, wide), wide)
        product = jnp.dot(
            tok[:, lhs_cols], held[d, rhs_rows, cols], preferred_element_type=F32
        )
        at = d * tiles + j
        if first:
            total[at] = product
        else:
            total[at] = total[at] + product

    def multiply(d, lhs_cols, rhs_rows, first):
        def tile(j, carry):
            multiply_tile(d, lhs_cols, rhs_rows, first, j)
            return carry

        lax.fori_loop(0, tiles, tile, 0)

    def project_dt():
        def arrived(k, carry):
            dt_arrival(k)
            return carry

        lax.fori_loop(1, n, arrived, 0)
        together = block // local

        def add(j, sums):
            cols = pl.ds(pl.multiple_of(j * block, block), block)
            piece = held_dt[j * together]
            for m in range(1, together):
                piece = piece + held_dt[j * together + m]
            return sums + lax.dot_general(
                tok[0:length, cols], piece, LAST, preferred_element_type=F32
            )

        sums = lax.fori_loop(0, depth // block, add, jnp.zeros((length, HEADS), F32))
        dt_out[...] = sums.astype(BF16)

    def step(s, carry):
        @pl.when(s >= 3)
        def _():
            for t in range(streams):
                for d in range(2):
                    core_arrival(d, t, s - 2)

        def part(t, inner):
            @pl.when(s < n)
            def _():
                for d in range(2):
                    ring_arrival(d, t, s)

                    @pl.when(s < n - 1)
                    def _():
                        ring_copy(d, t, s + 1).start()

                    side_copy(d, t, s).start()

            @pl.when((s >= 2) & (s <= n))
            def _():
                for d in range(2):
                    side_arrival(d, t, s - 1)
                    core_copy(d, t, s - 1).start()

            if incremental:
                for d in range(2):
                    owner = owner_of(d, s - 2)
                    at = pl.ds(pl.multiple_of(owner * local, 128), local)

                    @pl.when(s == 2)
                    def _():
                        multiply_tile(d, at, at, True, t)

                    @pl.when(s > 2)
                    def _():
                        multiply_tile(d, at, at, False, t)

            return inner

        lax.fori_loop(0, streams, part, 0)

        @pl.when(s == 1)
        def _():
            project_dt()

        return carry

    lax.fori_loop(1, n + 2, step, 0)
    if not incremental:
        for d in range(2):
            multiply(d, slice(0, 512), slice(0, 512), True)

            def more(j, carry):
                at = pl.ds(pl.multiple_of(j * 512, 512), 512)
                multiply(d, at, at, False)
                return carry

            lax.fori_loop(1, depth // 512, more, 0)

    for j in range(2 * tiles):
        cols = slice(j * wide, (j + 1) * wide)
        proj[:, cols] = total[j, 0:length].astype(BF16)
        tail[:, cols] = total[j, length:].astype(BF16)

    def drain(s, carry):
        for d in range(2):
            for t in range(streams):
                ring_copy(d, t, s).wait_send()
                side_copy(d, t, s).wait_send()
                core_copy(d, t, s).wait_send()
        dt_copy(s).wait_send()
        return carry

    lax.fori_loop(1, n, drain, 0)

    @pl.when(rank < ndev - 1)
    def _():
        tail_copy().wait_send()


def run_project(tokens, w_in, w_dt):
    n, n_out = lax.axis_size("inner"), lax.axis_size("outer")
    length, depth = tokens.shape
    local, xbc = w_in.shape
    block = max(local, 128)
    tail_rows = 16
    dt_block = w_dt.T
    if block != local:
        start = lax.rem(lax.axis_index("inner") * local, block)
        dt_block = lax.dynamic_update_slice(
            jnp.zeros((HEADS, block), BF16), dt_block, (jnp.int32(0), start)
        )
    streams = xbc // 4 // 128
    dma = pltpu.SemaphoreType.DMA
    vmem = pl.BlockSpec(memory_space=pltpu.VMEM)
    whole = pl.BlockSpec(memory_space=pl.ANY)
    return pl.pallas_call(
        partial(project_kernel, n, n_out),
        out_shape=(
            jax.ShapeDtypeStruct((length, xbc), BF16),
            jax.ShapeDtypeStruct((tail_rows, xbc), BF16),
            jax.ShapeDtypeStruct((length, HEADS), BF16),
        ),
        in_specs=[whole, whole, vmem],
        out_specs=(vmem, vmem, vmem),
        scratch_shapes=[
            pltpu.VMEM((length + tail_rows, depth), BF16),
            pltpu.VMEM((2, depth, xbc // 2), BF16),
            pltpu.VMEM((xbc // 256, length + tail_rows, 256), F32),
            pltpu.VMEM((n, HEADS, block), BF16),
            dma((2, streams, n)), dma((2, streams, n)),
            dma((2, streams, n)), dma((2, streams, n)),
            dma((2, streams, n)), dma((2, streams, n)),
            dma((n,)), dma((n,)), dma((3,)), dma(()), dma(()),
        ],
        compiler_params=pltpu.CompilerParams(
            collective_id=2, has_side_effects=True, vmem_limit_bytes=60 * 2**20
        ),
        name="project",
    )(tokens, w_in, dt_block)


def fused_kernel(
    n, n_out,
    tokens, w_in, w_dt, conv_w_in, conv_b_in, dt_bias_in, a_log_in, d_skip_in, gain_in,
    mixed_out, entry_all,
    conv_w, conv_b, dt_bias, a_log, d_skip, gain, mixed, entry_out,
    tail_rows_in, tail_send, tail_recv, decays,
    tok, held, total, held_dt, dt_acc, half_w, bias_row, gain_s, skip_row,
    conv, log_s, log_t, step_s, fac_s, reach_s, edge, scores, grow, local_s, y,
    send1, recv1, prefix, mid_send, mid_recv, start, send2, recv2, dec_send, dec_recv,
    ring_s, ring_r, side_s, side_r, core_s, core_r, dt_s, dt_r, dc_s, dc_r, misc, tail_s, tail_r,
    ss1, rs1, ssm, rsm, ss2, rs2, ssd, rsd, small, out_sems,
):
    length, depth = tokens.shape
    local, xbc = w_in.shape
    tail_rows = tok.shape[0] - length
    wide, lanes = 256, 128
    blocks = xbc // wide
    groups = HP // wide
    early = groups
    late = blocks - early
    steps = n // 2
    half = local // 2
    third = (half * 5 // 16) // 16 * 16
    chunks = length // CHUNK
    ndev = n * n_out
    team = ndev // 2
    rows = wide // team
    me = lax.axis_index("inner")
    core = lax.axis_index("outer")
    grp = lax.axis_index("grp")
    rank = core * n + me
    odd = lax.rem(me, 2)
    pos = jnp.where(odd == 0, lax.div(me, 2), n - lax.div(me + 1, 2))
    upper = lax.div(me, n // 2)
    base = upper * (n // 2)
    own = (me - base) * n_out + core
    slot = core * (n // 2) + me - base

    def index_at(q):
        q = lax.rem(q + 2 * n, n)
        return jnp.where(q < n // 2, 2 * q, 2 * n - 1 - 2 * q)

    def place(g):
        return {"inner": lax.rem(g, n), "outer": lax.div(g, n)}

    barrier = pltpu.get_barrier_semaphore()

    def greet(k, carry):
        pl.semaphore_signal(
            barrier, inc=1, device_id=place(lax.rem(rank + k, ndev)), device_id_type=MESH
        )
        return carry

    lax.fori_loop(1, ndev, greet, 0)
    pl.semaphore_signal(barrier, inc=1, device_id={"grp": 1 - grp}, device_id_type=MESH)

    own_rows = pl.ds(pl.multiple_of(me * local, local), local)

    def natural(q):
        return groups if q == 0 else (blocks - 1 if q == blocks - 1 else q - 1)

    load_tok = pltpu.make_async_copy(
        tokens, tok.at[pl.ds(tail_rows, length)], misc.at[blocks]
    )
    load_w = [
        pltpu.make_async_copy(
            w_in.at[:, pl.ds(natural(q) * wide, wide)],
            held.at[q, own_rows], misc.at[q],
        )
        for q in range(blocks)
    ]
    for copy in load_w:
        copy.start()
    load_small = [
        pltpu.make_async_copy(source, target, small.at[k])
        for k, (source, target) in enumerate((
            (w_dt, held_dt.at[me]), (conv_w_in, conv_w), (conv_b_in, conv_b),
            (dt_bias_in, dt_bias), (a_log_in, a_log), (d_skip_in, d_skip), (gain_in, gain),
            (tokens.at[pl.ds(length - tail_rows, tail_rows)], tail_rows_in),
        ))
    ]
    for copy in load_small:
        copy.start()

    @pl.when(rank == 0)
    def _():
        tok[0:tail_rows] = jnp.zeros((tail_rows, depth), BF16)

    def owner_of(d, s):
        return index_at(pos - s) if d == 0 else index_at(pos + s)

    def share(whole):
        return third if whole else half // 2

    def columns(d, whole):
        return slice(0, wide) if whole else slice(d * lanes, (d + 1) * lanes)

    def ring_between(d, q, s, source, whole):
        start = owner_of(d, source) * local + core * half + grp * share(whole)
        span = pl.ds(pl.multiple_of(start, 16), half - share(whole))
        part = held.at[q, span, columns(d, whole)]
        target = index_at(pos + 1) if d == 0 else index_at(pos - 1)
        return pltpu.make_async_remote_copy(
            src_ref=part, dst_ref=part, send_sem=ring_s.at[d, q, s],
            recv_sem=ring_r.at[d, q, s], device_id={"inner": target}, device_id_type=MESH,
        )

    def ring_copy(d, q, s, whole):
        return ring_between(d, q, s, s - 1, whole)

    def side_between(d, q, s, which, whole):
        start = owner_of(d, s) * local + core * half + which * (half - share(whole))
        span = pl.ds(pl.multiple_of(start, 16), share(whole))
        part = held.at[q, span, columns(d, whole)]
        return pltpu.make_async_remote_copy(
            src_ref=part, dst_ref=part, send_sem=side_s.at[d, q, s],
            recv_sem=side_r.at[d, q, s], device_id={"grp": 1 - grp}, device_id_type=MESH,
        )

    def core_between(d, q, s, which, whole):
        start = owner_of(d, s) * local + which * half
        part = held.at[q, pl.ds(pl.multiple_of(start, 16), half), columns(d, whole)]
        return pltpu.make_async_remote_copy(
            src_ref=part, dst_ref=part, send_sem=core_s.at[d, q, s],
            recv_sem=core_r.at[d, q, s], device_id={"outer": 1 - core}, device_id_type=MESH,
        )

    def dt_part(owner, which):
        return held_dt.at[owner, :, pl.ds(pl.multiple_of(which * half, 128), half)]

    def dt_copy(k):
        peer = lax.rem(me + k, n)
        return pltpu.make_async_remote_copy(
            src_ref=dt_part(me, core), dst_ref=dt_part(me, core), send_sem=dt_s.at[k],
            recv_sem=dt_r.at[me], device_id={"inner": peer}, device_id_type=MESH,
        )

    def dt_arrival(k):
        peer = lax.rem(me + k, n)
        pltpu.make_async_remote_copy(
            src_ref=dt_part(peer, core), dst_ref=dt_part(peer, core), send_sem=dt_s.at[k],
            recv_sem=dt_r.at[peer], device_id={"inner": peer}, device_id_type=MESH,
        ).wait_recv()

    def dt_core(owner, which):
        return pltpu.make_async_remote_copy(
            src_ref=dt_part(owner, which), dst_ref=dt_part(owner, which),
            send_sem=dc_s.at[owner], recv_sem=dc_r.at[owner],
            device_id={"outer": 1 - core}, device_id_type=MESH,
        )

    def tail_copy():
        return pltpu.make_async_remote_copy(
            src_ref=tail_send, dst_ref=tail_recv, send_sem=tail_s,
            recv_sem=tail_r, device_id=place(lax.rem(rank + 1, ndev)), device_id_type=MESH,
        )

    def decay_copy(g):
        return pltpu.make_async_remote_copy(
            src_ref=dec_send, dst_ref=dec_recv.at[rank], send_sem=ssd.at[g],
            recv_sem=rsd.at[rank], device_id=place(g), device_id_type=MESH,
        )

    def member(o):
        return {"inner": base + lax.div(o, n_out), "outer": lax.rem(o, n_out)}

    def member_at(k):
        return {"inner": base + lax.rem(k, n // 2), "outer": lax.div(k, n // 2)}

    def first_copy(j, o):
        return pltpu.make_async_remote_copy(
            src_ref=send1.at[j, o], dst_ref=recv1.at[j, slot], send_sem=ss1.at[j, o],
            recv_sem=rs1.at[j, slot], device_id=member(o), device_id_type=MESH,
        )

    def first_arrival(j, k):
        pltpu.make_async_remote_copy(
            src_ref=send1.at[j, k], dst_ref=recv1.at[j, k], send_sem=ss1.at[j, k],
            recv_sem=rs1.at[j, k], device_id=member_at(k), device_id_type=MESH,
        ).wait_recv()

    batches = [slice(j, j + 1) for j in range(groups)]

    def mid_copy(b, c):
        return pltpu.make_async_remote_copy(
            src_ref=mid_send.at[c, batches[b]], dst_ref=mid_recv.at[c, batches[b]],
            send_sem=ssm.at[b, c], recv_sem=rsm.at[b, c],
            device_id={"inner": me + n // 2 - upper * n}, device_id_type=MESH,
        )

    def second_copy(b, k):
        return pltpu.make_async_remote_copy(
            src_ref=send2.at[k, batches[b]], dst_ref=recv2.at[own, batches[b]],
            send_sem=ss2.at[b, k], recv_sem=rs2.at[b, own],
            device_id=member_at(k), device_id_type=MESH,
        )

    def second_arrival(b, o):
        pltpu.make_async_remote_copy(
            src_ref=send2.at[o, batches[b]], dst_ref=recv2.at[o, batches[b]],
            send_sem=ss2.at[b, o], recv_sem=rs2.at[b, o],
            device_id=member(o), device_id_type=MESH,
        ).wait_recv()

    def arrive(buffer, sems, r, peer):
        pltpu.make_async_remote_copy(
            src_ref=buffer.at[r], dst_ref=buffer.at[r], send_sem=sems.at[r],
            recv_sem=sems.at[r], device_id=peer, device_id_type=MESH,
        ).wait_recv()

    for copy in load_small:
        copy.wait()

    kept = tail_rows_in[...].astype(F32)[tail_rows - CONV :]
    part_cols = depth // CONV
    tail_send[...] = jnp.concatenate(
        [kept[:, k * part_cols : (k + 1) * part_cols] for k in range(CONV)], axis=0
    ).astype(BF16)

    half_w[...] = conv_w[...] * 0.5
    bias_row[...] = conv_b[...].reshape(1, xbc) * 0.5
    gain_s[...] = gain[...].reshape(1, HP)

    def spread_of(j, count):
        head = lax.rem(lax.broadcasted_iota(jnp.int32, (count, wide), 0), HEADS)
        col = lax.broadcasted_iota(jnp.int32, (count, wide), 1) // P_SIZE
        return (head == col + j * (wide // P_SIZE)).astype(F32).astype(BF16)

    def split(values):
        high = values.astype(BF16).astype(F32)
        lane = lax.broadcasted_iota(jnp.int32, values.shape, 1)
        return jnp.where(lane < HEADS, high, values - high).astype(BF16)

    skip = d_skip[...].reshape(1, HEADS)
    skip_high = skip.astype(BF16).astype(F32)
    for j in range(groups):
        skip_row[:, j * wide : (j + 1) * wide] = expand(
            skip - skip_high, spread_of(j, HEADS)
        ) + jnp.dot(skip_high.astype(BF16), spread_of(j, HEADS), preferred_element_type=F32)

    pl.semaphore_wait(barrier, ndev)

    @pl.when(rank < ndev - 1)
    def _():
        tail_copy().start()

    def send_dt(k, carry):
        dt_copy(k).start()
        return carry

    lax.fori_loop(1, n, send_dt, 0)
    for q in range(early):
        load_w[q].wait()
        for d in range(2):
            ring_copy(d, q, 1, True).start()
    load_tok.start()
    for q in range(early, blocks):
        load_w[q].wait()

    def multiply(q, shards, first):
        product = None if first else total[q]
        for owner in shards:
            at = pl.ds(pl.multiple_of(owner * local, local), local)
            term = jnp.dot(tok[:, at], held[q, at, :], preferred_element_type=F32)
            product = term if product is None else product + term
        total[q] = product

    all_parts = blocks * steps
    side_lag, core_lag = 3, 4
    second, third_turn = early, 2 * early + 1
    fifth = third_turn + (steps - 2) * blocks

    def item(i):
        full = jnp.maximum(i - third_turn, 0)
        t = jnp.where(i < second, 1, jnp.where(i < third_turn, 2, 3 + lax.div(full, blocks)))
        q = jnp.where(
            i < second, i, jnp.where(i < third_turn, i - second, lax.rem(full, blocks))
        )
        t = jnp.where(i < fifth, t, jnp.where(i < fifth + 2, steps + 1, steps + 2))
        q = jnp.where(i < fifth, q, jnp.where(i < fifth + 1, early, early + 1))
        return q, t - jnp.maximum(q - early + 1, 0)

    def exchange(i):
        q, s = item(i)

        @pl.when((i < all_parts) & (s < steps))
        def _():
            for d in range(2):
                ring_between(d, q, s, s, True).wait_recv()

                @pl.when(s < steps - 1)
                def _():
                    ring_copy(d, q, s + 1, True).start()

                @pl.when(s == steps - 1)
                def _():
                    ring_copy(d, q, s + 1, False).start()

                side_between(d, q, s, grp, True).start()

        @pl.when((i < all_parts) & (s == steps))
        def _():
            for d in range(2):
                ring_between(d, q, s, s, False).wait_recv()
                side_between(d, q, s, grp, False).start()

        for k in range(late):
            @pl.when(i == (early - 1, 2 * early)[k])
            def _():
                for d in range(2):
                    ring_copy(d, early + k, 1, True).start()

        q, s = item(jnp.maximum(i - side_lag, 0))
        for whole in (True, False):
            @pl.when((i >= side_lag) & (i < all_parts + side_lag) & ((s < steps) == whole))
            def _():
                for d in range(2):
                    side_between(d, q, s, 1 - grp, whole).wait_recv()
                    core_between(d, q, s, core, whole).start()

    def sent(q, s, whole):
        for d in range(2):
            ring_copy(d, q, s, whole).wait_send()
            side_between(d, q, s, grp, whole).wait_send()
            core_between(d, q, s, core, whole).wait_send()

    def accumulate(i):
        q, s = item(jnp.maximum(i - core_lag, 0))

        @pl.when((i >= core_lag) & (s < steps))
        def _():
            for d in range(2):
                core_between(d, q, s, 1 - core, True).wait_recv()
            sent(q, s, True)
            multiply(q, [owner_of(0, s), owner_of(1, s)], False)

        @pl.when((i >= core_lag) & (s == steps))
        def _():
            for d in range(2):
                core_between(d, q, s, 1 - core, False).wait_recv()
            sent(q, s, False)
            multiply(q, [owner_of(0, s)], False)

        @pl.when((i < early) | (i == 6) | (i == 10))
        def _():
            multiply(jnp.where(i < early, i, early + lax.div(jnp.maximum(i - 6, 0), 4)), [me], True)

    def add_dt(k):
        @pl.when(k != me)
        def _():
            dt_core(k, 1 - core).wait_recv()

        cols = pl.ds(pl.multiple_of(k * local, local), local)
        part = lax.dot_general(
            tok[tail_rows:, cols], held_dt[k], LAST, preferred_element_type=F32
        )

        @pl.when(k == 0)
        def _():
            dt_acc[...] = part

        @pl.when(k > 0)
        def _():
            dt_acc[...] = dt_acc[...] + part

    def early_part(i, carry):
        exchange(i)

        @pl.when((i == 0) & (rank > 0))
        def _():
            tail_copy().wait_recv()
            for k in range(CONV):
                rows_k = tail_recv[...].astype(F32)[k * CONV : (k + 1) * CONV]
                above = jnp.zeros((tail_rows - CONV, part_cols), F32)
                tok[0:tail_rows, k * part_cols : (k + 1) * part_cols] = jnp.concatenate(
                    [above, rows_k], axis=0
                ).astype(BF16)

        @pl.when(i == 0)
        def _():
            load_tok.wait()

        accumulate(i)

        @pl.when((i < n) & (i != me))
        def _():
            dt_arrival(lax.rem(i - me + n, n))
            dt_core(i, core).start()

        @pl.when(i >= 2)
        def _():
            add_dt(i - 2)

        return carry

    lax.fori_loop(0, 10, early_part, 0)

    row_id = lax.broadcasted_iota(jnp.int32, (CHUNK, CHUNK), 0)
    col_id = lax.broadcasted_iota(jnp.int32, (CHUNK, CHUNK), 1)
    causal = col_id <= row_id
    dt_raw = dt_acc[...].astype(BF16).astype(F32)
    step_one = jax.nn.softplus(dt_raw + dt_bias[...].reshape(1, HEADS))
    scaled = step_one * (-jnp.exp(a_log[...].reshape(1, HEADS)))
    scaled = jnp.concatenate([scaled, scaled], axis=1)
    step_size = jnp.concatenate([step_one, step_one], axis=1)
    before = jnp.zeros((1, 2 * HEADS), F32)
    lower = causal.astype(F32)
    for c in range(chunks):
        here = slice(c * CHUNK, (c + 1) * CHUNK)
        part = jnp.dot(
            lower, scaled[here], preferred_element_type=F32,
            precision=lax.Precision.HIGHEST,
        ) + before
        log_s[here] = part
        reach_s[here] = split(jnp.exp(part - before))
        before = part[CHUNK - 1 : CHUNK]
        fac_s[here] = split(jnp.exp(before - part) * step_size[here])
    flat = jnp.transpose(log_s[...])[0:HEADS]
    log_t[...] = jnp.transpose(log_s[...] - jnp.log(step_size))[0:HEADS]
    ends = [flat[:, (c + 1) * CHUNK - 1 : (c + 1) * CHUNK] for c in range(chunks)]
    dec_send[...] = jnp.zeros((1, 128), F32)
    dec_send[:, 0 : 2 * HEADS] = jnp.exp(before)
    dec_recv[rank] = dec_send[...]

    def tall_of(column):
        column = jnp.broadcast_to(column, (HEADS, 128)).reshape(HEADS, 1, 128)
        return jnp.broadcast_to(column, (HEADS, P_SIZE, 128)).reshape(HP, 128)

    for c in range(1, chunks):
        edge[0, c - 1] = tall_of(jnp.exp(ends[c] - ends[c - 1]))
        edge[1, c - 1] = tall_of(jnp.exp(ends[c - 1]))

    def send_decay(k, carry):
        decay_copy(lax.rem(rank + k, ndev)).start()
        return carry

    lax.fori_loop(1, ndev, send_decay, 0)

    def conv_column(block):
        q = jnp.where(block < groups, block + 1, (blocks - 1) * (block - groups))
        cols = pl.ds(pl.multiple_of(block * wide, wide), wide)

        def one(i, carry):
            start = pl.multiple_of(i * 128, 128)
            window = total[q, pl.ds(pl.multiple_of(start + tail_rows - 8, 8), 136), :]
            window = window.astype(BF16).astype(F32)
            acc = bias_row[:, cols]
            for k in range(CONV):
                acc = acc + half_w[k : k + 1, cols] * window[5 + k : 5 + k + 128]
            conv[pl.ds(start, 128), cols] = (acc + acc * jnp.tanh(acc)).astype(BF16)
            return carry

        lax.fori_loop(0, length // 128, one, 0)

    def score_all():
        def one(c, carry):
            here = pl.ds(pl.multiple_of(c * CHUNK, CHUNK), CHUNK)
            product = lax.dot_general(
                conv[here, HP + N :], conv[here, HP : HP + N], LAST,
                preferred_element_type=F32,
            )
            scores[c] = jnp.where(causal, product, 0.0)
            return carry

        lax.fori_loop(0, chunks, one, 0)

    heads_each = HEADS // groups

    def grow_heads(c, j):
        here = pl.ds(pl.multiple_of(c * CHUNK, CHUNK), CHUNK)
        log_c = log_s[here]
        for k in range(heads_each):
            h = j * heads_each + k
            gap = jnp.minimum(log_c[:, h : h + 1] - log_t[h : h + 1, here], 60.0)
            grow[h, c] = jnp.exp(gap)

    def contribute(j):
        cols = pl.ds(pl.multiple_of(j * wide, wide), wide)
        spread = spread_of(j, 2 * HEADS)
        state = None
        for c in range(chunks):
            here = slice(c * CHUNK, (c + 1) * CHUNK)
            factor = jnp.dot(fac_s[here], spread, preferred_element_type=F32)
            weighted = (factor * conv[here, cols].astype(F32)).astype(BF16)
            part = lax.dot_general(
                weighted, conv[here, HP : HP + N], FIRST, preferred_element_type=F32
            )
            if c > 0:
                local_s[c - 1, cols] = state
                scale = edge[0, c - 1, cols, :]
                part = part + jnp.concatenate([scale, scale], axis=1) * state
            state = part
        send1[j] = state.reshape(team, rows, N).astype(BF16)

        def send_one(o, inner):
            @pl.when(o != own)
            def _():
                first_copy(j, o).start()

            return inner

        lax.fori_loop(0, team, send_one, 0)

    def inside(j):
        cols = pl.ds(pl.multiple_of(j * wide, wide), wide)
        lane = lax.broadcasted_iota(jnp.int32, (1, wide), 1) // P_SIZE

        def one(c, carry):
            here = pl.ds(pl.multiple_of(c * CHUNK, CHUNK), CHUNK)
            x_rows = conv[here, cols]
            acc = skip_row[:, cols] * x_rows.astype(F32)
            score = scores[c]
            for k in range(heads_each):
                keep = (lane == k).astype(F32).astype(BF16)
                mixing = (score * grow[j * heads_each + k, c]).astype(BF16)
                acc = acc + jnp.dot(mixing, x_rows * keep, preferred_element_type=F32)
            y[here, cols] = acc
            return carry

        lax.fori_loop(0, chunks, one, 0)

    def decay_of(k, half_of, j):
        r = lax.div(k, n // 2) * n + half_of * (n // 2) + lax.rem(k, n // 2)
        return decays[j, pl.ds(r, 1), :]

    def combine(b):
        for j in range(groups)[batches[b]]:
            recv1[j, slot] = send1[j, own]

            def arrived(k, carry):
                @pl.when(k != slot)
                def _():
                    first_arrival(j, k)

                return carry

            lax.fori_loop(0, team, arrived, 0)
            for c in range(2):
                state = jnp.zeros((rows, N), F32)
                for m in range(n // 2):
                    k = c * (n // 2) + m
                    prefix[j, k] = state
                    state = decay_of(k, upper, j) * state + recv1[j, k].astype(F32)
                mid_send[c, j] = state.astype(BF16)
        mid_copy(b, 0).start()

        @pl.when(upper == 0)
        def _():
            mid_copy(b, 1).start()

    def product_of(c, half_of, j):
        result = decay_of(c * (n // 2), half_of, j)
        for m in range(1, n // 2):
            result = result * decay_of(c * (n // 2) + m, half_of, j)
        return result

    def distribute(b):
        mid_copy(b, 0).wait_recv()

        @pl.when(upper == 1)
        def _():
            mid_copy(b, 1).wait_recv()

        is_upper = upper == 1
        for j in range(groups)[batches[b]]:
            middle = mid_recv[0, j].astype(F32)
            ours = mid_send[0, j].astype(F32)
            lower_sum = jnp.where(is_upper, middle, ours)
            upper_sum = jnp.where(is_upper, ours, middle)
            block_end = product_of(0, 1, j) * lower_sum + upper_sum

            @pl.when(is_upper)
            def _():
                start[0, j] = middle
                start[1, j] = product_of(1, 0, j) * block_end + mid_recv[1, j].astype(F32)

            @pl.when(upper == 0)
            def _():
                start[0, j] = jnp.zeros((rows, N), F32)
                start[1, j] = block_end

        for k in range(team):
            for j in range(groups)[batches[b]]:
                state = start[k // (n // 2), j]
                send2[k, j] = (prefix[j, k] + state).astype(BF16)
                start[k // (n // 2), j] = decay_of(k, upper, j) * state

            @pl.when(k != slot)
            def _():
                second_copy(b, k).start()

        recv2[own, batches[b]] = send2[slot, batches[b]]

    def drain_dt(k, carry):
        dt_copy(k).wait_send()
        dt_core(lax.rem(me + k, n), core).wait_send()
        return carry

    def drain_decay(k, carry):
        decay_copy(lax.rem(rank + k, ndev)).wait_send()
        return carry

    def late_part(i, carry):
        exchange(i)
        accumulate(i)
        ready = fifth - blocks + core_lag + 1

        @pl.when(i == ready - 1)
        def _():
            conv_column(groups)

        @pl.when((i >= ready) & (i < ready + groups - 1))
        def _():
            conv_column(i - ready)
            contribute(i - ready)

        @pl.when(i == ready + groups - 2)
        def _():
            others()

        @pl.when(i == ready - 2)
        def _():
            lax.fori_loop(1, n, drain_dt, 0)

        @pl.when(i == all_parts)
        def _():
            lax.fori_loop(1, ndev, drain_decay, 0)

        for k in range(groups):
            @pl.when(i == 10 + 2 * k)
            def _():
                def one(c, inner):
                    grow_heads(c, k)
                    return inner

                lax.fori_loop(0, chunks, one, 0)

        for b, turn in enumerate((all_parts - 1, all_parts, all_parts + 2)):
            @pl.when(i == turn)
            def _():
                combine(b)

        @pl.when(i == fifth + core_lag)
        def _():
            conv_column(groups - 1)
            contribute(groups - 1)

        return carry

    def others():
        def one(k, carry):
            r = lax.rem(rank + k, ndev)
            arrive(dec_recv, rsd, r, place(r))
            return carry

        lax.fori_loop(1, ndev, one, 0)
        every = jnp.concatenate([dec_recv[r] for r in range(ndev)], axis=0)
        lane = lax.broadcasted_iota(jnp.int32, (ndev, 128), 1)
        for j in range(groups):
            head = j * heads_each + lax.div(own * rows, P_SIZE)
            column = jnp.sum(jnp.where(lane == head, every, 0.0), axis=1, keepdims=True)
            decays[j] = jnp.broadcast_to(column, (ndev, N))

    lax.fori_loop(10, all_parts + core_lag, late_part, 0)

    distribute(0)
    conv_column(groups + 1)
    score_all()

    def fill(j, carry):
        inside(j)
        return carry

    combine(groups - 1)
    lax.fori_loop(0, 1, fill, 0)
    distribute(1)
    distribute(2)
    lax.fori_loop(1, groups - 1, fill, 0)
    distribute(groups - 1)
    lax.fori_loop(groups - 1, groups, fill, 0)

    row_head = lax.broadcasted_iota(jnp.int32, (wide, wide), 0) // P_SIZE
    col_head = lax.broadcasted_iota(jnp.int32, (wide, wide), 1) // P_SIZE
    same = (row_head == col_head).astype(F32).astype(BF16)

    def out_copies(j):
        cols = pl.ds(pl.multiple_of(j * wide, wide), wide)
        return [
            pltpu.make_async_copy(
                mixed.at[:, cols], mixed_out.at[:, cols], out_sems.at[0, j]
            ),
            pltpu.make_async_copy(
                entry_out.at[cols], entry_all.at[cols], out_sems.at[1, j]
            ),
        ]

    def finish_group(j, carry):
        cols = pl.ds(pl.multiple_of(j * wide, wide), wide)
        entry = jnp.concatenate([recv2[o, j] for o in range(team)], axis=0).astype(F32)
        entry_out[cols] = entry.astype(BF16)
        spread = spread_of(j, 2 * HEADS)
        for c in range(chunks):
            here = slice(c * CHUNK, (c + 1) * CHUNK)
            state = entry
            if c > 0:
                scale = edge[1, c - 1, cols, :]
                state = local_s[c - 1, cols] + jnp.concatenate([scale, scale], axis=1) * entry
            carried = lax.dot_general(
                conv[here, HP + N :], state.astype(BF16), LAST, preferred_element_type=F32
            )
            reach = jnp.dot(reach_s[here], spread, preferred_element_type=F32)
            out = y[here, cols] + reach * carried
            square = (out * out).astype(BF16)
            sums = jnp.dot(square, same, preferred_element_type=F32)
            inv_rms = lax.rsqrt(sums * (1.0 / P_SIZE) + EPSILON)
            mixed[here, cols] = (out * inv_rms * gain_s[:, cols]).astype(BF16)
        for copy in out_copies(j):
            copy.start()
        return carry

    def wait_second(b):
        def one(o, carry):
            @pl.when(o != own)
            def _():
                second_arrival(b, o)

            return carry

        lax.fori_loop(0, team, one, 0)

    for j in range(groups):
        wait_second(j)
        lax.fori_loop(j, j + 1, finish_group, 0)

    def drain_out(j, carry):
        for copy in out_copies(j):
            copy.wait()
        return carry

    def drain_state(k, carry):
        @pl.when(k != own)
        def _():
            for j in range(groups):
                first_copy(j, k).wait_send()

        @pl.when(k != slot)
        def _():
            for b in range(groups):
                second_copy(b, k).wait_send()

        return carry

    lax.fori_loop(0, team, drain_state, 0)
    for b in range(groups):
        mid_copy(b, 0).wait_send()

    @pl.when(upper == 0)
    def _():
        for b in range(groups):
            mid_copy(b, 1).wait_send()

    @pl.when(rank < ndev - 1)
    def _():
        tail_copy().wait_send()

    lax.fori_loop(0, groups, drain_out, 0)


def run_fused(tokens, w_in, w_dt, conv_w, conv_b, dt_bias, a_log, d_skip, norm_gain):
    n, n_out = lax.axis_size("inner"), lax.axis_size("outer")
    ndev = n * n_out
    length, depth = tokens.shape
    local, xbc = w_in.shape
    team = ndev // 2
    groups = HP // 256
    rows = 256 // team
    tail_rows = 16
    blocks = xbc // 256
    chunks = length // CHUNK
    dma = pltpu.SemaphoreType.DMA
    whole = pl.BlockSpec(memory_space=pl.ANY)
    weight_sems = [dma((2, blocks, n // 2 + 1))] * 6
    first_sems = [dma((groups, team))] * 2
    swap_sems = [dma((groups, 2))] * 2
    second_sems = [dma((groups, team))] * 2
    rank_sems = [dma((ndev,))] * 2
    return pl.pallas_call(
        partial(fused_kernel, n, n_out),
        out_shape=(
            jax.ShapeDtypeStruct((length, HP), BF16),
            jax.ShapeDtypeStruct((HP, N), BF16),
        ),
        in_specs=[whole] * 9,
        out_specs=(whole, whole),
        scratch_shapes=[
            pltpu.VMEM((CONV, xbc), F32), pltpu.VMEM((xbc,), F32),
            pltpu.VMEM((HEADS,), F32), pltpu.VMEM((HEADS,), F32),
            pltpu.VMEM((HEADS,), F32), pltpu.VMEM((HP,), F32),
            pltpu.VMEM((length, HP), BF16), pltpu.VMEM((HP, N), BF16),
            pltpu.VMEM((tail_rows, depth), BF16),
            pltpu.VMEM((tail_rows, depth // 4), BF16),
            pltpu.VMEM((tail_rows, depth // 4), BF16),
            pltpu.VMEM((groups, ndev, N), F32),
            pltpu.VMEM((length + tail_rows, depth), BF16),
            pltpu.VMEM((blocks, depth, 256), BF16),
            pltpu.VMEM((blocks, length + tail_rows, 256), F32),
            pltpu.VMEM((n, HEADS, local), BF16),
            pltpu.VMEM((length, HEADS), F32),
            pltpu.VMEM((CONV, xbc), F32),
            pltpu.VMEM((1, xbc), F32),
            pltpu.VMEM((1, HP), F32),
            pltpu.VMEM((1, HP), F32),
            pltpu.VMEM((length, xbc), BF16),
            pltpu.VMEM((length, 2 * HEADS), F32),
            pltpu.VMEM((HEADS, length), F32),
            pltpu.VMEM((length, 2 * HEADS), F32),
            pltpu.VMEM((length, 2 * HEADS), BF16),
            pltpu.VMEM((length, 2 * HEADS), BF16),
            pltpu.VMEM((2, chunks - 1, HP, 128), F32),
            pltpu.VMEM((chunks, CHUNK, CHUNK), F32),
            pltpu.VMEM((HEADS, chunks, CHUNK, CHUNK), F32),
            pltpu.VMEM((chunks - 1, HP, N), F32),
            pltpu.VMEM((length, HP), F32),
            pltpu.VMEM((groups, team, rows, N), BF16),
            pltpu.VMEM((groups, team, rows, N), BF16),
            pltpu.VMEM((groups, team, rows, N), F32),
            pltpu.VMEM((2, groups, rows, N), BF16),
            pltpu.VMEM((2, groups, rows, N), BF16),
            pltpu.VMEM((2, groups, rows, N), F32),
            pltpu.VMEM((team, groups, rows, N), BF16),
            pltpu.VMEM((team, groups, rows, N), BF16),
            pltpu.VMEM((1, 128), F32),
            pltpu.VMEM((ndev, 1, 128), F32),
            *weight_sems,
            dma((n,)), dma((n,)), dma((n,)), dma((n,)), dma((blocks + 1,)), dma(()), dma(()),
            *first_sems, *swap_sems, *second_sems, *rank_sems, dma((8,)), dma((2, groups)),
        ],
        compiler_params=pltpu.CompilerParams(
            collective_id=3, has_side_effects=True, vmem_limit_bytes=62 * 2**20
        ),
        name="fused",
    )(
        tokens, w_in, w_dt.T, conv_w, conv_b, dt_bias, a_log, d_skip, norm_gain,
    )


def hand_over_kernel(
    mixed, entry, mixed_out, entry_out, held_m, held_e, wide_e, in_sems, out_sems
):
    parts = in_sems.shape[1]
    loads, stores = [], []
    arrays = ((entry, held_e, wide_e, entry_out), (mixed, held_m, held_m, mixed_out))
    for i, (source, held, ready, target) in enumerate(arrays):
        rows = source.shape[0] // parts
        for k in range(parts):
            at = pl.ds(k * rows, rows)
            loads.append(pltpu.make_async_copy(source.at[at], held.at[at], in_sems.at[i, k]))
            stores.append(pltpu.make_async_copy(ready.at[at], target.at[at], out_sems.at[i, k]))
    for load in loads:
        load.start()
    rows = entry.shape[0] // parts
    for k, (load, store) in enumerate(zip(loads, stores)):
        load.wait()
        if k < parts:
            at = slice(k * rows, (k + 1) * rows)
            wide_e[at] = held_e[at].astype(F32)
        store.start()
    for store in stores:
        store.wait()


def hand_over(mixed, entry):
    whole = pl.BlockSpec(memory_space=pl.ANY)
    sems = pltpu.SemaphoreType.DMA((2, 4))
    return pl.pallas_call(
        hand_over_kernel,
        out_shape=(
            jax.ShapeDtypeStruct(mixed.shape, mixed.dtype),
            jax.ShapeDtypeStruct(entry.shape, F32),
        ),
        in_specs=[whole, whole],
        out_specs=(whole, whole),
        scratch_shapes=[
            pltpu.VMEM(mixed.shape, mixed.dtype), pltpu.VMEM(entry.shape, entry.dtype),
            pltpu.VMEM(entry.shape, F32), sems, sems,
        ],
        name="hand_over",
    )(mixed, entry)


def per_device(tokens, w_in, w_dt, conv_w, conv_b, dt_bias, a_log, d_skip, norm_gain):
    own_rows = tokens.reshape(tokens.shape[1], tokens.shape[2])
    row_count = own_rows.shape[0]
    if w_in.shape[0] % 512 == 0 and lax.axis_size("inner") == 8:
        mixed, entry = run_fused(
            own_rows, w_in, w_dt, conv_w, conv_b, dt_bias, a_log, d_skip, norm_gain
        )
        mixed, entry = hand_over(mixed, entry)
    else:
        projected, tail, dt_raw = run_project(own_rows, w_in, w_dt)
        mixed, entry = run_scan(
            projected, tail, dt_raw, conv_w, conv_b, dt_bias, a_log, d_skip, norm_gain
        )
    return (
        mixed.reshape(1, row_count, HP),
        entry.reshape(1, 1, HEADS, P_SIZE, N),
    )


def solution(mesh):
    placed = (
        P(("grp", "outer"), "inner", None),
        P("inner", None),
        P("inner", None),
        P(), P(), P(), P(), P(), P(),
    )
    return jax.shard_map(
        per_device,
        mesh=mesh,
        in_specs=placed,
        out_specs=(
            P(("grp", "outer"), "inner", None),
            P(("grp", "outer"), "inner", None, None, None),
        ),
        check_vma=False,
    )
```

```python
from functools import partial

import jax
import jax.numpy as jnp
from jax import lax
from jax.experimental import pallas as pl
from jax.experimental.pallas import tpu as pltpu
from jax.sharding import PartitionSpec as P

HEADS = 16
P_SIZE = 64
N = 256
CONV = 4
HP = HEADS * P_SIZE
CHUNK = 256
EPSILON = 1e-05
MESH = pl.DeviceIdType.MESH
F32 = jnp.float32
BF16 = jnp.bfloat16
LAST = (((1,), (1,)), ((), ()))
FIRST = (((0,), (0,)), ((), ()))


def expand(values, spread):
    high = values.astype(BF16)
    low = (values - high.astype(F32)).astype(BF16)
    return jnp.dot(high, spread, preferred_element_type=F32) + jnp.dot(
        low, spread, preferred_element_type=F32
    )


def scan_kernel(
    n_in, ndev,
    proj, tail, dt_raw, conv_w, conv_b, dt_bias, a_log, d_skip, gain,
    mixed, entry_out,
    gain_s, bias_row, skip_row, pad, conv, log_s, log_t, step_s, y, states,
    send1, recv1, send2, recv2, dec_send, dec_recv,
    ss1, rs1, ss2, rs2, ssd, rsd,
):
    length = proj.shape[0]
    chunks = length // CHUNK
    rows = HP // ndev
    me = lax.axis_index("outer") * n_in + lax.axis_index("inner")

    def place(g):
        return {"inner": lax.rem(g, n_in), "outer": lax.div(g, n_in)}

    barrier = pltpu.get_barrier_semaphore()

    def greet(k, carry):
        pl.semaphore_signal(
            barrier, inc=1, device_id=place(lax.rem(me + k, ndev)), device_id_type=MESH
        )
        return carry

    lax.fori_loop(1, ndev, greet, 0)

    head_id = lax.broadcasted_iota(jnp.int32, (HEADS, HP), 0)
    col_head = lax.broadcasted_iota(jnp.int32, (HEADS, HP), 1) // P_SIZE
    spread = (head_id == col_head).astype(F32).astype(BF16)

    bias_row[...] = conv_b[...].reshape(1, conv_b.shape[0])
    gain_s[...] = gain[...].reshape(1, HP)
    skip = d_skip[...].reshape(1, HEADS)
    skip_high = skip.astype(BF16).astype(F32)
    skip_row[...] = expand(skip - skip_high, spread) + jnp.dot(
        skip_high.astype(BF16), spread, preferred_element_type=F32
    )
    step_size = jax.nn.softplus(dt_raw[...].astype(F32) + dt_bias[...].reshape(1, HEADS))
    scaled = step_size * (-jnp.exp(a_log[...].reshape(1, HEADS)))
    row_id = lax.broadcasted_iota(jnp.int32, (CHUNK, CHUNK), 0)
    col_id = lax.broadcasted_iota(jnp.int32, (CHUNK, CHUNK), 1)
    causal = col_id <= row_id
    lower = causal.astype(F32)
    step_s[...] = step_size
    before = jnp.zeros((1, HEADS), F32)
    for c in range(chunks):
        part = jnp.dot(
            lower,
            scaled[c * CHUNK : (c + 1) * CHUNK],
            preferred_element_type=F32,
            precision=lax.Precision.HIGHEST,
        ) + before
        log_s[c * CHUNK : (c + 1) * CHUNK] = part
        before = part[CHUNK - 1 : CHUNK]
    log_t[...] = jnp.transpose(log_s[...])
    dec_send[...] = jnp.broadcast_to(jnp.exp(log_t[:, length - 1 : length]), (HEADS, 128))

    pad[0:8] = tail[...].astype(F32)[8:16]
    pad[8:] = proj[...].astype(F32)
    wide = 256
    blocks = proj.shape[1] // wide

    def conv_block(t, carry):
        i, j = lax.div(t, blocks), lax.rem(t, blocks)
        cols = pl.ds(pl.multiple_of(j * wide, wide), wide)
        window = pad[pl.ds(pl.multiple_of(i * 128, 128), 136), cols]
        total = bias_row[:, cols]
        for k in range(CONV):
            total = total + conv_w[k : k + 1, cols] * window[5 + k : 5 + k + 128]
        conv[pl.ds(pl.multiple_of(i * 128, 128), 128), cols] = (
            total * jax.nn.sigmoid(total)
        ).astype(BF16)
        return carry

    row_blocks = length // 128

    def conv_column(j):
        def one(i, carry):
            return conv_block(i * blocks + j, carry)

        lax.fori_loop(0, row_blocks, one, 0)

    conv_column(HP // wide)

    def weighted_sum(stop):
        final = log_s[stop - 1 : stop]
        factor = jnp.exp(final - log_s[0:stop]) * step_s[0:stop]
        weighted = (expand(factor, spread) * conv[0:stop, 0:HP].astype(F32)).astype(BF16)
        return lax.dot_general(
            weighted, conv[0:stop, HP : HP + N], FIRST, preferred_element_type=F32
        )

    dec_recv[me] = dec_send[...]

    def decay_copy(g):
        return pltpu.make_async_remote_copy(
            src_ref=dec_send, dst_ref=dec_recv.at[me], send_sem=ssd.at[g],
            recv_sem=rsd.at[me], device_id=place(g), device_id_type=MESH,
        )

    def first_copy(g):
        return pltpu.make_async_remote_copy(
            src_ref=send1.at[g], dst_ref=recv1.at[me], send_sem=ss1.at[g],
            recv_sem=rs1.at[me], device_id=place(g), device_id_type=MESH,
        )

    def second_copy(g):
        return pltpu.make_async_remote_copy(
            src_ref=send2.at[g], dst_ref=recv2.at[me], send_sem=ss2.at[g],
            recv_sem=rs2.at[me], device_id=place(g), device_id_type=MESH,
        )

    pl.semaphore_wait(barrier, ndev - 1)

    def send_decay(k, carry):
        decay_copy(lax.rem(me + k, ndev)).start()
        return carry

    lax.fori_loop(1, ndev, send_decay, 0)

    groups = HP // wide
    owners = ndev // groups
    own_group = lax.div(me, owners)
    factor = jnp.exp(log_s[length - 1 : length] - log_s[...]) * step_s[...]

    def spread_of(j):
        head = lax.broadcasted_iota(jnp.int32, (HEADS, wide), 0)
        col = lax.broadcasted_iota(jnp.int32, (HEADS, wide), 1) // P_SIZE
        return (head == col + j * (wide // P_SIZE)).astype(F32).astype(BF16)

    def first_group(i, carry):
        j = lax.rem(own_group + 1 + i, groups)
        conv_column(j)
        cols = pl.ds(pl.multiple_of(j * wide, wide), wide)
        weighted = (expand(factor, spread_of(j)) * conv[:, cols].astype(F32)).astype(BF16)
        part = lax.dot_general(
            weighted, conv[:, HP : HP + N], FIRST, preferred_element_type=F32
        )
        send1[pl.ds(j * owners, owners)] = part.reshape(owners, rows, N).astype(BF16)

        def send_one(k, inner):
            g = j * owners + k

            @pl.when(g != me)
            def _():
                first_copy(g).start()

            return inner

        return lax.fori_loop(0, owners, send_one, carry)

    lax.fori_loop(0, groups, first_group, 0)
    recv1[me] = send1[me]
    conv_column(HP // wide + 1)

    states[0] = jnp.zeros((HP, N), BF16)
    for c in range(1, chunks):
        states[c] = weighted_sum(c * CHUNK).astype(BF16)

    def local_chunk(c, carry):
        start = pl.multiple_of(c * CHUNK, CHUNK)
        here = pl.ds(start, CHUNK)
        log_c = log_s[here]
        reached = log_s[pl.ds(pl.multiple_of(jnp.maximum(start - 8, 0), 8), 8)][7:8]
        reached = jnp.where(c > 0, reached, 0.0)
        c_rows = conv[here, HP + N :]
        b_rows = conv[here, HP : HP + N]
        scores = lax.dot_general(c_rows, b_rows, LAST, preferred_element_type=F32)
        scores = jnp.where(causal, scores, 0.0)
        x_rows = conv[here, 0:HP].astype(F32)
        driven = (expand(step_s[here], spread) * x_rows).astype(BF16)
        inter = lax.dot_general(c_rows, states[c], LAST, preferred_element_type=F32)
        y[here] = expand(jnp.exp(log_c - reached), spread) * inter + skip_row[...] * x_rows
        for h in range(0, HEADS, 2):
            pieces = []
            for k in (h, h + 1):
                gap = jnp.minimum(log_c[:, k : k + 1] - log_t[k : k + 1, here], 0.0)
                mixing = (scores * jnp.exp(gap)).astype(BF16)
                pieces.append(
                    jnp.dot(
                        mixing,
                        driven[:, k * P_SIZE : (k + 1) * P_SIZE],
                        preferred_element_type=F32,
                    )
                )
            both = slice(h * P_SIZE, (h + 2) * P_SIZE)
            y[here, both] = y[here, both] + jnp.concatenate(pieces, axis=1)
        return carry

    lax.fori_loop(0, chunks, local_chunk, 0)

    own_head = lax.div(me * rows, P_SIZE)

    def wait_from(copy_of, r):
        copy_of(r).wait_recv()

    def arrive(buffer, sems, r):
        pltpu.make_async_remote_copy(
            src_ref=buffer.at[r], dst_ref=buffer.at[r], send_sem=sems.at[r],
            recv_sem=sems.at[r], device_id=place(r), device_id_type=MESH,
        ).wait_recv()

    def advance(r, state):
        send2[r] = state.astype(BF16)

        @pl.when(r != me)
        def _():
            arrive(dec_recv, rsd, r)
            arrive(recv1, rs1, r)

        decay = dec_recv[r, pl.ds(own_head, 1), :]
        decay = jnp.concatenate([decay, decay], axis=1)
        return decay * state + recv1[r].astype(F32)

    lax.fori_loop(0, ndev, advance, jnp.zeros((rows, N), F32))

    def send_second(k, carry):
        second_copy(lax.rem(me + k, ndev)).start()
        return carry

    lax.fori_loop(1, ndev, send_second, 0)
    recv2[me] = send2[me]

    reach = jnp.exp(log_s[...])

    def last_group(i, carry):
        j = lax.rem(own_group + groups - 1 - i, groups)

        def wait_one(k, inner):
            g = j * owners + k

            @pl.when(g != me)
            def _():
                arrive(recv2, rs2, g)

            return inner

        lax.fori_loop(0, owners, wait_one, 0)
        cols = pl.ds(pl.multiple_of(j * wide, wide), wide)
        entry = recv2[pl.ds(j * owners, owners)].astype(F32).reshape(wide, N)
        entry_out[cols] = entry
        carried = lax.dot_general(
            conv[:, HP + N :], entry.astype(BF16), LAST, preferred_element_type=F32
        )
        spread_j = spread_of(j)
        out = y[:, cols] + expand(reach, spread_j) * carried
        square = out * out
        high = square.astype(BF16)
        low = (square - high.astype(F32)).astype(BF16)
        sums = lax.dot_general(high, spread_j, LAST, preferred_element_type=F32)
        sums = sums + lax.dot_general(low, spread_j, LAST, preferred_element_type=F32)
        inv_rms = lax.rsqrt(sums * (1.0 / P_SIZE) + EPSILON)
        mixed[:, cols] = (out * expand(inv_rms, spread_j) * gain_s[:, cols]).astype(BF16)
        return carry

    lax.fori_loop(0, groups, last_group, 0)

    def finish(k, carry):
        g = lax.rem(me + k, ndev)
        decay_copy(g).wait_send()
        first_copy(g).wait_send()
        second_copy(g).wait_send()
        return carry

    lax.fori_loop(1, ndev, finish, 0)


def run_scan(projected, tail, dt_raw, conv_w, conv_b, dt_bias, a_log, d_skip, norm_gain):
    n_in, n_out = lax.axis_size("inner"), lax.axis_size("outer")
    ndev = n_in * n_out
    length, xbc = projected.shape
    rows = HP // ndev
    dma = pltpu.SemaphoreType.DMA((ndev,))
    vmem = pl.BlockSpec(memory_space=pltpu.VMEM)
    return pl.pallas_call(
        partial(scan_kernel, n_in, ndev),
        out_shape=(
            jax.ShapeDtypeStruct((length, HP), BF16),
            jax.ShapeDtypeStruct((HP, N), F32),
        ),
        in_specs=[vmem] * 9,
        out_specs=(vmem, vmem),
        scratch_shapes=[
            pltpu.VMEM((1, HP), F32),
            pltpu.VMEM((1, xbc), F32),
            pltpu.VMEM((1, HP), F32),
            pltpu.VMEM((length + 8, xbc), F32),
            pltpu.VMEM((length, xbc), BF16),
            pltpu.VMEM((length, HEADS), F32),
            pltpu.VMEM((HEADS, length), F32),
            pltpu.VMEM((length, HEADS), F32),
            pltpu.VMEM((length, HP), F32),
            pltpu.VMEM((length // CHUNK, HP, N), BF16),
            pltpu.VMEM((ndev, rows, N), BF16),
            pltpu.VMEM((ndev, rows, N), BF16),
            pltpu.VMEM((ndev, rows, N), BF16),
            pltpu.VMEM((ndev, rows, N), BF16),
            pltpu.VMEM((HEADS, 128), F32),
            pltpu.VMEM((ndev, HEADS, 128), F32),
            dma, dma, dma, dma, dma, dma,
        ],
        compiler_params=pltpu.CompilerParams(
            collective_id=1, has_side_effects=True, vmem_limit_bytes=60 * 2**20
        ),
        name="scan",
    )(
        projected, tail, dt_raw, conv_w, conv_b, dt_bias, a_log, d_skip, norm_gain,
    )


def project_kernel(
    n, n_out,
    tokens, w_in, w_dt,
    proj, tail, dt_out,
    tok, held, total, held_dt,
    ring_s, ring_r, side_s, side_r, core_s, core_r, dt_s, dt_r, misc, tail_s, tail_r,
):
    length, depth = tokens.shape
    local, xbc = w_in.shape
    half = xbc // 2
    quarter = half // 2
    lanes = 128
    streams = quarter // lanes
    wide = 256
    tiles = half // wide
    third = (local * 5 // 16) // 16 * 16
    ring_rows = local - third
    tail_rows = tok.shape[0] - length
    block = held_dt.shape[2]
    ndev = n * n_out
    me = lax.axis_index("inner")
    core = lax.axis_index("outer")
    grp = lax.axis_index("grp")
    rank = core * n + me
    odd = lax.rem(me, 2)
    pos = jnp.where(odd == 0, lax.div(me, 2), n - lax.div(me + 1, 2))

    def index_at(q):
        q = lax.rem(q + 2 * n, n)
        return jnp.where(q < n // 2, 2 * q, 2 * n - 1 - 2 * q)

    def place(g):
        return {"inner": lax.rem(g, n), "outer": lax.div(g, n)}

    barrier = pltpu.get_barrier_semaphore()

    def greet(k, carry):
        pl.semaphore_signal(
            barrier, inc=1, device_id=place(lax.rem(rank + k, ndev)), device_id_type=MESH
        )
        return carry

    lax.fori_loop(1, ndev, greet, 0)
    pl.semaphore_signal(barrier, inc=1, device_id={"grp": 1 - grp}, device_id_type=MESH)

    def own_rows(owner):
        return pl.ds(pl.multiple_of(owner * local, 16), local)

    load_tok = pltpu.make_async_copy(tokens, tok.at[pl.ds(0, length)], misc.at[0])
    load_w = [
        pltpu.make_async_copy(
            w_in.at[:, pl.ds(d * half, half)], held.at[d, own_rows(me)], misc.at[1 + d]
        )
        for d in range(2)
    ]
    for copy in load_w:
        copy.start()
    load_tok.start()
    held_dt[me] = w_dt[...]

    @pl.when(rank == 0)
    def _():
        tok[length:] = jnp.zeros((tail_rows, depth), BF16)

    def ring_copy(d, t, s):
        owner = index_at(pos - (s - 1)) if d == 0 else index_at(pos + (s - 1))
        target = index_at(pos + 1) if d == 0 else index_at(pos - 1)
        rows = pl.ds(pl.multiple_of(owner * local + grp * third, 16), ring_rows)
        cols = pl.ds(pl.multiple_of(core * quarter + t * lanes, lanes), lanes)
        part = held.at[d, rows, cols]
        return pltpu.make_async_remote_copy(
            src_ref=part, dst_ref=part, send_sem=ring_s.at[d, t, s],
            recv_sem=ring_r.at[d, t, s], device_id={"inner": target}, device_id_type=MESH,
        )

    def owner_of(d, s):
        return index_at(pos - s) if d == 0 else index_at(pos + s)

    def chunk_cols(which, t):
        return pl.ds(pl.multiple_of(which * quarter + t * lanes, lanes), lanes)

    def side_rows(d, s, which):
        start = owner_of(d, s) * local + which * ring_rows
        return pl.ds(pl.multiple_of(start, 16), third)

    def side_between(d, t, s, which):
        part = held.at[d, side_rows(d, s, which), chunk_cols(core, t)]
        return pltpu.make_async_remote_copy(
            src_ref=part, dst_ref=part, send_sem=side_s.at[d, t, s],
            recv_sem=side_r.at[d, t, s], device_id={"grp": 1 - grp}, device_id_type=MESH,
        )

    def core_between(d, t, s, which):
        part = held.at[d, own_rows(owner_of(d, s)), chunk_cols(which, t)]
        return pltpu.make_async_remote_copy(
            src_ref=part, dst_ref=part, send_sem=core_s.at[d, t, s],
            recv_sem=core_r.at[d, t, s], device_id={"outer": 1 - core}, device_id_type=MESH,
        )

    def side_copy(d, t, s):
        return side_between(d, t, s, grp)

    def core_copy(d, t, s):
        return core_between(d, t, s, core)

    def ring_arrival(d, t, s):
        start = owner_of(d, s) * local + grp * third
        rows = pl.ds(pl.multiple_of(start, 16), ring_rows)
        part = held.at[d, rows, chunk_cols(core, t)]
        pltpu.make_async_remote_copy(
            src_ref=part, dst_ref=part, send_sem=ring_s.at[d, t, s],
            recv_sem=ring_r.at[d, t, s], device_id={"inner": index_at(pos + 1)},
            device_id_type=MESH,
        ).wait_recv()

    def side_arrival(d, t, s):
        side_between(d, t, s, 1 - grp).wait_recv()

    def core_arrival(d, t, s):
        core_between(d, t, s, 1 - core).wait_recv()

    def dt_copy(k):
        peer = lax.rem(me + k, n)
        return pltpu.make_async_remote_copy(
            src_ref=w_dt, dst_ref=held_dt.at[me], send_sem=dt_s.at[k],
            recv_sem=dt_r.at[me], device_id={"inner": peer}, device_id_type=MESH,
        )

    def dt_arrival(k):
        peer = lax.rem(me + k, n)
        pltpu.make_async_remote_copy(
            src_ref=w_dt, dst_ref=held_dt.at[peer], send_sem=dt_s.at[k],
            recv_sem=dt_r.at[peer], device_id={"inner": peer}, device_id_type=MESH,
        ).wait_recv()

    def tail_copy():
        return pltpu.make_async_remote_copy(
            src_ref=tokens.at[pl.ds(length - tail_rows, tail_rows)],
            dst_ref=tok.at[pl.ds(length, tail_rows)], send_sem=tail_s,
            recv_sem=tail_r, device_id=place(lax.rem(rank + 1, ndev)), device_id_type=MESH,
        )

    pl.semaphore_wait(barrier, ndev)

    @pl.when(rank < ndev - 1)
    def _():
        tail_copy().start()

    for d in range(2):
        load_w[d].wait()
        for t in range(streams):
            ring_copy(d, t, 1).start()

    def send_dt(k, carry):
        dt_copy(k).start()
        return carry

    lax.fori_loop(1, n, send_dt, 0)
    load_tok.wait()

    @pl.when(rank > 0)
    def _():
        tail_copy().wait_recv()

    incremental = local % 128 == 0

    def multiply_tile(d, lhs_cols, rhs_rows, first, j):
        cols = pl.ds(pl.multiple_of(j * wide, wide), wide)
        product = jnp.dot(
            tok[:, lhs_cols], held[d, rhs_rows, cols], preferred_element_type=F32
        )
        at = d * tiles + j
        if first:
            total[at] = product
        else:
            total[at] = total[at] + product

    def multiply(d, lhs_cols, rhs_rows, first):
        def tile(j, carry):
            multiply_tile(d, lhs_cols, rhs_rows, first, j)
            return carry

        lax.fori_loop(0, tiles, tile, 0)

    def project_dt():
        def arrived(k, carry):
            dt_arrival(k)
            return carry

        lax.fori_loop(1, n, arrived, 0)
        together = block // local

        def add(j, sums):
            cols = pl.ds(pl.multiple_of(j * block, block), block)
            piece = held_dt[j * together]
            for m in range(1, together):
                piece = piece + held_dt[j * together + m]
            return sums + lax.dot_general(
                tok[0:length, cols], piece, LAST, preferred_element_type=F32
            )

        sums = lax.fori_loop(0, depth // block, add, jnp.zeros((length, HEADS), F32))
        dt_out[...] = sums.astype(BF16)

    def step(s, carry):
        @pl.when(s >= 3)
        def _():
            for t in range(streams):
                for d in range(2):
                    core_arrival(d, t, s - 2)

        def part(t, inner):
            @pl.when(s < n)
            def _():
                for d in range(2):
                    ring_arrival(d, t, s)

                    @pl.when(s < n - 1)
                    def _():
                        ring_copy(d, t, s + 1).start()

                    side_copy(d, t, s).start()

            @pl.when((s >= 2) & (s <= n))
            def _():
                for d in range(2):
                    side_arrival(d, t, s - 1)
                    core_copy(d, t, s - 1).start()

            if incremental:
                for d in range(2):
                    owner = owner_of(d, s - 2)
                    at = pl.ds(pl.multiple_of(owner * local, 128), local)

                    @pl.when(s == 2)
                    def _():
                        multiply_tile(d, at, at, True, t)

                    @pl.when(s > 2)
                    def _():
                        multiply_tile(d, at, at, False, t)

            return inner

        lax.fori_loop(0, streams, part, 0)

        @pl.when(s == 1)
        def _():
            project_dt()

        return carry

    lax.fori_loop(1, n + 2, step, 0)
    if not incremental:
        for d in range(2):
            multiply(d, slice(0, 512), slice(0, 512), True)

            def more(j, carry):
                at = pl.ds(pl.multiple_of(j * 512, 512), 512)
                multiply(d, at, at, False)
                return carry

            lax.fori_loop(1, depth // 512, more, 0)

    for j in range(2 * tiles):
        cols = slice(j * wide, (j + 1) * wide)
        proj[:, cols] = total[j, 0:length].astype(BF16)
        tail[:, cols] = total[j, length:].astype(BF16)

    def drain(s, carry):
        for d in range(2):
            for t in range(streams):
                ring_copy(d, t, s).wait_send()
                side_copy(d, t, s).wait_send()
                core_copy(d, t, s).wait_send()
        dt_copy(s).wait_send()
        return carry

    lax.fori_loop(1, n, drain, 0)

    @pl.when(rank < ndev - 1)
    def _():
        tail_copy().wait_send()


def run_project(tokens, w_in, w_dt):
    n, n_out = lax.axis_size("inner"), lax.axis_size("outer")
    length, depth = tokens.shape
    local, xbc = w_in.shape
    block = max(local, 128)
    tail_rows = 16
    dt_block = w_dt.T
    if block != local:
        start = lax.rem(lax.axis_index("inner") * local, block)
        dt_block = lax.dynamic_update_slice(
            jnp.zeros((HEADS, block), BF16), dt_block, (jnp.int32(0), start)
        )
    streams = xbc // 4 // 128
    dma = pltpu.SemaphoreType.DMA
    vmem = pl.BlockSpec(memory_space=pltpu.VMEM)
    whole = pl.BlockSpec(memory_space=pl.ANY)
    return pl.pallas_call(
        partial(project_kernel, n, n_out),
        out_shape=(
            jax.ShapeDtypeStruct((length, xbc), BF16),
            jax.ShapeDtypeStruct((tail_rows, xbc), BF16),
            jax.ShapeDtypeStruct((length, HEADS), BF16),
        ),
        in_specs=[whole, whole, vmem],
        out_specs=(vmem, vmem, vmem),
        scratch_shapes=[
            pltpu.VMEM((length + tail_rows, depth), BF16),
            pltpu.VMEM((2, depth, xbc // 2), BF16),
            pltpu.VMEM((xbc // 256, length + tail_rows, 256), F32),
            pltpu.VMEM((n, HEADS, block), BF16),
            dma((2, streams, n)), dma((2, streams, n)),
            dma((2, streams, n)), dma((2, streams, n)),
            dma((2, streams, n)), dma((2, streams, n)),
            dma((n,)), dma((n,)), dma((3,)), dma(()), dma(()),
        ],
        compiler_params=pltpu.CompilerParams(
            collective_id=2, has_side_effects=True, vmem_limit_bytes=60 * 2**20
        ),
        name="project",
    )(tokens, w_in, dt_block)


def fused_kernel(
    n, n_out,
    tokens, w_in, w_dt, conv_w_in, conv_b_in, dt_bias_in, a_log_in, d_skip_in, gain_in,
    mixed_out, entry_all,
    conv_w, conv_b, dt_bias, a_log, d_skip, gain, mixed, entry_out,
    tail_rows_in, tail_send, tail_recv, decays,
    tok, held, total, held_dt, dt_acc, half_w, bias_row, gain_s, skip_row,
    conv, log_s, log_t, step_s, fac_s, reach_s, reach_all, edge, scores, grow, local_s, y,
    send1, recv1, prefix, mid_send, mid_recv, start, send2, recv2, dec_send, dec_recv,
    ring_s, ring_r, side_s, side_r, core_s, core_r, dt_s, dt_r, dc_s, dc_r, misc, tail_s, tail_r,
    ss1, rs1, ssm, rsm, ss2, rs2, ssd, rsd, small, out_sems,
):
    length, depth = tokens.shape
    local, xbc = w_in.shape
    tail_rows = tok.shape[0] - length
    wide, lanes = 256, 128
    blocks = xbc // wide
    groups = HP // wide
    early = groups
    late = blocks - early
    steps = n // 2
    half = local // 2
    third = (half * 5 // 16) // 16 * 16
    chunks = length // CHUNK
    ndev = n * n_out
    team = ndev // 2
    rows = wide // team
    me = lax.axis_index("inner")
    core = lax.axis_index("outer")
    grp = lax.axis_index("grp")
    rank = core * n + me
    odd = lax.rem(me, 2)
    pos = jnp.where(odd == 0, lax.div(me, 2), n - lax.div(me + 1, 2))
    upper = lax.div(me, n // 2)
    base = upper * (n // 2)
    own = (me - base) * n_out + core
    slot = core * (n // 2) + me - base

    def index_at(q):
        q = lax.rem(q + 2 * n, n)
        return jnp.where(q < n // 2, 2 * q, 2 * n - 1 - 2 * q)

    def place(g):
        return {"inner": lax.rem(g, n), "outer": lax.div(g, n)}

    barrier = pltpu.get_barrier_semaphore()

    def greet(k, carry):
        pl.semaphore_signal(
            barrier, inc=1, device_id=place(lax.rem(rank + k, ndev)), device_id_type=MESH
        )
        return carry

    lax.fori_loop(1, ndev, greet, 0)
    pl.semaphore_signal(barrier, inc=1, device_id={"grp": 1 - grp}, device_id_type=MESH)

    own_rows = pl.ds(pl.multiple_of(me * local, local), local)

    def natural(q):
        return groups if q == 0 else (blocks - 1 if q == blocks - 1 else q - 1)

    load_tok = pltpu.make_async_copy(
        tokens, tok.at[pl.ds(tail_rows, length)], misc.at[blocks]
    )
    load_w = [
        pltpu.make_async_copy(
            w_in.at[:, pl.ds(natural(q) * wide, wide)],
            held.at[q, own_rows], misc.at[q],
        )
        for q in range(blocks)
    ]
    for copy in load_w:
        copy.start()
    load_small = [
        pltpu.make_async_copy(source, target, small.at[k])
        for k, (source, target) in enumerate((
            (w_dt, held_dt.at[me]), (conv_w_in, conv_w), (conv_b_in, conv_b),
            (dt_bias_in, dt_bias), (a_log_in, a_log), (d_skip_in, d_skip), (gain_in, gain),
            (tokens.at[pl.ds(length - tail_rows, tail_rows)], tail_rows_in),
        ))
    ]
    for copy in load_small:
        copy.start()

    @pl.when(rank == 0)
    def _():
        tok[0:tail_rows] = jnp.zeros((tail_rows, depth), BF16)

    def owner_of(d, s):
        return index_at(pos - s) if d == 0 else index_at(pos + s)

    def share(whole):
        return third if whole else half // 2

    def columns(d, whole):
        return slice(0, wide) if whole else slice(d * lanes, (d + 1) * lanes)

    def ring_between(d, q, s, source, whole):
        start = owner_of(d, source) * local + core * half + grp * share(whole)
        span = pl.ds(pl.multiple_of(start, 16), half - share(whole))
        part = held.at[q, span, columns(d, whole)]
        target = index_at(pos + 1) if d == 0 else index_at(pos - 1)
        return pltpu.make_async_remote_copy(
            src_ref=part, dst_ref=part, send_sem=ring_s.at[d, q, s],
            recv_sem=ring_r.at[d, q, s], device_id={"inner": target}, device_id_type=MESH,
        )

    def ring_copy(d, q, s, whole):
        return ring_between(d, q, s, s - 1, whole)

    def side_between(d, q, s, which, whole):
        start = owner_of(d, s) * local + core * half + which * (half - share(whole))
        span = pl.ds(pl.multiple_of(start, 16), share(whole))
        part = held.at[q, span, columns(d, whole)]
        return pltpu.make_async_remote_copy(
            src_ref=part, dst_ref=part, send_sem=side_s.at[d, q, s],
            recv_sem=side_r.at[d, q, s], device_id={"grp": 1 - grp}, device_id_type=MESH,
        )

    def core_between(d, q, s, which, whole):
        start = owner_of(d, s) * local + which * half
        part = held.at[q, pl.ds(pl.multiple_of(start, 16), half), columns(d, whole)]
        return pltpu.make_async_remote_copy(
            src_ref=part, dst_ref=part, send_sem=core_s.at[d, q, s],
            recv_sem=core_r.at[d, q, s], device_id={"outer": 1 - core}, device_id_type=MESH,
        )

    def dt_part(owner, which):
        return held_dt.at[owner, :, pl.ds(pl.multiple_of(which * half, 128), half)]

    def dt_copy(k):
        peer = lax.rem(me + k, n)
        return pltpu.make_async_remote_copy(
            src_ref=dt_part(me, core), dst_ref=dt_part(me, core), send_sem=dt_s.at[k],
            recv_sem=dt_r.at[me], device_id={"inner": peer}, device_id_type=MESH,
        )

    def dt_arrival(k):
        peer = lax.rem(me + k, n)
        pltpu.make_async_remote_copy(
            src_ref=dt_part(peer, core), dst_ref=dt_part(peer, core), send_sem=dt_s.at[k],
            recv_sem=dt_r.at[peer], device_id={"inner": peer}, device_id_type=MESH,
        ).wait_recv()

    def dt_core(owner, which):
        return pltpu.make_async_remote_copy(
            src_ref=dt_part(owner, which), dst_ref=dt_part(owner, which),
            send_sem=dc_s.at[owner], recv_sem=dc_r.at[owner],
            device_id={"outer": 1 - core}, device_id_type=MESH,
        )

    def tail_copy():
        return pltpu.make_async_remote_copy(
            src_ref=tail_send, dst_ref=tail_recv, send_sem=tail_s,
            recv_sem=tail_r, device_id=place(lax.rem(rank + 1, ndev)), device_id_type=MESH,
        )

    def decay_copy(g):
        return pltpu.make_async_remote_copy(
            src_ref=dec_send, dst_ref=dec_recv.at[rank], send_sem=ssd.at[g],
            recv_sem=rsd.at[rank], device_id=place(g), device_id_type=MESH,
        )

    def member(o):
        return {"inner": base + lax.div(o, n_out), "outer": lax.rem(o, n_out)}

    def member_at(k):
        return {"inner": base + lax.rem(k, n // 2), "outer": lax.div(k, n // 2)}

    def first_copy(j, o):
        return pltpu.make_async_remote_copy(
            src_ref=send1.at[j, o], dst_ref=recv1.at[j, slot], send_sem=ss1.at[j, o],
            recv_sem=rs1.at[j, slot], device_id=member(o), device_id_type=MESH,
        )

    def first_arrival(j, k):
        pltpu.make_async_remote_copy(
            src_ref=send1.at[j, k], dst_ref=recv1.at[j, k], send_sem=ss1.at[j, k],
            recv_sem=rs1.at[j, k], device_id=member_at(k), device_id_type=MESH,
        ).wait_recv()

    batches = [slice(j, j + 1) for j in range(groups)]

    def mid_copy(b, c):
        return pltpu.make_async_remote_copy(
            src_ref=mid_send.at[c, batches[b]], dst_ref=mid_recv.at[c, batches[b]],
            send_sem=ssm.at[b, c], recv_sem=rsm.at[b, c],
            device_id={"inner": me + n // 2 - upper * n}, device_id_type=MESH,
        )

    def second_copy(b, k):
        return pltpu.make_async_remote_copy(
            src_ref=send2.at[k, batches[b]], dst_ref=recv2.at[own, batches[b]],
            send_sem=ss2.at[b, k], recv_sem=rs2.at[b, own],
            device_id=member_at(k), device_id_type=MESH,
        )

    def second_arrival(b, o):
        pltpu.make_async_remote_copy(
            src_ref=send2.at[o, batches[b]], dst_ref=recv2.at[o, batches[b]],
            send_sem=ss2.at[b, o], recv_sem=rs2.at[b, o],
            device_id=member(o), device_id_type=MESH,
        ).wait_recv()

    def arrive(buffer, sems, r, peer):
        pltpu.make_async_remote_copy(
            src_ref=buffer.at[r], dst_ref=buffer.at[r], send_sem=sems.at[r],
            recv_sem=sems.at[r], device_id=peer, device_id_type=MESH,
        ).wait_recv()

    for copy in load_small:
        copy.wait()

    kept = tail_rows_in[...].astype(F32)[tail_rows - CONV :]
    part_cols = depth // CONV
    tail_send[...] = jnp.concatenate(
        [kept[:, k * part_cols : (k + 1) * part_cols] for k in range(CONV)], axis=0
    ).astype(BF16)

    half_w[...] = conv_w[...] * 0.5
    bias_row[...] = conv_b[...].reshape(1, xbc) * 0.5
    gain_s[...] = gain[...].reshape(1, HP)

    def spread_of(j, count):
        head = lax.rem(lax.broadcasted_iota(jnp.int32, (count, wide), 0), HEADS)
        col = lax.broadcasted_iota(jnp.int32, (count, wide), 1) // P_SIZE
        return (head == col + j * (wide // P_SIZE)).astype(F32).astype(BF16)

    def split(values):
        high = values.astype(BF16).astype(F32)
        lane = lax.broadcasted_iota(jnp.int32, values.shape, 1)
        return jnp.where(lane < HEADS, high, values - high).astype(BF16)

    skip = d_skip[...].reshape(1, HEADS)
    skip_high = skip.astype(BF16).astype(F32)
    for j in range(groups):
        skip_row[:, j * wide : (j + 1) * wide] = expand(
            skip - skip_high, spread_of(j, HEADS)
        ) + jnp.dot(skip_high.astype(BF16), spread_of(j, HEADS), preferred_element_type=F32)

    pl.semaphore_wait(barrier, ndev)

    @pl.when(rank < ndev - 1)
    def _():
        tail_copy().start()

    def send_dt(k, carry):
        dt_copy(k).start()
        return carry

    lax.fori_loop(1, n, send_dt, 0)
    for q in range(early):
        load_w[q].wait()
        for d in range(2):
            ring_copy(d, q, 1, True).start()
    load_tok.start()
    for q in range(early, blocks):
        load_w[q].wait()

    def multiply(q, shards, first):
        product = None if first else total[q]
        for owner in shards:
            at = pl.ds(pl.multiple_of(owner * local, local), local)
            term = jnp.dot(tok[:, at], held[q, at, :], preferred_element_type=F32)
            product = term if product is None else product + term
        total[q] = product

    all_parts = blocks * steps
    side_lag, core_lag = 3, 4
    second, third_turn = early, 2 * early + 1
    fifth = third_turn + (steps - 2) * blocks

    def item(i):
        full = jnp.maximum(i - third_turn, 0)
        t = jnp.where(i < second, 1, jnp.where(i < third_turn, 2, 3 + lax.div(full, blocks)))
        q = jnp.where(
            i < second, i, jnp.where(i < third_turn, i - second, lax.rem(full, blocks))
        )
        t = jnp.where(i < fifth, t, jnp.where(i < fifth + 2, steps + 1, steps + 2))
        q = jnp.where(i < fifth, q, jnp.where(i < fifth + 1, early, early + 1))
        return q, t - jnp.maximum(q - early + 1, 0)

    def exchange(i):
        q, s = item(i)

        @pl.when((i < all_parts) & (s < steps))
        def _():
            for d in range(2):
                ring_between(d, q, s, s, True).wait_recv()

                @pl.when(s < steps - 1)
                def _():
                    ring_copy(d, q, s + 1, True).start()

                @pl.when(s == steps - 1)
                def _():
                    ring_copy(d, q, s + 1, False).start()

                side_between(d, q, s, grp, True).start()

        @pl.when((i < all_parts) & (s == steps))
        def _():
            for d in range(2):
                ring_between(d, q, s, s, False).wait_recv()
                side_between(d, q, s, grp, False).start()

        for k in range(late):
            @pl.when(i == (early - 1, 2 * early)[k])
            def _():
                for d in range(2):
                    ring_copy(d, early + k, 1, True).start()

        q, s = item(jnp.maximum(i - side_lag, 0))
        for whole in (True, False):
            @pl.when((i >= side_lag) & (i < all_parts + side_lag) & ((s < steps) == whole))
            def _():
                for d in range(2):
                    side_between(d, q, s, 1 - grp, whole).wait_recv()
                    core_between(d, q, s, core, whole).start()

    def sent(q, s, whole):
        for d in range(2):
            ring_copy(d, q, s, whole).wait_send()
            side_between(d, q, s, grp, whole).wait_send()
            core_between(d, q, s, core, whole).wait_send()

    def accumulate(i):
        q, s = item(jnp.maximum(i - core_lag, 0))

        @pl.when((i >= core_lag) & (s < steps))
        def _():
            for d in range(2):
                core_between(d, q, s, 1 - core, True).wait_recv()
            sent(q, s, True)
            multiply(q, [owner_of(0, s), owner_of(1, s)], False)

        @pl.when((i >= core_lag) & (s == steps))
        def _():
            for d in range(2):
                core_between(d, q, s, 1 - core, False).wait_recv()
            sent(q, s, False)
            multiply(q, [owner_of(0, s)], False)

        @pl.when((i < early) | (i == 6) | (i == 10))
        def _():
            multiply(jnp.where(i < early, i, early + lax.div(jnp.maximum(i - 6, 0), 4)), [me], True)

    def add_dt(k):
        @pl.when(k != me)
        def _():
            dt_core(k, 1 - core).wait_recv()

        cols = pl.ds(pl.multiple_of(k * local, local), local)
        part = lax.dot_general(
            tok[tail_rows:, cols], held_dt[k], LAST, preferred_element_type=F32
        )

        @pl.when(k == 0)
        def _():
            dt_acc[...] = part

        @pl.when(k > 0)
        def _():
            dt_acc[...] = dt_acc[...] + part

    def early_part(i, carry):
        exchange(i)

        @pl.when((i == 0) & (rank > 0))
        def _():
            tail_copy().wait_recv()
            for k in range(CONV):
                rows_k = tail_recv[...].astype(F32)[k * CONV : (k + 1) * CONV]
                above = jnp.zeros((tail_rows - CONV, part_cols), F32)
                tok[0:tail_rows, k * part_cols : (k + 1) * part_cols] = jnp.concatenate(
                    [above, rows_k], axis=0
                ).astype(BF16)

        @pl.when(i == 0)
        def _():
            load_tok.wait()

        accumulate(i)

        @pl.when((i < n) & (i != me))
        def _():
            dt_arrival(lax.rem(i - me + n, n))
            dt_core(i, core).start()

        @pl.when(i >= 2)
        def _():
            add_dt(i - 2)

        return carry

    lax.fori_loop(0, 10, early_part, 0)

    row_id = lax.broadcasted_iota(jnp.int32, (CHUNK, CHUNK), 0)
    col_id = lax.broadcasted_iota(jnp.int32, (CHUNK, CHUNK), 1)
    causal = col_id <= row_id
    dt_raw = dt_acc[...].astype(BF16).astype(F32)
    step_one = jax.nn.softplus(dt_raw + dt_bias[...].reshape(1, HEADS))
    scaled = step_one * (-jnp.exp(a_log[...].reshape(1, HEADS)))
    scaled = jnp.concatenate([scaled, scaled], axis=1)
    step_size = jnp.concatenate([step_one, step_one], axis=1)
    before = jnp.zeros((1, 2 * HEADS), F32)
    lower = causal.astype(F32)
    for c in range(chunks):
        here = slice(c * CHUNK, (c + 1) * CHUNK)
        part = jnp.dot(
            lower, scaled[here], preferred_element_type=F32,
            precision=lax.Precision.HIGHEST,
        ) + before
        log_s[here] = part
        reach_s[here] = split(jnp.exp(part - before))
        before = part[CHUNK - 1 : CHUNK]
        fac_s[here] = split(jnp.exp(before - part) * step_size[here])
    flat = jnp.transpose(log_s[...])[0:HEADS]
    log_t[...] = jnp.transpose(log_s[...] - jnp.log(step_size))[0:HEADS]
    ends = [flat[:, (c + 1) * CHUNK - 1 : (c + 1) * CHUNK] for c in range(chunks)]
    dec_send[...] = jnp.zeros((1, 128), F32)
    dec_send[:, 0 : 2 * HEADS] = jnp.exp(before)
    dec_recv[rank] = dec_send[...]

    def tall_of(column):
        column = jnp.broadcast_to(column, (HEADS, 128)).reshape(HEADS, 1, 128)
        return jnp.broadcast_to(column, (HEADS, P_SIZE, 128)).reshape(HP, 128)

    for c in range(1, chunks):
        edge[0, c - 1] = tall_of(jnp.exp(ends[c] - ends[c - 1]))
        edge[1, c - 1] = tall_of(jnp.exp(ends[c - 1]))

    def send_decay(k, carry):
        decay_copy(lax.rem(rank + k, ndev)).start()
        return carry

    lax.fori_loop(1, ndev, send_decay, 0)

    def conv_column(block):
        q = jnp.where(block < groups, block + 1, (blocks - 1) * (block - groups))
        cols = pl.ds(pl.multiple_of(block * wide, wide), wide)

        def one(i, carry):
            start = pl.multiple_of(i * 128, 128)
            window = total[q, pl.ds(pl.multiple_of(start + tail_rows - 8, 8), 136), :]
            window = window.astype(BF16).astype(F32)
            acc = bias_row[:, cols]
            for k in range(CONV):
                acc = acc + half_w[k : k + 1, cols] * window[5 + k : 5 + k + 128]
            conv[pl.ds(start, 128), cols] = (acc + acc * jnp.tanh(acc)).astype(BF16)
            return carry

        lax.fori_loop(0, length // 128, one, 0)

    def score_all():
        def one(c, carry):
            here = pl.ds(pl.multiple_of(c * CHUNK, CHUNK), CHUNK)
            product = lax.dot_general(
                conv[here, HP + N :], conv[here, HP : HP + N], LAST,
                preferred_element_type=F32,
            )
            scores[c] = jnp.where(causal, product, 0.0)
            return carry

        lax.fori_loop(0, chunks, one, 0)

    heads_each = HEADS // groups

    def grow_heads(c, j):
        here = pl.ds(pl.multiple_of(c * CHUNK, CHUNK), CHUNK)
        log_c = log_s[here]
        for k in range(heads_each):
            h = j * heads_each + k
            gap = jnp.minimum(log_c[:, h : h + 1] - log_t[h : h + 1, here], 60.0)
            grow[h, c] = jnp.exp(gap)

    def contribute(j):
        cols = pl.ds(pl.multiple_of(j * wide, wide), wide)
        spread = spread_of(j, 2 * HEADS)
        state = None
        for c in range(chunks):
            here = slice(c * CHUNK, (c + 1) * CHUNK)
            factor = jnp.dot(fac_s[here], spread, preferred_element_type=F32)
            weighted = (factor * conv[here, cols].astype(F32)).astype(BF16)
            part = lax.dot_general(
                weighted, conv[here, HP : HP + N], FIRST, preferred_element_type=F32
            )
            if c > 0:
                local_s[c - 1, cols] = state
                scale = edge[0, c - 1, cols, :]
                part = part + jnp.concatenate([scale, scale], axis=1) * state
            state = part
        send1[j] = state.reshape(team, rows, N).astype(BF16)

        def send_one(o, inner):
            @pl.when(o != own)
            def _():
                first_copy(j, o).start()

            return inner

        lax.fori_loop(0, team, send_one, 0)

    def inside(j):
        cols = pl.ds(pl.multiple_of(j * wide, wide), wide)
        lane = lax.broadcasted_iota(jnp.int32, (1, wide), 1) // P_SIZE

        def one(c, carry):
            here = pl.ds(pl.multiple_of(c * CHUNK, CHUNK), CHUNK)
            x_rows = conv[here, cols]
            acc = skip_row[:, cols] * x_rows.astype(F32)
            score = scores[c]
            for k in range(heads_each):
                keep = (lane == k).astype(F32).astype(BF16)
                mixing = (score * grow[j * heads_each + k, c]).astype(BF16)
                acc = acc + jnp.dot(mixing, x_rows * keep, preferred_element_type=F32)
            y[here, cols] = acc
            return carry

        lax.fori_loop(0, chunks, one, 0)

    def decay_of(k, half_of, j):
        r = lax.div(k, n // 2) * n + half_of * (n // 2) + lax.rem(k, n // 2)
        return decays[j, pl.ds(r, 1), :]

    def combine(b):
        for j in range(groups)[batches[b]]:
            recv1[j, slot] = send1[j, own]

            def arrived(k, carry):
                @pl.when(k != slot)
                def _():
                    first_arrival(j, k)

                return carry

            lax.fori_loop(0, team, arrived, 0)
            for c in range(2):
                state = jnp.zeros((rows, N), F32)
                for m in range(n // 2):
                    k = c * (n // 2) + m
                    prefix[j, k] = state
                    state = decay_of(k, upper, j) * state + recv1[j, k].astype(F32)
                mid_send[c, j] = state.astype(BF16)
        mid_copy(b, 0).start()

        @pl.when(upper == 0)
        def _():
            mid_copy(b, 1).start()

    def product_of(c, half_of, j):
        result = decay_of(c * (n // 2), half_of, j)
        for m in range(1, n // 2):
            result = result * decay_of(c * (n // 2) + m, half_of, j)
        return result

    def distribute(b):
        mid_copy(b, 0).wait_recv()

        @pl.when(upper == 1)
        def _():
            mid_copy(b, 1).wait_recv()

        is_upper = upper == 1
        for j in range(groups)[batches[b]]:
            middle = mid_recv[0, j].astype(F32)
            ours = mid_send[0, j].astype(F32)
            lower_sum = jnp.where(is_upper, middle, ours)
            upper_sum = jnp.where(is_upper, ours, middle)
            block_end = product_of(0, 1, j) * lower_sum + upper_sum

            @pl.when(is_upper)
            def _():
                start[0, j] = middle
                start[1, j] = product_of(1, 0, j) * block_end + mid_recv[1, j].astype(F32)

            @pl.when(upper == 0)
            def _():
                start[0, j] = jnp.zeros((rows, N), F32)
                start[1, j] = block_end

        for k in range(team):
            for j in range(groups)[batches[b]]:
                state = start[k // (n // 2), j]
                send2[k, j] = (prefix[j, k] + state).astype(BF16)
                start[k // (n // 2), j] = decay_of(k, upper, j) * state

            @pl.when(k != slot)
            def _():
                second_copy(b, k).start()

        recv2[own, batches[b]] = send2[slot, batches[b]]

    def drain_dt(k, carry):
        dt_copy(k).wait_send()
        dt_core(lax.rem(me + k, n), core).wait_send()
        return carry

    def drain_decay(k, carry):
        decay_copy(lax.rem(rank + k, ndev)).wait_send()
        return carry

    def late_part(i, carry):
        exchange(i)
        accumulate(i)
        ready = fifth - blocks + core_lag + 1

        @pl.when(i == ready - 1)
        def _():
            conv_column(groups)

        @pl.when((i >= ready) & (i < ready + groups - 1))
        def _():
            conv_column(i - ready)
            contribute(i - ready)

        @pl.when(i == ready + groups - 2)
        def _():
            others()

        @pl.when(i == ready - 2)
        def _():
            lax.fori_loop(1, n, drain_dt, 0)

        @pl.when(i == all_parts)
        def _():
            lax.fori_loop(1, ndev, drain_decay, 0)

        for k in range(groups):
            @pl.when(i == 10 + 2 * k)
            def _():
                def one(c, inner):
                    grow_heads(c, k)
                    return inner

                lax.fori_loop(0, chunks, one, 0)

            @pl.when(i == 11 + 2 * k)
            def _():
                spread = spread_of(k, 2 * HEADS)
                for c in range(chunks):
                    here = slice(c * CHUNK, (c + 1) * CHUNK)
                    reach_all[here, k * wide : (k + 1) * wide] = jnp.dot(
                        reach_s[here], spread, preferred_element_type=F32
                    )

        for b, turn in enumerate((all_parts - 1, all_parts, all_parts + 2)):
            @pl.when(i == turn)
            def _():
                combine(b)

        @pl.when(i == fifth + core_lag)
        def _():
            conv_column(groups - 1)
            contribute(groups - 1)

        return carry

    def others():
        def one(k, carry):
            r = lax.rem(rank + k, ndev)
            arrive(dec_recv, rsd, r, place(r))
            return carry

        lax.fori_loop(1, ndev, one, 0)
        every = jnp.concatenate([dec_recv[r] for r in range(ndev)], axis=0)
        lane = lax.broadcasted_iota(jnp.int32, (ndev, 128), 1)
        for j in range(groups):
            head = j * heads_each + lax.div(own * rows, P_SIZE)
            column = jnp.sum(jnp.where(lane == head, every, 0.0), axis=1, keepdims=True)
            decays[j] = jnp.broadcast_to(column, (ndev, N))

    lax.fori_loop(10, all_parts + core_lag, late_part, 0)

    distribute(0)
    conv_column(groups + 1)
    score_all()

    def fill(j, carry):
        inside(j)
        return carry

    combine(groups - 1)
    lax.fori_loop(0, 1, fill, 0)
    distribute(1)
    distribute(2)
    lax.fori_loop(1, groups - 1, fill, 0)
    distribute(groups - 1)
    lax.fori_loop(groups - 1, groups, fill, 0)

    row_head = lax.broadcasted_iota(jnp.int32, (wide, wide), 0) // P_SIZE
    col_head = lax.broadcasted_iota(jnp.int32, (wide, wide), 1) // P_SIZE
    same = (row_head == col_head).astype(F32).astype(BF16)

    def out_copies(j):
        cols = pl.ds(pl.multiple_of(j * wide, wide), wide)
        return [
            pltpu.make_async_copy(
                mixed.at[:, cols], mixed_out.at[:, cols], out_sems.at[0, j]
            ),
            pltpu.make_async_copy(
                entry_out.at[cols], entry_all.at[cols], out_sems.at[1, j]
            ),
        ]

    def finish_group(j, carry):
        cols = pl.ds(pl.multiple_of(j * wide, wide), wide)
        entry = jnp.concatenate([recv2[o, j] for o in range(team)], axis=0).astype(F32)
        entry_out[cols] = entry.astype(BF16)
        for c in range(chunks):
            here = slice(c * CHUNK, (c + 1) * CHUNK)
            state = entry
            if c > 0:
                scale = edge[1, c - 1, cols, :]
                state = local_s[c - 1, cols] + jnp.concatenate([scale, scale], axis=1) * entry
            carried = lax.dot_general(
                conv[here, HP + N :], state.astype(BF16), LAST, preferred_element_type=F32
            )
            out = y[here, cols] + reach_all[here, cols] * carried
            square = (out * out).astype(BF16)
            sums = jnp.dot(square, same, preferred_element_type=F32)
            inv_rms = lax.rsqrt(sums * (1.0 / P_SIZE) + EPSILON)
            mixed[here, cols] = (out * inv_rms * gain_s[:, cols]).astype(BF16)
        for copy in out_copies(j):
            copy.start()
        return carry

    def wait_second(b):
        def one(o, carry):
            @pl.when(o != own)
            def _():
                second_arrival(b, o)

            return carry

        lax.fori_loop(0, team, one, 0)

    def drain_first(k, carry):
        @pl.when(k != own)
        def _():
            for j in range(groups):
                first_copy(j, k).wait_send()

        return carry

    def drain_second(b):
        def one(k, carry):
            @pl.when(k != slot)
            def _():
                second_copy(b, k).wait_send()

            return carry

        lax.fori_loop(0, team, one, 0)

    def drain_swap(b):
        mid_copy(b, 0).wait_send()

        @pl.when(upper == 0)
        def _():
            mid_copy(b, 1).wait_send()

    for j in range(groups):
        if j == groups - 1:
            lax.fori_loop(0, team, drain_first, 0)
            for b in range(groups - 1):
                drain_second(b)
                drain_swap(b)

            @pl.when(rank < ndev - 1)
            def _():
                tail_copy().wait_send()

        wait_second(j)
        lax.fori_loop(j, j + 1, finish_group, 0)

    def drain_out(j, carry):
        for copy in out_copies(j):
            copy.wait()
        return carry

    drain_swap(groups - 1)
    drain_second(groups - 1)
    lax.fori_loop(0, groups, drain_out, 0)


def run_fused(tokens, w_in, w_dt, conv_w, conv_b, dt_bias, a_log, d_skip, norm_gain):
    n, n_out = lax.axis_size("inner"), lax.axis_size("outer")
    ndev = n * n_out
    length, depth = tokens.shape
    local, xbc = w_in.shape
    team = ndev // 2
    groups = HP // 256
    rows = 256 // team
    tail_rows = 16
    blocks = xbc // 256
    chunks = length // CHUNK
    dma = pltpu.SemaphoreType.DMA
    whole = pl.BlockSpec(memory_space=pl.ANY)
    weight_sems = [dma((2, blocks, n // 2 + 1))] * 6
    first_sems = [dma((groups, team))] * 2
    swap_sems = [dma((groups, 2))] * 2
    second_sems = [dma((groups, team))] * 2
    rank_sems = [dma((ndev,))] * 2
    return pl.pallas_call(
        partial(fused_kernel, n, n_out),
        out_shape=(
            jax.ShapeDtypeStruct((length, HP), BF16),
            jax.ShapeDtypeStruct((HP, N), BF16),
        ),
        in_specs=[whole] * 9,
        out_specs=(whole, whole),
        scratch_shapes=[
            pltpu.VMEM((CONV, xbc), F32), pltpu.VMEM((xbc,), F32),
            pltpu.VMEM((HEADS,), F32), pltpu.VMEM((HEADS,), F32),
            pltpu.VMEM((HEADS,), F32), pltpu.VMEM((HP,), F32),
            pltpu.VMEM((length, HP), BF16), pltpu.VMEM((HP, N), BF16),
            pltpu.VMEM((tail_rows, depth), BF16),
            pltpu.VMEM((tail_rows, depth // 4), BF16),
            pltpu.VMEM((tail_rows, depth // 4), BF16),
            pltpu.VMEM((groups, ndev, N), F32),
            pltpu.VMEM((length + tail_rows, depth), BF16),
            pltpu.VMEM((blocks, depth, 256), BF16),
            pltpu.VMEM((blocks, length + tail_rows, 256), F32),
            pltpu.VMEM((n, HEADS, local), BF16),
            pltpu.VMEM((length, HEADS), F32),
            pltpu.VMEM((CONV, xbc), F32),
            pltpu.VMEM((1, xbc), F32),
            pltpu.VMEM((1, HP), F32),
            pltpu.VMEM((1, HP), F32),
            pltpu.VMEM((length, xbc), BF16),
            pltpu.VMEM((length, 2 * HEADS), F32),
            pltpu.VMEM((HEADS, length), F32),
            pltpu.VMEM((length, 2 * HEADS), F32),
            pltpu.VMEM((length, 2 * HEADS), BF16),
            pltpu.VMEM((length, 2 * HEADS), BF16),
            pltpu.VMEM((length, HP), F32),
            pltpu.VMEM((2, chunks - 1, HP, 128), F32),
            pltpu.VMEM((chunks, CHUNK, CHUNK), F32),
            pltpu.VMEM((HEADS, chunks, CHUNK, CHUNK), F32),
            pltpu.VMEM((chunks - 1, HP, N), F32),
            pltpu.VMEM((length, HP), F32),
            pltpu.VMEM((groups, team, rows, N), BF16),
            pltpu.VMEM((groups, team, rows, N), BF16),
            pltpu.VMEM((groups, team, rows, N), F32),
            pltpu.VMEM((2, groups, rows, N), BF16),
            pltpu.VMEM((2, groups, rows, N), BF16),
            pltpu.VMEM((2, groups, rows, N), F32),
            pltpu.VMEM((team, groups, rows, N), BF16),
            pltpu.VMEM((team, groups, rows, N), BF16),
            pltpu.VMEM((1, 128), F32),
            pltpu.VMEM((ndev, 1, 128), F32),
            *weight_sems,
            dma((n,)), dma((n,)), dma((n,)), dma((n,)), dma((blocks + 1,)), dma(()), dma(()),
            *first_sems, *swap_sems, *second_sems, *rank_sems, dma((8,)), dma((2, groups)),
        ],
        compiler_params=pltpu.CompilerParams(
            collective_id=3, has_side_effects=True, vmem_limit_bytes=62 * 2**20
        ),
        name="fused",
    )(
        tokens, w_in, w_dt.T, conv_w, conv_b, dt_bias, a_log, d_skip, norm_gain,
    )


def hand_over_kernel(
    mixed, entry, mixed_out, entry_out, held_m, held_e, wide_e, in_sems, out_sems
):
    parts = in_sems.shape[1]
    loads, stores = [], []
    arrays = ((entry, held_e, wide_e, entry_out), (mixed, held_m, held_m, mixed_out))
    for i, (source, held, ready, target) in enumerate(arrays):
        rows = source.shape[0] // parts
        for k in range(parts):
            at = pl.ds(k * rows, rows)
            loads.append(pltpu.make_async_copy(source.at[at], held.at[at], in_sems.at[i, k]))
            stores.append(pltpu.make_async_copy(ready.at[at], target.at[at], out_sems.at[i, k]))
    for load in loads:
        load.start()
    rows = entry.shape[0] // parts
    for k, (load, store) in enumerate(zip(loads, stores)):
        load.wait()
        if k < parts:
            at = slice(k * rows, (k + 1) * rows)
            wide_e[at] = held_e[at].astype(F32)
        store.start()
    for store in stores:
        store.wait()


def hand_over(mixed, entry):
    whole = pl.BlockSpec(memory_space=pl.ANY)
    sems = pltpu.SemaphoreType.DMA((2, 4))
    return pl.pallas_call(
        hand_over_kernel,
        out_shape=(
            jax.ShapeDtypeStruct(mixed.shape, mixed.dtype),
            jax.ShapeDtypeStruct(entry.shape, F32),
        ),
        in_specs=[whole, whole],
        out_specs=(whole, whole),
        scratch_shapes=[
            pltpu.VMEM(mixed.shape, mixed.dtype), pltpu.VMEM(entry.shape, entry.dtype),
            pltpu.VMEM(entry.shape, F32), sems, sems,
        ],
        name="hand_over",
    )(mixed, entry)


def per_device(tokens, w_in, w_dt, conv_w, conv_b, dt_bias, a_log, d_skip, norm_gain):
    own_rows = tokens.reshape(tokens.shape[1], tokens.shape[2])
    row_count = own_rows.shape[0]
    if w_in.shape[0] % 512 == 0 and lax.axis_size("inner") == 8:
        mixed, entry = run_fused(
            own_rows, w_in, w_dt, conv_w, conv_b, dt_bias, a_log, d_skip, norm_gain
        )
        mixed, entry = hand_over(mixed, entry)
    else:
        projected, tail, dt_raw = run_project(own_rows, w_in, w_dt)
        mixed, entry = run_scan(
            projected, tail, dt_raw, conv_w, conv_b, dt_bias, a_log, d_skip, norm_gain
        )
    return (
        mixed.reshape(1, row_count, HP),
        entry.reshape(1, 1, HEADS, P_SIZE, N),
    )


def solution(mesh):
    placed = (
        P(("grp", "outer"), "inner", None),
        P("inner", None),
        P("inner", None),
        P(), P(), P(), P(), P(), P(),
    )
    return jax.shard_map(
        per_device,
        mesh=mesh,
        in_specs=placed,
        out_specs=(
            P(("grp", "outer"), "inner", None),
            P(("grp", "outer"), "inner", None, None, None),
        ),
        check_vma=False,
    )
```

```python
from functools import partial

import jax
import jax.numpy as jnp
from jax import lax
from jax.experimental import pallas as pl
from jax.experimental.pallas import tpu as pltpu
from jax.sharding import PartitionSpec as P

HEADS = 16
P_SIZE = 64
N = 256
CONV = 4
HP = HEADS * P_SIZE
CHUNK = 256
EPSILON = 1e-05
MESH = pl.DeviceIdType.MESH
F32 = jnp.float32
BF16 = jnp.bfloat16
LAST = (((1,), (1,)), ((), ()))
FIRST = (((0,), (0,)), ((), ()))


def expand(values, spread):
    high = values.astype(BF16)
    low = (values - high.astype(F32)).astype(BF16)
    return jnp.dot(high, spread, preferred_element_type=F32) + jnp.dot(
        low, spread, preferred_element_type=F32
    )


def scan_kernel(
    n_in, ndev,
    proj, tail, dt_raw, conv_w, conv_b, dt_bias, a_log, d_skip, gain,
    mixed, entry_out,
    gain_s, bias_row, skip_row, pad, conv, log_s, log_t, step_s, y, states,
    send1, recv1, send2, recv2, dec_send, dec_recv,
    ss1, rs1, ss2, rs2, ssd, rsd,
):
    length = proj.shape[0]
    chunks = length // CHUNK
    rows = HP // ndev
    me = lax.axis_index("outer") * n_in + lax.axis_index("inner")

    def place(g):
        return {"inner": lax.rem(g, n_in), "outer": lax.div(g, n_in)}

    barrier = pltpu.get_barrier_semaphore()

    def greet(k, carry):
        pl.semaphore_signal(
            barrier, inc=1, device_id=place(lax.rem(me + k, ndev)), device_id_type=MESH
        )
        return carry

    lax.fori_loop(1, ndev, greet, 0)

    head_id = lax.broadcasted_iota(jnp.int32, (HEADS, HP), 0)
    col_head = lax.broadcasted_iota(jnp.int32, (HEADS, HP), 1) // P_SIZE
    spread = (head_id == col_head).astype(F32).astype(BF16)

    bias_row[...] = conv_b[...].reshape(1, conv_b.shape[0])
    gain_s[...] = gain[...].reshape(1, HP)
    skip = d_skip[...].reshape(1, HEADS)
    skip_high = skip.astype(BF16).astype(F32)
    skip_row[...] = expand(skip - skip_high, spread) + jnp.dot(
        skip_high.astype(BF16), spread, preferred_element_type=F32
    )
    step_size = jax.nn.softplus(dt_raw[...].astype(F32) + dt_bias[...].reshape(1, HEADS))
    scaled = step_size * (-jnp.exp(a_log[...].reshape(1, HEADS)))
    row_id = lax.broadcasted_iota(jnp.int32, (CHUNK, CHUNK), 0)
    col_id = lax.broadcasted_iota(jnp.int32, (CHUNK, CHUNK), 1)
    causal = col_id <= row_id
    lower = causal.astype(F32)
    step_s[...] = step_size
    before = jnp.zeros((1, HEADS), F32)
    for c in range(chunks):
        part = jnp.dot(
            lower,
            scaled[c * CHUNK : (c + 1) * CHUNK],
            preferred_element_type=F32,
            precision=lax.Precision.HIGHEST,
        ) + before
        log_s[c * CHUNK : (c + 1) * CHUNK] = part
        before = part[CHUNK - 1 : CHUNK]
    log_t[...] = jnp.transpose(log_s[...])
    dec_send[...] = jnp.broadcast_to(jnp.exp(log_t[:, length - 1 : length]), (HEADS, 128))

    pad[0:8] = tail[...].astype(F32)[8:16]
    pad[8:] = proj[...].astype(F32)
    wide = 256
    blocks = proj.shape[1] // wide

    def conv_block(t, carry):
        i, j = lax.div(t, blocks), lax.rem(t, blocks)
        cols = pl.ds(pl.multiple_of(j * wide, wide), wide)
        window = pad[pl.ds(pl.multiple_of(i * 128, 128), 136), cols]
        total = bias_row[:, cols]
        for k in range(CONV):
            total = total + conv_w[k : k + 1, cols] * window[5 + k : 5 + k + 128]
        conv[pl.ds(pl.multiple_of(i * 128, 128), 128), cols] = (
            total * jax.nn.sigmoid(total)
        ).astype(BF16)
        return carry

    row_blocks = length // 128

    def conv_column(j):
        def one(i, carry):
            return conv_block(i * blocks + j, carry)

        lax.fori_loop(0, row_blocks, one, 0)

    conv_column(HP // wide)

    def weighted_sum(stop):
        final = log_s[stop - 1 : stop]
        factor = jnp.exp(final - log_s[0:stop]) * step_s[0:stop]
        weighted = (expand(factor, spread) * conv[0:stop, 0:HP].astype(F32)).astype(BF16)
        return lax.dot_general(
            weighted, conv[0:stop, HP : HP + N], FIRST, preferred_element_type=F32
        )

    dec_recv[me] = dec_send[...]

    def decay_copy(g):
        return pltpu.make_async_remote_copy(
            src_ref=dec_send, dst_ref=dec_recv.at[me], send_sem=ssd.at[g],
            recv_sem=rsd.at[me], device_id=place(g), device_id_type=MESH,
        )

    def first_copy(g):
        return pltpu.make_async_remote_copy(
            src_ref=send1.at[g], dst_ref=recv1.at[me], send_sem=ss1.at[g],
            recv_sem=rs1.at[me], device_id=place(g), device_id_type=MESH,
        )

    def second_copy(g):
        return pltpu.make_async_remote_copy(
            src_ref=send2.at[g], dst_ref=recv2.at[me], send_sem=ss2.at[g],
            recv_sem=rs2.at[me], device_id=place(g), device_id_type=MESH,
        )

    pl.semaphore_wait(barrier, ndev - 1)

    def send_decay(k, carry):
        decay_copy(lax.rem(me + k, ndev)).start()
        return carry

    lax.fori_loop(1, ndev, send_decay, 0)

    groups = HP // wide
    owners = ndev // groups
    own_group = lax.div(me, owners)
    factor = jnp.exp(log_s[length - 1 : length] - log_s[...]) * step_s[...]

    def spread_of(j):
        head = lax.broadcasted_iota(jnp.int32, (HEADS, wide), 0)
        col = lax.broadcasted_iota(jnp.int32, (HEADS, wide), 1) // P_SIZE
        return (head == col + j * (wide // P_SIZE)).astype(F32).astype(BF16)

    def first_group(i, carry):
        j = lax.rem(own_group + 1 + i, groups)
        conv_column(j)
        cols = pl.ds(pl.multiple_of(j * wide, wide), wide)
        weighted = (expand(factor, spread_of(j)) * conv[:, cols].astype(F32)).astype(BF16)
        part = lax.dot_general(
            weighted, conv[:, HP : HP + N], FIRST, preferred_element_type=F32
        )
        send1[pl.ds(j * owners, owners)] = part.reshape(owners, rows, N).astype(BF16)

        def send_one(k, inner):
            g = j * owners + k

            @pl.when(g != me)
            def _():
                first_copy(g).start()

            return inner

        return lax.fori_loop(0, owners, send_one, carry)

    lax.fori_loop(0, groups, first_group, 0)
    recv1[me] = send1[me]
    conv_column(HP // wide + 1)

    states[0] = jnp.zeros((HP, N), BF16)
    for c in range(1, chunks):
        states[c] = weighted_sum(c * CHUNK).astype(BF16)

    def local_chunk(c, carry):
        start = pl.multiple_of(c * CHUNK, CHUNK)
        here = pl.ds(start, CHUNK)
        log_c = log_s[here]
        reached = log_s[pl.ds(pl.multiple_of(jnp.maximum(start - 8, 0), 8), 8)][7:8]
        reached = jnp.where(c > 0, reached, 0.0)
        c_rows = conv[here, HP + N :]
        b_rows = conv[here, HP : HP + N]
        scores = lax.dot_general(c_rows, b_rows, LAST, preferred_element_type=F32)
        scores = jnp.where(causal, scores, 0.0)
        x_rows = conv[here, 0:HP].astype(F32)
        driven = (expand(step_s[here], spread) * x_rows).astype(BF16)
        inter = lax.dot_general(c_rows, states[c], LAST, preferred_element_type=F32)
        y[here] = expand(jnp.exp(log_c - reached), spread) * inter + skip_row[...] * x_rows
        for h in range(0, HEADS, 2):
            pieces = []
            for k in (h, h + 1):
                gap = jnp.minimum(log_c[:, k : k + 1] - log_t[k : k + 1, here], 0.0)
                mixing = (scores * jnp.exp(gap)).astype(BF16)
                pieces.append(
                    jnp.dot(
                        mixing,
                        driven[:, k * P_SIZE : (k + 1) * P_SIZE],
                        preferred_element_type=F32,
                    )
                )
            both = slice(h * P_SIZE, (h + 2) * P_SIZE)
            y[here, both] = y[here, both] + jnp.concatenate(pieces, axis=1)
        return carry

    lax.fori_loop(0, chunks, local_chunk, 0)

    own_head = lax.div(me * rows, P_SIZE)

    def wait_from(copy_of, r):
        copy_of(r).wait_recv()

    def arrive(buffer, sems, r):
        pltpu.make_async_remote_copy(
            src_ref=buffer.at[r], dst_ref=buffer.at[r], send_sem=sems.at[r],
            recv_sem=sems.at[r], device_id=place(r), device_id_type=MESH,
        ).wait_recv()

    def advance(r, state):
        send2[r] = state.astype(BF16)

        @pl.when(r != me)
        def _():
            arrive(dec_recv, rsd, r)
            arrive(recv1, rs1, r)

        decay = dec_recv[r, pl.ds(own_head, 1), :]
        decay = jnp.concatenate([decay, decay], axis=1)
        return decay * state + recv1[r].astype(F32)

    lax.fori_loop(0, ndev, advance, jnp.zeros((rows, N), F32))

    def send_second(k, carry):
        second_copy(lax.rem(me + k, ndev)).start()
        return carry

    lax.fori_loop(1, ndev, send_second, 0)
    recv2[me] = send2[me]

    reach = jnp.exp(log_s[...])

    def last_group(i, carry):
        j = lax.rem(own_group + groups - 1 - i, groups)

        def wait_one(k, inner):
            g = j * owners + k

            @pl.when(g != me)
            def _():
                arrive(recv2, rs2, g)

            return inner

        lax.fori_loop(0, owners, wait_one, 0)
        cols = pl.ds(pl.multiple_of(j * wide, wide), wide)
        entry = recv2[pl.ds(j * owners, owners)].astype(F32).reshape(wide, N)
        entry_out[cols] = entry
        carried = lax.dot_general(
            conv[:, HP + N :], entry.astype(BF16), LAST, preferred_element_type=F32
        )
        spread_j = spread_of(j)
        out = y[:, cols] + expand(reach, spread_j) * carried
        square = out * out
        high = square.astype(BF16)
        low = (square - high.astype(F32)).astype(BF16)
        sums = lax.dot_general(high, spread_j, LAST, preferred_element_type=F32)
        sums = sums + lax.dot_general(low, spread_j, LAST, preferred_element_type=F32)
        inv_rms = lax.rsqrt(sums * (1.0 / P_SIZE) + EPSILON)
        mixed[:, cols] = (out * expand(inv_rms, spread_j) * gain_s[:, cols]).astype(BF16)
        return carry

    lax.fori_loop(0, groups, last_group, 0)

    def finish(k, carry):
        g = lax.rem(me + k, ndev)
        decay_copy(g).wait_send()
        first_copy(g).wait_send()
        second_copy(g).wait_send()
        return carry

    lax.fori_loop(1, ndev, finish, 0)


def run_scan(projected, tail, dt_raw, conv_w, conv_b, dt_bias, a_log, d_skip, norm_gain):
    n_in, n_out = lax.axis_size("inner"), lax.axis_size("outer")
    ndev = n_in * n_out
    length, xbc = projected.shape
    rows = HP // ndev
    dma = pltpu.SemaphoreType.DMA((ndev,))
    vmem = pl.BlockSpec(memory_space=pltpu.VMEM)
    return pl.pallas_call(
        partial(scan_kernel, n_in, ndev),
        out_shape=(
            jax.ShapeDtypeStruct((length, HP), BF16),
            jax.ShapeDtypeStruct((HP, N), F32),
        ),
        in_specs=[vmem] * 9,
        out_specs=(vmem, vmem),
        scratch_shapes=[
            pltpu.VMEM((1, HP), F32),
            pltpu.VMEM((1, xbc), F32),
            pltpu.VMEM((1, HP), F32),
            pltpu.VMEM((length + 8, xbc), F32),
            pltpu.VMEM((length, xbc), BF16),
            pltpu.VMEM((length, HEADS), F32),
            pltpu.VMEM((HEADS, length), F32),
            pltpu.VMEM((length, HEADS), F32),
            pltpu.VMEM((length, HP), F32),
            pltpu.VMEM((length // CHUNK, HP, N), BF16),
            pltpu.VMEM((ndev, rows, N), BF16),
            pltpu.VMEM((ndev, rows, N), BF16),
            pltpu.VMEM((ndev, rows, N), BF16),
            pltpu.VMEM((ndev, rows, N), BF16),
            pltpu.VMEM((HEADS, 128), F32),
            pltpu.VMEM((ndev, HEADS, 128), F32),
            dma, dma, dma, dma, dma, dma,
        ],
        compiler_params=pltpu.CompilerParams(
            collective_id=1, has_side_effects=True, vmem_limit_bytes=60 * 2**20
        ),
        name="scan",
    )(
        projected, tail, dt_raw, conv_w, conv_b, dt_bias, a_log, d_skip, norm_gain,
    )


def project_kernel(
    n, n_out,
    tokens, w_in, w_dt,
    proj, tail, dt_out,
    tok, held, total, held_dt,
    ring_s, ring_r, side_s, side_r, core_s, core_r, dt_s, dt_r, misc, tail_s, tail_r,
):
    length, depth = tokens.shape
    local, xbc = w_in.shape
    half = xbc // 2
    quarter = half // 2
    lanes = 128
    streams = quarter // lanes
    wide = 256
    tiles = half // wide
    third = (local * 5 // 16) // 16 * 16
    ring_rows = local - third
    tail_rows = tok.shape[0] - length
    block = held_dt.shape[2]
    ndev = n * n_out
    me = lax.axis_index("inner")
    core = lax.axis_index("outer")
    grp = lax.axis_index("grp")
    rank = core * n + me
    odd = lax.rem(me, 2)
    pos = jnp.where(odd == 0, lax.div(me, 2), n - lax.div(me + 1, 2))

    def index_at(q):
        q = lax.rem(q + 2 * n, n)
        return jnp.where(q < n // 2, 2 * q, 2 * n - 1 - 2 * q)

    def place(g):
        return {"inner": lax.rem(g, n), "outer": lax.div(g, n)}

    barrier = pltpu.get_barrier_semaphore()

    def greet(k, carry):
        pl.semaphore_signal(
            barrier, inc=1, device_id=place(lax.rem(rank + k, ndev)), device_id_type=MESH
        )
        return carry

    lax.fori_loop(1, ndev, greet, 0)
    pl.semaphore_signal(barrier, inc=1, device_id={"grp": 1 - grp}, device_id_type=MESH)

    def own_rows(owner):
        return pl.ds(pl.multiple_of(owner * local, 16), local)

    load_tok = pltpu.make_async_copy(tokens, tok.at[pl.ds(0, length)], misc.at[0])
    load_w = [
        pltpu.make_async_copy(
            w_in.at[:, pl.ds(d * half, half)], held.at[d, own_rows(me)], misc.at[1 + d]
        )
        for d in range(2)
    ]
    for copy in load_w:
        copy.start()
    load_tok.start()
    held_dt[me] = w_dt[...]

    @pl.when(rank == 0)
    def _():
        tok[length:] = jnp.zeros((tail_rows, depth), BF16)

    def ring_copy(d, t, s):
        owner = index_at(pos - (s - 1)) if d == 0 else index_at(pos + (s - 1))
        target = index_at(pos + 1) if d == 0 else index_at(pos - 1)
        rows = pl.ds(pl.multiple_of(owner * local + grp * third, 16), ring_rows)
        cols = pl.ds(pl.multiple_of(core * quarter + t * lanes, lanes), lanes)
        part = held.at[d, rows, cols]
        return pltpu.make_async_remote_copy(
            src_ref=part, dst_ref=part, send_sem=ring_s.at[d, t, s],
            recv_sem=ring_r.at[d, t, s], device_id={"inner": target}, device_id_type=MESH,
        )

    def owner_of(d, s):
        return index_at(pos - s) if d == 0 else index_at(pos + s)

    def chunk_cols(which, t):
        return pl.ds(pl.multiple_of(which * quarter + t * lanes, lanes), lanes)

    def side_rows(d, s, which):
        start = owner_of(d, s) * local + which * ring_rows
        return pl.ds(pl.multiple_of(start, 16), third)

    def side_between(d, t, s, which):
        part = held.at[d, side_rows(d, s, which), chunk_cols(core, t)]
        return pltpu.make_async_remote_copy(
            src_ref=part, dst_ref=part, send_sem=side_s.at[d, t, s],
            recv_sem=side_r.at[d, t, s], device_id={"grp": 1 - grp}, device_id_type=MESH,
        )

    def core_between(d, t, s, which):
        part = held.at[d, own_rows(owner_of(d, s)), chunk_cols(which, t)]
        return pltpu.make_async_remote_copy(
            src_ref=part, dst_ref=part, send_sem=core_s.at[d, t, s],
            recv_sem=core_r.at[d, t, s], device_id={"outer": 1 - core}, device_id_type=MESH,
        )

    def side_copy(d, t, s):
        return side_between(d, t, s, grp)

    def core_copy(d, t, s):
        return core_between(d, t, s, core)

    def ring_arrival(d, t, s):
        start = owner_of(d, s) * local + grp * third
        rows = pl.ds(pl.multiple_of(start, 16), ring_rows)
        part = held.at[d, rows, chunk_cols(core, t)]
        pltpu.make_async_remote_copy(
            src_ref=part, dst_ref=part, send_sem=ring_s.at[d, t, s],
            recv_sem=ring_r.at[d, t, s], device_id={"inner": index_at(pos + 1)},
            device_id_type=MESH,
        ).wait_recv()

    def side_arrival(d, t, s):
        side_between(d, t, s, 1 - grp).wait_recv()

    def core_arrival(d, t, s):
        core_between(d, t, s, 1 - core).wait_recv()

    def dt_copy(k):
        peer = lax.rem(me + k, n)
        return pltpu.make_async_remote_copy(
            src_ref=w_dt, dst_ref=held_dt.at[me], send_sem=dt_s.at[k],
            recv_sem=dt_r.at[me], device_id={"inner": peer}, device_id_type=MESH,
        )

    def dt_arrival(k):
        peer = lax.rem(me + k, n)
        pltpu.make_async_remote_copy(
            src_ref=w_dt, dst_ref=held_dt.at[peer], send_sem=dt_s.at[k],
            recv_sem=dt_r.at[peer], device_id={"inner": peer}, device_id_type=MESH,
        ).wait_recv()

    def tail_copy():
        return pltpu.make_async_remote_copy(
            src_ref=tokens.at[pl.ds(length - tail_rows, tail_rows)],
            dst_ref=tok.at[pl.ds(length, tail_rows)], send_sem=tail_s,
            recv_sem=tail_r, device_id=place(lax.rem(rank + 1, ndev)), device_id_type=MESH,
        )

    pl.semaphore_wait(barrier, ndev)

    @pl.when(rank < ndev - 1)
    def _():
        tail_copy().start()

    for d in range(2):
        load_w[d].wait()
        for t in range(streams):
            ring_copy(d, t, 1).start()

    def send_dt(k, carry):
        dt_copy(k).start()
        return carry

    lax.fori_loop(1, n, send_dt, 0)
    load_tok.wait()

    @pl.when(rank > 0)
    def _():
        tail_copy().wait_recv()

    incremental = local % 128 == 0

    def multiply_tile(d, lhs_cols, rhs_rows, first, j):
        cols = pl.ds(pl.multiple_of(j * wide, wide), wide)
        product = jnp.dot(
            tok[:, lhs_cols], held[d, rhs_rows, cols], preferred_element_type=F32
        )
        at = d * tiles + j
        if first:
            total[at] = product
        else:
            total[at] = total[at] + product

    def multiply(d, lhs_cols, rhs_rows, first):
        def tile(j, carry):
            multiply_tile(d, lhs_cols, rhs_rows, first, j)
            return carry

        lax.fori_loop(0, tiles, tile, 0)

    def project_dt():
        def arrived(k, carry):
            dt_arrival(k)
            return carry

        lax.fori_loop(1, n, arrived, 0)
        together = block // local

        def add(j, sums):
            cols = pl.ds(pl.multiple_of(j * block, block), block)
            piece = held_dt[j * together]
            for m in range(1, together):
                piece = piece + held_dt[j * together + m]
            return sums + lax.dot_general(
                tok[0:length, cols], piece, LAST, preferred_element_type=F32
            )

        sums = lax.fori_loop(0, depth // block, add, jnp.zeros((length, HEADS), F32))
        dt_out[...] = sums.astype(BF16)

    def step(s, carry):
        @pl.when(s >= 3)
        def _():
            for t in range(streams):
                for d in range(2):
                    core_arrival(d, t, s - 2)

        def part(t, inner):
            @pl.when(s < n)
            def _():
                for d in range(2):
                    ring_arrival(d, t, s)

                    @pl.when(s < n - 1)
                    def _():
                        ring_copy(d, t, s + 1).start()

                    side_copy(d, t, s).start()

            @pl.when((s >= 2) & (s <= n))
            def _():
                for d in range(2):
                    side_arrival(d, t, s - 1)
                    core_copy(d, t, s - 1).start()

            if incremental:
                for d in range(2):
                    owner = owner_of(d, s - 2)
                    at = pl.ds(pl.multiple_of(owner * local, 128), local)

                    @pl.when(s == 2)
                    def _():
                        multiply_tile(d, at, at, True, t)

                    @pl.when(s > 2)
                    def _():
                        multiply_tile(d, at, at, False, t)

            return inner

        lax.fori_loop(0, streams, part, 0)

        @pl.when(s == 1)
        def _():
            project_dt()

        return carry

    lax.fori_loop(1, n + 2, step, 0)
    if not incremental:
        for d in range(2):
            multiply(d, slice(0, 512), slice(0, 512), True)

            def more(j, carry):
                at = pl.ds(pl.multiple_of(j * 512, 512), 512)
                multiply(d, at, at, False)
                return carry

            lax.fori_loop(1, depth // 512, more, 0)

    for j in range(2 * tiles):
        cols = slice(j * wide, (j + 1) * wide)
        proj[:, cols] = total[j, 0:length].astype(BF16)
        tail[:, cols] = total[j, length:].astype(BF16)

    def drain(s, carry):
        for d in range(2):
            for t in range(streams):
                ring_copy(d, t, s).wait_send()
                side_copy(d, t, s).wait_send()
                core_copy(d, t, s).wait_send()
        dt_copy(s).wait_send()
        return carry

    lax.fori_loop(1, n, drain, 0)

    @pl.when(rank < ndev - 1)
    def _():
        tail_copy().wait_send()


def run_project(tokens, w_in, w_dt):
    n, n_out = lax.axis_size("inner"), lax.axis_size("outer")
    length, depth = tokens.shape
    local, xbc = w_in.shape
    block = max(local, 128)
    tail_rows = 16
    dt_block = w_dt.T
    if block != local:
        start = lax.rem(lax.axis_index("inner") * local, block)
        dt_block = lax.dynamic_update_slice(
            jnp.zeros((HEADS, block), BF16), dt_block, (jnp.int32(0), start)
        )
    streams = xbc // 4 // 128
    dma = pltpu.SemaphoreType.DMA
    vmem = pl.BlockSpec(memory_space=pltpu.VMEM)
    whole = pl.BlockSpec(memory_space=pl.ANY)
    return pl.pallas_call(
        partial(project_kernel, n, n_out),
        out_shape=(
            jax.ShapeDtypeStruct((length, xbc), BF16),
            jax.ShapeDtypeStruct((tail_rows, xbc), BF16),
            jax.ShapeDtypeStruct((length, HEADS), BF16),
        ),
        in_specs=[whole, whole, vmem],
        out_specs=(vmem, vmem, vmem),
        scratch_shapes=[
            pltpu.VMEM((length + tail_rows, depth), BF16),
            pltpu.VMEM((2, depth, xbc // 2), BF16),
            pltpu.VMEM((xbc // 256, length + tail_rows, 256), F32),
            pltpu.VMEM((n, HEADS, block), BF16),
            dma((2, streams, n)), dma((2, streams, n)),
            dma((2, streams, n)), dma((2, streams, n)),
            dma((2, streams, n)), dma((2, streams, n)),
            dma((n,)), dma((n,)), dma((3,)), dma(()), dma(()),
        ],
        compiler_params=pltpu.CompilerParams(
            collective_id=2, has_side_effects=True, vmem_limit_bytes=60 * 2**20
        ),
        name="project",
    )(tokens, w_in, dt_block)


def fused_kernel(
    n, n_out,
    tokens, w_in, w_dt, conv_w_in, conv_b_in, dt_bias_in, a_log_in, d_skip_in, gain_in,
    mixed_out, entry_all,
    conv_w, conv_b, dt_bias, a_log, d_skip, gain, mixed, entry_out,
    tail_rows_in, tail_send, tail_recv, decays,
    tok, held, total, held_dt, dt_acc, half_w, bias_row, gain_s, skip_row,
    conv, log_s, log_t, step_s, fac_s, reach_s, reach_all, edge, scores, grow, local_s, y,
    send1, recv1, prefix, mid_send, mid_recv, start, send2, recv2, dec_send, dec_recv,
    ring_s, ring_r, side_s, side_r, core_s, core_r, dt_s, dt_r, dc_s, dc_r, misc, tail_s, tail_r,
    ss1, rs1, ssm, rsm, ss2, rs2, ssd, rsd, small, out_sems,
):
    length, depth = tokens.shape
    local, xbc = w_in.shape
    tail_rows = tok.shape[0] - length
    wide, lanes = 256, 128
    blocks = xbc // wide
    groups = HP // wide
    early = groups
    late = blocks - early
    steps = n // 2
    half = local // 2
    third = (half * 5 // 16) // 16 * 16
    chunks = length // CHUNK
    ndev = n * n_out
    team = ndev // 2
    rows = wide // team
    me = lax.axis_index("inner")
    core = lax.axis_index("outer")
    grp = lax.axis_index("grp")
    rank = core * n + me
    odd = lax.rem(me, 2)
    pos = jnp.where(odd == 0, lax.div(me, 2), n - lax.div(me + 1, 2))
    upper = lax.div(me, n // 2)
    base = upper * (n // 2)
    own = (me - base) * n_out + core
    slot = core * (n // 2) + me - base

    def index_at(q):
        q = lax.rem(q + 2 * n, n)
        return jnp.where(q < n // 2, 2 * q, 2 * n - 1 - 2 * q)

    def place(g):
        return {"inner": lax.rem(g, n), "outer": lax.div(g, n)}

    barrier = pltpu.get_barrier_semaphore()

    def greet(k, carry):
        pl.semaphore_signal(
            barrier, inc=1, device_id=place(lax.rem(rank + k, ndev)), device_id_type=MESH
        )
        return carry

    lax.fori_loop(1, ndev, greet, 0)
    pl.semaphore_signal(barrier, inc=1, device_id={"grp": 1 - grp}, device_id_type=MESH)

    own_rows = pl.ds(pl.multiple_of(me * local, local), local)

    def natural(q):
        return groups if q == 0 else (blocks - 1 if q == blocks - 1 else q - 1)

    load_tok = pltpu.make_async_copy(
        tokens, tok.at[pl.ds(tail_rows, length)], misc.at[blocks]
    )
    load_w = [
        pltpu.make_async_copy(
            w_in.at[:, pl.ds(natural(q) * wide, wide)],
            held.at[q, own_rows], misc.at[q],
        )
        for q in range(blocks)
    ]
    for copy in load_w:
        copy.start()
    load_small = [
        pltpu.make_async_copy(source, target, small.at[k])
        for k, (source, target) in enumerate((
            (w_dt, held_dt.at[me]), (conv_w_in, conv_w), (conv_b_in, conv_b),
            (dt_bias_in, dt_bias), (a_log_in, a_log), (d_skip_in, d_skip), (gain_in, gain),
            (tokens.at[pl.ds(length - tail_rows, tail_rows)], tail_rows_in),
        ))
    ]
    for copy in load_small:
        copy.start()

    @pl.when(rank == 0)
    def _():
        tok[0:tail_rows] = jnp.zeros((tail_rows, depth), BF16)

    def owner_of(d, s):
        return index_at(pos - s) if d == 0 else index_at(pos + s)

    def share(whole):
        return third if whole else half // 2

    def columns(d, whole):
        return slice(0, wide) if whole else slice(d * lanes, (d + 1) * lanes)

    def ring_between(d, q, s, source, whole):
        start = owner_of(d, source) * local + core * half + grp * share(whole)
        span = pl.ds(pl.multiple_of(start, 16), half - share(whole))
        part = held.at[q, span, columns(d, whole)]
        target = index_at(pos + 1) if d == 0 else index_at(pos - 1)
        return pltpu.make_async_remote_copy(
            src_ref=part, dst_ref=part, send_sem=ring_s.at[d, q, s],
            recv_sem=ring_r.at[d, q, s], device_id={"inner": target}, device_id_type=MESH,
        )

    def ring_copy(d, q, s, whole):
        return ring_between(d, q, s, s - 1, whole)

    def side_between(d, q, s, which, whole):
        start = owner_of(d, s) * local + core * half + which * (half - share(whole))
        span = pl.ds(pl.multiple_of(start, 16), share(whole))
        part = held.at[q, span, columns(d, whole)]
        return pltpu.make_async_remote_copy(
            src_ref=part, dst_ref=part, send_sem=side_s.at[d, q, s],
            recv_sem=side_r.at[d, q, s], device_id={"grp": 1 - grp}, device_id_type=MESH,
        )

    def core_between(d, q, s, which, whole):
        start = owner_of(d, s) * local + which * half
        part = held.at[q, pl.ds(pl.multiple_of(start, 16), half), columns(d, whole)]
        return pltpu.make_async_remote_copy(
            src_ref=part, dst_ref=part, send_sem=core_s.at[d, q, s],
            recv_sem=core_r.at[d, q, s], device_id={"outer": 1 - core}, device_id_type=MESH,
        )

    def dt_part(owner, which):
        return held_dt.at[owner, :, pl.ds(pl.multiple_of(which * half, 128), half)]

    def dt_copy(k):
        peer = lax.rem(me + k, n)
        return pltpu.make_async_remote_copy(
            src_ref=dt_part(me, core), dst_ref=dt_part(me, core), send_sem=dt_s.at[k],
            recv_sem=dt_r.at[me], device_id={"inner": peer}, device_id_type=MESH,
        )

    def dt_arrival(k):
        peer = lax.rem(me + k, n)
        pltpu.make_async_remote_copy(
            src_ref=dt_part(peer, core), dst_ref=dt_part(peer, core), send_sem=dt_s.at[k],
            recv_sem=dt_r.at[peer], device_id={"inner": peer}, device_id_type=MESH,
        ).wait_recv()

    def dt_core(owner, which):
        return pltpu.make_async_remote_copy(
            src_ref=dt_part(owner, which), dst_ref=dt_part(owner, which),
            send_sem=dc_s.at[owner], recv_sem=dc_r.at[owner],
            device_id={"outer": 1 - core}, device_id_type=MESH,
        )

    def tail_copy():
        return pltpu.make_async_remote_copy(
            src_ref=tail_send, dst_ref=tail_recv, send_sem=tail_s,
            recv_sem=tail_r, device_id=place(lax.rem(rank + 1, ndev)), device_id_type=MESH,
        )

    def decay_copy(g):
        return pltpu.make_async_remote_copy(
            src_ref=dec_send, dst_ref=dec_recv.at[rank], send_sem=ssd.at[g],
            recv_sem=rsd.at[rank], device_id=place(g), device_id_type=MESH,
        )

    def member(o):
        return {"inner": base + lax.div(o, n_out), "outer": lax.rem(o, n_out)}

    def member_at(k):
        return {"inner": base + lax.rem(k, n // 2), "outer": lax.div(k, n // 2)}

    def first_copy(j, o):
        return pltpu.make_async_remote_copy(
            src_ref=send1.at[j, o], dst_ref=recv1.at[j, slot], send_sem=ss1.at[j, o],
            recv_sem=rs1.at[j, slot], device_id=member(o), device_id_type=MESH,
        )

    def first_arrival(j, k):
        pltpu.make_async_remote_copy(
            src_ref=send1.at[j, k], dst_ref=recv1.at[j, k], send_sem=ss1.at[j, k],
            recv_sem=rs1.at[j, k], device_id=member_at(k), device_id_type=MESH,
        ).wait_recv()

    batches = [slice(j, j + 1) for j in range(groups)]

    def mid_copy(b, c):
        return pltpu.make_async_remote_copy(
            src_ref=mid_send.at[c, batches[b]], dst_ref=mid_recv.at[c, batches[b]],
            send_sem=ssm.at[b, c], recv_sem=rsm.at[b, c],
            device_id={"inner": me + n // 2 - upper * n}, device_id_type=MESH,
        )

    def second_copy(b, k):
        return pltpu.make_async_remote_copy(
            src_ref=send2.at[k, batches[b]], dst_ref=recv2.at[own, batches[b]],
            send_sem=ss2.at[b, k], recv_sem=rs2.at[b, own],
            device_id=member_at(k), device_id_type=MESH,
        )

    def second_arrival(b, o):
        pltpu.make_async_remote_copy(
            src_ref=send2.at[o, batches[b]], dst_ref=recv2.at[o, batches[b]],
            send_sem=ss2.at[b, o], recv_sem=rs2.at[b, o],
            device_id=member(o), device_id_type=MESH,
        ).wait_recv()

    def arrive(buffer, sems, r, peer):
        pltpu.make_async_remote_copy(
            src_ref=buffer.at[r], dst_ref=buffer.at[r], send_sem=sems.at[r],
            recv_sem=sems.at[r], device_id=peer, device_id_type=MESH,
        ).wait_recv()

    for copy in load_small:
        copy.wait()

    kept = tail_rows_in[...].astype(F32)[tail_rows - CONV :]
    part_cols = depth // CONV
    tail_send[...] = jnp.concatenate(
        [kept[:, k * part_cols : (k + 1) * part_cols] for k in range(CONV)], axis=0
    ).astype(BF16)

    half_w[...] = conv_w[...] * 0.5
    bias_row[...] = conv_b[...].reshape(1, xbc) * 0.5
    gain_s[...] = gain[...].reshape(1, HP)

    def spread_of(j, count):
        head = lax.rem(lax.broadcasted_iota(jnp.int32, (count, wide), 0), HEADS)
        col = lax.broadcasted_iota(jnp.int32, (count, wide), 1) // P_SIZE
        return (head == col + j * (wide // P_SIZE)).astype(F32).astype(BF16)

    def split(values):
        high = values.astype(BF16).astype(F32)
        lane = lax.broadcasted_iota(jnp.int32, values.shape, 1)
        return jnp.where(lane < HEADS, high, values - high).astype(BF16)

    skip = d_skip[...].reshape(1, HEADS)
    skip_high = skip.astype(BF16).astype(F32)
    for j in range(groups):
        skip_row[:, j * wide : (j + 1) * wide] = expand(
            skip - skip_high, spread_of(j, HEADS)
        ) + jnp.dot(skip_high.astype(BF16), spread_of(j, HEADS), preferred_element_type=F32)

    pl.semaphore_wait(barrier, ndev)

    @pl.when(rank < ndev - 1)
    def _():
        tail_copy().start()

    def send_dt(k, carry):
        dt_copy(k).start()
        return carry

    lax.fori_loop(1, n, send_dt, 0)
    for q in range(early):
        load_w[q].wait()
        for d in range(2):
            ring_copy(d, q, 1, True).start()
    load_tok.start()
    for q in range(early, blocks):
        load_w[q].wait()

    def multiply(q, shards, first):
        product = None if first else total[q]
        for owner in shards:
            at = pl.ds(pl.multiple_of(owner * local, local), local)
            term = jnp.dot(tok[:, at], held[q, at, :], preferred_element_type=F32)
            product = term if product is None else product + term
        total[q] = product

    all_parts = blocks * steps
    side_lag, core_lag = 3, 4
    second, third_turn = early, 2 * early + 1
    fifth = third_turn + (steps - 2) * blocks

    def item(i):
        full = jnp.maximum(i - third_turn, 0)
        t = jnp.where(i < second, 1, jnp.where(i < third_turn, 2, 3 + lax.div(full, blocks)))
        q = jnp.where(
            i < second, i, jnp.where(i < third_turn, i - second, lax.rem(full, blocks))
        )
        t = jnp.where(i < fifth, t, jnp.where(i < fifth + 2, steps + 1, steps + 2))
        q = jnp.where(i < fifth, q, jnp.where(i < fifth + 1, early, early + 1))
        return q, t - jnp.maximum(q - early + 1, 0)

    def exchange(i):
        q, s = item(i)

        @pl.when((i < all_parts) & (s < steps))
        def _():
            for d in range(2):
                ring_between(d, q, s, s, True).wait_recv()

                @pl.when(s < steps - 1)
                def _():
                    ring_copy(d, q, s + 1, True).start()

                @pl.when(s == steps - 1)
                def _():
                    ring_copy(d, q, s + 1, False).start()

                side_between(d, q, s, grp, True).start()

        @pl.when((i < all_parts) & (s == steps))
        def _():
            for d in range(2):
                ring_between(d, q, s, s, False).wait_recv()
                side_between(d, q, s, grp, False).start()

        for k in range(late):
            @pl.when(i == (early - 1, 2 * early)[k])
            def _():
                for d in range(2):
                    ring_copy(d, early + k, 1, True).start()

        q, s = item(jnp.maximum(i - side_lag, 0))
        for whole in (True, False):
            @pl.when((i >= side_lag) & (i < all_parts + side_lag) & ((s < steps) == whole))
            def _():
                for d in range(2):
                    side_between(d, q, s, 1 - grp, whole).wait_recv()
                    core_between(d, q, s, core, whole).start()

    def sent(q, s, whole):
        for d in range(2):
            ring_copy(d, q, s, whole).wait_send()
            side_between(d, q, s, grp, whole).wait_send()
            core_between(d, q, s, core, whole).wait_send()

    def accumulate(i):
        q, s = item(jnp.maximum(i - core_lag, 0))

        @pl.when((i >= core_lag) & (s < steps))
        def _():
            for d in range(2):
                core_between(d, q, s, 1 - core, True).wait_recv()
            sent(q, s, True)
            multiply(q, [owner_of(0, s), owner_of(1, s)], False)

        @pl.when((i >= core_lag) & (s == steps))
        def _():
            for d in range(2):
                core_between(d, q, s, 1 - core, False).wait_recv()
            sent(q, s, False)
            multiply(q, [owner_of(0, s)], False)

        @pl.when((i < early) | (i == 6) | (i == 10))
        def _():
            multiply(jnp.where(i < early, i, early + lax.div(jnp.maximum(i - 6, 0), 4)), [me], True)

    def add_dt(k):
        @pl.when(k != me)
        def _():
            dt_core(k, 1 - core).wait_recv()

        cols = pl.ds(pl.multiple_of(k * local, local), local)
        part = lax.dot_general(
            tok[tail_rows:, cols], held_dt[k], LAST, preferred_element_type=F32
        )

        @pl.when(k == 0)
        def _():
            dt_acc[...] = part

        @pl.when(k > 0)
        def _():
            dt_acc[...] = dt_acc[...] + part

    def early_part(i, carry):
        exchange(i)

        @pl.when((i == 0) & (rank > 0))
        def _():
            tail_copy().wait_recv()
            for k in range(CONV):
                rows_k = tail_recv[...].astype(F32)[k * CONV : (k + 1) * CONV]
                above = jnp.zeros((tail_rows - CONV, part_cols), F32)
                tok[0:tail_rows, k * part_cols : (k + 1) * part_cols] = jnp.concatenate(
                    [above, rows_k], axis=0
                ).astype(BF16)

        @pl.when(i == 0)
        def _():
            load_tok.wait()

        accumulate(i)

        @pl.when((i < n) & (i != me))
        def _():
            dt_arrival(lax.rem(i - me + n, n))
            dt_core(i, core).start()

        @pl.when(i >= 2)
        def _():
            add_dt(i - 2)

        return carry

    lax.fori_loop(0, 10, early_part, 0)

    row_id = lax.broadcasted_iota(jnp.int32, (CHUNK, CHUNK), 0)
    col_id = lax.broadcasted_iota(jnp.int32, (CHUNK, CHUNK), 1)
    causal = col_id <= row_id
    dt_raw = dt_acc[...].astype(BF16).astype(F32)
    step_one = jax.nn.softplus(dt_raw + dt_bias[...].reshape(1, HEADS))
    scaled = step_one * (-jnp.exp(a_log[...].reshape(1, HEADS)))
    scaled = jnp.concatenate([scaled, scaled], axis=1)
    step_size = jnp.concatenate([step_one, step_one], axis=1)
    before = jnp.zeros((1, 2 * HEADS), F32)
    lower = causal.astype(F32)
    for c in range(chunks):
        here = slice(c * CHUNK, (c + 1) * CHUNK)
        part = jnp.dot(
            lower, scaled[here], preferred_element_type=F32,
            precision=lax.Precision.HIGHEST,
        ) + before
        log_s[here] = part
        reach_s[here] = split(jnp.exp(part - before))
        before = part[CHUNK - 1 : CHUNK]
        fac_s[here] = split(jnp.exp(before - part) * step_size[here])
    flat = jnp.transpose(log_s[...])[0:HEADS]
    log_t[...] = jnp.transpose(log_s[...] - jnp.log(step_size))[0:HEADS]
    ends = [flat[:, (c + 1) * CHUNK - 1 : (c + 1) * CHUNK] for c in range(chunks)]
    dec_send[...] = jnp.zeros((1, 128), F32)
    dec_send[:, 0 : 2 * HEADS] = jnp.exp(before)
    dec_recv[rank] = dec_send[...]

    def tall_of(column):
        column = jnp.broadcast_to(column, (HEADS, 128)).reshape(HEADS, 1, 128)
        return jnp.broadcast_to(column, (HEADS, P_SIZE, 128)).reshape(HP, 128)

    for c in range(1, chunks):
        edge[0, c - 1] = tall_of(jnp.exp(ends[c] - ends[c - 1]))
        edge[1, c - 1] = tall_of(jnp.exp(ends[c - 1]))

    def send_decay(k, carry):
        decay_copy(lax.rem(rank + k, ndev)).start()
        return carry

    lax.fori_loop(1, ndev, send_decay, 0)

    def conv_column(block):
        q = jnp.where(block < groups, block + 1, (blocks - 1) * (block - groups))
        cols = pl.ds(pl.multiple_of(block * wide, wide), wide)

        def one(i, carry):
            start = pl.multiple_of(i * 128, 128)
            window = total[q, pl.ds(pl.multiple_of(start + tail_rows - 8, 8), 136), :]
            window = window.astype(BF16).astype(F32)
            acc = bias_row[:, cols]
            for k in range(CONV):
                acc = acc + half_w[k : k + 1, cols] * window[5 + k : 5 + k + 128]
            conv[pl.ds(start, 128), cols] = (acc + acc * jnp.tanh(acc)).astype(BF16)
            return carry

        lax.fori_loop(0, length // 128, one, 0)

    def score_all():
        def one(c, carry):
            here = pl.ds(pl.multiple_of(c * CHUNK, CHUNK), CHUNK)
            product = lax.dot_general(
                conv[here, HP + N :], conv[here, HP : HP + N], LAST,
                preferred_element_type=F32,
            )
            scores[c] = jnp.where(causal, product, 0.0)
            return carry

        lax.fori_loop(0, chunks, one, 0)

    heads_each = HEADS // groups

    def grow_heads(c, j):
        here = pl.ds(pl.multiple_of(c * CHUNK, CHUNK), CHUNK)
        log_c = log_s[here]
        for k in range(heads_each):
            h = j * heads_each + k
            gap = jnp.minimum(log_c[:, h : h + 1] - log_t[h : h + 1, here], 60.0)
            grow[h, c] = jnp.exp(gap)

    def contribute(j):
        cols = pl.ds(pl.multiple_of(j * wide, wide), wide)
        spread = spread_of(j, 2 * HEADS)
        state = None
        for c in range(chunks):
            here = slice(c * CHUNK, (c + 1) * CHUNK)
            factor = jnp.dot(fac_s[here], spread, preferred_element_type=F32)
            weighted = (factor * conv[here, cols].astype(F32)).astype(BF16)
            part = lax.dot_general(
                weighted, conv[here, HP : HP + N], FIRST, preferred_element_type=F32
            )
            if c > 0:
                local_s[c - 1, cols] = state
                scale = edge[0, c - 1, cols, :]
                part = part + jnp.concatenate([scale, scale], axis=1) * state
            state = part
        send1[j] = state.reshape(team, rows, N).astype(BF16)

        def send_one(o, inner):
            @pl.when(o != own)
            def _():
                first_copy(j, o).start()

            return inner

        lax.fori_loop(0, team, send_one, 0)

    def inside(j):
        cols = pl.ds(pl.multiple_of(j * wide, wide), wide)
        lane = lax.broadcasted_iota(jnp.int32, (1, wide), 1) // P_SIZE

        def one(c, carry):
            here = pl.ds(pl.multiple_of(c * CHUNK, CHUNK), CHUNK)
            x_rows = conv[here, cols]
            acc = skip_row[:, cols] * x_rows.astype(F32)
            score = scores[c]
            for k in range(heads_each):
                keep = (lane == k).astype(F32).astype(BF16)
                mixing = (score * grow[j * heads_each + k, c]).astype(BF16)
                acc = acc + jnp.dot(mixing, x_rows * keep, preferred_element_type=F32)
            y[here, cols] = acc
            return carry

        lax.fori_loop(0, chunks, one, 0)

    def decay_of(k, half_of, j):
        r = lax.div(k, n // 2) * n + half_of * (n // 2) + lax.rem(k, n // 2)
        return decays[j, pl.ds(r, 1), :]

    def combine(b):
        for j in range(groups)[batches[b]]:
            recv1[j, slot] = send1[j, own]

            def arrived(k, carry):
                @pl.when(k != slot)
                def _():
                    first_arrival(j, k)

                return carry

            lax.fori_loop(0, team, arrived, 0)
            for c in range(2):
                state = jnp.zeros((rows, N), F32)
                for m in range(n // 2):
                    k = c * (n // 2) + m
                    prefix[j, k] = state
                    state = decay_of(k, upper, j) * state + recv1[j, k].astype(F32)
                mid_send[c, j] = state.astype(BF16)
        mid_copy(b, 0).start()

        @pl.when(upper == 0)
        def _():
            mid_copy(b, 1).start()

    def product_of(c, half_of, j):
        result = decay_of(c * (n // 2), half_of, j)
        for m in range(1, n // 2):
            result = result * decay_of(c * (n // 2) + m, half_of, j)
        return result

    def distribute(b):
        mid_copy(b, 0).wait_recv()

        @pl.when(upper == 1)
        def _():
            mid_copy(b, 1).wait_recv()

        is_upper = upper == 1
        for j in range(groups)[batches[b]]:
            middle = mid_recv[0, j].astype(F32)
            ours = mid_send[0, j].astype(F32)
            lower_sum = jnp.where(is_upper, middle, ours)
            upper_sum = jnp.where(is_upper, ours, middle)
            block_end = product_of(0, 1, j) * lower_sum + upper_sum

            @pl.when(is_upper)
            def _():
                start[0, j] = middle
                start[1, j] = product_of(1, 0, j) * block_end + mid_recv[1, j].astype(F32)

            @pl.when(upper == 0)
            def _():
                start[0, j] = jnp.zeros((rows, N), F32)
                start[1, j] = block_end

        for k in range(team):
            for j in range(groups)[batches[b]]:
                state = start[k // (n // 2), j]
                send2[k, j] = (prefix[j, k] + state).astype(BF16)
                start[k // (n // 2), j] = decay_of(k, upper, j) * state

            @pl.when(k != slot)
            def _():
                second_copy(b, k).start()

        recv2[own, batches[b]] = send2[slot, batches[b]]

    def drain_dt(k, carry):
        dt_copy(k).wait_send()
        dt_core(lax.rem(me + k, n), core).wait_send()
        return carry

    def drain_decay(k, carry):
        decay_copy(lax.rem(rank + k, ndev)).wait_send()
        return carry

    def late_part(i, carry):
        exchange(i)
        accumulate(i)
        ready = fifth - blocks + core_lag + 1

        @pl.when(i == ready - 1)
        def _():
            conv_column(groups)

        @pl.when((i >= ready) & (i < ready + groups - 1))
        def _():
            conv_column(i - ready)
            contribute(i - ready)

        @pl.when(i == ready + groups - 2)
        def _():
            others()

        @pl.when(i == ready - 2)
        def _():
            lax.fori_loop(1, n, drain_dt, 0)

        @pl.when(i == all_parts)
        def _():
            lax.fori_loop(1, ndev, drain_decay, 0)

        for k in range(groups):
            @pl.when(i == 10 + 2 * k)
            def _():
                def one(c, inner):
                    grow_heads(c, k)
                    return inner

                lax.fori_loop(0, chunks, one, 0)

            @pl.when(i == 11 + 2 * k)
            def _():
                spread = spread_of(k, 2 * HEADS)
                for c in range(chunks):
                    here = slice(c * CHUNK, (c + 1) * CHUNK)
                    reach_all[here, k * wide : (k + 1) * wide] = jnp.dot(
                        reach_s[here], spread, preferred_element_type=F32
                    )

        for b, turn in enumerate((all_parts - 1, all_parts, all_parts + 2)):
            @pl.when(i == turn)
            def _():
                combine(b)

        @pl.when(i == fifth + core_lag)
        def _():
            conv_column(groups - 1)
            contribute(groups - 1)

        return carry

    def others():
        def one(k, carry):
            r = lax.rem(rank + k, ndev)
            arrive(dec_recv, rsd, r, place(r))
            return carry

        lax.fori_loop(1, ndev, one, 0)
        every = jnp.concatenate([dec_recv[r] for r in range(ndev)], axis=0)
        lane = lax.broadcasted_iota(jnp.int32, (ndev, 128), 1)
        for j in range(groups):
            head = j * heads_each + lax.div(own * rows, P_SIZE)
            column = jnp.sum(jnp.where(lane == head, every, 0.0), axis=1, keepdims=True)
            decays[j] = jnp.broadcast_to(column, (ndev, N))

    lax.fori_loop(10, all_parts + core_lag, late_part, 0)

    conv_column(groups + 1)
    distribute(0)
    score_all()

    def fill(j, carry):
        inside(j)
        return carry

    combine(groups - 1)
    lax.fori_loop(0, 1, fill, 0)
    distribute(1)
    lax.fori_loop(1, 2, fill, 0)
    distribute(2)
    lax.fori_loop(2, groups - 1, fill, 0)
    distribute(groups - 1)
    lax.fori_loop(groups - 1, groups, fill, 0)

    row_head = lax.broadcasted_iota(jnp.int32, (wide, wide), 0) // P_SIZE
    col_head = lax.broadcasted_iota(jnp.int32, (wide, wide), 1) // P_SIZE
    same = (row_head == col_head).astype(F32).astype(BF16)

    def out_copies(j):
        cols = pl.ds(pl.multiple_of(j * wide, wide), wide)
        return [
            pltpu.make_async_copy(
                mixed.at[:, cols], mixed_out.at[:, cols], out_sems.at[0, j]
            ),
            pltpu.make_async_copy(
                entry_out.at[cols], entry_all.at[cols], out_sems.at[1, j]
            ),
        ]

    def finish_group(j, carry):
        cols = pl.ds(pl.multiple_of(j * wide, wide), wide)
        entry = jnp.concatenate([recv2[o, j] for o in range(team)], axis=0).astype(F32)
        entry_out[cols] = entry.astype(BF16)
        for c in range(chunks):
            here = slice(c * CHUNK, (c + 1) * CHUNK)
            state = entry
            if c > 0:
                scale = edge[1, c - 1, cols, :]
                state = local_s[c - 1, cols] + jnp.concatenate([scale, scale], axis=1) * entry
            carried = lax.dot_general(
                conv[here, HP + N :], state.astype(BF16), LAST, preferred_element_type=F32
            )
            out = y[here, cols] + reach_all[here, cols] * carried
            square = (out * out).astype(BF16)
            sums = jnp.dot(square, same, preferred_element_type=F32)
            inv_rms = lax.rsqrt(sums * (1.0 / P_SIZE) + EPSILON)
            mixed[here, cols] = (out * inv_rms * gain_s[:, cols]).astype(BF16)
        for copy in out_copies(j):
            copy.start()
        return carry

    def wait_second(b):
        def one(o, carry):
            @pl.when(o != own)
            def _():
                second_arrival(b, o)

            return carry

        lax.fori_loop(0, team, one, 0)

    def drain_first(k, carry):
        @pl.when(k != own)
        def _():
            for j in range(groups):
                first_copy(j, k).wait_send()

        return carry

    def drain_second(b):
        def one(k, carry):
            @pl.when(k != slot)
            def _():
                second_copy(b, k).wait_send()

            return carry

        lax.fori_loop(0, team, one, 0)

    def drain_swap(b):
        mid_copy(b, 0).wait_send()

        @pl.when(upper == 0)
        def _():
            mid_copy(b, 1).wait_send()

    for j in range(groups):
        if j == groups - 1:
            lax.fori_loop(0, team, drain_first, 0)
            for b in range(groups - 1):
                drain_second(b)
                drain_swap(b)

            @pl.when(rank < ndev - 1)
            def _():
                tail_copy().wait_send()

        wait_second(j)
        lax.fori_loop(j, j + 1, finish_group, 0)

    def drain_out(j, carry):
        for copy in out_copies(j):
            copy.wait()
        return carry

    drain_swap(groups - 1)
    drain_second(groups - 1)
    lax.fori_loop(0, groups, drain_out, 0)


def run_fused(tokens, w_in, w_dt, conv_w, conv_b, dt_bias, a_log, d_skip, norm_gain):
    n, n_out = lax.axis_size("inner"), lax.axis_size("outer")
    ndev = n * n_out
    length, depth = tokens.shape
    local, xbc = w_in.shape
    team = ndev // 2
    groups = HP // 256
    rows = 256 // team
    tail_rows = 16
    blocks = xbc // 256
    chunks = length // CHUNK
    dma = pltpu.SemaphoreType.DMA
    whole = pl.BlockSpec(memory_space=pl.ANY)
    weight_sems = [dma((2, blocks, n // 2 + 1))] * 6
    first_sems = [dma((groups, team))] * 2
    swap_sems = [dma((groups, 2))] * 2
    second_sems = [dma((groups, team))] * 2
    rank_sems = [dma((ndev,))] * 2
    return pl.pallas_call(
        partial(fused_kernel, n, n_out),
        out_shape=(
            jax.ShapeDtypeStruct((length, HP), BF16),
            jax.ShapeDtypeStruct((HP, N), BF16),
        ),
        in_specs=[whole] * 9,
        out_specs=(whole, whole),
        scratch_shapes=[
            pltpu.VMEM((CONV, xbc), F32), pltpu.VMEM((xbc,), F32),
            pltpu.VMEM((HEADS,), F32), pltpu.VMEM((HEADS,), F32),
            pltpu.VMEM((HEADS,), F32), pltpu.VMEM((HP,), F32),
            pltpu.VMEM((length, HP), BF16), pltpu.VMEM((HP, N), BF16),
            pltpu.VMEM((tail_rows, depth), BF16),
            pltpu.VMEM((tail_rows, depth // 4), BF16),
            pltpu.VMEM((tail_rows, depth // 4), BF16),
            pltpu.VMEM((groups, ndev, N), F32),
            pltpu.VMEM((length + tail_rows, depth), BF16),
            pltpu.VMEM((blocks, depth, 256), BF16),
            pltpu.VMEM((blocks, length + tail_rows, 256), F32),
            pltpu.VMEM((n, HEADS, local), BF16),
            pltpu.VMEM((length, HEADS), F32),
            pltpu.VMEM((CONV, xbc), F32),
            pltpu.VMEM((1, xbc), F32),
            pltpu.VMEM((1, HP), F32),
            pltpu.VMEM((1, HP), F32),
            pltpu.VMEM((length, xbc), BF16),
            pltpu.VMEM((length, 2 * HEADS), F32),
            pltpu.VMEM((HEADS, length), F32),
            pltpu.VMEM((length, 2 * HEADS), F32),
            pltpu.VMEM((length, 2 * HEADS), BF16),
            pltpu.VMEM((length, 2 * HEADS), BF16),
            pltpu.VMEM((length, HP), F32),
            pltpu.VMEM((2, chunks - 1, HP, 128), F32),
            pltpu.VMEM((chunks, CHUNK, CHUNK), F32),
            pltpu.VMEM((HEADS, chunks, CHUNK, CHUNK), F32),
            pltpu.VMEM((chunks - 1, HP, N), F32),
            pltpu.VMEM((length, HP), F32),
            pltpu.VMEM((groups, team, rows, N), BF16),
            pltpu.VMEM((groups, team, rows, N), BF16),
            pltpu.VMEM((groups, team, rows, N), F32),
            pltpu.VMEM((2, groups, rows, N), BF16),
            pltpu.VMEM((2, groups, rows, N), BF16),
            pltpu.VMEM((2, groups, rows, N), F32),
            pltpu.VMEM((team, groups, rows, N), BF16),
            pltpu.VMEM((team, groups, rows, N), BF16),
            pltpu.VMEM((1, 128), F32),
            pltpu.VMEM((ndev, 1, 128), F32),
            *weight_sems,
            dma((n,)), dma((n,)), dma((n,)), dma((n,)), dma((blocks + 1,)), dma(()), dma(()),
            *first_sems, *swap_sems, *second_sems, *rank_sems, dma((8,)), dma((2, groups)),
        ],
        compiler_params=pltpu.CompilerParams(
            collective_id=3, has_side_effects=True, vmem_limit_bytes=62 * 2**20
        ),
        name="fused",
    )(
        tokens, w_in, w_dt.T, conv_w, conv_b, dt_bias, a_log, d_skip, norm_gain,
    )


def hand_over_kernel(
    mixed, entry, mixed_out, entry_out, held_m, held_e, wide_e, in_sems, out_sems
):
    parts = in_sems.shape[1]
    loads, stores = [], []
    arrays = ((entry, held_e, wide_e, entry_out), (mixed, held_m, held_m, mixed_out))
    for i, (source, held, ready, target) in enumerate(arrays):
        rows = source.shape[0] // parts
        for k in range(parts):
            at = pl.ds(k * rows, rows)
            loads.append(pltpu.make_async_copy(source.at[at], held.at[at], in_sems.at[i, k]))
            stores.append(pltpu.make_async_copy(ready.at[at], target.at[at], out_sems.at[i, k]))
    for load in loads:
        load.start()
    rows = entry.shape[0] // parts
    for k, (load, store) in enumerate(zip(loads, stores)):
        load.wait()
        if k < parts:
            at = slice(k * rows, (k + 1) * rows)
            wide_e[at] = held_e[at].astype(F32)
        store.start()
    for store in stores:
        store.wait()


def hand_over(mixed, entry):
    whole = pl.BlockSpec(memory_space=pl.ANY)
    sems = pltpu.SemaphoreType.DMA((2, 4))
    return pl.pallas_call(
        hand_over_kernel,
        out_shape=(
            jax.ShapeDtypeStruct(mixed.shape, mixed.dtype),
            jax.ShapeDtypeStruct(entry.shape, F32),
        ),
        in_specs=[whole, whole],
        out_specs=(whole, whole),
        scratch_shapes=[
            pltpu.VMEM(mixed.shape, mixed.dtype), pltpu.VMEM(entry.shape, entry.dtype),
            pltpu.VMEM(entry.shape, F32), sems, sems,
        ],
        name="hand_over",
    )(mixed, entry)


def per_device(tokens, w_in, w_dt, conv_w, conv_b, dt_bias, a_log, d_skip, norm_gain):
    own_rows = tokens.reshape(tokens.shape[1], tokens.shape[2])
    row_count = own_rows.shape[0]
    if w_in.shape[0] % 512 == 0 and lax.axis_size("inner") == 8:
        mixed, entry = run_fused(
            own_rows, w_in, w_dt, conv_w, conv_b, dt_bias, a_log, d_skip, norm_gain
        )
        mixed, entry = hand_over(mixed, entry)
    else:
        projected, tail, dt_raw = run_project(own_rows, w_in, w_dt)
        mixed, entry = run_scan(
            projected, tail, dt_raw, conv_w, conv_b, dt_bias, a_log, d_skip, norm_gain
        )
    return (
        mixed.reshape(1, row_count, HP),
        entry.reshape(1, 1, HEADS, P_SIZE, N),
    )


def solution(mesh):
    placed = (
        P(("grp", "outer"), "inner", None),
        P("inner", None),
        P("inner", None),
        P(), P(), P(), P(), P(), P(),
    )
    return jax.shard_map(
        per_device,
        mesh=mesh,
        in_specs=placed,
        out_specs=(
            P(("grp", "outer"), "inner", None),
            P(("grp", "outer"), "inner", None, None, None),
        ),
        check_vma=False,
    )
```
